32 devices in a mesh: lat: 8 (over z, y), lon: 4 (over x, core).
Axes of the slice: x: 2, y: 2, z: 4, core: 2. Of those that a mesh axis runs over, the one named last changes fastest.
Arguments:
- right_side: float32 [480, 4, 4096], P('lat', None, 'lon'), may hold values from -6 to 6
- lon_coef: float32 [480], replicated, may hold values from 5 to 500
- lat_coef: float32 [479], replicated, may hold values from 200 to 2000
- level_scale: float32 [4], replicated, may hold values from 0.5 to 4
Outputs:
- solution_grid: float32 [480, 4, 4096], P('lat', None, 'lon')
The draws below stay inside these ranges and needn't reach their ends.
All inputs are finite; a program needn't handle non-finite values.
Results may differ from the reference program's by a relative error of at most 0.0003.
Values sent between devices are 32-bit elements; how exact they have to be, the bound alone decides.
No kernel may reach another device: no remote copies, remote signals or barrier semaphores. Data moves between devices by JAX's collectives and lax.ppermute only.
A program may use at most 128 MiB of HBM per device.

```python
import math
import jax
import jax.numpy as jnp
from jax import lax

NLON = 4096
LAT_DEV = 60
LEVELS = 4
OV = 8
ITERS = 2
NLAT = 480
N_LAT = 8


def level_of(stream_key, shape, shards, low, top_value):
    def one(position, parts):
        steps = jax.random.uniform(jax.random.fold_in(jax.random.fold_in(stream_key, 6), position), (parts,), jnp.float32, low / len(shards), top_value / len(shards))
        return jnp.repeat(jnp.exp(steps), shape[position] // parts).reshape((-1,) + (1,) * (len(shape) - position - 1))

    loudness = one(*shards[0])
    for cut in shards[1:]:
        loudness = loudness * one(*cut)
    return loudness


def gaussian(stream_key, shape, width, reach, cuts=(), held_as=jnp.bfloat16):
    factor_of = level_of(stream_key, shape, cuts, -0.22, 0.18) if cuts else 1.0
    array = jax.random.normal(stream_key, shape, jnp.float32) * width * factor_of
    return jnp.minimum(jnp.maximum(array, -reach), reach).astype(held_as)


def setup_inputs(seed: int = 0) -> dict:
    arg_keys = jax.random.split(jax.random.key(seed), 5)
    right_side = gaussian(arg_keys[0], (NLAT, LEVELS, NLON), 1.0, 6.0, ((0, 8), (2, 4)), jnp.float32)
    lon_coef = jnp.clip(jnp.exp(jax.random.uniform(arg_keys[1], (NLAT,), jnp.float32, math.log(5.0), math.log(500.0))), 5.0, 500.0)
    lat_coef = jnp.clip(jnp.exp(jax.random.uniform(arg_keys[2], (NLAT - 1,), jnp.float32, math.log(200.0), math.log(2000.0))), 200.0, 2000.0)
    level_scale = jnp.clip(jnp.exp(jax.random.uniform(arg_keys[3], (LEVELS,), jnp.float32, math.log(0.5), math.log(4.0))), 0.5, 4.0)
    return dict(right_side=right_side, lon_coef=lon_coef, lat_coef=lat_coef, level_scale=level_scale)


TWO_PI = 2.0 * math.pi


def forward_transform(grid_field):
    middle = NLON // 2
    coeffs = jnp.fft.rfft(grid_field, axis=2)
    return jnp.concatenate([coeffs.real, coeffs.imag[:, :, 1:middle]], axis=2).astype(jnp.float32)


def inverse_transform(spectral):
    middle = NLON // 2
    zero_col = jnp.zeros(spectral.shape[:2] + (1,), spectral.dtype)
    real_part = spectral[:, :, :middle + 1]
    imag_part = jnp.concatenate([zero_col, spectral[:, :, middle + 1:], zero_col], axis=2)
    return jnp.fft.irfft(real_part + 1j * imag_part, n=NLON, axis=2).astype(jnp.float32)


def eigenvalues():
    coef_index = jnp.arange(NLON, dtype=jnp.int32)
    middle = NLON // 2
    wavenumber = jnp.where(coef_index <= middle, coef_index, coef_index - middle)
    return 2.0 - 2.0 * jnp.cos(wavenumber.astype(jnp.float32) * (TWO_PI / NLON))


def band_operator(lon_window, couple_low, couple_high, level_scale, eigenvalue):
    level_factor = level_scale[None, :, None]
    main_diag = 1.0 + level_factor * (lon_window[:, None, None] * eigenvalue[None, None, :]
                                      + couple_low[:, None, None] + couple_high[:, None, None])
    sub_diag = jnp.broadcast_to(-level_factor * couple_low[:, None, None], main_diag.shape)
    super_diag = jnp.broadcast_to(-level_factor * couple_high[:, None, None], main_diag.shape)
    return main_diag, sub_diag, super_diag


def band_solve(sub_diag, main_diag, super_diag, right_part):
    zero_state = jnp.zeros(right_part.shape[1:], jnp.float32)

    def eliminate(state, row_values):
        ratio_prev, value_prev = state
        below_coef, middle_coef, above_coef, right_value = row_values
        divisor = middle_coef - below_coef * ratio_prev
        ratio_next = above_coef / divisor
        value_next = (right_value - below_coef * value_prev) / divisor
        return (ratio_next, value_next), (ratio_next, value_next)

    _, (ratios, values) = lax.scan(eliminate, (zero_state, zero_state), (sub_diag, main_diag, super_diag, right_part))

    def substitute(following, row_values):
        ratio_here, value_here = row_values
        current = value_here - ratio_here * following
        return current, current

    _, result_rows = lax.scan(substitute, zero_state, (ratios, values), reverse=True)
    return result_rows


def reference(right_side, lon_coef, lat_coef, level_scale):
    spectral = forward_transform(right_side)
    eigenvalue = eigenvalues()
    extent = LAT_DEV + 2 * OV
    lon_padded = jnp.pad(lon_coef, (OV, OV))
    lat_padded = jnp.pad(lat_coef, (OV + 1, OV + 2))
    full_main, full_sub, full_super = band_operator(lon_coef, lat_padded[OV:OV + NLAT],
                                                    lat_padded[OV + 1:OV + 1 + NLAT], level_scale, eigenvalue)
    iterate = jnp.zeros_like(spectral)
    for sweep_index in range(ITERS):
        padded = jnp.pad(iterate, ((1, 1), (0, 0), (0, 0)))
        residual = spectral - (full_main * iterate + full_sub * padded[:-2] + full_super * padded[2:])
        residual_padded = jnp.pad(residual, ((OV, OV), (0, 0), (0, 0)))

        def solve_band(band_index):
            row_first = (band_index * LAT_DEV).astype(jnp.int32)
            lon_window = lax.dynamic_slice_in_dim(lon_padded, row_first, extent)
            couple_low = lax.dynamic_slice_in_dim(lat_padded, row_first, extent)
            couple_high = lax.dynamic_slice_in_dim(lat_padded, row_first + 1, extent)
            main_diag, sub_diag, super_diag = band_operator(lon_window, couple_low, couple_high, level_scale, eigenvalue)
            right_part = lax.dynamic_slice_in_dim(residual_padded, row_first, extent, 0)
            correction = band_solve(sub_diag, main_diag, super_diag, right_part)
            return correction[OV:OV + LAT_DEV]

        corrections = lax.map(solve_band, jnp.arange(N_LAT, dtype=jnp.int32))
        iterate = iterate + corrections.reshape(NLAT, LEVELS, NLON)
    return inverse_transform(iterate)
```

```python
import functools
import math

import jax
import jax.numpy as jnp
import numpy as np
from jax import lax
from jax.experimental import pallas as pl
from jax.experimental.pallas import tpu as pltpu
from jax.sharding import PartitionSpec as P

NLON = 4096
OV = 8
N1 = 32
N2 = 128
GROUPS = 16
BLOCK = 8

VMEM = pltpu.VMEM
SMEM = pltpu.SMEM


def numpy_split(table):
    import ml_dtypes

    table = np.asarray(table, np.float32)
    high = table.astype(ml_dtypes.bfloat16)
    low = (table - high.astype(np.float32)).astype(ml_dtypes.bfloat16)
    return high, low


def tables():
    j1 = np.arange(N1)
    j2 = np.arange(N2)
    k2 = np.arange(N2)
    digit = np.arange(GROUPS)
    small = np.zeros((N1, N1))
    small[:GROUPS] = np.cos(2 * np.pi * np.outer(digit, j1) / N1)
    small[GROUPS] = np.cos(np.pi * j1)
    small[GROUPS + 1 :] = -np.sin(2 * np.pi * np.outer(digit[1:], j1) / N1)
    first = np.kron(np.eye(BLOCK), small)
    angle = 2 * np.pi * np.outer(digit, j2) / NLON
    turn_cos = np.cos(angle)
    turn_sin = np.sin(angle)
    phase = 2 * np.pi * (np.outer(j2, k2) % N2) / N2
    cosine, sine = np.cos(phase), np.sin(phase)
    second = np.block([[cosine, -sine], [sine, cosine]])
    special = np.zeros((2 * N2, 2 * N2))
    half = N2 // 2
    special[:N2, : half + 1] = np.cos(2 * np.pi * np.outer(j2, np.arange(half + 1)) / N2)
    special[:N2, half + 1 : N2] = -np.sin(2 * np.pi * np.outer(j2, np.arange(1, half)) / N2)
    odd = 2 * np.pi * np.outer(j2, 1 + 2 * np.arange(half)) / (2 * N2)
    special[N2:, N2 : N2 + half] = np.cos(odd)
    special[N2:, N2 + half :] = -np.sin(odd)
    weight = np.full(2 * N2, 2.0 / NLON)
    weight[0] = 1.0 / NLON
    weight[half] = 1.0 / NLON
    second_back = second.T * (2.0 / NLON)
    special_back = weight[:, None] * special.T
    wave = np.zeros((GROUPS, 2 * N2))
    wave[:, :N2] = digit[:, None] + N1 * k2[None, :]
    wave[:, N2:] = wave[:, :N2]
    lane = np.arange(N2)
    wave[0, :N2] = np.where(lane <= half, N1 * lane, N1 * (lane - half))
    wave[0, N2:] = 16 + N1 * (lane % half)
    eigen = 2.0 - 2.0 * np.cos(2 * np.pi * wave / NLON)
    pair = lambda t: np.concatenate(numpy_split(t), axis=0)
    return dict(
        first=pair(first),
        first_back=pair(first.T),
        second=pair(second),
        second_back=pair(second_back),
        special=pair(special),
        special_back=pair(special_back),
        turn=np.concatenate([turn_cos, turn_sin], axis=0).astype(np.float32),
        eigen=np.stack([eigen[:, :N2], eigen[:, N2:]]).astype(np.float32),
    )


def halves(value):
    high = value.astype(jnp.bfloat16)
    low = (value - high.astype(jnp.float32)).astype(jnp.bfloat16)
    return high, low


def dot(a, b):
    return lax.dot_general(a, b, (((1,), (0,)), ((), ())), preferred_element_type=jnp.float32)


def product_right(value, table_ref):
    size = table_ref.shape[0] // 2
    high, low = halves(value)
    table_high = table_ref[:size, :]
    return dot(high, table_high) + dot(low, table_high) + dot(high, table_ref[size:, :])


def product_left(table_ref, value):
    size = table_ref.shape[0] // 2
    high, low = halves(value)
    both = dot(table_ref[...], high)
    return both[:size] + both[size:] + dot(table_ref[:size, :], low)


def lanes_apart(value, rows):
    real = value[:, :N2].reshape(rows, GROUPS, N2)
    imag = value[:, N2:].reshape(rows, GROUPS, N2)
    return jnp.concatenate([real, imag], axis=1).reshape(rows * 2 * GROUPS, N2)


def lanes_together(value, rows):
    both = value.reshape(rows, 2 * GROUPS, N2)
    return jnp.concatenate([both[:, :GROUPS], both[:, GROUPS:]], axis=2).reshape(rows * GROUPS, 2 * N2)


def load_zeroth(ref, rows):
    return jnp.concatenate(
        [ref[pl.ds(0, rows, stride=2 * GROUPS), :], ref[pl.ds(GROUPS, rows, stride=2 * GROUPS), :]], axis=1
    )


def store_zeroth(ref, rows, value):
    ref[pl.ds(0, rows, stride=2 * GROUPS), :] = value[:, :N2]
    ref[pl.ds(GROUPS, rows, stride=2 * GROUPS), :] = value[:, N2:]


def forward_rows(points_ref, rows, first_ref, turn_ref, second_ref, special_ref, mid_ref, out_ref):
    padded = points_ref.shape[0]
    turn_cos = turn_ref[:GROUPS, :][None]
    turn_sin = turn_ref[GROUPS:, :][None]
    for pair in range(padded // (2 * BLOCK)):
        base = pair * 2 * BLOCK
        left = points_ref[base : base + BLOCK].reshape(BLOCK * N1, N2)
        right = points_ref[base + BLOCK : base + 2 * BLOCK].reshape(BLOCK * N1, N2)
        value = product_left(first_ref, jnp.concatenate([left, right], axis=1))
        for side in range(2):
            digits = value[:, side * N2 : (side + 1) * N2].reshape(BLOCK, N1, N2)
            real, imag = digits[:, :GROUPS], digits[:, GROUPS:]
            turned = jnp.concatenate(
                [real * turn_cos + imag * turn_sin, imag * turn_cos - real * turn_sin], axis=1
            )
            at = (base + side * BLOCK) * N1
            mid_ref[at : at + BLOCK * N1, :] = turned.reshape(BLOCK * N1, N2)
    result = product_right(lanes_together(mid_ref[...], padded), second_ref)
    out_ref[...] = lanes_apart(result, padded)[: rows * N1]
    store_zeroth(out_ref, rows, product_right(load_zeroth(mid_ref, padded), special_ref)[:rows])


def backward_rows(spec_ref, rows, first_ref, turn_ref, second_ref, special_ref, mid_ref, out_ref):
    padded = out_ref.shape[0]
    turn_cos = turn_ref[:GROUPS, :][None]
    turn_sin = turn_ref[GROUPS:, :][None]
    result = product_right(lanes_together(spec_ref[...], rows), second_ref)
    mid_ref[: rows * N1, :] = lanes_apart(result, rows)
    if padded > rows:
        mid_ref[rows * N1 :, :] = jnp.zeros(((padded - rows) * N1, N2), jnp.float32)
    store_zeroth(mid_ref, rows, product_right(load_zeroth(spec_ref, rows), special_ref))
    for pair in range(padded // (2 * BLOCK)):
        base = pair * 2 * BLOCK
        sides = []
        for side in range(2):
            at = (base + side * BLOCK) * N1
            both = mid_ref[at : at + BLOCK * N1, :].reshape(BLOCK, N1, N2)
            real, imag = both[:, :GROUPS], both[:, GROUPS:]
            digits = jnp.concatenate(
                [real * turn_cos - imag * turn_sin, imag * turn_cos + real * turn_sin], axis=1
            )
            sides.append(digits.reshape(BLOCK * N1, N2))
        value = product_left(first_ref, jnp.concatenate(sides, axis=1))
        out_ref[base : base + BLOCK] = value[:, :N2].reshape(BLOCK, N1, N2)
        out_ref[base + BLOCK : base + 2 * BLOCK] = value[:, N2:].reshape(BLOCK, N1, N2)


def factor_kernel(rows, lon_ref, couple_ref, eigen_ref, ratio_ref, inverse_ref, edge_ref):
    eigen = eigen_ref[...]
    groups = eigen.shape[0]
    half = rows // 2
    last = rows + 2 * OV - 1

    def plain(e):
        return 1.0 + lon_ref[e] * eigen

    def put(ref, index, value):
        ref[index * groups : (index + 1) * groups, :] = value

    def chain(start, stop, step, into):
        excess = inverse = None
        for e in range(start, stop + step, step):
            before = couple_ref[e] if step > 0 else couple_ref[e + 1]
            after = couple_ref[e + 1] if step > 0 else couple_ref[e]
            if inverse is None:
                ratio = None
                excess = plain(e) + before
            else:
                ratio = before * inverse
                excess = plain(e) + ratio * excess
            divisor = after + excess
            inverse = 1.0 / divisor
            into(e, ratio, inverse, excess, divisor)

    kept = {}

    def top(e, ratio, inverse, excess, divisor):
        if e == OV - 1:
            put(edge_ref, 0, inverse)
        if e >= OV:
            put(ratio_ref, e - OV, ratio)
            put(inverse_ref, e - OV, inverse)
        if e == OV + half - 1:
            kept["top"] = excess, divisor

    def bottom(e, ratio, inverse, excess, divisor):
        if e == OV + rows:
            put(edge_ref, 1, inverse)
        if e < OV + rows:
            put(ratio_ref, e - OV, ratio)
            put(inverse_ref, e - OV, inverse)
        if e == OV + half:
            kept["bottom"] = excess, divisor

    def next_band(e, ratio, inverse, excess, divisor):
        if ratio is not None:
            put(edge_ref, 7 + e - rows - 1, ratio)
        if e == OV + rows - 1:
            put(edge_ref, 5, inverse)

    def previous_band(e, ratio, inverse, excess, divisor):
        if ratio is not None:
            put(edge_ref, 14 + e - OV, ratio)
        if e == OV:
            put(edge_ref, 6, inverse)

    chain(rows, OV + rows - 1, 1, next_band)
    chain(2 * OV - 1, OV, -1, previous_band)
    chain(0, OV + half - 1, 1, top)
    chain(last, OV + half, -1, bottom)
    excess_top, divisor_top = kept["top"]
    excess_bottom, divisor_bottom = kept["bottom"]
    between = couple_ref[OV + half]
    inverse = 1.0 / (between * (excess_top + excess_bottom) + excess_top * excess_bottom)
    put(edge_ref, 2, divisor_bottom * inverse)
    put(edge_ref, 3, divisor_top * inverse)
    put(edge_ref, 4, between * inverse)


def edge_sums(low_rows, high_rows, edge_ref, groups):
    def edge(index):
        return edge_ref[index * groups : (index + 1) * groups, :]

    top = high_rows(0)
    for i in range(1, OV):
        top = high_rows(i) + edge(7 + i - 1) * top
    bottom = low_rows(OV - 1)
    for i in range(OV - 2, -1, -1):
        bottom = low_rows(i) + edge(14 + i) * bottom
    return top, bottom


def swap_out(parity, up, down, even_ref, odd_ref):
    is_even = parity == 0
    even_ref[...] = jnp.where(is_even, up, down)
    odd_ref[...] = jnp.where(is_even, down, up)


def swap_in(parity, even, odd):
    is_even = parity == 0
    return jnp.where(is_even, odd, even), jnp.where(is_even, even, odd)


def solve_first(rows, groups, right_side_row, from_low, from_high, ratio_ref, inverse_ref, edge_ref, out_ref):
    half = rows // 2

    def at(ref, index):
        return ref[index * groups : (index + 1) * groups, :]

    def put(index, value):
        out_ref[index * groups : (index + 1) * groups, :] = value

    low, high = from_low, from_high
    for i in range(half):
        j = rows - 1 - i
        low = right_side_row(i) + at(ratio_ref, i) * low
        high = right_side_row(j) + at(ratio_ref, j) * high
        put(i, low)
        put(j, high)
    meet(rows, groups, low, high, ratio_ref, inverse_ref, edge_ref, at, lambda i: at(out_ref, i), put)


def meet(rows, groups, low, high, ratio_ref, inverse_ref, edge_ref, at, value, put):
    half = rows // 2
    between = at(edge_ref, 4)
    x_low = at(edge_ref, 2) * low + between * high
    x_high = at(edge_ref, 3) * high + between * low
    put(half - 1, x_low)
    put(half, x_high)
    for i in range(half - 2, -1, -1):
        j = rows - 1 - i
        x_low = value(i) * at(inverse_ref, i) + at(ratio_ref, i + 1) * x_low
        x_high = value(j) * at(inverse_ref, j) + at(ratio_ref, j - 1) * x_high
        put(i, x_low)
        put(j, x_high)


def solve_second(
    rows, groups, couple_low, couple_high, own_top, own_bottom, got_top, got_bottom, sent_top, sent_bottom,
    from_low, from_high, ratio_ref, inverse_ref, edge_ref, first_ref, out_ref, mid_ref,
):
    half = rows // 2

    def at(ref, index):
        return ref[index * groups : (index + 1) * groups, :]

    beyond_low = (got_top + couple_low * own_top) * at(edge_ref, 0)
    beyond_high = (got_bottom + couple_high * own_bottom) * at(edge_ref, 1)
    theirs_low = (sent_bottom + couple_low * from_low) * at(edge_ref, 6)
    theirs_high = (sent_top + couple_high * from_high) * at(edge_ref, 5)
    low = couple_low * (own_top - theirs_low)
    high = couple_high * (own_bottom - theirs_high)
    for i in range(half):
        j = rows - 1 - i
        low = at(ratio_ref, i) * low
        high = at(ratio_ref, j) * high
        if i == 0:
            low = low + couple_low * (from_low - beyond_low)
            high = high + couple_high * (from_high - beyond_high)
        mid_ref[i * groups : (i + 1) * groups, :] = low
        mid_ref[j * groups : (j + 1) * groups, :] = high

    def put(index, value):
        rows_at = slice(index * groups, (index + 1) * groups)
        out_ref[rows_at, :] = first_ref[rows_at, :] + value

    meet(rows, groups, low, high, ratio_ref, inverse_ref, edge_ref, at, lambda i: at(mid_ref, i), put)


def call(body, outs, ins, spaces, scratch, flops, name):
    nbytes = sum(x.size * x.dtype.itemsize for x in ins) + sum(4 * math.prod(s) for s in outs)
    out = pl.pallas_call(
        body,
        out_shape=[jax.ShapeDtypeStruct(s, jnp.float32) for s in outs],
        in_specs=[pl.BlockSpec(memory_space=s) for s in spaces],
        out_specs=[pl.BlockSpec(memory_space=VMEM) for _ in outs],
        scratch_shapes=scratch,
        compiler_params=pltpu.CompilerParams(vmem_limit_bytes=48 << 20),
        cost_estimate=pl.CostEstimate(flops=flops, bytes_accessed=nbytes, transcendentals=0),
        name=name,
    )(*ins)
    return out


def pad_rows(rows):
    return -(-rows // (2 * BLOCK)) * 2 * BLOCK


def swap(value_even, value_odd):
    count = lax.axis_size("lat")
    even = [(i, i ^ 1) for i in range(count) if (i ^ 1) < count]
    odd = [(i, ((i + 1) ^ 1) - 1) for i in range(1, count) if ((i + 1) ^ 1) - 1 < count]
    return lax.ppermute(value_even, "lat", even), lax.ppermute(value_odd, "lat", odd)


def on_device(right_side, lon_coef, lat_coef, level_scale):
    rows, levels, lon_count = right_side.shape
    lon_size = lax.axis_size("lon")
    assert lon_size % levels == 0 and N1 % lon_size == 0 and rows % 2 == 0
    sharers = lon_size // levels
    groups = 2 * GROUPS // sharers
    part_rows = rows // sharers
    digits = N1 // lon_size
    const = {k: jnp.asarray(v) for k, v in tables().items()}
    lon_at = lax.axis_index("lon")
    lat_at = lax.axis_index("lat")
    level = lon_at // sharers
    parity = (lat_at % 2).astype(jnp.int32)
    row_first = lat_at * rows
    extent = rows + 2 * OV
    scale = lax.dynamic_index_in_dim(level_scale, level, 0, False)
    lon_window = scale * lax.dynamic_slice_in_dim(jnp.pad(lon_coef, (OV, OV)), row_first, extent)
    couple = scale * lax.dynamic_slice_in_dim(
        jnp.pad(lat_coef, (OV + 1, OV + 2)), row_first, extent + 1
    )
    eigen = const["eigen"]
    if sharers > 1:
        eigen = lax.dynamic_slice_in_dim(eigen, (lon_at % sharers) * (groups // 2), groups // 2, axis=1)
    eigen = eigen.reshape(groups, N2)
    wide = N2
    block = (rows * groups, wide)
    row = (groups, wide)
    ratio, inverse, edge = call(
        functools.partial(factor_kernel, rows),
        [block, block, (21 * groups, wide)],
        [lon_window, couple, eigen],
        [SMEM, SMEM, VMEM],
        [],
        rows * groups * wide * 20,
        "factor",
    )
    if sharers == 1:
        pieces = exchange_levels(right_side, lon_at)
    else:
        pieces = None
        send = right_side.reshape(sharers, part_rows, levels, lon_count).transpose(2, 0, 1, 3)
        send = send.reshape(lon_size, part_rows, digits, N2)
        got = lax.all_to_all(send, "lon", 0, 0, tiled=True)
        points = got.transpose(1, 0, 2, 3).reshape(part_rows, N1, N2)
    if sharers == 1:
        points = place_pieces(pieces, lon_at, digits)
    padded = pad_rows(part_rows)

    def transform(points_ref, first_ref, turn_ref, second_ref, special_ref, out_ref, full_ref, mid_ref):
        full_ref[:part_rows] = points_ref[...]
        if padded > part_rows:
            full_ref[part_rows:] = jnp.zeros((padded - part_rows, N1, N2), jnp.float32)
        forward_rows(full_ref, part_rows, first_ref, turn_ref, second_ref, special_ref, mid_ref, out_ref)

    (spectral,) = call(
        transform,
        [(part_rows * N1, wide)],
        [points, const["first"], const["turn"], const["second"], const["special"]],
        [VMEM] * 5,
        [pltpu.VMEM((padded, N1, N2), jnp.float32), pltpu.VMEM((padded * N1, wide), jnp.float32)],
        part_rows * NLON * 256 * 4,
        "transform",
    )
    if sharers > 1:
        spectral = to_coefs(spectral, sharers, part_rows, groups)
    parity_arg = parity.reshape(1)

    def edges(parity_ref, spec_ref, edge_ref, top_ref, bottom_ref, even_ref, odd_ref):
        def spec_row(i):
            return spec_ref[i * groups : (i + 1) * groups, :]

        top, bottom = edge_sums(spec_row, lambda i: spec_row(rows - OV + i), edge_ref, groups)
        top_ref[...] = top
        bottom_ref[...] = bottom
        swap_out(parity_ref[0], top, bottom, even_ref, odd_ref)

    sent_top, sent_bottom, even, odd = call(
        edges, [row] * 4, [parity_arg, spectral, edge], [SMEM, VMEM, VMEM], [], groups * wide * 32, "edges"
    )
    even, odd = swap(even, odd)

    def first(parity_ref, spec_ref, even_ref, odd_ref, ratio_ref, inverse_ref, edge_ref, out_ref, e_ref, o_ref):
        low, high = swap_in(parity_ref[0], even_ref[...], odd_ref[...])
        solve_first(
            rows, groups, lambda i: spec_ref[i * groups : (i + 1) * groups, :], low, high,
            ratio_ref, inverse_ref, edge_ref, out_ref,
        )
        swap_out(parity_ref[0], out_ref[(rows - 1) * groups :, :], out_ref[:groups, :], e_ref, o_ref)

    iterate, even2, odd2 = call(
        first, [block, row, row], [parity_arg, spectral, even, odd, ratio, inverse, edge],
        [SMEM] + [VMEM] * 6, [], rows * groups * wide * 8, "first_solve",
    )
    even2, odd2 = swap(even2, odd2)

    def second(
        parity_ref, couple_ref, first_ref, even_ref, odd_ref, even2_ref, odd2_ref, top_ref, bottom_ref,
        ratio_ref, inverse_ref, edge_ref, out_ref, mid_ref,
    ):
        got_top, got_bottom = swap_in(parity_ref[0], even_ref[...], odd_ref[...])
        low, high = swap_in(parity_ref[0], even2_ref[...], odd2_ref[...])
        solve_second(
            rows, groups, couple_ref[OV], couple_ref[OV + rows],
            first_ref[:groups, :], first_ref[(rows - 1) * groups :, :],
            got_top, got_bottom, top_ref[...], bottom_ref[...], low, high,
            ratio_ref, inverse_ref, edge_ref, first_ref, out_ref, mid_ref,
        )

    (iterate,) = call(
        second, [block],
        [parity_arg, couple, iterate, even, odd, even2, odd2, sent_top, sent_bottom, ratio, inverse, edge],
        [SMEM, SMEM] + [VMEM] * 10, [pltpu.VMEM(block, jnp.float32)], rows * groups * wide * 8, "second_solve",
    )
    if sharers > 1:
        iterate = to_rows(iterate, sharers, part_rows, groups)

    def back(spec_ref, first_ref, turn_ref, second_ref, special_ref, out_ref, mid_ref, full_ref):
        backward_rows(spec_ref, part_rows, first_ref, turn_ref, second_ref, special_ref, mid_ref, full_ref)
        out_ref[...] = full_ref[:part_rows]

    (points,) = call(
        back,
        [(part_rows, N1, N2)],
        [iterate, const["first_back"], const["turn"], const["second_back"], const["special_back"]],
        [VMEM] * 5,
        [pltpu.VMEM((padded * N1, wide), jnp.float32), pltpu.VMEM((padded, N1, N2), jnp.float32)],
        part_rows * NLON * 256 * 4,
        "back_transform",
    )
    if sharers == 1:
        return return_levels(points, lon_at, digits, right_side.shape)
    send = points.reshape(part_rows, lon_size, digits, N2).transpose(1, 0, 2, 3)
    got = lax.all_to_all(send, "lon", 0, 0, tiled=True)
    got = got.reshape(levels, sharers, part_rows, lon_count).transpose(1, 2, 0, 3)
    return got.reshape(rows, levels, lon_count)


def exchange_levels(right_side, lon_at):
    rows, levels, lon_count = right_side.shape
    size = levels
    pieces = []
    for mask in range(size):
        piece = lax.dynamic_index_in_dim(right_side, lon_at ^ mask, 1, False)
        piece = piece.reshape(rows, lon_count // N2, N2)
        if mask:
            piece = lax.ppermute(piece, "lon", [(d, d ^ mask) for d in range(size)])
        pieces.append(piece)
    return pieces


def place_pieces(pieces, lon_at, digits):
    stacked = jnp.stack(pieces, axis=1)
    order = lon_at ^ jnp.arange(len(pieces))
    stacked = jnp.take(stacked, order, axis=1)
    return stacked.reshape(stacked.shape[0], N1, N2)


def return_levels(points, lon_at, digits, shape):
    rows, levels, lon_count = shape
    size = levels
    parts = points.reshape(rows, size, digits, N2)
    pieces = []
    for mask in range(size):
        piece = lax.dynamic_index_in_dim(parts, lon_at ^ mask, 1, False)
        if mask:
            piece = lax.ppermute(piece, "lon", [(d, d ^ mask) for d in range(size)])
        pieces.append(piece.reshape(rows, lon_count))
    stacked = jnp.stack(pieces, axis=1)
    return jnp.take(stacked, lon_at ^ jnp.arange(size), axis=1)


def level_groups(sharers):
    size = lax.axis_size("lon")
    return [[first + i for i in range(sharers)] for first in range(0, size, sharers)]


def to_coefs(spectral, sharers, part_rows, groups):
    send = spectral.reshape(part_rows, 2, sharers, groups // 2, N2).transpose(2, 0, 1, 3, 4)
    got = lax.all_to_all(
        send, "lon", 0, 0, tiled=True, axis_index_groups=level_groups(sharers)
    )
    return got.reshape(sharers * part_rows * groups, N2)


def to_rows(values, sharers, part_rows, groups):
    send = values.reshape(sharers, part_rows, 2, groups // 2, N2)
    got = lax.all_to_all(
        send, "lon", 0, 0, tiled=True, axis_index_groups=level_groups(sharers)
    )
    return got.transpose(1, 2, 0, 3, 4).reshape(part_rows * N1, N2)


def solution(mesh):
    return jax.shard_map(
        on_device,
        mesh=mesh,
        in_specs=(P("lat", None, "lon"), P(), P(), P()),
        out_specs=P("lat", None, "lon"),
        check_vma=False,
    )
```

```python
import functools
import math

import jax
import jax.numpy as jnp
import numpy as np
from jax import lax
from jax.experimental import pallas as pl
from jax.experimental.pallas import tpu as pltpu
from jax.sharding import PartitionSpec as P

NLON = 4096
OV = 8
N1 = 32
N2 = 128
GROUPS = 16
BLOCK = 8

VMEM = pltpu.VMEM
SMEM = pltpu.SMEM


def numpy_split(table):
    import ml_dtypes

    table = np.asarray(table, np.float32)
    high = table.astype(ml_dtypes.bfloat16)
    low = (table - high.astype(np.float32)).astype(ml_dtypes.bfloat16)
    return high, low


def tables():
    j1 = np.arange(N1)
    j2 = np.arange(N2)
    k2 = np.arange(N2)
    digit = np.arange(GROUPS)
    small = np.zeros((N1, N1))
    small[:GROUPS] = np.cos(2 * np.pi * np.outer(digit, j1) / N1)
    small[GROUPS] = np.cos(np.pi * j1)
    small[GROUPS + 1 :] = -np.sin(2 * np.pi * np.outer(digit[1:], j1) / N1)
    first = np.kron(np.eye(BLOCK), small)
    angle = 2 * np.pi * np.outer(digit, j2) / NLON
    turn_cos = np.cos(angle)
    turn_sin = np.sin(angle)
    phase = 2 * np.pi * (np.outer(j2, k2) % N2) / N2
    cosine, sine = np.cos(phase), np.sin(phase)
    second = np.block([[cosine, -sine], [sine, cosine]])
    special = np.zeros((2 * N2, 2 * N2))
    half = N2 // 2
    special[:N2, : half + 1] = np.cos(2 * np.pi * np.outer(j2, np.arange(half + 1)) / N2)
    special[:N2, half + 1 : N2] = -np.sin(2 * np.pi * np.outer(j2, np.arange(1, half)) / N2)
    odd = 2 * np.pi * np.outer(j2, 1 + 2 * np.arange(half)) / (2 * N2)
    special[N2:, N2 : N2 + half] = np.cos(odd)
    special[N2:, N2 + half :] = -np.sin(odd)
    weight = np.full(2 * N2, 2.0 / NLON)
    weight[0] = 1.0 / NLON
    weight[half] = 1.0 / NLON
    second_back = second.T * (2.0 / NLON)
    special_back = weight[:, None] * special.T
    wave = np.zeros((GROUPS, 2 * N2))
    wave[:, :N2] = digit[:, None] + N1 * k2[None, :]
    wave[:, N2:] = wave[:, :N2]
    lane = np.arange(N2)
    wave[0, :N2] = np.where(lane <= half, N1 * lane, N1 * (lane - half))
    wave[0, N2:] = 16 + N1 * (lane % half)
    eigen = 2.0 - 2.0 * np.cos(2 * np.pi * wave / NLON)
    pair = lambda t: np.concatenate(numpy_split(t), axis=0)
    return dict(
        first=pair(first),
        first_back=pair(first.T),
        second=pair(second),
        second_back=pair(second_back),
        special=pair(special),
        special_back=pair(special_back),
        turn=np.concatenate([turn_cos, turn_sin], axis=0).astype(np.float32),
        eigen=np.stack([eigen[:, :N2], eigen[:, N2:]]).astype(np.float32),
    )


def halves(value):
    high = value.astype(jnp.bfloat16)
    low = (value - high.astype(jnp.float32)).astype(jnp.bfloat16)
    return high, low


def dot(a, b):
    return lax.dot_general(a, b, (((1,), (0,)), ((), ())), preferred_element_type=jnp.float32)


def product_right(value, table_ref):
    size = table_ref.shape[0] // 2
    high, low = halves(value)
    table_high = table_ref[:size, :]
    return dot(high, table_high) + dot(low, table_high) + dot(high, table_ref[size:, :])


def product_left(table_ref, value):
    size = table_ref.shape[0] // 2
    high, low = halves(value)
    both = dot(table_ref[...], high)
    return both[:size] + both[size:] + dot(table_ref[:size, :], low)


def lanes_apart(value, rows):
    real = value[:, :N2].reshape(rows, GROUPS, N2)
    imag = value[:, N2:].reshape(rows, GROUPS, N2)
    return jnp.concatenate([real, imag], axis=1).reshape(rows * 2 * GROUPS, N2)


def lanes_together(value, rows):
    both = value.reshape(rows, 2 * GROUPS, N2)
    return jnp.concatenate([both[:, :GROUPS], both[:, GROUPS:]], axis=2).reshape(rows * GROUPS, 2 * N2)


def load_zeroth(ref, rows):
    return jnp.concatenate(
        [ref[pl.ds(0, rows, stride=2 * GROUPS), :], ref[pl.ds(GROUPS, rows, stride=2 * GROUPS), :]], axis=1
    )


def store_zeroth(ref, rows, value):
    ref[pl.ds(0, rows, stride=2 * GROUPS), :] = value[:, :N2]
    ref[pl.ds(GROUPS, rows, stride=2 * GROUPS), :] = value[:, N2:]


def forward_rows(points_ref, rows, first_ref, turn_ref, second_ref, special_ref, mid_ref, out_ref):
    padded = points_ref.shape[0]
    turn_cos = turn_ref[:GROUPS, :][None]
    turn_sin = turn_ref[GROUPS:, :][None]
    for pair in range(padded // (2 * BLOCK)):
        base = pair * 2 * BLOCK
        left = points_ref[base : base + BLOCK].reshape(BLOCK * N1, N2)
        right = points_ref[base + BLOCK : base + 2 * BLOCK].reshape(BLOCK * N1, N2)
        value = product_left(first_ref, jnp.concatenate([left, right], axis=1))
        for side in range(2):
            digits = value[:, side * N2 : (side + 1) * N2].reshape(BLOCK, N1, N2)
            real, imag = digits[:, :GROUPS], digits[:, GROUPS:]
            turned = jnp.concatenate(
                [real * turn_cos + imag * turn_sin, imag * turn_cos - real * turn_sin], axis=1
            )
            at = (base + side * BLOCK) * N1
            mid_ref[at : at + BLOCK * N1, :] = turned.reshape(BLOCK * N1, N2)
    result = product_right(lanes_together(mid_ref[...], padded), second_ref)
    out_ref[...] = lanes_apart(result, padded)[: rows * N1]
    store_zeroth(out_ref, rows, product_right(load_zeroth(mid_ref, padded), special_ref)[:rows])


def backward_rows(spec_ref, rows, first_ref, turn_ref, second_ref, special_ref, mid_ref, out_ref):
    padded = out_ref.shape[0]
    turn_cos = turn_ref[:GROUPS, :][None]
    turn_sin = turn_ref[GROUPS:, :][None]
    result = product_right(lanes_together(spec_ref[...], rows), second_ref)
    mid_ref[: rows * N1, :] = lanes_apart(result, rows)
    if padded > rows:
        mid_ref[rows * N1 :, :] = jnp.zeros(((padded - rows) * N1, N2), jnp.float32)
    store_zeroth(mid_ref, rows, product_right(load_zeroth(spec_ref, rows), special_ref))
    for pair in range(padded // (2 * BLOCK)):
        base = pair * 2 * BLOCK
        sides = []
        for side in range(2):
            at = (base + side * BLOCK) * N1
            both = mid_ref[at : at + BLOCK * N1, :].reshape(BLOCK, N1, N2)
            real, imag = both[:, :GROUPS], both[:, GROUPS:]
            digits = jnp.concatenate(
                [real * turn_cos - imag * turn_sin, imag * turn_cos + real * turn_sin], axis=1
            )
            sides.append(digits.reshape(BLOCK * N1, N2))
        value = product_left(first_ref, jnp.concatenate(sides, axis=1))
        out_ref[base : base + BLOCK] = value[:, :N2].reshape(BLOCK, N1, N2)
        out_ref[base + BLOCK : base + 2 * BLOCK] = value[:, N2:].reshape(BLOCK, N1, N2)


def factor_kernel(rows, lon_ref, couple_ref, eigen_ref, ratio_ref, inverse_ref, edge_ref):
    eigen = eigen_ref[...]
    groups = eigen.shape[0]
    half = rows // 2
    last = rows + 2 * OV - 1

    def plain(e):
        return 1.0 + lon_ref[e] * eigen

    def put(ref, index, value):
        ref[index * groups : (index + 1) * groups, :] = value

    def chain(start, stop, step, into):
        excess = inverse = None
        for e in range(start, stop + step, step):
            before = couple_ref[e] if step > 0 else couple_ref[e + 1]
            after = couple_ref[e + 1] if step > 0 else couple_ref[e]
            if inverse is None:
                ratio = None
                excess = plain(e) + before
            else:
                ratio = before * inverse
                excess = plain(e) + ratio * excess
            divisor = after + excess
            inverse = 1.0 / divisor
            into(e, ratio, inverse, excess, divisor)

    kept = {}

    def top(e, ratio, inverse, excess, divisor):
        if e == OV - 1:
            put(edge_ref, 0, inverse)
        if e >= OV:
            put(ratio_ref, e - OV, ratio)
            put(inverse_ref, e - OV, inverse)
        if e == OV + half - 1:
            kept["top"] = excess, divisor

    def bottom(e, ratio, inverse, excess, divisor):
        if e == OV + rows:
            put(edge_ref, 1, inverse)
        if e < OV + rows:
            put(ratio_ref, e - OV, ratio)
            put(inverse_ref, e - OV, inverse)
        if e == OV + half:
            kept["bottom"] = excess, divisor

    def next_band(e, ratio, inverse, excess, divisor):
        if ratio is not None:
            put(edge_ref, 7 + e - rows - 1, ratio)
        if e == OV + rows - 1:
            put(edge_ref, 5, inverse)

    def previous_band(e, ratio, inverse, excess, divisor):
        if ratio is not None:
            put(edge_ref, 14 + e - OV, ratio)
        if e == OV:
            put(edge_ref, 6, inverse)

    chain(rows, OV + rows - 1, 1, next_band)
    chain(2 * OV - 1, OV, -1, previous_band)
    chain(0, OV + half - 1, 1, top)
    chain(last, OV + half, -1, bottom)
    excess_top, divisor_top = kept["top"]
    excess_bottom, divisor_bottom = kept["bottom"]
    between = couple_ref[OV + half]
    inverse = 1.0 / (between * (excess_top + excess_bottom) + excess_top * excess_bottom)
    put(edge_ref, 2, divisor_bottom * inverse)
    put(edge_ref, 3, divisor_top * inverse)
    put(edge_ref, 4, between * inverse)


def edge_sums(low_rows, high_rows, edge_ref, groups):
    def edge(index):
        return edge_ref[index * groups : (index + 1) * groups, :]

    top = high_rows(0)
    for i in range(1, OV):
        top = high_rows(i) + edge(7 + i - 1) * top
    bottom = low_rows(OV - 1)
    for i in range(OV - 2, -1, -1):
        bottom = low_rows(i) + edge(14 + i) * bottom
    return top, bottom


def swap_out(parity, up, down, even_ref, odd_ref):
    is_even = parity == 0
    even_ref[...] = jnp.where(is_even, up, down)
    odd_ref[...] = jnp.where(is_even, down, up)


def swap_in(parity, even, odd):
    is_even = parity == 0
    return jnp.where(is_even, odd, even), jnp.where(is_even, even, odd)


def solve_first(rows, groups, right_side_row, from_low, from_high, ratio_ref, inverse_ref, edge_ref, out_ref):
    half = rows // 2

    def at(ref, index):
        return ref[index * groups : (index + 1) * groups, :]

    def put(index, value):
        out_ref[index * groups : (index + 1) * groups, :] = value

    low, high = from_low, from_high
    for i in range(half):
        j = rows - 1 - i
        low = right_side_row(i) + at(ratio_ref, i) * low
        high = right_side_row(j) + at(ratio_ref, j) * high
        put(i, low)
        put(j, high)
    meet(rows, groups, low, high, ratio_ref, inverse_ref, edge_ref, at, lambda i: at(out_ref, i), put)


def meet(rows, groups, low, high, ratio_ref, inverse_ref, edge_ref, at, value, put):
    half = rows // 2
    between = at(edge_ref, 4)
    x_low = at(edge_ref, 2) * low + between * high
    x_high = at(edge_ref, 3) * high + between * low
    put(half - 1, x_low)
    put(half, x_high)
    for i in range(half - 2, -1, -1):
        j = rows - 1 - i
        x_low = value(i) * at(inverse_ref, i) + at(ratio_ref, i + 1) * x_low
        x_high = value(j) * at(inverse_ref, j) + at(ratio_ref, j - 1) * x_high
        put(i, x_low)
        put(j, x_high)


def solve_second(
    rows, groups, couple_low, couple_high, own_top, own_bottom, got_top, got_bottom, sent_top, sent_bottom,
    from_low, from_high, ratio_ref, inverse_ref, edge_ref, first_ref, out_ref, mid_ref,
):
    half = rows // 2

    def at(ref, index):
        return ref[index * groups : (index + 1) * groups, :]

    beyond_low = (got_top + couple_low * own_top) * at(edge_ref, 0)
    beyond_high = (got_bottom + couple_high * own_bottom) * at(edge_ref, 1)
    theirs_low = (sent_bottom + couple_low * from_low) * at(edge_ref, 6)
    theirs_high = (sent_top + couple_high * from_high) * at(edge_ref, 5)
    low = couple_low * (own_top - theirs_low)
    high = couple_high * (own_bottom - theirs_high)
    for i in range(half):
        j = rows - 1 - i
        low = at(ratio_ref, i) * low
        high = at(ratio_ref, j) * high
        if i == 0:
            low = low + couple_low * (from_low - beyond_low)
            high = high + couple_high * (from_high - beyond_high)
        mid_ref[i * groups : (i + 1) * groups, :] = low
        mid_ref[j * groups : (j + 1) * groups, :] = high

    def put(index, value):
        rows_at = slice(index * groups, (index + 1) * groups)
        out_ref[rows_at, :] = first_ref[rows_at, :] + value

    meet(rows, groups, low, high, ratio_ref, inverse_ref, edge_ref, at, lambda i: at(mid_ref, i), put)


def call(body, outs, ins, spaces, scratch, flops, name):
    nbytes = sum(x.size * x.dtype.itemsize for x in ins) + sum(4 * math.prod(s) for s in outs)
    out = pl.pallas_call(
        body,
        out_shape=[jax.ShapeDtypeStruct(s, jnp.float32) for s in outs],
        in_specs=[pl.BlockSpec(memory_space=s) for s in spaces],
        out_specs=[pl.BlockSpec(memory_space=VMEM) for _ in outs],
        scratch_shapes=scratch,
        compiler_params=pltpu.CompilerParams(vmem_limit_bytes=48 << 20),
        cost_estimate=pl.CostEstimate(flops=flops, bytes_accessed=nbytes, transcendentals=0),
        name=name,
    )(*ins)
    return out


def pad_rows(rows):
    return -(-rows // (2 * BLOCK)) * 2 * BLOCK


def swap(value_even, value_odd):
    count = lax.axis_size("lat")
    even = [(i, i ^ 1) for i in range(count) if (i ^ 1) < count]
    odd = [(i, ((i + 1) ^ 1) - 1) for i in range(1, count) if ((i + 1) ^ 1) - 1 < count]
    return lax.ppermute(value_even, "lat", even), lax.ppermute(value_odd, "lat", odd)


def swap_levels(pieces):
    size = len(pieces)
    return [pieces[0]] + [
        lax.ppermute(pieces[mask], "lon", [(d, d ^ mask) for d in range(size)]) for mask in range(1, size)
    ]


def operator_parts(rows, level, lon_coef, lat_coef, level_scale):
    row_first = lax.axis_index("lat") * rows
    extent = rows + 2 * OV
    scale = lax.dynamic_index_in_dim(level_scale, level, 0, False)
    lon_window = scale * lax.dynamic_slice_in_dim(jnp.pad(lon_coef, (OV, OV)), row_first, extent)
    couple = scale * lax.dynamic_slice_in_dim(
        jnp.pad(lat_coef, (OV + 1, OV + 2)), row_first, extent + 1
    )
    return lon_window, couple


def factor(rows, groups, lon_window, couple, eigen):
    block = (rows * groups, N2)
    return call(
        functools.partial(factor_kernel, rows),
        [block, block, (21 * groups, N2)],
        [lon_window, couple, eigen],
        [SMEM, SMEM, VMEM],
        [],
        rows * groups * N2 * 20,
        "factor",
    )


def vmem(*shape):
    return pltpu.VMEM(shape, jnp.float32)


def rows_of(ref, groups, first=0):
    return lambda i: ref[(i - first) * groups : (i - first + 1) * groups, :]


def fill(full_ref, pieces, where, rows):
    padded = full_ref.shape[0]
    width = N1 // len(pieces)
    for mask, piece in enumerate(pieces):
        at = pl.multiple_of((where ^ mask) * width, width)
        full_ref[:rows, pl.ds(at, width), :] = piece[...].reshape(rows, width, N2)
    if padded > rows:
        full_ref[rows:] = jnp.zeros((padded - rows, N1, N2), jnp.float32)


def on_device(right_side, lon_coef, lat_coef, level_scale):
    const = {k: jnp.asarray(v) for k, v in tables().items()}
    if lax.axis_size("lon") != right_side.shape[1]:
        return shared_levels(const, right_side, lon_coef, lat_coef, level_scale)
    return whole_levels(const, right_side, lon_coef, lat_coef, level_scale)


def whole_levels(const, right_side, lon_coef, lat_coef, level_scale):
    rows, levels, lon_count = right_side.shape
    digits = N1 // levels
    groups = 2 * GROUPS
    lon_at = lax.axis_index("lon").astype(jnp.int32)
    parity = (lax.axis_index("lat") % 2).astype(jnp.int32)
    place = jnp.stack([lon_at, parity])
    lon_window, couple = operator_parts(rows, lon_at, lon_coef, lat_coef, level_scale)
    ratio, inverse, edge = factor(rows, groups, lon_window, couple, const["eigen"].reshape(groups, N2))
    block = (rows * groups, N2)
    row = (groups, N2)
    ends = 2 * OV
    inner = rows - ends
    by_row = right_side.reshape(rows, levels, digits, N2).transpose(0, 2, 1, 3).reshape(-1, N2)

    def pack(place_ref, in_ref, *out_refs):
        for mask in range(levels):
            level = place_ref[0] ^ mask
            end_ref, inner_ref = out_refs[2 * mask : 2 * mask + 2]
            span = OV * digits
            end_ref[:span, :] = in_ref[pl.ds(level, span, stride=levels), :]
            inner_ref[...] = in_ref[pl.ds(level + levels * span, inner * digits, stride=levels), :]
            end_ref[span:, :] = in_ref[pl.ds(level + levels * (rows - OV) * digits, span, stride=levels), :]

    packed = call(
        pack, [(ends * digits, N2), (inner * digits, N2)] * levels, [place, by_row], [SMEM, VMEM], [], 0, "pack"
    )
    end_pieces = swap_levels(packed[0::2])
    inner_pieces = swap_levels(packed[1::2])
    forward = [const["first"], const["turn"], const["second"], const["special"]]
    pad_ends, pad_inner = pad_rows(ends), pad_rows(inner)

    def ends_body(place_ref, *refs):
        pieces, refs = refs[:levels], refs[levels:]
        tables_in, edge_ref = refs[:4], refs[4]
        spec_ref, top_ref, bottom_ref, even_ref, odd_ref, full_ref, mid_ref = refs[5:]
        fill(full_ref, pieces, place_ref[0], ends)
        forward_rows(full_ref, ends, *tables_in, mid_ref, spec_ref)
        top, bottom = edge_sums(rows_of(spec_ref, groups), rows_of(spec_ref, groups, -OV), edge_ref, groups)
        top_ref[...] = top
        bottom_ref[...] = bottom
        swap_out(place_ref[1], top, bottom, even_ref, odd_ref)

    end_spectral, sent_top, sent_bottom, even, odd = call(
        ends_body,
        [(ends * groups, N2)] + [row] * 4,
        [place, *end_pieces, *forward, edge],
        [SMEM] + [VMEM] * (levels + 5),
        [vmem(pad_ends, N1, N2), vmem(pad_ends * N1, N2)],
        ends * NLON * 256 * 4,
        "ends",
    )
    even, odd = swap(even, odd)

    def inner_body(place_ref, *refs):
        pieces, refs = refs[:levels], refs[levels:]
        tables_in, refs = refs[:4], refs[4:]
        ends_ref, even_ref, odd_ref, ratio_ref, inverse_ref, edge_ref = refs[:6]
        out_ref, even_out, odd_out, full_ref, mid_ref, spec_ref = refs[6:]
        fill(full_ref, pieces, place_ref[0], inner)
        forward_rows(full_ref, inner, *tables_in, mid_ref, spec_ref)
        low, high = swap_in(place_ref[1], even_ref[...], odd_ref[...])

        def spec_row(i):
            if i < OV:
                return rows_of(ends_ref, groups)(i)
            if i >= rows - OV:
                return rows_of(ends_ref, groups, rows - ends)(i)
            return rows_of(spec_ref, groups, OV)(i)

        solve_first(rows, groups, spec_row, low, high, ratio_ref, inverse_ref, edge_ref, out_ref)
        swap_out(place_ref[1], out_ref[(rows - 1) * groups :, :], out_ref[:groups, :], even_out, odd_out)

    iterate, even2, odd2 = call(
        inner_body,
        [block, row, row],
        [place, *inner_pieces, *forward, end_spectral, even, odd, ratio, inverse, edge],
        [SMEM] + [VMEM] * (levels + 10),
        [vmem(pad_inner, N1, N2), vmem(pad_inner * N1, N2), vmem(inner * N1, N2)],
        inner * NLON * 256 * 4,
        "inner",
    )
    even2, odd2 = swap(even2, odd2)
    pad_all = pad_rows(rows)

    def second_body(place_ref, couple_ref, *refs):
        first_ref, even_ref, odd_ref, even2_ref, odd2_ref, top_ref, bottom_ref = refs[:7]
        ratio_ref, inverse_ref, edge_ref = refs[7:10]
        tables_in = refs[10:14]
        out_refs = refs[14 : 14 + levels]
        sum_ref, mid_ref, full_ref = refs[14 + levels :]
        second_part(
            rows, groups, place_ref[1], couple_ref, first_ref, even_ref, odd_ref, even2_ref, odd2_ref,
            top_ref, bottom_ref, ratio_ref, inverse_ref, edge_ref, sum_ref, mid_ref,
        )
        backward_rows(sum_ref, rows, *tables_in, mid_ref, full_ref)
        for mask in range(levels):
            at = pl.multiple_of((place_ref[0] ^ mask) * digits, digits)
            out_refs[mask][...] = full_ref[:rows, pl.ds(at, digits), :].reshape(rows * digits, N2)

    backward = [const["first_back"], const["turn"], const["second_back"], const["special_back"]]
    pieces = call(
        second_body,
        [(rows * digits, N2)] * levels,
        [place, couple, iterate, even, odd, even2, odd2, sent_top, sent_bottom, ratio, inverse, edge, *backward],
        [SMEM, SMEM] + [VMEM] * 14,
        [vmem(*block), vmem(pad_all * N1, N2), vmem(pad_all, N1, N2)],
        rows * NLON * 256 * 4,
        "second",
    )
    pieces = swap_levels(pieces)

    def unpack(place_ref, *refs):
        out_ref = refs[levels]
        for mask in range(levels):
            out_ref[pl.ds(place_ref[0] ^ mask, rows * digits, stride=levels), :] = refs[mask][...]

    (out,) = call(
        unpack, [(rows * levels * digits, N2)], [place, *pieces], [SMEM] + [VMEM] * levels, [], 0, "unpack"
    )
    return out.reshape(rows, digits, levels, N2).transpose(0, 2, 1, 3).reshape(right_side.shape)


def second_part(
    rows, groups, parity, couple_ref, first_ref, even_ref, odd_ref, even2_ref, odd2_ref, top_ref, bottom_ref,
    ratio_ref, inverse_ref, edge_ref, out_ref, mid_ref,
):
    got_top, got_bottom = swap_in(parity, even_ref[...], odd_ref[...])
    low, high = swap_in(parity, even2_ref[...], odd2_ref[...])
    solve_second(
        rows, groups, couple_ref[OV], couple_ref[OV + rows],
        first_ref[:groups, :], first_ref[(rows - 1) * groups :, :],
        got_top, got_bottom, top_ref[...], bottom_ref[...], low, high,
        ratio_ref, inverse_ref, edge_ref, first_ref, out_ref, mid_ref,
    )


def shared_levels(const, right_side, lon_coef, lat_coef, level_scale):
    rows, levels, lon_count = right_side.shape
    lon_size = lax.axis_size("lon")
    assert lon_size % levels == 0 and GROUPS % (lon_size // levels) == 0 and rows % (lon_size // levels) == 0
    sharers = lon_size // levels
    groups = 2 * GROUPS // sharers
    part_rows = rows // sharers
    digits = N1 // lon_size
    lon_at = lax.axis_index("lon")
    parity = (lax.axis_index("lat") % 2).astype(jnp.int32).reshape(1)
    lon_window, couple = operator_parts(rows, lon_at // sharers, lon_coef, lat_coef, level_scale)
    eigen = lax.dynamic_slice_in_dim(
        const["eigen"], (lon_at % sharers) * (groups // 2), groups // 2, axis=1
    ).reshape(groups, N2)
    ratio, inverse, edge = factor(rows, groups, lon_window, couple, eigen)
    block = (rows * groups, N2)
    row = (groups, N2)
    send = right_side.reshape(sharers, part_rows, levels, lon_count).transpose(2, 0, 1, 3)
    send = send.reshape(lon_size, part_rows, digits, N2)
    got = lax.all_to_all(send, "lon", 0, 0, tiled=True)
    points = got.transpose(1, 0, 2, 3).reshape(part_rows, N1, N2)
    padded = pad_rows(part_rows)

    def transform(points_ref, first_ref, turn_ref, second_ref, special_ref, out_ref, full_ref, mid_ref):
        full_ref[:part_rows] = points_ref[...]
        if padded > part_rows:
            full_ref[part_rows:] = jnp.zeros((padded - part_rows, N1, N2), jnp.float32)
        forward_rows(full_ref, part_rows, first_ref, turn_ref, second_ref, special_ref, mid_ref, out_ref)

    (spectral,) = call(
        transform,
        [(part_rows * N1, N2)],
        [points, const["first"], const["turn"], const["second"], const["special"]],
        [VMEM] * 5,
        [vmem(padded, N1, N2), vmem(padded * N1, N2)],
        part_rows * NLON * 256 * 4,
        "transform",
    )
    spectral = to_coefs(spectral, sharers, part_rows, groups)

    def edges(parity_ref, spec_ref, edge_ref, top_ref, bottom_ref, even_ref, odd_ref):
        top, bottom = edge_sums(
            rows_of(spec_ref, groups), rows_of(spec_ref, groups, OV - rows), edge_ref, groups
        )
        top_ref[...] = top
        bottom_ref[...] = bottom
        swap_out(parity_ref[0], top, bottom, even_ref, odd_ref)

    sent_top, sent_bottom, even, odd = call(
        edges, [row] * 4, [parity, spectral, edge], [SMEM, VMEM, VMEM], [], groups * N2 * 32, "edges"
    )
    even, odd = swap(even, odd)

    def first(parity_ref, spec_ref, even_ref, odd_ref, ratio_ref, inverse_ref, edge_ref, out_ref, e_ref, o_ref):
        low, high = swap_in(parity_ref[0], even_ref[...], odd_ref[...])
        solve_first(
            rows, groups, rows_of(spec_ref, groups), low, high, ratio_ref, inverse_ref, edge_ref, out_ref
        )
        swap_out(parity_ref[0], out_ref[(rows - 1) * groups :, :], out_ref[:groups, :], e_ref, o_ref)

    iterate, even2, odd2 = call(
        first,
        [block, row, row],
        [parity, spectral, even, odd, ratio, inverse, edge],
        [SMEM] + [VMEM] * 6,
        [],
        rows * groups * N2 * 8,
        "first_solve",
    )
    even2, odd2 = swap(even2, odd2)

    def second(parity_ref, *refs):
        second_part(rows, groups, parity_ref[0], *refs)

    (iterate,) = call(
        second,
        [block],
        [parity, couple, iterate, even, odd, even2, odd2, sent_top, sent_bottom, ratio, inverse, edge],
        [SMEM, SMEM] + [VMEM] * 10,
        [vmem(*block)],
        rows * groups * N2 * 8,
        "second_solve",
    )
    iterate = to_rows(iterate, sharers, part_rows, groups)

    def back(spec_ref, first_ref, turn_ref, second_ref, special_ref, out_ref, mid_ref, full_ref):
        backward_rows(spec_ref, part_rows, first_ref, turn_ref, second_ref, special_ref, mid_ref, full_ref)
        out_ref[...] = full_ref[:part_rows]

    (points,) = call(
        back,
        [(part_rows, N1, N2)],
        [iterate, const["first_back"], const["turn"], const["second_back"], const["special_back"]],
        [VMEM] * 5,
        [vmem(padded * N1, N2), vmem(padded, N1, N2)],
        part_rows * NLON * 256 * 4,
        "back_transform",
    )
    send = points.reshape(part_rows, lon_size, digits, N2).transpose(1, 0, 2, 3)
    got = lax.all_to_all(send, "lon", 0, 0, tiled=True)
    got = got.reshape(levels, sharers, part_rows, lon_count).transpose(1, 2, 0, 3)
    return got.reshape(rows, levels, lon_count)


def level_groups(sharers):
    size = lax.axis_size("lon")
    return [[first + i for i in range(sharers)] for first in range(0, size, sharers)]


def to_coefs(spectral, sharers, part_rows, groups):
    send = spectral.reshape(part_rows, 2, sharers, groups // 2, N2).transpose(2, 0, 1, 3, 4)
    got = lax.all_to_all(
        send, "lon", 0, 0, tiled=True, axis_index_groups=level_groups(sharers)
    )
    return got.reshape(sharers * part_rows * groups, N2)


def to_rows(values, sharers, part_rows, groups):
    send = values.reshape(sharers, part_rows, 2, groups // 2, N2)
    got = lax.all_to_all(
        send, "lon", 0, 0, tiled=True, axis_index_groups=level_groups(sharers)
    )
    return got.transpose(1, 2, 0, 3, 4).reshape(part_rows * N1, N2)


def solution(mesh):
    return jax.shard_map(
        on_device,
        mesh=mesh,
        in_specs=(P("lat", None, "lon"), P(), P(), P()),
        out_specs=P("lat", None, "lon"),
        check_vma=False,
    )
```

```python
import functools
import math

import jax
import jax.numpy as jnp
import numpy as np
from jax import lax
from jax.experimental import pallas as pl
from jax.experimental.pallas import tpu as pltpu
from jax.sharding import PartitionSpec as P

NLON = 4096
OV = 8
N1 = 32
N2 = 128
GROUPS = 16
BLOCK = 8

VMEM = pltpu.VMEM
SMEM = pltpu.SMEM


def numpy_split(table):
    import ml_dtypes

    table = np.asarray(table, np.float32)
    high = table.astype(ml_dtypes.bfloat16)
    low = (table - high.astype(np.float32)).astype(ml_dtypes.bfloat16)
    return high, low


def tables(levels):
    j1 = np.arange(N1)
    j2 = np.arange(N2)
    k2 = np.arange(N2)
    digit = np.arange(GROUPS)
    small = np.zeros((N1, N1))
    small[:GROUPS] = np.cos(2 * np.pi * np.outer(digit, j1) / N1)
    small[GROUPS] = np.cos(np.pi * j1)
    small[GROUPS + 1 :] = -np.sin(2 * np.pi * np.outer(digit[1:], j1) / N1)
    first = np.kron(np.eye(BLOCK), small)
    angle = 2 * np.pi * np.outer(digit, j2) / NLON
    turn_cos = np.cos(angle)
    turn_sin = np.sin(angle)
    phase = 2 * np.pi * (np.outer(j2, k2) % N2) / N2
    cosine, sine = np.cos(phase), np.sin(phase)
    second = np.block([[cosine, -sine], [sine, cosine]])
    special = np.zeros((2 * N2, 2 * N2))
    half = N2 // 2
    special[:N2, : half + 1] = np.cos(2 * np.pi * np.outer(j2, np.arange(half + 1)) / N2)
    special[:N2, half + 1 : N2] = -np.sin(2 * np.pi * np.outer(j2, np.arange(1, half)) / N2)
    odd = 2 * np.pi * np.outer(j2, 1 + 2 * np.arange(half)) / (2 * N2)
    special[N2:, N2 : N2 + half] = np.cos(odd)
    special[N2:, N2 + half :] = -np.sin(odd)
    weight = np.full(2 * N2, 2.0 / NLON)
    weight[0] = 1.0 / NLON
    weight[half] = 1.0 / NLON
    second_back = second.T * (2.0 / NLON)
    special_back = weight[:, None] * special.T
    wave = np.zeros((GROUPS, 2 * N2))
    wave[:, :N2] = digit[:, None] + N1 * k2[None, :]
    wave[:, N2:] = wave[:, :N2]
    lane = np.arange(N2)
    wave[0, :N2] = np.where(lane <= half, N1 * lane, N1 * (lane - half))
    wave[0, N2:] = 16 + N1 * (lane % half)
    eigen = 2.0 - 2.0 * np.cos(2 * np.pi * wave / NLON)
    pair = lambda t: np.concatenate(numpy_split(t), axis=0)
    width = N1 // levels
    part = [pair(np.kron(np.eye(BLOCK), small.T[at : at + width])) for at in range(0, N1, width)]
    return dict(
        first_back_part=np.concatenate(part, axis=0),
        first=pair(first),
        first_back=pair(first.T),
        second=pair(second),
        second_back=pair(second_back),
        special=pair(special),
        special_back=pair(special_back),
        turn=np.concatenate([turn_cos, turn_sin], axis=0).astype(np.float32),
        eigen=np.stack([eigen[:, :N2], eigen[:, N2:]]).astype(np.float32),
    )


def halves(value):
    high = value.astype(jnp.bfloat16)
    low = (value - high.astype(jnp.float32)).astype(jnp.bfloat16)
    return high, low


def dot(a, b):
    return lax.dot_general(a, b, (((1,), (0,)), ((), ())), preferred_element_type=jnp.float32)


def product_right(value, table_ref):
    size = table_ref.shape[0] // 2
    high, low = halves(value)
    table_high = table_ref[:size, :]
    return dot(high, table_high) + dot(low, table_high) + dot(high, table_ref[size:, :])


def product_left(table_ref, value):
    size = table_ref.shape[0] // 2
    high, low = halves(value)
    both = dot(table_ref[...], high)
    return both[:size] + both[size:] + dot(table_ref[:size, :], low)


def lanes_apart(value, rows):
    real = value[:, :N2].reshape(rows, GROUPS, N2)
    imag = value[:, N2:].reshape(rows, GROUPS, N2)
    return jnp.concatenate([real, imag], axis=1).reshape(rows * 2 * GROUPS, N2)


def lanes_together(value, rows):
    both = value.reshape(rows, 2 * GROUPS, N2)
    return jnp.concatenate([both[:, :GROUPS], both[:, GROUPS:]], axis=2).reshape(rows * GROUPS, 2 * N2)


def load_zeroth(ref, rows):
    return jnp.concatenate(
        [ref[pl.ds(0, rows, stride=2 * GROUPS), :], ref[pl.ds(GROUPS, rows, stride=2 * GROUPS), :]], axis=1
    )


def store_zeroth(ref, rows, value):
    ref[pl.ds(0, rows, stride=2 * GROUPS), :] = value[:, :N2]
    ref[pl.ds(GROUPS, rows, stride=2 * GROUPS), :] = value[:, N2:]


def forward_rows(points_ref, rows, first_ref, turn_ref, second_ref, special_ref, mid_ref, out_ref):
    padded = points_ref.shape[0]
    turn_cos = turn_ref[:GROUPS, :][None]
    turn_sin = turn_ref[GROUPS:, :][None]
    for pair in range(padded // (2 * BLOCK)):
        base = pair * 2 * BLOCK
        left = points_ref[base : base + BLOCK].reshape(BLOCK * N1, N2)
        right = points_ref[base + BLOCK : base + 2 * BLOCK].reshape(BLOCK * N1, N2)
        value = product_left(first_ref, jnp.concatenate([left, right], axis=1))
        for side in range(2):
            digits = value[:, side * N2 : (side + 1) * N2].reshape(BLOCK, N1, N2)
            real, imag = digits[:, :GROUPS], digits[:, GROUPS:]
            turned = jnp.concatenate(
                [real * turn_cos + imag * turn_sin, imag * turn_cos - real * turn_sin], axis=1
            )
            at = (base + side * BLOCK) * N1
            mid_ref[at : at + BLOCK * N1, :] = turned.reshape(BLOCK * N1, N2)
    result = product_right(lanes_together(mid_ref[...], padded), second_ref)
    out_ref[...] = lanes_apart(result, padded)[: rows * N1]
    store_zeroth(out_ref, rows, product_right(load_zeroth(mid_ref, padded), special_ref)[:rows])


def spectral_back(spec_ref, rows, padded, second_ref, special_ref, mid_ref):
    result = product_right(lanes_together(spec_ref[...], rows), second_ref)
    mid_ref[: rows * N1, :] = lanes_apart(result, rows)
    if padded > rows:
        mid_ref[rows * N1 : padded * N1, :] = jnp.zeros(((padded - rows) * N1, N2), jnp.float32)
    store_zeroth(mid_ref, rows, product_right(load_zeroth(spec_ref, rows), special_ref))


def digits_back(mid_ref, pair, turn_ref, first_ref):
    turn_cos = turn_ref[:GROUPS, :][None]
    turn_sin = turn_ref[GROUPS:, :][None]
    sides = []
    for side in range(2):
        at = (2 * pair + side) * BLOCK * N1
        both = mid_ref[at : at + BLOCK * N1, :].reshape(BLOCK, N1, N2)
        real, imag = both[:, :GROUPS], both[:, GROUPS:]
        turned = jnp.concatenate(
            [real * turn_cos - imag * turn_sin, imag * turn_cos + real * turn_sin], axis=1
        )
        sides.append(turned.reshape(BLOCK * N1, N2))
    return product_left(first_ref, jnp.concatenate(sides, axis=1))


def backward_rows(spec_ref, rows, first_ref, turn_ref, second_ref, special_ref, mid_ref, out_ref):
    padded = out_ref.shape[0]
    spectral_back(spec_ref, rows, padded, second_ref, special_ref, mid_ref)
    for pair in range(padded // (2 * BLOCK)):
        base = pair * 2 * BLOCK
        value = digits_back(mid_ref, pair, turn_ref, first_ref)
        out_ref[base : base + BLOCK] = value[:, :N2].reshape(BLOCK, N1, N2)
        out_ref[base + BLOCK : base + 2 * BLOCK] = value[:, N2:].reshape(BLOCK, N1, N2)


def factor_kernel(rows, lon_ref, couple_ref, eigen_ref, ratio_ref, inverse_ref, edge_ref):
    eigen = eigen_ref[...]
    groups = eigen.shape[0]
    half = rows // 2
    last = rows + 2 * OV - 1

    def plain(e):
        return 1.0 + lon_ref[e] * eigen

    def put(ref, index, value):
        ref[index * groups : (index + 1) * groups, :] = value

    def chain(start, stop, step, into):
        excess = inverse = None
        for e in range(start, stop + step, step):
            before = couple_ref[e] if step > 0 else couple_ref[e + 1]
            after = couple_ref[e + 1] if step > 0 else couple_ref[e]
            if inverse is None:
                ratio = None
                excess = plain(e) + before
            else:
                ratio = before * inverse
                excess = plain(e) + ratio * excess
            divisor = after + excess
            inverse = 1.0 / divisor
            into(e, ratio, inverse, excess, divisor)

    kept = {}

    def top(e, ratio, inverse, excess, divisor):
        if e == OV - 1:
            put(edge_ref, 0, inverse)
        if e >= OV:
            put(ratio_ref, e - OV, ratio)
            put(inverse_ref, e - OV, inverse)
        if e == OV + half - 1:
            kept["top"] = excess, divisor

    def bottom(e, ratio, inverse, excess, divisor):
        if e == OV + rows:
            put(edge_ref, 1, inverse)
        if e < OV + rows:
            put(ratio_ref, e - OV, ratio)
            put(inverse_ref, e - OV, inverse)
        if e == OV + half:
            kept["bottom"] = excess, divisor

    def next_band(e, ratio, inverse, excess, divisor):
        if ratio is not None:
            put(edge_ref, 7 + e - rows - 1, ratio)
        if e == OV + rows - 1:
            put(edge_ref, 5, inverse)

    def previous_band(e, ratio, inverse, excess, divisor):
        if ratio is not None:
            put(edge_ref, 14 + e - OV, ratio)
        if e == OV:
            put(edge_ref, 6, inverse)

    chain(rows, OV + rows - 1, 1, next_band)
    chain(2 * OV - 1, OV, -1, previous_band)
    chain(0, OV + half - 1, 1, top)
    chain(last, OV + half, -1, bottom)
    excess_top, divisor_top = kept["top"]
    excess_bottom, divisor_bottom = kept["bottom"]
    between = couple_ref[OV + half]
    inverse = 1.0 / (between * (excess_top + excess_bottom) + excess_top * excess_bottom)
    put(edge_ref, 2, divisor_bottom * inverse)
    put(edge_ref, 3, divisor_top * inverse)
    put(edge_ref, 4, between * inverse)


def edge_sums(low_rows, high_rows, edge_ref, groups):
    def edge(index):
        return edge_ref[index * groups : (index + 1) * groups, :]

    top = high_rows(0)
    for i in range(1, OV):
        top = high_rows(i) + edge(7 + i - 1) * top
    bottom = low_rows(OV - 1)
    for i in range(OV - 2, -1, -1):
        bottom = low_rows(i) + edge(14 + i) * bottom
    return top, bottom


def swap_out(parity, up, down, even_ref, odd_ref):
    is_even = parity == 0
    even_ref[...] = jnp.where(is_even, up, down)
    odd_ref[...] = jnp.where(is_even, down, up)


def swap_in(parity, even, odd):
    is_even = parity == 0
    return jnp.where(is_even, odd, even), jnp.where(is_even, even, odd)


def solve_first(rows, groups, right_side_row, from_low, from_high, ratio_ref, inverse_ref, edge_ref, out_ref):
    half = rows // 2

    def at(ref, index):
        return ref[index * groups : (index + 1) * groups, :]

    def put(index, value):
        out_ref[index * groups : (index + 1) * groups, :] = value

    low, high = from_low, from_high
    for i in range(half):
        j = rows - 1 - i
        low = right_side_row(i) + at(ratio_ref, i) * low
        high = right_side_row(j) + at(ratio_ref, j) * high
        put(i, low)
        put(j, high)
    meet(rows, groups, low, high, ratio_ref, inverse_ref, edge_ref, at, lambda i: at(out_ref, i), put)


def meet(rows, groups, low, high, ratio_ref, inverse_ref, edge_ref, at, value, put):
    half = rows // 2
    between = at(edge_ref, 4)
    x_low = at(edge_ref, 2) * low + between * high
    x_high = at(edge_ref, 3) * high + between * low
    put(half - 1, x_low)
    put(half, x_high)
    for i in range(half - 2, -1, -1):
        j = rows - 1 - i
        x_low = value(i) * at(inverse_ref, i) + at(ratio_ref, i + 1) * x_low
        x_high = value(j) * at(inverse_ref, j) + at(ratio_ref, j - 1) * x_high
        put(i, x_low)
        put(j, x_high)


def sigmas(
    couple_low, couple_high, own_top, own_bottom, got_top, got_bottom, sent_top, sent_bottom, from_low, from_high,
    ratio_first, ratio_last, edge_ref,
):
    groups = own_top.shape[0]

    def edge(index):
        return edge_ref[index * groups : (index + 1) * groups, :]

    beyond_low = (got_top + couple_low * own_top) * edge(0)
    beyond_high = (got_bottom + couple_high * own_bottom) * edge(1)
    theirs_low = (sent_bottom + couple_low * from_low) * edge(6)
    theirs_high = (sent_top + couple_high * from_high) * edge(5)
    low = ratio_first * (couple_low * (own_top - theirs_low)) + couple_low * (from_low - beyond_low)
    high = ratio_last * (couple_high * (own_bottom - theirs_high)) + couple_high * (from_high - beyond_high)
    return low, high


def solve_second(
    rows, groups, couple_low, couple_high, own_top, own_bottom, got_top, got_bottom, sent_top, sent_bottom,
    from_low, from_high, ratio_ref, inverse_ref, edge_ref, first_ref, out_ref, mid_ref,
):
    half = rows // 2

    def at(ref, index):
        return ref[index * groups : (index + 1) * groups, :]

    low, high = sigmas(
        couple_low, couple_high, own_top, own_bottom, got_top, got_bottom, sent_top, sent_bottom,
        from_low, from_high, at(ratio_ref, 0), at(ratio_ref, rows - 1), edge_ref,
    )
    for i in range(half):
        j = rows - 1 - i
        if i:
            low = at(ratio_ref, i) * low
            high = at(ratio_ref, j) * high
        mid_ref[i * groups : (i + 1) * groups, :] = low
        mid_ref[j * groups : (j + 1) * groups, :] = high

    def put(index, value):
        rows_at = slice(index * groups, (index + 1) * groups)
        out_ref[rows_at, :] = first_ref[rows_at, :] + value

    meet(rows, groups, low, high, ratio_ref, inverse_ref, edge_ref, at, lambda i: at(mid_ref, i), put)


def call(body, outs, ins, spaces, scratch, flops, name, out_spaces=None, aliases=None):
    nbytes = sum(x.size * x.dtype.itemsize for x in ins) + sum(4 * math.prod(s) for s in outs)
    out = pl.pallas_call(
        body,
        out_shape=[jax.ShapeDtypeStruct(s, jnp.float32) for s in outs],
        in_specs=[pl.BlockSpec(memory_space=s) for s in spaces],
        out_specs=[pl.BlockSpec(memory_space=s) for s in out_spaces or [VMEM] * len(outs)],
        input_output_aliases=aliases or {},
        scratch_shapes=scratch,
        compiler_params=pltpu.CompilerParams(vmem_limit_bytes=48 << 20),
        cost_estimate=pl.CostEstimate(flops=flops, bytes_accessed=nbytes, transcendentals=0),
        name=name,
    )(*ins)
    return out


def pad_rows(rows):
    return -(-rows // (2 * BLOCK)) * 2 * BLOCK


def swap(value_even, value_odd):
    count = lax.axis_size("lat")
    even = [(i, i ^ 1) for i in range(count) if (i ^ 1) < count]
    odd = [(i, ((i + 1) ^ 1) - 1) for i in range(1, count) if ((i + 1) ^ 1) - 1 < count]
    return lax.ppermute(value_even, "lat", even), lax.ppermute(value_odd, "lat", odd)


def send_level(piece, mask, size):
    return lax.ppermute(piece, "lon", [(d, d ^ mask) for d in range(size)])


def swap_levels(pieces):
    return [pieces[0]] + [send_level(pieces[mask], mask, len(pieces)) for mask in range(1, len(pieces))]


def operator_parts(rows, lon_coef, lat_coef, level_scale):
    row_first = lax.axis_index("lat") * rows
    extent = rows + 2 * OV
    lon_window = lax.dynamic_slice_in_dim(jnp.pad(lon_coef, (OV, OV)), row_first, extent)
    couple = lax.dynamic_slice_in_dim(jnp.pad(lat_coef, (OV + 1, OV + 2)), row_first, extent + 1)
    return level_scale[:, None] * lon_window[None], level_scale[:, None] * couple[None]


def factor(rows, groups, lon_window, couple, eigen):
    block = (rows * groups, N2)
    return call(
        functools.partial(factor_kernel, rows),
        [block, block, (21 * groups, N2)],
        [lon_window, couple, eigen],
        [SMEM, SMEM, VMEM],
        [],
        rows * groups * N2 * 20,
        "factor",
    )


def vmem(*shape):
    return pltpu.VMEM(shape, jnp.float32)


def rows_of(ref, groups, first=0):
    return lambda i: ref[(i - first) * groups : (i - first + 1) * groups, :]


def on_device(right_side, lon_coef, lat_coef, level_scale):
    const = {k: jnp.asarray(v) for k, v in tables(right_side.shape[1]).items()}
    if lax.axis_size("lon") != right_side.shape[1]:
        return shared_levels(const, right_side, lon_coef, lat_coef, level_scale)
    return whole_levels(const, right_side, lon_coef, lat_coef, level_scale)


def early_rows(rows):
    return rows // 2 + 2


def influence_kernel(rows, early, levels, lon_ref, couple_ref, eigen_ref, phi_ref, psi_ref, ratio_ref, value_ref):
    eigen = eigen_ref[...]
    groups = eigen.shape[0]
    half = rows // 2
    span = early * groups

    def at(ref, index):
        return ref[index * groups : (index + 1) * groups, :]

    def put(ref, index, value):
        ref[index * groups : (index + 1) * groups, :] = value

    def one_level(level, carry):
        def plain(e):
            return 1.0 + lon_ref[level, e] * eigen

        low = high = None
        low_inverse = high_inverse = low_value = high_value = None
        for i in range(-OV, half):
            j = rows - 1 - i
            e, f = i + OV, j + OV
            if low is None:
                low = plain(e) + couple_ref[level, e]
                high = plain(f) + couple_ref[level, f + 1]
            else:
                low_ratio = couple_ref[level, e] * low_inverse
                high_ratio = couple_ref[level, f + 1] * high_inverse
                low = plain(e) + low_ratio * low
                high = plain(f) + high_ratio * high
            low_divisor = couple_ref[level, e + 1] + low
            high_divisor = couple_ref[level, f] + high
            low_inverse = 1.0 / low_divisor
            high_inverse = 1.0 / high_divisor
            if i == 0:
                low_value = high_value = jnp.ones_like(eigen)
            elif i > 0:
                low_value = low_ratio * low_value
                high_value = high_ratio * high_value
            if i >= 0:
                put(ratio_ref, i, low_ratio)
                put(value_ref, i, low_value * low_inverse)
                if j < early:
                    put(ratio_ref, j, high_ratio)
                    put(value_ref, j, high_value * high_inverse)
        between = couple_ref[level, OV + half]
        inverse = 1.0 / (between * (low + high) + low * high)

        def place(ref, index, value):
            ref[pl.ds(pl.multiple_of(level * span + index * groups, groups), groups), :] = value

        phi = high_divisor * inverse * low_value
        psi = between * inverse * high_value
        phi_down = between * inverse * low_value
        psi_down = low_divisor * inverse * high_value
        place(phi_ref, half - 1, phi)
        place(psi_ref, half - 1, psi)
        for i in range(half - 2, -1, -1):
            ratio = at(ratio_ref, i + 1)
            phi = at(value_ref, i) + ratio * phi
            psi = ratio * psi
            place(phi_ref, i, phi)
            place(psi_ref, i, psi)
        place(phi_ref, half, phi_down)
        place(psi_ref, half, psi_down)
        for j in range(half + 1, early):
            ratio = at(ratio_ref, j - 1)
            phi_down = ratio * phi_down
            psi_down = at(value_ref, j) + ratio * psi_down
            place(phi_ref, j, phi_down)
            place(psi_ref, j, psi_down)
        return carry

    lax.fori_loop(0, levels, one_level, 0)


def whole_levels(const, right_side, lon_coef, lat_coef, level_scale):
    rows, levels, lon_count = right_side.shape
    digits = N1 // levels
    groups = 2 * GROUPS
    lon_at = lax.axis_index("lon").astype(jnp.int32)
    parity = (lax.axis_index("lat") % 2).astype(jnp.int32)
    place = jnp.stack([lon_at, parity])
    half = rows // 2
    early = early_rows(rows)
    late = rows - early
    eigen = const["eigen"].reshape(groups, N2)
    lon_all, couple_all = operator_parts(rows, lon_coef, lat_coef, level_scale)
    lon_window = lax.dynamic_index_in_dim(lon_all, lon_at, 0, False)
    couple = lax.dynamic_index_in_dim(couple_all, lon_at, 0, False)
    ratio, inverse, edge = factor(rows, groups, lon_window, couple, eigen)
    phi, psi = call(
        functools.partial(influence_kernel, rows, early, levels),
        [(levels * early * groups, N2)] * 2,
        [lon_all, couple_all, eigen],
        [SMEM, SMEM, VMEM],
        [vmem(early * groups, N2), vmem(early * groups, N2)],
        levels * rows * groups * N2 * 20,
        "influence",
    )
    row = (groups, N2)
    ends = 2 * OV
    inner = rows - ends
    span = OV * digits
    by_row = right_side.reshape(rows, levels, digits, N2).transpose(0, 2, 1, 3).reshape(-1, N2)

    far = list(range(2, levels))

    def pack_ends(place_ref, in_ref, *refs):
        out_refs, (low_ref, high_ref, sems) = refs[:-3], refs[-3:]
        low = pltpu.make_async_copy(in_ref.at[pl.ds(0, levels * span), :], low_ref, sems.at[0])
        high = pltpu.make_async_copy(
            in_ref.at[pl.ds(levels * (rows - OV) * digits, levels * span), :], high_ref, sems.at[1]
        )
        low.start()
        high.start()
        low.wait()
        high.wait()
        for out_ref, mask in zip(out_refs, [0] + far):
            level = place_ref[0] ^ mask
            out_ref[:span, :] = low_ref[pl.ds(level, span, stride=levels), :]
            out_ref[span:, :] = high_ref[pl.ds(level, span, stride=levels), :]

    end_packed = call(
        pack_ends,
        [(ends * digits, N2)] * (1 + len(far)),
        [place, by_row],
        [SMEM, pltpu.HBM],
        [vmem(levels * span, N2), vmem(levels * span, N2), pltpu.SemaphoreType.DMA((2,))],
        0,
        "pack_ends",
    )

    def pack(place_ref, in_ref, after_ref, *out_refs):
        del after_ref
        for mask, out_ref in enumerate(out_refs):
            level = place_ref[0] ^ mask
            skip = 0 if mask == 1 else span
            out_ref[...] = in_ref[pl.ds(level + levels * skip, out_ref.shape[0], stride=levels), :]

    packed = call(
        pack,
        [((rows if mask == 1 else inner) * digits, N2) for mask in range(levels)],
        [place, by_row, end_packed[0]],
        [SMEM, VMEM, pl.ANY],
        [],
        0,
        "pack",
    )
    end_pieces = [end_packed[0], None] + [send_level(p, m, levels) for p, m in zip(end_packed[1:], far)]
    near = send_level(packed[1], 1, levels)
    end_pieces[1] = near
    inner_pieces = [packed[0], near] + [send_level(packed[m], m, levels) for m in far]
    forward = [const["first"], const["turn"], const["second"], const["special"]]
    pad_ends, pad_inner = pad_rows(ends), pad_rows(inner)

    def ends_body(place_ref, *refs):
        pieces, refs = refs[:levels], refs[levels:]
        tables_in, edge_ref = refs[:4], refs[4]
        spec_ref, top_ref, bottom_ref, even_ref, odd_ref, full_ref, mid_ref = refs[5:]
        for mask, piece in enumerate(pieces):
            at = pl.multiple_of((place_ref[0] ^ mask) * digits, digits)
            last = piece.shape[0] - span
            full_ref[:OV, pl.ds(at, digits), :] = piece[:span, :].reshape(OV, digits, N2)
            full_ref[OV:ends, pl.ds(at, digits), :] = piece[last:, :].reshape(OV, digits, N2)
        forward_rows(full_ref, ends, *tables_in, mid_ref, spec_ref)
        top, bottom = edge_sums(rows_of(spec_ref, groups), rows_of(spec_ref, groups, -OV), edge_ref, groups)
        top_ref[...] = top
        bottom_ref[...] = bottom
        swap_out(place_ref[1], top, bottom, even_ref, odd_ref)

    end_spectral, sent_top, sent_bottom, even, odd = call(
        ends_body,
        [(ends * groups, N2)] + [row] * 4,
        [place, *end_pieces, *forward, edge],
        [SMEM] + [VMEM] * (levels + 5),
        [vmem(pad_ends, N1, N2), vmem(pad_ends * N1, N2)],
        ends * NLON * 256 * 4,
        "ends",
    )
    even, odd = swap(even, odd)
    backward = [const["first_back"], const["turn"], const["second_back"], const["special_back"]]
    pad_early, pad_late = pad_rows(early), pad_rows(late)

    def spread(place_ref, full_ref, count, out_refs):
        for mask, out_ref in enumerate(out_refs):
            at = pl.multiple_of((place_ref[0] ^ mask) * digits, digits)
            out_ref[: count * digits, :] = full_ref[:count, pl.ds(at, digits), :].reshape(count * digits, N2)

    def inner_body(place_ref, *refs):
        pieces, refs = refs[:levels], refs[levels + 1 :]
        tables_in, back_in, refs = refs[:4], refs[4:7], refs[7:]
        ends_ref, even_ref, odd_ref, ratio_ref, inverse_ref, edge_ref = refs[:6]
        late_ref, top_ref, even_out, odd_out = refs[6:10]
        early_refs, refs = refs[10 : 10 + levels], refs[10 + levels :]
        full_ref, mid_ref, spec_ref, sum_ref, back_full_ref, back_mid_ref = refs
        for mask, piece in enumerate(pieces):
            at = pl.multiple_of((place_ref[0] ^ mask) * digits, digits)
            skip = span if mask == 1 else 0
            full_ref[:inner, pl.ds(at, digits), :] = piece[skip : skip + inner * digits, :].reshape(
                inner, digits, N2
            )
        if pad_inner > inner:
            full_ref[inner:] = jnp.zeros((pad_inner - inner, N1, N2), jnp.float32)
        forward_rows(full_ref, inner, *tables_in, mid_ref, spec_ref)
        low, high = swap_in(place_ref[1], even_ref[...], odd_ref[...])

        def spec_row(i):
            if i < OV:
                return rows_of(ends_ref, groups)(i)
            if i >= rows - OV:
                return rows_of(ends_ref, groups, rows - ends)(i)
            return rows_of(spec_ref, groups, OV)(i)

        solve_first(rows, groups, spec_row, low, high, ratio_ref, inverse_ref, edge_ref, sum_ref)
        top = sum_ref[:groups, :]
        top_ref[...] = top
        late_ref[...] = sum_ref[early * groups :, :]
        swap_out(place_ref[1], sum_ref[(rows - 1) * groups :, :], top, even_out, odd_out)
        early_sum = sum_ref.at[pl.ds(0, early * groups), :]
        backward_rows(early_sum, early, back_in[0], tables_in[1], back_in[1], back_in[2], back_mid_ref, back_full_ref)
        spread(place_ref, back_full_ref, early, early_refs)

    late_first, own_top, even2, odd2, *early_pieces = call(
        inner_body,
        [(late * groups, N2), row, row, row] + [(early * digits, N2)] * levels,
        [
            place, *inner_pieces, phi, *forward, backward[0], backward[2], backward[3],
            end_spectral, even, odd, ratio, inverse, edge,
        ],
        [SMEM] + [VMEM] * levels + [pl.ANY] + [VMEM] * 13,
        [
            vmem(pad_inner, N1, N2), vmem(pad_inner * N1, N2), vmem(inner * N1, N2), vmem(rows * groups, N2),
            vmem(pad_early, N1, N2), vmem(pad_early * N1, N2),
        ],
        (inner + early) * NLON * 256 * 4,
        "inner",
    )
    early_pieces = swap_levels(early_pieces)
    even2, odd2 = swap(even2, odd2)

    def second_body(place_ref, couple_ref, *refs):
        first_ref, own_top_ref, even_ref, odd_ref, even2_ref, odd2_ref, top_ref, bottom_ref = refs[:8]
        ratio_ref, inverse_ref, edge_ref = refs[8:11]
        tables_in, refs = refs[11:15], refs[15 + len(far) :]
        sigma_ref, late_refs = refs[0], refs[1 : 1 + levels]
        sum_ref, mid_ref, full_ref = refs[1 + levels :]
        got_top, got_bottom = swap_in(place_ref[1], even_ref[...], odd_ref[...])
        from_low, from_high = swap_in(place_ref[1], even2_ref[...], odd2_ref[...])
        low, high = sigmas(
            couple_ref[OV], couple_ref[OV + rows], own_top_ref[...], first_ref[(late - 1) * groups :, :],
            got_top, got_bottom, top_ref[...], bottom_ref[...], from_low, from_high,
            ratio_ref[:groups, :], ratio_ref[(rows - 1) * groups :, :], edge_ref,
        )
        sigma_ref[:groups, :] = low
        sigma_ref[groups:, :] = high
        late_refs[1][late * digits : late * digits + groups, :] = low
        late_refs[1][late * digits + groups :, :] = high

        def at(ref, index):
            return ref[index * groups : (index + 1) * groups, :]

        for i in range(half):
            j = rows - 1 - i
            if i:
                low = at(ratio_ref, i) * low
                high = at(ratio_ref, j) * high
            mid_ref[(j - half) * groups : (j - half + 1) * groups, :] = high
        x_high = at(edge_ref, 3) * high + at(edge_ref, 4) * low
        for j in range(half, rows):
            if j > half:
                x_high = at(mid_ref, j - half) * at(inverse_ref, j) + at(ratio_ref, j - 1) * x_high
            if j >= early:
                here = slice((j - early) * groups, (j - early + 1) * groups)
                sum_ref[here, :] = first_ref[here, :] + x_high
        backward_rows(sum_ref, late, *tables_in, mid_ref, full_ref)
        spread(place_ref, full_ref, late, late_refs)

    sigma, *late_pieces = call(
        second_body,
        [(2 * groups, N2)]
        + [(late * digits + (2 * groups if mask == 1 else 0), N2) for mask in range(levels)],
        [
            place, couple, late_first, own_top, even, odd, even2, odd2, sent_top, sent_bottom,
            ratio, inverse, edge, *backward, *early_pieces[2:],
        ],
        [SMEM, SMEM] + [VMEM] * 15 + [pl.ANY] * len(far),
        [vmem(late * groups, N2), vmem(max(pad_late, half) * N1, N2), vmem(pad_late, N1, N2)],
        late * NLON * 256 * 4,
        "second",
    )
    late_pieces = swap_levels(late_pieces)
    sigma_pieces = [sigma, late_pieces[1]] + [send_level(sigma, mask, levels) for mask in far]
    total = rows * levels * digits
    early_total = early * levels * digits
    part = const["first_back_part"]

    def correct(place_ref, *refs):
        pieces, sigma_refs, refs = refs[:levels], refs[levels : 2 * levels], refs[2 * levels :]
        phi_ref, psi_ref, part_ref, turn_ref, second_ref, special_ref = refs[:6]
        out_ref, sum_ref, mid_ref, done_ref, sem = refs[6:]
        part_rows = part_ref.shape[0] // levels
        mine = part_ref.at[pl.ds(pl.multiple_of(place_ref[0] * part_rows, part_rows), part_rows), :]
        size = early * groups
        for mask in range(levels):
            level = place_ref[0] ^ mask
            last = sigma_refs[mask].shape[0]
            low = sigma_refs[mask][last - 2 * groups : last - groups, :]
            high = sigma_refs[mask][last - groups :, :]
            first = pl.multiple_of(level * size, size)
            phi_all = phi_ref[pl.ds(first, size), :].reshape(early, groups, N2)
            psi_all = psi_ref[pl.ds(first, size), :].reshape(early, groups, N2)
            sum_ref[...] = (phi_all * low[None] + psi_all * high[None]).reshape(size, N2)
            spectral_back(sum_ref, early, pad_early, second_ref, special_ref, mid_ref)
            for pair in range(pad_early // (2 * BLOCK)):
                value = digits_back(mid_ref, pair, turn_ref, mine)
                for side in range(2):
                    begin = (2 * pair + side) * BLOCK
                    count = min(BLOCK, early - begin)
                    if count <= 0:
                        continue
                    lines = count * digits
                    whole = pieces[mask][begin * digits : begin * digits + lines, :]
                    done_ref[pl.ds(level + begin * digits * levels, lines, stride=levels), :] = (
                        whole + value[:lines, side * N2 : (side + 1) * N2]
                    )
        copy = pltpu.make_async_copy(done_ref, out_ref.at[pl.ds(0, early_total), :], sem)
        copy.start()
        copy.wait()

    (out,) = call(
        correct,
        [(total, N2)],
        [place, *early_pieces, *sigma_pieces, phi, psi, part, const["turn"], backward[2], backward[3]],
        [SMEM] + [VMEM] * (2 * levels + 6),
        [
            vmem(early * groups, N2), vmem(pad_early * N1, N2), vmem(early_total, N2), pltpu.SemaphoreType.DMA,
        ],
        levels * early * NLON * 256 * 3,
        "correct",
        out_spaces=[pl.ANY],
    )

    def unpack(place_ref, *refs):
        pieces = refs[:levels]
        out_ref, done_ref, sem = refs[levels + 1 :]
        for mask in range(levels):
            done_ref[pl.ds(place_ref[0] ^ mask, late * digits, stride=levels), :] = pieces[mask][: late * digits, :]
        copy = pltpu.make_async_copy(
            done_ref, out_ref.at[pl.ds(early_total, total - early_total), :], sem
        )
        copy.start()
        copy.wait()

    (out,) = call(
        unpack,
        [(total, N2)],
        [place, *late_pieces, out],
        [SMEM] + [VMEM] * levels + [pl.ANY],
        [vmem(total - early_total, N2), pltpu.SemaphoreType.DMA],
        0,
        "unpack",
        out_spaces=[pl.ANY],
        aliases={levels + 1: 0},
    )
    return out.reshape(rows, digits, levels, N2).transpose(0, 2, 1, 3).reshape(right_side.shape)


def second_part(
    rows, groups, parity, couple_ref, first_ref, even_ref, odd_ref, even2_ref, odd2_ref, top_ref, bottom_ref,
    ratio_ref, inverse_ref, edge_ref, out_ref, mid_ref,
):
    got_top, got_bottom = swap_in(parity, even_ref[...], odd_ref[...])
    low, high = swap_in(parity, even2_ref[...], odd2_ref[...])
    solve_second(
        rows, groups, couple_ref[OV], couple_ref[OV + rows],
        first_ref[:groups, :], first_ref[(rows - 1) * groups :, :],
        got_top, got_bottom, top_ref[...], bottom_ref[...], low, high,
        ratio_ref, inverse_ref, edge_ref, first_ref, out_ref, mid_ref,
    )


def shared_levels(const, right_side, lon_coef, lat_coef, level_scale):
    rows, levels, lon_count = right_side.shape
    lon_size = lax.axis_size("lon")
    assert lon_size % levels == 0 and GROUPS % (lon_size // levels) == 0 and rows % (lon_size // levels) == 0
    sharers = lon_size // levels
    groups = 2 * GROUPS // sharers
    part_rows = rows // sharers
    digits = N1 // lon_size
    lon_at = lax.axis_index("lon")
    parity = (lax.axis_index("lat") % 2).astype(jnp.int32).reshape(1)
    lon_window, couple = operator_parts(rows, lon_coef, lat_coef, level_scale)
    lon_window = lax.dynamic_index_in_dim(lon_window, lon_at // sharers, 0, False)
    couple = lax.dynamic_index_in_dim(couple, lon_at // sharers, 0, False)
    eigen = lax.dynamic_slice_in_dim(
        const["eigen"], (lon_at % sharers) * (groups // 2), groups // 2, axis=1
    ).reshape(groups, N2)
    ratio, inverse, edge = factor(rows, groups, lon_window, couple, eigen)
    block = (rows * groups, N2)
    row = (groups, N2)
    send = right_side.reshape(sharers, part_rows, levels, lon_count).transpose(2, 0, 1, 3)
    send = send.reshape(lon_size, part_rows, digits, N2)
    got = lax.all_to_all(send, "lon", 0, 0, tiled=True)
    points = got.transpose(1, 0, 2, 3).reshape(part_rows, N1, N2)
    padded = pad_rows(part_rows)

    def transform(points_ref, first_ref, turn_ref, second_ref, special_ref, out_ref, full_ref, mid_ref):
        full_ref[:part_rows] = points_ref[...]
        if padded > part_rows:
            full_ref[part_rows:] = jnp.zeros((padded - part_rows, N1, N2), jnp.float32)
        forward_rows(full_ref, part_rows, first_ref, turn_ref, second_ref, special_ref, mid_ref, out_ref)

    (spectral,) = call(
        transform,
        [(part_rows * N1, N2)],
        [points, const["first"], const["turn"], const["second"], const["special"]],
        [VMEM] * 5,
        [vmem(padded, N1, N2), vmem(padded * N1, N2)],
        part_rows * NLON * 256 * 4,
        "transform",
    )
    spectral = to_coefs(spectral, sharers, part_rows, groups)

    def edges(parity_ref, spec_ref, edge_ref, top_ref, bottom_ref, even_ref, odd_ref):
        top, bottom = edge_sums(
            rows_of(spec_ref, groups), rows_of(spec_ref, groups, OV - rows), edge_ref, groups
        )
        top_ref[...] = top
        bottom_ref[...] = bottom
        swap_out(parity_ref[0], top, bottom, even_ref, odd_ref)

    sent_top, sent_bottom, even, odd = call(
        edges, [row] * 4, [parity, spectral, edge], [SMEM, VMEM, VMEM], [], groups * N2 * 32, "edges"
    )
    even, odd = swap(even, odd)

    def first(parity_ref, spec_ref, even_ref, odd_ref, ratio_ref, inverse_ref, edge_ref, out_ref, e_ref, o_ref):
        low, high = swap_in(parity_ref[0], even_ref[...], odd_ref[...])
        solve_first(
            rows, groups, rows_of(spec_ref, groups), low, high, ratio_ref, inverse_ref, edge_ref, out_ref
        )
        swap_out(parity_ref[0], out_ref[(rows - 1) * groups :, :], out_ref[:groups, :], e_ref, o_ref)

    iterate, even2, odd2 = call(
        first,
        [block, row, row],
        [parity, spectral, even, odd, ratio, inverse, edge],
        [SMEM] + [VMEM] * 6,
        [],
        rows * groups * N2 * 8,
        "first_solve",
    )
    even2, odd2 = swap(even2, odd2)

    def second(parity_ref, *refs):
        second_part(rows, groups, parity_ref[0], *refs)

    (iterate,) = call(
        second,
        [block],
        [parity, couple, iterate, even, odd, even2, odd2, sent_top, sent_bottom, ratio, inverse, edge],
        [SMEM, SMEM] + [VMEM] * 10,
        [vmem(*block)],
        rows * groups * N2 * 8,
        "second_solve",
    )
    iterate = to_rows(iterate, sharers, part_rows, groups)

    def back(spec_ref, first_ref, turn_ref, second_ref, special_ref, out_ref, mid_ref, full_ref):
        backward_rows(spec_ref, part_rows, first_ref, turn_ref, second_ref, special_ref, mid_ref, full_ref)
        out_ref[...] = full_ref[:part_rows]

    (points,) = call(
        back,
        [(part_rows, N1, N2)],
        [iterate, const["first_back"], const["turn"], const["second_back"], const["special_back"]],
        [VMEM] * 5,
        [vmem(padded * N1, N2), vmem(padded, N1, N2)],
        part_rows * NLON * 256 * 4,
        "back_transform",
    )
    send = points.reshape(part_rows, lon_size, digits, N2).transpose(1, 0, 2, 3)
    got = lax.all_to_all(send, "lon", 0, 0, tiled=True)
    got = got.reshape(levels, sharers, part_rows, lon_count).transpose(1, 2, 0, 3)
    return got.reshape(rows, levels, lon_count)


def level_groups(sharers):
    size = lax.axis_size("lon")
    return [[first + i for i in range(sharers)] for first in range(0, size, sharers)]


def to_coefs(spectral, sharers, part_rows, groups):
    send = spectral.reshape(part_rows, 2, sharers, groups // 2, N2).transpose(2, 0, 1, 3, 4)
    got = lax.all_to_all(
        send, "lon", 0, 0, tiled=True, axis_index_groups=level_groups(sharers)
    )
    return got.reshape(sharers * part_rows * groups, N2)


def to_rows(values, sharers, part_rows, groups):
    send = values.reshape(sharers, part_rows, 2, groups // 2, N2)
    got = lax.all_to_all(
        send, "lon", 0, 0, tiled=True, axis_index_groups=level_groups(sharers)
    )
    return got.transpose(1, 2, 0, 3, 4).reshape(part_rows * N1, N2)


def solution(mesh):
    return jax.shard_map(
        on_device,
        mesh=mesh,
        in_specs=(P("lat", None, "lon"), P(), P(), P()),
        out_specs=P("lat", None, "lon"),
        check_vma=False,
    )
```

```python
import functools
import math

import jax
import jax.numpy as jnp
import numpy as np
from jax import lax
from jax.experimental import pallas as pl
from jax.experimental.pallas import tpu as pltpu
from jax.sharding import PartitionSpec as P

NLON = 4096
OV = 8
N1 = 32
N2 = 128
GROUPS = 16
BLOCK = 8

VMEM = pltpu.VMEM
SMEM = pltpu.SMEM


def numpy_split(table):
    import ml_dtypes

    table = np.asarray(table, np.float32)
    high = table.astype(ml_dtypes.bfloat16)
    low = (table - high.astype(np.float32)).astype(ml_dtypes.bfloat16)
    return high, low


def tables(levels):
    j1 = np.arange(N1)
    j2 = np.arange(N2)
    k2 = np.arange(N2)
    digit = np.arange(GROUPS)
    small = np.zeros((N1, N1))
    small[:GROUPS] = np.cos(2 * np.pi * np.outer(digit, j1) / N1)
    small[GROUPS] = np.cos(np.pi * j1)
    small[GROUPS + 1 :] = -np.sin(2 * np.pi * np.outer(digit[1:], j1) / N1)
    first = np.kron(np.eye(BLOCK), small)
    angle = 2 * np.pi * np.outer(digit, j2) / NLON
    turn_cos = np.cos(angle)
    turn_sin = np.sin(angle)
    phase = 2 * np.pi * (np.outer(j2, k2) % N2) / N2
    cosine, sine = np.cos(phase), np.sin(phase)
    second = np.block([[cosine, -sine], [sine, cosine]])
    special = np.zeros((2 * N2, 2 * N2))
    half = N2 // 2
    special[:N2, : half + 1] = np.cos(2 * np.pi * np.outer(j2, np.arange(half + 1)) / N2)
    special[:N2, half + 1 : N2] = -np.sin(2 * np.pi * np.outer(j2, np.arange(1, half)) / N2)
    odd = 2 * np.pi * np.outer(j2, 1 + 2 * np.arange(half)) / (2 * N2)
    special[N2:, N2 : N2 + half] = np.cos(odd)
    special[N2:, N2 + half :] = -np.sin(odd)
    weight = np.full(2 * N2, 2.0 / NLON)
    weight[0] = 1.0 / NLON
    weight[half] = 1.0 / NLON
    second_back = second.T * (2.0 / NLON)
    special_back = weight[:, None] * special.T
    wave = np.zeros((GROUPS, 2 * N2))
    wave[:, :N2] = digit[:, None] + N1 * k2[None, :]
    wave[:, N2:] = wave[:, :N2]
    lane = np.arange(N2)
    wave[0, :N2] = np.where(lane <= half, N1 * lane, N1 * (lane - half))
    wave[0, N2:] = 16 + N1 * (lane % half)
    eigen = 2.0 - 2.0 * np.cos(2 * np.pi * wave / NLON)
    pair = lambda t: np.concatenate(numpy_split(t), axis=0)
    width = N1 // levels
    part = [pair(np.kron(np.eye(BLOCK), small.T[at : at + width])) for at in range(0, N1, width)]
    return dict(
        first_back_part=np.concatenate(part, axis=0),
        first=pair(first),
        first_back=pair(first.T),
        second=pair(second),
        second_back=pair(second_back),
        special=pair(special),
        special_back=pair(special_back),
        turn=np.concatenate([turn_cos, turn_sin], axis=0).astype(np.float32),
        eigen=np.stack([eigen[:, :N2], eigen[:, N2:]]).astype(np.float32),
    )


def halves(value):
    high = value.astype(jnp.bfloat16)
    low = (value - high.astype(jnp.float32)).astype(jnp.bfloat16)
    return high, low


def dot(a, b):
    return lax.dot_general(a, b, (((1,), (0,)), ((), ())), preferred_element_type=jnp.float32)


def product_right(value, table_ref):
    size = table_ref.shape[0] // 2
    high, low = halves(value)
    table_high = table_ref[:size, :]
    return dot(high, table_high) + dot(low, table_high) + dot(high, table_ref[size:, :])


def product_left(table_ref, value):
    size = table_ref.shape[0] // 2
    high, low = halves(value)
    both = dot(table_ref[...], high)
    return both[:size] + both[size:] + dot(table_ref[:size, :], low)


def lanes_apart(value, rows):
    real = value[:, :N2].reshape(rows, GROUPS, N2)
    imag = value[:, N2:].reshape(rows, GROUPS, N2)
    return jnp.concatenate([real, imag], axis=1).reshape(rows * 2 * GROUPS, N2)


def lanes_together(value, rows):
    both = value.reshape(rows, 2 * GROUPS, N2)
    return jnp.concatenate([both[:, :GROUPS], both[:, GROUPS:]], axis=2).reshape(rows * GROUPS, 2 * N2)


def load_zeroth(ref, rows):
    return jnp.concatenate(
        [ref[pl.ds(0, rows, stride=2 * GROUPS), :], ref[pl.ds(GROUPS, rows, stride=2 * GROUPS), :]], axis=1
    )


def store_zeroth(ref, rows, value):
    ref[pl.ds(0, rows, stride=2 * GROUPS), :] = value[:, :N2]
    ref[pl.ds(GROUPS, rows, stride=2 * GROUPS), :] = value[:, N2:]


def forward_rows(points_ref, rows, first_ref, turn_ref, second_ref, special_ref, mid_ref, out_ref):
    padded = points_ref.shape[0]
    turn_cos = turn_ref[:GROUPS, :][None]
    turn_sin = turn_ref[GROUPS:, :][None]
    for pair in range(padded // (2 * BLOCK)):
        base = pair * 2 * BLOCK
        left = points_ref[base : base + BLOCK].reshape(BLOCK * N1, N2)
        right = points_ref[base + BLOCK : base + 2 * BLOCK].reshape(BLOCK * N1, N2)
        value = product_left(first_ref, jnp.concatenate([left, right], axis=1))
        for side in range(2):
            digits = value[:, side * N2 : (side + 1) * N2].reshape(BLOCK, N1, N2)
            real, imag = digits[:, :GROUPS], digits[:, GROUPS:]
            turned = jnp.concatenate(
                [real * turn_cos + imag * turn_sin, imag * turn_cos - real * turn_sin], axis=1
            )
            at = (base + side * BLOCK) * N1
            mid_ref[at : at + BLOCK * N1, :] = turned.reshape(BLOCK * N1, N2)
    result = product_right(lanes_together(mid_ref[...], padded), second_ref)
    out_ref[...] = lanes_apart(result, padded)[: rows * N1]
    store_zeroth(out_ref, rows, product_right(load_zeroth(mid_ref, padded), special_ref)[:rows])


def spectral_back(spec_ref, rows, padded, second_ref, special_ref, mid_ref):
    result = product_right(lanes_together(spec_ref[...], rows), second_ref)
    mid_ref[: rows * N1, :] = lanes_apart(result, rows)
    if padded > rows:
        mid_ref[rows * N1 : padded * N1, :] = jnp.zeros(((padded - rows) * N1, N2), jnp.float32)
    store_zeroth(mid_ref, rows, product_right(load_zeroth(spec_ref, rows), special_ref))


def digits_back(mid_ref, pair, turn_ref, first_ref):
    turn_cos = turn_ref[:GROUPS, :][None]
    turn_sin = turn_ref[GROUPS:, :][None]
    sides = []
    for side in range(2):
        at = (2 * pair + side) * BLOCK * N1
        both = mid_ref[at : at + BLOCK * N1, :].reshape(BLOCK, N1, N2)
        real, imag = both[:, :GROUPS], both[:, GROUPS:]
        turned = jnp.concatenate(
            [real * turn_cos - imag * turn_sin, imag * turn_cos + real * turn_sin], axis=1
        )
        sides.append(turned.reshape(BLOCK * N1, N2))
    return product_left(first_ref, jnp.concatenate(sides, axis=1))


def backward_rows(spec_ref, rows, first_ref, turn_ref, second_ref, special_ref, mid_ref, out_ref):
    padded = out_ref.shape[0]
    spectral_back(spec_ref, rows, padded, second_ref, special_ref, mid_ref)
    for pair in range(padded // (2 * BLOCK)):
        base = pair * 2 * BLOCK
        value = digits_back(mid_ref, pair, turn_ref, first_ref)
        out_ref[base : base + BLOCK] = value[:, :N2].reshape(BLOCK, N1, N2)
        out_ref[base + BLOCK : base + 2 * BLOCK] = value[:, N2:].reshape(BLOCK, N1, N2)


def factor_kernel(rows, lon_ref, couple_ref, eigen_ref, ratio_ref, inverse_ref, edge_ref):
    eigen = eigen_ref[...]
    groups = eigen.shape[0]
    half = rows // 2
    last = rows + 2 * OV - 1

    def plain(e):
        return 1.0 + lon_ref[e] * eigen

    def put(ref, index, value):
        ref[index * groups : (index + 1) * groups, :] = value

    def chain(start, stop, step, into):
        excess = inverse = None
        for e in range(start, stop + step, step):
            before = couple_ref[e] if step > 0 else couple_ref[e + 1]
            after = couple_ref[e + 1] if step > 0 else couple_ref[e]
            if inverse is None:
                ratio = None
                excess = plain(e) + before
            else:
                ratio = before * inverse
                excess = plain(e) + ratio * excess
            divisor = after + excess
            inverse = 1.0 / divisor
            into(e, ratio, inverse, excess, divisor)

    kept = {}

    def top(e, ratio, inverse, excess, divisor):
        if e == OV - 1:
            put(edge_ref, 0, inverse)
        if e >= OV:
            put(ratio_ref, e - OV, ratio)
            put(inverse_ref, e - OV, inverse)
        if e == OV + half - 1:
            kept["top"] = excess, divisor

    def bottom(e, ratio, inverse, excess, divisor):
        if e == OV + rows:
            put(edge_ref, 1, inverse)
        if e < OV + rows:
            put(ratio_ref, e - OV, ratio)
            put(inverse_ref, e - OV, inverse)
        if e == OV + half:
            kept["bottom"] = excess, divisor

    def next_band(e, ratio, inverse, excess, divisor):
        if ratio is not None:
            put(edge_ref, 7 + e - rows - 1, ratio)
        if e == OV + rows - 1:
            put(edge_ref, 5, inverse)

    def previous_band(e, ratio, inverse, excess, divisor):
        if ratio is not None:
            put(edge_ref, 14 + e - OV, ratio)
        if e == OV:
            put(edge_ref, 6, inverse)

    chain(rows, OV + rows - 1, 1, next_band)
    chain(2 * OV - 1, OV, -1, previous_band)
    chain(0, OV + half - 1, 1, top)
    chain(last, OV + half, -1, bottom)
    excess_top, divisor_top = kept["top"]
    excess_bottom, divisor_bottom = kept["bottom"]
    between = couple_ref[OV + half]
    inverse = 1.0 / (between * (excess_top + excess_bottom) + excess_top * excess_bottom)
    put(edge_ref, 2, divisor_bottom * inverse)
    put(edge_ref, 3, divisor_top * inverse)
    put(edge_ref, 4, between * inverse)


def edge_sums(low_rows, high_rows, next_ratio, previous_ratio):
    top = high_rows(0)
    for i in range(1, OV):
        top = high_rows(i) + next_ratio(i - 1) * top
    bottom = low_rows(OV - 1)
    for i in range(OV - 2, -1, -1):
        bottom = low_rows(i) + previous_ratio(i) * bottom
    return top, bottom


def swap_out(parity, up, down, even_ref, odd_ref):
    is_even = parity == 0
    even_ref[...] = jnp.where(is_even, up, down)
    odd_ref[...] = jnp.where(is_even, down, up)


def swap_in(parity, even, odd):
    is_even = parity == 0
    return jnp.where(is_even, odd, even), jnp.where(is_even, even, odd)


def solve_first(rows, groups, right_side_row, from_low, from_high, ratio_ref, inverse_ref, edge_ref, out_ref):
    half = rows // 2

    def at(ref, index):
        return ref[index * groups : (index + 1) * groups, :]

    def put(index, value):
        out_ref[index * groups : (index + 1) * groups, :] = value

    low, high = from_low, from_high
    for i in range(half):
        j = rows - 1 - i
        low = right_side_row(i) + at(ratio_ref, i) * low
        high = right_side_row(j) + at(ratio_ref, j) * high
        put(i, low)
        put(j, high)
    meet(rows, groups, low, high, ratio_ref, inverse_ref, edge_ref, at, lambda i: at(out_ref, i), put)


def meet(rows, groups, low, high, ratio_ref, inverse_ref, edge_ref, at, value, put):
    half = rows // 2
    between = at(edge_ref, 4)
    x_low = at(edge_ref, 2) * low + between * high
    x_high = at(edge_ref, 3) * high + between * low
    put(half - 1, x_low)
    put(half, x_high)
    for i in range(half - 2, -1, -1):
        j = rows - 1 - i
        x_low = value(i) * at(inverse_ref, i) + at(ratio_ref, i + 1) * x_low
        x_high = value(j) * at(inverse_ref, j) + at(ratio_ref, j - 1) * x_high
        put(i, x_low)
        put(j, x_high)


def sigmas(
    couple_low, couple_high, own_top, own_bottom, got_top, got_bottom, sent_top, sent_bottom, from_low, from_high,
    ratio_first, ratio_last, edge_ref, next_inverse, previous_inverse,
):
    groups = own_top.shape[0]

    def edge(index):
        return edge_ref[index * groups : (index + 1) * groups, :]

    beyond_low = (got_top + couple_low * own_top) * edge(0)
    beyond_high = (got_bottom + couple_high * own_bottom) * edge(1)
    theirs_low = (sent_bottom + couple_low * from_low) * previous_inverse
    theirs_high = (sent_top + couple_high * from_high) * next_inverse
    low = ratio_first * (couple_low * (own_top - theirs_low)) + couple_low * (from_low - beyond_low)
    high = ratio_last * (couple_high * (own_bottom - theirs_high)) + couple_high * (from_high - beyond_high)
    return low, high


def solve_second(
    rows, groups, couple_low, couple_high, own_top, own_bottom, got_top, got_bottom, sent_top, sent_bottom,
    from_low, from_high, ratio_ref, inverse_ref, edge_ref, first_ref, out_ref, mid_ref,
):
    half = rows // 2

    def at(ref, index):
        return ref[index * groups : (index + 1) * groups, :]

    low, high = sigmas(
        couple_low, couple_high, own_top, own_bottom, got_top, got_bottom, sent_top, sent_bottom,
        from_low, from_high, at(ratio_ref, 0), at(ratio_ref, rows - 1), edge_ref, at(edge_ref, 5), at(edge_ref, 6),
    )
    for i in range(half):
        j = rows - 1 - i
        if i:
            low = at(ratio_ref, i) * low
            high = at(ratio_ref, j) * high
        mid_ref[i * groups : (i + 1) * groups, :] = low
        mid_ref[j * groups : (j + 1) * groups, :] = high

    def put(index, value):
        rows_at = slice(index * groups, (index + 1) * groups)
        out_ref[rows_at, :] = first_ref[rows_at, :] + value

    meet(rows, groups, low, high, ratio_ref, inverse_ref, edge_ref, at, lambda i: at(mid_ref, i), put)


def call(body, outs, ins, spaces, scratch, flops, name, out_spaces=None, aliases=None, limit=48):
    nbytes = sum(x.size * x.dtype.itemsize for x in ins) + sum(4 * math.prod(s) for s in outs)
    out = pl.pallas_call(
        body,
        out_shape=[jax.ShapeDtypeStruct(s, jnp.float32) for s in outs],
        in_specs=[pl.BlockSpec(memory_space=s) for s in spaces],
        out_specs=[pl.BlockSpec(memory_space=s) for s in out_spaces or [VMEM] * len(outs)],
        input_output_aliases=aliases or {},
        scratch_shapes=scratch,
        compiler_params=pltpu.CompilerParams(vmem_limit_bytes=limit << 20),
        cost_estimate=pl.CostEstimate(flops=flops, bytes_accessed=nbytes, transcendentals=0),
        name=name,
    )(*ins)
    return out


def pad_rows(rows):
    return -(-rows // (2 * BLOCK)) * 2 * BLOCK


def swap(value_even, value_odd):
    count = lax.axis_size("lat")
    even = [(i, i ^ 1) for i in range(count) if (i ^ 1) < count]
    odd = [(i, ((i + 1) ^ 1) - 1) for i in range(1, count) if ((i + 1) ^ 1) - 1 < count]
    return lax.ppermute(value_even, "lat", even), lax.ppermute(value_odd, "lat", odd)


def send_level(piece, mask, size):
    return lax.ppermute(piece, "lon", [(d, d ^ mask) for d in range(size)])


def swap_levels(pieces):
    return [pieces[0]] + [send_level(pieces[mask], mask, len(pieces)) for mask in range(1, len(pieces))]


def operator_parts(rows, lon_coef, lat_coef, level_scale):
    row_first = lax.axis_index("lat") * rows
    extent = rows + 2 * OV
    lon_window = lax.dynamic_slice_in_dim(jnp.pad(lon_coef, (OV, OV)), row_first, extent)
    couple = lax.dynamic_slice_in_dim(jnp.pad(lat_coef, (OV + 1, OV + 2)), row_first, extent + 1)
    return level_scale[:, None] * lon_window[None], level_scale[:, None] * couple[None]


def factor(rows, groups, lon_window, couple, eigen):
    block = (rows * groups, N2)
    return call(
        functools.partial(factor_kernel, rows),
        [block, block, (21 * groups, N2)],
        [lon_window, couple, eigen],
        [SMEM, SMEM, VMEM],
        [],
        rows * groups * N2 * 20,
        "factor",
    )


def vmem(*shape):
    return pltpu.VMEM(shape, jnp.float32)


def rows_of(ref, groups, first=0):
    return lambda i: ref[(i - first) * groups : (i - first + 1) * groups, :]


def on_device(right_side, lon_coef, lat_coef, level_scale):
    const = {k: jnp.asarray(v) for k, v in tables(right_side.shape[1]).items()}
    if lax.axis_size("lon") != right_side.shape[1]:
        return shared_levels(const, right_side, lon_coef, lat_coef, level_scale)
    return whole_levels(const, right_side, lon_coef, lat_coef, level_scale)


def early_rows(rows):
    return rows // 2 + 2


def edge_kernel(rows, level_ref, lon_ref, couple_ref, eigen_ref, out_ref):
    eigen = eigen_ref[...]
    groups = eigen.shape[0]
    level = level_ref[0]
    low = high = low_inverse = high_inverse = None
    for i in range(OV):
        e, f = rows + i, 2 * OV - 1 - i
        if i == 0:
            low = 1.0 + lon_ref[level, e] * eigen + couple_ref[level, e]
            high = 1.0 + lon_ref[level, f] * eigen + couple_ref[level, f + 1]
        else:
            low_ratio = couple_ref[level, e] * low_inverse
            high_ratio = couple_ref[level, f + 1] * high_inverse
            out_ref[(i - 1) * groups : i * groups, :] = low_ratio
            out_ref[(OV + i - 1) * groups : (OV + i) * groups, :] = high_ratio
            low = 1.0 + lon_ref[level, e] * eigen + low_ratio * low
            high = 1.0 + lon_ref[level, f] * eigen + high_ratio * high
        low_inverse = 1.0 / (couple_ref[level, e + 1] + low)
        high_inverse = 1.0 / (couple_ref[level, f] + high)
    out_ref[(OV - 1) * groups : OV * groups, :] = low_inverse
    out_ref[(2 * OV - 1) * groups :, :] = high_inverse


def level_response(rows, early, level, lon_ref, couple_ref, eigen, put_ratio, put_inverse, keep, tables):
    half = rows // 2
    ratio_at, value_at, put_value, put_phi, put_psi = tables

    def plain(e):
        return 1.0 + lon_ref[level, e] * eigen

    low = high = None
    low_inverse = high_inverse = low_value = high_value = None
    for i in range(-OV, half):
        j = rows - 1 - i
        e, f = i + OV, j + OV
        if low is None:
            low = plain(e) + couple_ref[level, e]
            high = plain(f) + couple_ref[level, f + 1]
        else:
            low_ratio = couple_ref[level, e] * low_inverse
            high_ratio = couple_ref[level, f + 1] * high_inverse
            low = plain(e) + low_ratio * low
            high = plain(f) + high_ratio * high
        low_divisor = couple_ref[level, e + 1] + low
        high_divisor = couple_ref[level, f] + high
        low_inverse = 1.0 / low_divisor
        high_inverse = 1.0 / high_divisor
        if i == -1:
            keep(0, low_inverse)
            keep(1, high_inverse)
        if i == 0:
            low_value = high_value = jnp.ones_like(eigen)
        elif i > 0:
            low_value = low_ratio * low_value
            high_value = high_ratio * high_value
        if i >= 0:
            put_ratio(i, low_ratio)
            put_ratio(j, high_ratio)
            put_inverse(i, low_inverse)
            put_inverse(j, high_inverse)
            put_value(i, low_value * low_inverse)
            if j < early:
                put_value(j, high_value * high_inverse)
    between = couple_ref[level, OV + half]
    inverse = 1.0 / (between * (low + high) + low * high)
    across = between * inverse
    high_inverse = high_divisor * inverse
    low_inverse = low_divisor * inverse
    keep(2, high_inverse)
    keep(3, low_inverse)
    keep(4, across)
    phi = high_inverse * low_value
    psi = across * high_value
    phi_down = across * low_value
    psi_down = low_inverse * high_value
    put_phi(half - 1, phi)
    put_psi(half - 1, psi)
    for i in range(half - 2, -1, -1):
        ratio = ratio_at(i + 1)
        phi = value_at(i) + ratio * phi
        psi = ratio * psi
        put_phi(i, phi)
        put_psi(i, psi)
    put_phi(half, phi_down)
    put_psi(half, psi_down)
    for j in range(half + 1, early):
        ratio = ratio_at(j - 1)
        phi_down = ratio * phi_down
        psi_down = value_at(j) + ratio * psi_down
        put_phi(j, phi_down)
        put_psi(j, psi_down)


def getter(ref, groups):
    return lambda index: ref[index * groups : (index + 1) * groups, :]


def putter(ref, groups, first=0):
    def put(index, value):
        at = first + index * groups
        ref[pl.ds(at if isinstance(at, int) else pl.multiple_of(at, groups), groups), :] = value

    return put


def own_kernel(
    rows, early, place_ref, lon_ref, couple_ref, eigen_ref, ratio_ref, inverse_ref, edge_ref, phi_ref, psi_ref, value_ref
):
    groups = eigen_ref.shape[0]
    level_response(
        rows, early, place_ref[0], lon_ref, couple_ref, eigen_ref[...], putter(ratio_ref, groups),
        putter(inverse_ref, groups), putter(edge_ref, groups),
        (
            getter(ratio_ref, groups), getter(value_ref, groups), putter(value_ref, groups),
            putter(phi_ref, groups), putter(psi_ref, groups),
        ),
    )


def partners_kernel(
    rows, early, levels, place_ref, lon_ref, couple_ref, eigen_ref, after_ref, phi_ref, psi_ref, kept_ref, value_ref
):
    del after_ref
    eigen = eigen_ref[...]
    groups = eigen.shape[0]

    def partner(mask, carry):
        def nothing(index, value):
            pass

        put_kept = putter(kept_ref, groups)

        def put_ratio(index, value):
            if index < early:
                put_kept(index, value)

        first = (mask - 1) * (early * groups)
        level_response(
            rows, early, place_ref[0] ^ mask, lon_ref, couple_ref, eigen, put_ratio, nothing, nothing,
            (
                getter(kept_ref, groups), getter(value_ref, groups), putter(value_ref, groups),
                putter(phi_ref, groups, first), putter(psi_ref, groups, first),
            ),
        )
        return carry

    lax.fori_loop(1, levels, partner, 0)


def whole_levels(const, right_side, lon_coef, lat_coef, level_scale):
    rows, levels, lon_count = right_side.shape
    digits = N1 // levels
    groups = 2 * GROUPS
    lon_at = lax.axis_index("lon").astype(jnp.int32)
    parity = (lax.axis_index("lat") % 2).astype(jnp.int32)
    place = jnp.stack([lon_at, parity])
    half = rows // 2
    early = early_rows(rows)
    late = rows - early
    eigen = const["eigen"].reshape(groups, N2)
    lon_all, couple_all = operator_parts(rows, lon_coef, lat_coef, level_scale)
    (around,) = call(
        functools.partial(edge_kernel, rows),
        [(2 * OV * groups, N2)],
        [place, lon_all, couple_all, eigen],
        [SMEM, SMEM, SMEM, VMEM],
        [],
        16 * groups * N2 * 20,
        "edge",
    )
    block = (rows * groups, N2)
    early_block = (early * groups, N2)
    ratio, inverse, edge, phi, psi = call(
        functools.partial(own_kernel, rows, early),
        [block, block, (5 * groups, N2), early_block, early_block],
        [place, lon_all, couple_all, eigen],
        [SMEM, SMEM, SMEM, VMEM],
        [vmem(*early_block)],
        rows * groups * N2 * 20,
        "own",
    )
    row = (groups, N2)
    ends = 2 * OV
    inner = rows - ends
    span = OV * digits
    by_row = right_side.reshape(rows, levels, digits, N2).transpose(0, 2, 1, 3).reshape(-1, N2)

    far = list(range(2, levels))

    def pack_ends(place_ref, in_ref, *refs):
        out_refs, (low_ref, high_ref, sems) = refs[:-3], refs[-3:]
        low = pltpu.make_async_copy(in_ref.at[pl.ds(0, levels * span), :], low_ref, sems.at[0])
        high = pltpu.make_async_copy(
            in_ref.at[pl.ds(levels * (rows - OV) * digits, levels * span), :], high_ref, sems.at[1]
        )
        low.start()
        high.start()
        low.wait()
        high.wait()
        for out_ref, mask in zip(out_refs, [0] + far):
            level = place_ref[0] ^ mask
            out_ref[:span, :] = low_ref[pl.ds(level, span, stride=levels), :]
            out_ref[span:, :] = high_ref[pl.ds(level, span, stride=levels), :]

    end_packed = call(
        pack_ends,
        [(ends * digits, N2)] * (1 + len(far)),
        [place, by_row],
        [SMEM, pltpu.HBM],
        [vmem(levels * span, N2), vmem(levels * span, N2), pltpu.SemaphoreType.DMA((2,))],
        0,
        "pack_ends",
        limit=58,
    )

    def pack(place_ref, in_ref, after_ref, *out_refs):
        del after_ref
        for mask, out_ref in enumerate(out_refs):
            level = place_ref[0] ^ mask
            skip = 0 if mask == 1 else span
            out_ref[...] = in_ref[pl.ds(level + levels * skip, out_ref.shape[0], stride=levels), :]

    packed = call(
        pack,
        [((rows if mask == 1 else inner) * digits, N2) for mask in range(levels)],
        [place, by_row, end_packed[0]],
        [SMEM, VMEM, pl.ANY],
        [],
        0,
        "pack",
    )
    end_pieces = [end_packed[0], None] + [send_level(p, m, levels) for p, m in zip(end_packed[1:], far)]
    near = send_level(packed[1], 1, levels)
    end_pieces[1] = near
    inner_pieces = [packed[0], near] + [send_level(packed[m], m, levels) for m in far]
    forward = [const["first"], const["turn"], const["second"], const["special"]]
    pad_ends, pad_inner = pad_rows(ends), pad_rows(inner)

    def ends_body(place_ref, *refs):
        pieces, refs = refs[:levels], refs[levels:]
        tables_in, edge_ref = refs[:4], refs[4]
        spec_ref, top_ref, bottom_ref, even_ref, odd_ref, full_ref, mid_ref = refs[5:]
        for mask, piece in enumerate(pieces):
            at = pl.multiple_of((place_ref[0] ^ mask) * digits, digits)
            last = piece.shape[0] - span
            full_ref[:OV, pl.ds(at, digits), :] = piece[:span, :].reshape(OV, digits, N2)
            full_ref[OV:ends, pl.ds(at, digits), :] = piece[last:, :].reshape(OV, digits, N2)
        forward_rows(full_ref, ends, *tables_in, mid_ref, spec_ref)
        top, bottom = edge_sums(
            rows_of(spec_ref, groups), rows_of(spec_ref, groups, -OV),
            rows_of(edge_ref, groups), lambda i: edge_ref[(2 * OV - 2 - i) * groups : (2 * OV - 1 - i) * groups, :],
        )
        top_ref[...] = top
        bottom_ref[...] = bottom
        swap_out(place_ref[1], top, bottom, even_ref, odd_ref)

    end_spectral, sent_top, sent_bottom, even, odd = call(
        ends_body,
        [(ends * groups, N2)] + [row] * 4,
        [place, *end_pieces, *forward, around],
        [SMEM] + [VMEM] * (levels + 5),
        [vmem(pad_ends, N1, N2), vmem(pad_ends * N1, N2)],
        ends * NLON * 256 * 4,
        "ends",
    )
    even, odd = swap(even, odd)
    backward = [const["first_back"], const["turn"], const["second_back"], const["special_back"]]
    pad_early, pad_late = pad_rows(early), pad_rows(late)

    def spread(place_ref, full_ref, count, out_refs):
        for mask, out_ref in enumerate(out_refs):
            at = pl.multiple_of((place_ref[0] ^ mask) * digits, digits)
            out_ref[: count * digits, :] = full_ref[:count, pl.ds(at, digits), :].reshape(count * digits, N2)

    def inner_body(place_ref, *refs):
        pieces, refs = refs[:levels], refs[levels:]
        tables_in, back_in, refs = refs[:4], refs[4:7], refs[7:]
        ends_ref, even_ref, odd_ref, ratio_ref, inverse_ref, edge_ref = refs[:6]
        late_ref, top_ref, even_out, odd_out = refs[6:10]
        early_refs, refs = refs[10 : 10 + levels], refs[10 + levels :]
        full_ref, mid_ref, spec_ref, sum_ref, back_full_ref, back_mid_ref = refs
        for mask, piece in enumerate(pieces):
            at = pl.multiple_of((place_ref[0] ^ mask) * digits, digits)
            skip = span if mask == 1 else 0
            full_ref[:inner, pl.ds(at, digits), :] = piece[skip : skip + inner * digits, :].reshape(
                inner, digits, N2
            )
        if pad_inner > inner:
            full_ref[inner:] = jnp.zeros((pad_inner - inner, N1, N2), jnp.float32)
        forward_rows(full_ref, inner, *tables_in, mid_ref, spec_ref)
        low, high = swap_in(place_ref[1], even_ref[...], odd_ref[...])

        def spec_row(i):
            if i < OV:
                return rows_of(ends_ref, groups)(i)
            if i >= rows - OV:
                return rows_of(ends_ref, groups, rows - ends)(i)
            return rows_of(spec_ref, groups, OV)(i)

        solve_first(rows, groups, spec_row, low, high, ratio_ref, inverse_ref, edge_ref, sum_ref)
        top = sum_ref[:groups, :]
        top_ref[...] = top
        late_ref[...] = sum_ref[early * groups :, :]
        swap_out(place_ref[1], sum_ref[(rows - 1) * groups :, :], top, even_out, odd_out)
        early_sum = sum_ref.at[pl.ds(0, early * groups), :]
        backward_rows(early_sum, early, back_in[0], tables_in[1], back_in[1], back_in[2], back_mid_ref, back_full_ref)
        spread(place_ref, back_full_ref, early, early_refs)

    late_first, own_top, even2, odd2, *early_pieces = call(
        inner_body,
        [(late * groups, N2), row, row, row] + [(early * digits, N2)] * levels,
        [
            place, *inner_pieces, *forward, backward[0], backward[2], backward[3],
            end_spectral, even, odd, ratio, inverse, edge,
        ],
        [SMEM] + [VMEM] * (levels + 13),
        [
            vmem(pad_inner, N1, N2), vmem(pad_inner * N1, N2), vmem(inner * N1, N2), vmem(rows * groups, N2),
            vmem(pad_early, N1, N2), vmem(pad_early * N1, N2),
        ],
        (inner + early) * NLON * 256 * 4,
        "inner",
    )
    early_pieces = swap_levels(early_pieces)
    even2, odd2 = swap(even2, odd2)

    def sigma_body(place_ref, couple_ref, *refs):
        first_ref, own_top_ref, even_ref, odd_ref, even2_ref, odd2_ref, top_ref, bottom_ref = refs[:8]
        ratio_ref, edge_ref, around_ref = refs[8:11]
        sigma_ref = refs[-1]
        level = place_ref[0]
        got_top, got_bottom = swap_in(place_ref[1], even_ref[...], odd_ref[...])
        from_low, from_high = swap_in(place_ref[1], even2_ref[...], odd2_ref[...])
        low, high = sigmas(
            couple_ref[level, OV], couple_ref[level, OV + rows], own_top_ref[...], first_ref[(late - 1) * groups :, :],
            got_top, got_bottom, top_ref[...], bottom_ref[...], from_low, from_high,
            ratio_ref[:groups, :], ratio_ref[(rows - 1) * groups :, :], edge_ref,
            around_ref[(OV - 1) * groups : OV * groups, :], around_ref[(2 * OV - 1) * groups :, :],
        )
        sigma_ref[:groups, :] = low
        sigma_ref[groups:, :] = high

    (sigma,) = call(
        sigma_body,
        [(2 * groups, N2)],
        [
            place, couple_all, late_first, own_top, even, odd, even2, odd2, sent_top, sent_bottom, ratio, edge, around,
            *early_pieces[1:],
        ],
        [SMEM, SMEM] + [VMEM] * 11 + [pl.ANY] * (levels - 1),
        [],
        groups * N2 * 40,
        "sigma",
    )
    far_sigma = [send_level(sigma, mask, levels) for mask in far]
    phi_others, psi_others = call(
        functools.partial(partners_kernel, rows, early, levels),
        [((levels - 1) * early * groups, N2)] * 2,
        [place, lon_all, couple_all, eigen, sigma],
        [SMEM, SMEM, SMEM, VMEM, pl.ANY],
        [vmem(*early_block), vmem(*early_block)],
        (levels - 1) * rows * groups * N2 * 20,
        "partners",
    )

    def second_body(place_ref, *refs):
        sigma_ref, first_ref, ratio_ref, inverse_ref, edge_ref = refs[:5]
        tables_in, refs = refs[5:9], refs[9:]
        late_refs = refs[:levels]
        sum_ref, mid_ref, full_ref = refs[levels:]
        low, high = sigma_ref[:groups, :], sigma_ref[groups:, :]

        def at(ref, index):
            return ref[index * groups : (index + 1) * groups, :]

        for i in range(half):
            j = rows - 1 - i
            if i:
                low = at(ratio_ref, i) * low
                high = at(ratio_ref, j) * high
            mid_ref[(j - half) * groups : (j - half + 1) * groups, :] = high
        x_high = at(edge_ref, 3) * high + at(edge_ref, 4) * low
        for j in range(half, rows):
            if j > half:
                x_high = at(mid_ref, j - half) * at(inverse_ref, j) + at(ratio_ref, j - 1) * x_high
            if j >= early:
                here = slice((j - early) * groups, (j - early + 1) * groups)
                sum_ref[here, :] = first_ref[here, :] + x_high
        backward_rows(sum_ref, late, *tables_in, mid_ref, full_ref)
        spread(place_ref, full_ref, late, late_refs)
        late_refs[1][late * digits :, :] = sigma_ref[...]

    late_pieces = call(
        second_body,
        [(late * digits + (2 * groups if mask == 1 else 0), N2) for mask in range(levels)],
        [place, sigma, late_first, ratio, inverse, edge, *backward],
        [SMEM] + [VMEM] * 9,
        [vmem(late * groups, N2), vmem(max(pad_late, half) * N1, N2), vmem(pad_late, N1, N2)],
        late * NLON * 256 * 4,
        "second",
    )
    late_pieces = swap_levels(late_pieces)
    sigma_pieces = [sigma, late_pieces[1], *far_sigma]
    total = rows * levels * digits
    early_total = early * levels * digits
    part = const["first_back_part"]

    def correct(place_ref, *refs):
        pieces, sigma_refs, refs = refs[:levels], refs[levels : 2 * levels], refs[2 * levels :]
        phi_ref, psi_ref, phi_others_ref, psi_others_ref, part_ref, turn_ref, second_ref, special_ref = refs[:8]
        out_ref, sum_ref, mid_ref, done_ref, sem = refs[8:]
        part_rows = part_ref.shape[0] // levels
        mine = part_ref.at[pl.ds(pl.multiple_of(place_ref[0] * part_rows, part_rows), part_rows), :]
        size = early * groups
        for mask in range(levels):
            level = place_ref[0] ^ mask
            last = sigma_refs[mask].shape[0]
            low = sigma_refs[mask][last - 2 * groups : last - groups, :]
            high = sigma_refs[mask][last - groups :, :]
            first = (mask - 1) * size
            phi_all = phi_others_ref[first : first + size, :] if mask else phi_ref[...]
            psi_all = psi_others_ref[first : first + size, :] if mask else psi_ref[...]
            phi_all = phi_all.reshape(early, groups, N2)
            psi_all = psi_all.reshape(early, groups, N2)
            sum_ref[...] = (phi_all * low[None] + psi_all * high[None]).reshape(size, N2)
            spectral_back(sum_ref, early, pad_early, second_ref, special_ref, mid_ref)
            for pair in range(pad_early // (2 * BLOCK)):
                value = digits_back(mid_ref, pair, turn_ref, mine)
                for side in range(2):
                    begin = (2 * pair + side) * BLOCK
                    count = min(BLOCK, early - begin)
                    if count <= 0:
                        continue
                    lines = count * digits
                    whole = pieces[mask][begin * digits : begin * digits + lines, :]
                    done_ref[pl.ds(level + begin * digits * levels, lines, stride=levels), :] = (
                        whole + value[:lines, side * N2 : (side + 1) * N2]
                    )
        copy = pltpu.make_async_copy(done_ref, out_ref.at[pl.ds(0, early_total), :], sem)
        copy.start()
        copy.wait()

    (out,) = call(
        correct,
        [(total, N2)],
        [place, *early_pieces, *sigma_pieces, phi, psi, phi_others, psi_others, part, const["turn"], *backward[2:]],
        [SMEM] + [VMEM] * (2 * levels + 8),
        [
            vmem(early * groups, N2), vmem(pad_early * N1, N2), vmem(early_total, N2), pltpu.SemaphoreType.DMA,
        ],
        levels * early * NLON * 256 * 40,
        "correct",
        out_spaces=[pl.ANY],
    )

    chunks = 4

    def unpack(place_ref, *refs):
        pieces = refs[:levels]
        out_ref, done_ref, sems = refs[levels + 1 :]
        lines = late * digits // chunks
        copies = []
        for chunk in range(chunks):
            for mask in range(levels):
                first = (place_ref[0] ^ mask) + chunk * lines * levels
                done_ref[pl.ds(first, lines, stride=levels), :] = pieces[mask][chunk * lines : (chunk + 1) * lines, :]
            here = pl.ds(chunk * lines * levels, lines * levels)
            there = pl.ds(early_total + chunk * lines * levels, lines * levels)
            copy = pltpu.make_async_copy(done_ref.at[here, :], out_ref.at[there, :], sems.at[chunk])
            copy.start()
            copies.append(copy)
        for copy in copies:
            copy.wait()

    (out,) = call(
        unpack,
        [(total, N2)],
        [place, *late_pieces, out],
        [SMEM] + [VMEM] * levels + [pl.ANY],
        [vmem(total - early_total, N2), pltpu.SemaphoreType.DMA((chunks,))],
        0,
        "unpack",
        out_spaces=[pl.ANY],
        aliases={levels + 1: 0},
    )
    return out.reshape(rows, digits, levels, N2).transpose(0, 2, 1, 3).reshape(right_side.shape)


def second_part(
    rows, groups, parity, couple_ref, first_ref, even_ref, odd_ref, even2_ref, odd2_ref, top_ref, bottom_ref,
    ratio_ref, inverse_ref, edge_ref, out_ref, mid_ref,
):
    got_top, got_bottom = swap_in(parity, even_ref[...], odd_ref[...])
    low, high = swap_in(parity, even2_ref[...], odd2_ref[...])
    solve_second(
        rows, groups, couple_ref[OV], couple_ref[OV + rows],
        first_ref[:groups, :], first_ref[(rows - 1) * groups :, :],
        got_top, got_bottom, top_ref[...], bottom_ref[...], low, high,
        ratio_ref, inverse_ref, edge_ref, first_ref, out_ref, mid_ref,
    )


def shared_levels(const, right_side, lon_coef, lat_coef, level_scale):
    rows, levels, lon_count = right_side.shape
    lon_size = lax.axis_size("lon")
    assert lon_size % levels == 0 and GROUPS % (lon_size // levels) == 0 and rows % (lon_size // levels) == 0
    sharers = lon_size // levels
    groups = 2 * GROUPS // sharers
    part_rows = rows // sharers
    digits = N1 // lon_size
    lon_at = lax.axis_index("lon")
    parity = (lax.axis_index("lat") % 2).astype(jnp.int32).reshape(1)
    lon_window, couple = operator_parts(rows, lon_coef, lat_coef, level_scale)
    lon_window = lax.dynamic_index_in_dim(lon_window, lon_at // sharers, 0, False)
    couple = lax.dynamic_index_in_dim(couple, lon_at // sharers, 0, False)
    eigen = lax.dynamic_slice_in_dim(
        const["eigen"], (lon_at % sharers) * (groups // 2), groups // 2, axis=1
    ).reshape(groups, N2)
    ratio, inverse, edge = factor(rows, groups, lon_window, couple, eigen)
    block = (rows * groups, N2)
    row = (groups, N2)
    send = right_side.reshape(sharers, part_rows, levels, lon_count).transpose(2, 0, 1, 3)
    send = send.reshape(lon_size, part_rows, digits, N2)
    got = lax.all_to_all(send, "lon", 0, 0, tiled=True)
    points = got.transpose(1, 0, 2, 3).reshape(part_rows, N1, N2)
    padded = pad_rows(part_rows)

    def transform(points_ref, first_ref, turn_ref, second_ref, special_ref, out_ref, full_ref, mid_ref):
        full_ref[:part_rows] = points_ref[...]
        if padded > part_rows:
            full_ref[part_rows:] = jnp.zeros((padded - part_rows, N1, N2), jnp.float32)
        forward_rows(full_ref, part_rows, first_ref, turn_ref, second_ref, special_ref, mid_ref, out_ref)

    (spectral,) = call(
        transform,
        [(part_rows * N1, N2)],
        [points, const["first"], const["turn"], const["second"], const["special"]],
        [VMEM] * 5,
        [vmem(padded, N1, N2), vmem(padded * N1, N2)],
        part_rows * NLON * 256 * 4,
        "transform",
    )
    spectral = to_coefs(spectral, sharers, part_rows, groups)

    def edges(parity_ref, spec_ref, edge_ref, top_ref, bottom_ref, even_ref, odd_ref):
        top, bottom = edge_sums(
            rows_of(spec_ref, groups), rows_of(spec_ref, groups, OV - rows),
            rows_of(edge_ref, groups, -7), rows_of(edge_ref, groups, -14),
        )
        top_ref[...] = top
        bottom_ref[...] = bottom
        swap_out(parity_ref[0], top, bottom, even_ref, odd_ref)

    sent_top, sent_bottom, even, odd = call(
        edges, [row] * 4, [parity, spectral, edge], [SMEM, VMEM, VMEM], [], groups * N2 * 32, "edges"
    )
    even, odd = swap(even, odd)

    def first(parity_ref, spec_ref, even_ref, odd_ref, ratio_ref, inverse_ref, edge_ref, out_ref, e_ref, o_ref):
        low, high = swap_in(parity_ref[0], even_ref[...], odd_ref[...])
        solve_first(
            rows, groups, rows_of(spec_ref, groups), low, high, ratio_ref, inverse_ref, edge_ref, out_ref
        )
        swap_out(parity_ref[0], out_ref[(rows - 1) * groups :, :], out_ref[:groups, :], e_ref, o_ref)

    iterate, even2, odd2 = call(
        first,
        [block, row, row],
        [parity, spectral, even, odd, ratio, inverse, edge],
        [SMEM] + [VMEM] * 6,
        [],
        rows * groups * N2 * 8,
        "first_solve",
    )
    even2, odd2 = swap(even2, odd2)

    def second(parity_ref, *refs):
        second_part(rows, groups, parity_ref[0], *refs)

    (iterate,) = call(
        second,
        [block],
        [parity, couple, iterate, even, odd, even2, odd2, sent_top, sent_bottom, ratio, inverse, edge],
        [SMEM, SMEM] + [VMEM] * 10,
        [vmem(*block)],
        rows * groups * N2 * 8,
        "second_solve",
    )
    iterate = to_rows(iterate, sharers, part_rows, groups)

    def back(spec_ref, first_ref, turn_ref, second_ref, special_ref, out_ref, mid_ref, full_ref):
        backward_rows(spec_ref, part_rows, first_ref, turn_ref, second_ref, special_ref, mid_ref, full_ref)
        out_ref[...] = full_ref[:part_rows]

    (points,) = call(
        back,
        [(part_rows, N1, N2)],
        [iterate, const["first_back"], const["turn"], const["second_back"], const["special_back"]],
        [VMEM] * 5,
        [vmem(padded * N1, N2), vmem(padded, N1, N2)],
        part_rows * NLON * 256 * 4,
        "back_transform",
    )
    send = points.reshape(part_rows, lon_size, digits, N2).transpose(1, 0, 2, 3)
    got = lax.all_to_all(send, "lon", 0, 0, tiled=True)
    got = got.reshape(levels, sharers, part_rows, lon_count).transpose(1, 2, 0, 3)
    return got.reshape(rows, levels, lon_count)


def level_groups(sharers):
    size = lax.axis_size("lon")
    return [[first + i for i in range(sharers)] for first in range(0, size, sharers)]


def to_coefs(spectral, sharers, part_rows, groups):
    send = spectral.reshape(part_rows, 2, sharers, groups // 2, N2).transpose(2, 0, 1, 3, 4)
    got = lax.all_to_all(
        send, "lon", 0, 0, tiled=True, axis_index_groups=level_groups(sharers)
    )
    return got.reshape(sharers * part_rows * groups, N2)


def to_rows(values, sharers, part_rows, groups):
    send = values.reshape(sharers, part_rows, 2, groups // 2, N2)
    got = lax.all_to_all(
        send, "lon", 0, 0, tiled=True, axis_index_groups=level_groups(sharers)
    )
    return got.transpose(1, 2, 0, 3, 4).reshape(part_rows * N1, N2)


def solution(mesh):
    return jax.shard_map(
        on_device,
        mesh=mesh,
        in_specs=(P("lat", None, "lon"), P(), P(), P()),
        out_specs=P("lat", None, "lon"),
        check_vma=False,
    )
```

```python
import functools
import math

import jax
import jax.numpy as jnp
import numpy as np
from jax import lax
from jax.experimental import pallas as pl
from jax.experimental.pallas import tpu as pltpu
from jax.sharding import PartitionSpec as P

NLON = 4096
OV = 8
N1 = 32
N2 = 128
GROUPS = 16
BLOCK = 8

VMEM = pltpu.VMEM
SMEM = pltpu.SMEM


def numpy_split(table):
    import ml_dtypes

    table = np.asarray(table, np.float32)
    high = table.astype(ml_dtypes.bfloat16)
    low = (table - high.astype(np.float32)).astype(ml_dtypes.bfloat16)
    return high, low


def tables(levels):
    j1 = np.arange(N1)
    j2 = np.arange(N2)
    k2 = np.arange(N2)
    digit = np.arange(GROUPS)
    small = np.zeros((N1, N1))
    small[:GROUPS] = np.cos(2 * np.pi * np.outer(digit, j1) / N1)
    small[GROUPS] = np.cos(np.pi * j1)
    small[GROUPS + 1 :] = -np.sin(2 * np.pi * np.outer(digit[1:], j1) / N1)
    first = np.kron(np.eye(BLOCK), small)
    angle = 2 * np.pi * np.outer(digit, j2) / NLON
    turn_cos = np.cos(angle)
    turn_sin = np.sin(angle)
    phase = 2 * np.pi * (np.outer(j2, k2) % N2) / N2
    cosine, sine = np.cos(phase), np.sin(phase)
    second = np.block([[cosine, -sine], [sine, cosine]])
    special = np.zeros((2 * N2, 2 * N2))
    half = N2 // 2
    special[:N2, : half + 1] = np.cos(2 * np.pi * np.outer(j2, np.arange(half + 1)) / N2)
    special[:N2, half + 1 : N2] = -np.sin(2 * np.pi * np.outer(j2, np.arange(1, half)) / N2)
    odd = 2 * np.pi * np.outer(j2, 1 + 2 * np.arange(half)) / (2 * N2)
    special[N2:, N2 : N2 + half] = np.cos(odd)
    special[N2:, N2 + half :] = -np.sin(odd)
    weight = np.full(2 * N2, 2.0 / NLON)
    weight[0] = 1.0 / NLON
    weight[half] = 1.0 / NLON
    second_back = second.T * (2.0 / NLON)
    special_back = weight[:, None] * special.T
    wave = np.zeros((GROUPS, 2 * N2))
    wave[:, :N2] = digit[:, None] + N1 * k2[None, :]
    wave[:, N2:] = wave[:, :N2]
    lane = np.arange(N2)
    wave[0, :N2] = np.where(lane <= half, N1 * lane, N1 * (lane - half))
    wave[0, N2:] = 16 + N1 * (lane % half)
    eigen = 2.0 - 2.0 * np.cos(2 * np.pi * wave / NLON)
    pair = lambda t: np.concatenate(numpy_split(t), axis=0)
    width = N1 // levels
    part = [pair(np.kron(np.eye(BLOCK), small.T[at : at + width])) for at in range(0, N1, width)]
    return dict(
        first_back_part=np.concatenate(part, axis=0),
        first=pair(first),
        first_back=pair(first.T),
        second=pair(second),
        second_back=pair(second_back),
        special=pair(special),
        special_back=pair(special_back),
        turn=np.concatenate([turn_cos, turn_sin], axis=0).astype(np.float32),
        eigen=np.stack([eigen[:, :N2], eigen[:, N2:]]).astype(np.float32),
    )


def halves(value):
    high = value.astype(jnp.bfloat16)
    low = (value - high.astype(jnp.float32)).astype(jnp.bfloat16)
    return high, low


def dot(a, b):
    return lax.dot_general(a, b, (((1,), (0,)), ((), ())), preferred_element_type=jnp.float32)


def product_right(value, table_ref):
    size = table_ref.shape[0] // 2
    high, low = halves(value)
    table_high = table_ref[:size, :]
    return dot(high, table_high) + dot(low, table_high) + dot(high, table_ref[size:, :])


def product_left(table_ref, value):
    size = table_ref.shape[0] // 2
    high, low = halves(value)
    both = dot(table_ref[...], high)
    return both[:size] + both[size:] + dot(table_ref[:size, :], low)


def lanes_apart(value, rows):
    real = value[:, :N2].reshape(rows, GROUPS, N2)
    imag = value[:, N2:].reshape(rows, GROUPS, N2)
    return jnp.concatenate([real, imag], axis=1).reshape(rows * 2 * GROUPS, N2)


def lanes_together(value, rows):
    both = value.reshape(rows, 2 * GROUPS, N2)
    return jnp.concatenate([both[:, :GROUPS], both[:, GROUPS:]], axis=2).reshape(rows * GROUPS, 2 * N2)


def load_zeroth(ref, rows):
    return jnp.concatenate(
        [ref[pl.ds(0, rows, stride=2 * GROUPS), :], ref[pl.ds(GROUPS, rows, stride=2 * GROUPS), :]], axis=1
    )


def store_zeroth(ref, rows, value):
    ref[pl.ds(0, rows, stride=2 * GROUPS), :] = value[:, :N2]
    ref[pl.ds(GROUPS, rows, stride=2 * GROUPS), :] = value[:, N2:]


def forward_rows(points_ref, rows, first_ref, turn_ref, second_ref, special_ref, mid_ref, out_ref):
    padded = points_ref.shape[0]
    turn_cos = turn_ref[:GROUPS, :][None]
    turn_sin = turn_ref[GROUPS:, :][None]
    for pair in range(padded // (2 * BLOCK)):
        base = pair * 2 * BLOCK
        left = points_ref[base : base + BLOCK].reshape(BLOCK * N1, N2)
        right = points_ref[base + BLOCK : base + 2 * BLOCK].reshape(BLOCK * N1, N2)
        value = product_left(first_ref, jnp.concatenate([left, right], axis=1))
        for side in range(2):
            digits = value[:, side * N2 : (side + 1) * N2].reshape(BLOCK, N1, N2)
            real, imag = digits[:, :GROUPS], digits[:, GROUPS:]
            turned = jnp.concatenate(
                [real * turn_cos + imag * turn_sin, imag * turn_cos - real * turn_sin], axis=1
            )
            at = (base + side * BLOCK) * N1
            mid_ref[at : at + BLOCK * N1, :] = turned.reshape(BLOCK * N1, N2)
    result = product_right(lanes_together(mid_ref[...], padded), second_ref)
    out_ref[...] = lanes_apart(result, padded)[: rows * N1]
    store_zeroth(out_ref, rows, product_right(load_zeroth(mid_ref, padded), special_ref)[:rows])


def spectral_back(spec_ref, rows, padded, second_ref, special_ref, mid_ref):
    result = product_right(lanes_together(spec_ref[...], rows), second_ref)
    mid_ref[: rows * N1, :] = lanes_apart(result, rows)
    if padded > rows:
        mid_ref[rows * N1 : padded * N1, :] = jnp.zeros(((padded - rows) * N1, N2), jnp.float32)
    store_zeroth(mid_ref, rows, product_right(load_zeroth(spec_ref, rows), special_ref))


def digits_back(mid_ref, pair, turn_ref, first_ref):
    turn_cos = turn_ref[:GROUPS, :][None]
    turn_sin = turn_ref[GROUPS:, :][None]
    sides = []
    for side in range(2):
        at = (2 * pair + side) * BLOCK * N1
        both = mid_ref[at : at + BLOCK * N1, :].reshape(BLOCK, N1, N2)
        real, imag = both[:, :GROUPS], both[:, GROUPS:]
        turned = jnp.concatenate(
            [real * turn_cos - imag * turn_sin, imag * turn_cos + real * turn_sin], axis=1
        )
        sides.append(turned.reshape(BLOCK * N1, N2))
    return product_left(first_ref, jnp.concatenate(sides, axis=1))


def backward_rows(spec_ref, rows, first_ref, turn_ref, second_ref, special_ref, mid_ref, out_ref):
    padded = out_ref.shape[0]
    spectral_back(spec_ref, rows, padded, second_ref, special_ref, mid_ref)
    for pair in range(padded // (2 * BLOCK)):
        base = pair * 2 * BLOCK
        value = digits_back(mid_ref, pair, turn_ref, first_ref)
        out_ref[base : base + BLOCK] = value[:, :N2].reshape(BLOCK, N1, N2)
        out_ref[base + BLOCK : base + 2 * BLOCK] = value[:, N2:].reshape(BLOCK, N1, N2)


def factor_kernel(rows, lon_ref, couple_ref, eigen_ref, ratio_ref, inverse_ref, edge_ref):
    eigen = eigen_ref[...]
    groups = eigen.shape[0]
    half = rows // 2
    last = rows + 2 * OV - 1

    def plain(e):
        return 1.0 + lon_ref[e] * eigen

    def put(ref, index, value):
        ref[index * groups : (index + 1) * groups, :] = value

    def chain(start, stop, step, into):
        excess = inverse = None
        for e in range(start, stop + step, step):
            before = couple_ref[e] if step > 0 else couple_ref[e + 1]
            after = couple_ref[e + 1] if step > 0 else couple_ref[e]
            if inverse is None:
                ratio = None
                excess = plain(e) + before
            else:
                ratio = before * inverse
                excess = plain(e) + ratio * excess
            divisor = after + excess
            inverse = 1.0 / divisor
            into(e, ratio, inverse, excess, divisor)

    kept = {}

    def top(e, ratio, inverse, excess, divisor):
        if e == OV - 1:
            put(edge_ref, 0, inverse)
        if e >= OV:
            put(ratio_ref, e - OV, ratio)
            put(inverse_ref, e - OV, inverse)
        if e == OV + half - 1:
            kept["top"] = excess, divisor

    def bottom(e, ratio, inverse, excess, divisor):
        if e == OV + rows:
            put(edge_ref, 1, inverse)
        if e < OV + rows:
            put(ratio_ref, e - OV, ratio)
            put(inverse_ref, e - OV, inverse)
        if e == OV + half:
            kept["bottom"] = excess, divisor

    def next_band(e, ratio, inverse, excess, divisor):
        if ratio is not None:
            put(edge_ref, 7 + e - rows - 1, ratio)
        if e == OV + rows - 1:
            put(edge_ref, 5, inverse)

    def previous_band(e, ratio, inverse, excess, divisor):
        if ratio is not None:
            put(edge_ref, 14 + e - OV, ratio)
        if e == OV:
            put(edge_ref, 6, inverse)

    chain(rows, OV + rows - 1, 1, next_band)
    chain(2 * OV - 1, OV, -1, previous_band)
    chain(0, OV + half - 1, 1, top)
    chain(last, OV + half, -1, bottom)
    excess_top, divisor_top = kept["top"]
    excess_bottom, divisor_bottom = kept["bottom"]
    between = couple_ref[OV + half]
    inverse = 1.0 / (between * (excess_top + excess_bottom) + excess_top * excess_bottom)
    put(edge_ref, 2, divisor_bottom * inverse)
    put(edge_ref, 3, divisor_top * inverse)
    put(edge_ref, 4, between * inverse)


def edge_sums(low_rows, high_rows, next_ratio, previous_ratio):
    top = high_rows(0)
    for i in range(1, OV):
        top = high_rows(i) + next_ratio(i - 1) * top
    bottom = low_rows(OV - 1)
    for i in range(OV - 2, -1, -1):
        bottom = low_rows(i) + previous_ratio(i) * bottom
    return top, bottom


def swap_out(parity, up, down, even_ref, odd_ref):
    is_even = parity == 0
    even_ref[...] = jnp.where(is_even, up, down)
    odd_ref[...] = jnp.where(is_even, down, up)


def swap_in(parity, even, odd):
    is_even = parity == 0
    return jnp.where(is_even, odd, even), jnp.where(is_even, even, odd)


def solve_first(rows, groups, right_side_row, from_low, from_high, ratio_ref, inverse_ref, edge_ref, out_ref):
    half = rows // 2

    def at(ref, index):
        return ref[index * groups : (index + 1) * groups, :]

    def put(index, value):
        out_ref[index * groups : (index + 1) * groups, :] = value

    low, high = from_low, from_high
    for i in range(half):
        j = rows - 1 - i
        low = right_side_row(i) + at(ratio_ref, i) * low
        high = right_side_row(j) + at(ratio_ref, j) * high
        put(i, low)
        put(j, high)
    meet(rows, groups, low, high, ratio_ref, inverse_ref, edge_ref, at, lambda i: at(out_ref, i), put)


def meet(rows, groups, low, high, ratio_ref, inverse_ref, edge_ref, at, value, put):
    half = rows // 2
    between = at(edge_ref, 4)
    x_low = at(edge_ref, 2) * low + between * high
    x_high = at(edge_ref, 3) * high + between * low
    put(half - 1, x_low)
    put(half, x_high)
    for i in range(half - 2, -1, -1):
        j = rows - 1 - i
        x_low = value(i) * at(inverse_ref, i) + at(ratio_ref, i + 1) * x_low
        x_high = value(j) * at(inverse_ref, j) + at(ratio_ref, j - 1) * x_high
        put(i, x_low)
        put(j, x_high)


def sigmas(
    couple_low, couple_high, own_top, own_bottom, got_top, got_bottom, sent_top, sent_bottom, from_low, from_high,
    ratio_first, ratio_last, edge_ref, next_inverse, previous_inverse,
):
    groups = own_top.shape[0]

    def edge(index):
        return edge_ref[index * groups : (index + 1) * groups, :]

    beyond_low = (got_top + couple_low * own_top) * edge(0)
    beyond_high = (got_bottom + couple_high * own_bottom) * edge(1)
    theirs_low = (sent_bottom + couple_low * from_low) * previous_inverse
    theirs_high = (sent_top + couple_high * from_high) * next_inverse
    low = ratio_first * (couple_low * (own_top - theirs_low)) + couple_low * (from_low - beyond_low)
    high = ratio_last * (couple_high * (own_bottom - theirs_high)) + couple_high * (from_high - beyond_high)
    return low, high


def solve_second(
    rows, groups, couple_low, couple_high, own_top, own_bottom, got_top, got_bottom, sent_top, sent_bottom,
    from_low, from_high, ratio_ref, inverse_ref, edge_ref, first_ref, out_ref, mid_ref,
):
    half = rows // 2

    def at(ref, index):
        return ref[index * groups : (index + 1) * groups, :]

    low, high = sigmas(
        couple_low, couple_high, own_top, own_bottom, got_top, got_bottom, sent_top, sent_bottom,
        from_low, from_high, at(ratio_ref, 0), at(ratio_ref, rows - 1), edge_ref, at(edge_ref, 5), at(edge_ref, 6),
    )
    for i in range(half):
        j = rows - 1 - i
        if i:
            low = at(ratio_ref, i) * low
            high = at(ratio_ref, j) * high
        mid_ref[i * groups : (i + 1) * groups, :] = low
        mid_ref[j * groups : (j + 1) * groups, :] = high

    def put(index, value):
        rows_at = slice(index * groups, (index + 1) * groups)
        out_ref[rows_at, :] = first_ref[rows_at, :] + value

    meet(rows, groups, low, high, ratio_ref, inverse_ref, edge_ref, at, lambda i: at(mid_ref, i), put)


def call(body, outs, ins, spaces, scratch, flops, name, out_spaces=None, aliases=None):
    nbytes = sum(x.size * x.dtype.itemsize for x in ins) + sum(4 * math.prod(s) for s in outs)
    out = pl.pallas_call(
        body,
        out_shape=[jax.ShapeDtypeStruct(s, jnp.float32) for s in outs],
        in_specs=[pl.BlockSpec(memory_space=s) for s in spaces],
        out_specs=[pl.BlockSpec(memory_space=s) for s in out_spaces or [VMEM] * len(outs)],
        input_output_aliases=aliases or {},
        scratch_shapes=scratch,
        compiler_params=pltpu.CompilerParams(vmem_limit_bytes=48 << 20),
        cost_estimate=pl.CostEstimate(flops=flops, bytes_accessed=nbytes, transcendentals=0),
        name=name,
    )(*ins)
    return out


def pad_rows(rows):
    return -(-rows // (2 * BLOCK)) * 2 * BLOCK


def swap(value_even, value_odd):
    count = lax.axis_size("lat")
    even = [(i, i ^ 1) for i in range(count) if (i ^ 1) < count]
    odd = [(i, ((i + 1) ^ 1) - 1) for i in range(1, count) if ((i + 1) ^ 1) - 1 < count]
    value_odd = lax.ppermute(value_odd, "lat", odd)
    return lax.ppermute(value_even, "lat", even), value_odd


def send_level(piece, mask, size):
    return lax.ppermute(piece, "lon", [(d, d ^ mask) for d in range(size)])


def swap_levels(pieces):
    return [pieces[0]] + [send_level(pieces[mask], mask, len(pieces)) for mask in range(1, len(pieces))]


def operator_parts(rows, lon_coef, lat_coef, level_scale):
    row_first = lax.axis_index("lat") * rows
    extent = rows + 2 * OV
    lon_window = lax.dynamic_slice_in_dim(jnp.pad(lon_coef, (OV, OV)), row_first, extent)
    couple = lax.dynamic_slice_in_dim(jnp.pad(lat_coef, (OV + 1, OV + 2)), row_first, extent + 1)
    return level_scale[:, None] * lon_window[None], level_scale[:, None] * couple[None]


def factor(rows, groups, lon_window, couple, eigen):
    block = (rows * groups, N2)
    return call(
        functools.partial(factor_kernel, rows),
        [block, block, (21 * groups, N2)],
        [lon_window, couple, eigen],
        [SMEM, SMEM, VMEM],
        [],
        rows * groups * N2 * 20,
        "factor",
    )


def vmem(*shape):
    return pltpu.VMEM(shape, jnp.float32)


def rows_of(ref, groups, first=0):
    return lambda i: ref[(i - first) * groups : (i - first + 1) * groups, :]


def on_device(right_side, lon_coef, lat_coef, level_scale):
    const = {k: jnp.asarray(v) for k, v in tables(right_side.shape[1]).items()}
    if lax.axis_size("lon") != right_side.shape[1]:
        return shared_levels(const, right_side, lon_coef, lat_coef, level_scale)
    return whole_levels(const, right_side, lon_coef, lat_coef, level_scale)


def early_rows(rows):
    return rows // 2 + 2


def inverses(one, other):
    inverse = 1.0 / (one * other)
    return other * inverse, one * inverse


def edge_kernel(rows, level_ref, lon_ref, couple_ref, eigen_ref, out_ref):
    eigen = eigen_ref[...]
    groups = eigen.shape[0]
    level = level_ref[0]
    low = high = low_inverse = high_inverse = None
    for i in range(OV):
        e, f = rows + i, 2 * OV - 1 - i
        if i == 0:
            low = 1.0 + lon_ref[level, e] * eigen + couple_ref[level, e]
            high = 1.0 + lon_ref[level, f] * eigen + couple_ref[level, f + 1]
        else:
            low_ratio = couple_ref[level, e] * low_inverse
            high_ratio = couple_ref[level, f + 1] * high_inverse
            out_ref[(i - 1) * groups : i * groups, :] = low_ratio
            out_ref[(OV + i - 1) * groups : (OV + i) * groups, :] = high_ratio
            low = 1.0 + lon_ref[level, e] * eigen + low_ratio * low
            high = 1.0 + lon_ref[level, f] * eigen + high_ratio * high
        low_inverse, high_inverse = inverses(couple_ref[level, e + 1] + low, couple_ref[level, f] + high)
    out_ref[(OV - 1) * groups : OV * groups, :] = low_inverse
    out_ref[(2 * OV - 1) * groups :, :] = high_inverse


def level_response(rows, early, level, lon_ref, couple_ref, eigen, put_ratio, put_inverse, keep, tables):
    half = rows // 2
    ratio_at, value_at, put_value, put_phi, put_psi = tables

    def plain(e):
        return 1.0 + lon_ref[level, e] * eigen

    low = high = None
    low_inverse = high_inverse = low_value = high_value = None
    for i in range(-OV, half):
        j = rows - 1 - i
        e, f = i + OV, j + OV
        if low is None:
            low = plain(e) + couple_ref[level, e]
            high = plain(f) + couple_ref[level, f + 1]
        else:
            low_ratio = couple_ref[level, e] * low_inverse
            high_ratio = couple_ref[level, f + 1] * high_inverse
            low = plain(e) + low_ratio * low
            high = plain(f) + high_ratio * high
        low_divisor = couple_ref[level, e + 1] + low
        high_divisor = couple_ref[level, f] + high
        low_inverse, high_inverse = inverses(low_divisor, high_divisor)
        if i == -1:
            keep(0, low_inverse)
            keep(1, high_inverse)
        if i == 0:
            low_value = high_value = jnp.ones_like(eigen)
        elif i > 0:
            low_value = low_ratio * low_value
            high_value = high_ratio * high_value
        if i >= 0:
            put_ratio(i, low_ratio)
            put_ratio(j, high_ratio)
            put_inverse(i, low_inverse)
            put_inverse(j, high_inverse)
            put_value(i, low_value * low_inverse)
            if j < early:
                put_value(j, high_value * high_inverse)
    between = couple_ref[level, OV + half]
    inverse = 1.0 / (between * (low + high) + low * high)
    across = between * inverse
    high_inverse = high_divisor * inverse
    low_inverse = low_divisor * inverse
    keep(2, high_inverse)
    keep(3, low_inverse)
    keep(4, across)
    phi = high_inverse * low_value
    psi = across * high_value
    phi_down = across * low_value
    psi_down = low_inverse * high_value
    put_phi(half - 1, phi)
    put_psi(half - 1, psi)
    for i in range(half - 2, -1, -1):
        ratio = ratio_at(i + 1)
        phi = value_at(i) + ratio * phi
        psi = ratio * psi
        put_phi(i, phi)
        put_psi(i, psi)
    put_phi(half, phi_down)
    put_psi(half, psi_down)
    for j in range(half + 1, early):
        ratio = ratio_at(j - 1)
        phi_down = ratio * phi_down
        psi_down = value_at(j) + ratio * psi_down
        put_phi(j, phi_down)
        put_psi(j, psi_down)


def getter(ref, groups):
    return lambda index: ref[index * groups : (index + 1) * groups, :]


def putter(ref, groups, first=0):
    def put(index, value):
        at = first + index * groups
        ref[pl.ds(at if isinstance(at, int) else pl.multiple_of(at, groups), groups), :] = value

    return put


def own_kernel(
    rows, early, place_ref, lon_ref, couple_ref, eigen_ref, ratio_ref, inverse_ref, edge_ref, phi_ref, psi_ref, value_ref
):
    groups = eigen_ref.shape[0]
    level_response(
        rows, early, place_ref[0], lon_ref, couple_ref, eigen_ref[...], putter(ratio_ref, groups),
        putter(inverse_ref, groups), putter(edge_ref, groups),
        (
            getter(ratio_ref, groups), getter(value_ref, groups), putter(value_ref, groups),
            putter(phi_ref, groups), putter(psi_ref, groups),
        ),
    )


def partners_kernel(
    rows, early, levels, place_ref, lon_ref, couple_ref, eigen_ref, after_ref, phi_ref, psi_ref, token_ref, kept_ref, value_ref
):
    token_ref[...] = after_ref[...]
    eigen = eigen_ref[...]
    groups = eigen.shape[0]

    def partner(mask, carry):
        def nothing(index, value):
            pass

        put_kept = putter(kept_ref, groups)

        def put_ratio(index, value):
            if index < early:
                put_kept(index, value)

        first = (mask - 1) * (early * groups)
        level_response(
            rows, early, place_ref[0] ^ mask, lon_ref, couple_ref, eigen, put_ratio, nothing, nothing,
            (
                getter(kept_ref, groups), getter(value_ref, groups), putter(value_ref, groups),
                putter(phi_ref, groups, first), putter(psi_ref, groups, first),
            ),
        )
        return carry

    lax.fori_loop(1, levels, partner, 0)


def whole_levels(const, right_side, lon_coef, lat_coef, level_scale):
    rows, levels, lon_count = right_side.shape
    digits = N1 // levels
    groups = 2 * GROUPS
    lon_at = lax.axis_index("lon").astype(jnp.int32)
    parity = (lax.axis_index("lat") % 2).astype(jnp.int32)
    place = jnp.stack([lon_at, parity])
    half = rows // 2
    early = early_rows(rows)
    late = rows - early
    eigen = const["eigen"].reshape(groups, N2)
    lon_all, couple_all = operator_parts(rows, lon_coef, lat_coef, level_scale)
    (around,) = call(
        functools.partial(edge_kernel, rows),
        [(2 * OV * groups, N2)],
        [place, lon_all, couple_all, eigen],
        [SMEM, SMEM, SMEM, VMEM],
        [],
        16 * groups * N2 * 20,
        "edge",
    )
    block = (rows * groups, N2)
    early_block = (early * groups, N2)
    ratio, inverse, edge, phi, psi = call(
        functools.partial(own_kernel, rows, early),
        [block, block, (5 * groups, N2), early_block, early_block],
        [place, lon_all, couple_all, eigen],
        [SMEM, SMEM, SMEM, VMEM],
        [vmem(*early_block)],
        rows * groups * N2 * 20,
        "own",
    )
    row = (groups, N2)
    ends = 2 * OV
    inner = rows - ends
    span = OV * digits
    by_row = right_side.reshape(rows, levels, digits, N2).transpose(0, 2, 1, 3).reshape(-1, N2)

    far = list(range(2, levels))

    def pack_ends(place_ref, low_ref, high_ref, *out_refs):
        for out_ref, mask in zip(out_refs, [0] + far):
            level = place_ref[0] ^ mask
            out_ref[:span, :] = low_ref[pl.ds(level, span, stride=levels), :]
            out_ref[span:, :] = high_ref[pl.ds(level, span, stride=levels), :]

    end_packed = call(
        pack_ends,
        [(ends * digits, N2)] * (1 + len(far)),
        [place, by_row[: levels * span], by_row[levels * (rows - OV) * digits :]],
        [SMEM, VMEM, VMEM],
        [],
        0,
        "pack_ends",
    )

    def pack(place_ref, in_ref, after_ref, *out_refs):
        del after_ref
        for mask, out_ref in enumerate(out_refs):
            level = place_ref[0] ^ mask
            skip = 0 if mask == 1 else span
            out_ref[...] = in_ref[pl.ds(level + levels * skip, out_ref.shape[0], stride=levels), :]

    packed = call(
        pack,
        [((rows if mask == 1 else inner) * digits, N2) for mask in range(levels)],
        [place, by_row, end_packed[0]],
        [SMEM, VMEM, pl.ANY],
        [],
        0,
        "pack",
    )
    end_pieces = [end_packed[0], None] + [send_level(p, m, levels) for p, m in zip(end_packed[1:], far)]
    near = send_level(packed[1], 1, levels)
    end_pieces[1] = near
    inner_pieces = [packed[0], near] + [send_level(packed[m], m, levels) for m in far]
    forward = [const["first"], const["turn"], const["second"], const["special"]]
    pad_ends, pad_inner = pad_rows(ends), pad_rows(inner)

    def ends_body(place_ref, *refs):
        pieces, refs = refs[:levels], refs[levels:]
        tables_in, edge_ref = refs[:4], refs[4]
        spec_ref, top_ref, bottom_ref, even_ref, odd_ref, full_ref, mid_ref = refs[5:]
        for mask, piece in enumerate(pieces):
            at = pl.multiple_of((place_ref[0] ^ mask) * digits, digits)
            last = piece.shape[0] - span
            full_ref[:OV, pl.ds(at, digits), :] = piece[:span, :].reshape(OV, digits, N2)
            full_ref[OV:ends, pl.ds(at, digits), :] = piece[last:, :].reshape(OV, digits, N2)
        forward_rows(full_ref, ends, *tables_in, mid_ref, spec_ref)
        top, bottom = edge_sums(
            rows_of(spec_ref, groups), rows_of(spec_ref, groups, -OV),
            rows_of(edge_ref, groups), lambda i: edge_ref[(2 * OV - 2 - i) * groups : (2 * OV - 1 - i) * groups, :],
        )
        top_ref[...] = top
        bottom_ref[...] = bottom
        swap_out(place_ref[1], top, bottom, even_ref, odd_ref)

    end_spectral, sent_top, sent_bottom, even, odd = call(
        ends_body,
        [(ends * groups, N2)] + [row] * 4,
        [place, *end_pieces, *forward, around],
        [SMEM] + [VMEM] * (levels + 5),
        [vmem(pad_ends, N1, N2), vmem(pad_ends * N1, N2)],
        ends * NLON * 256 * 4,
        "ends",
    )
    even, odd = swap(even, odd)
    backward = [const["first_back"], const["turn"], const["second_back"], const["special_back"]]
    pad_early, pad_late = pad_rows(early), pad_rows(late)

    def spread(place_ref, full_ref, count, out_refs):
        for mask, out_ref in enumerate(out_refs):
            at = pl.multiple_of((place_ref[0] ^ mask) * digits, digits)
            out_ref[: count * digits, :] = full_ref[:count, pl.ds(at, digits), :].reshape(count * digits, N2)

    def inner_body(place_ref, *refs):
        pieces, refs = refs[:levels], refs[levels:]
        tables_in, back_in, refs = refs[:4], refs[4:7], refs[7:]
        ends_ref, even_ref, odd_ref, ratio_ref, inverse_ref, edge_ref = refs[:6]
        late_ref, top_ref, even_out, odd_out = refs[6:10]
        early_refs, refs = refs[10 : 10 + levels], refs[10 + levels :]
        full_ref, mid_ref, spec_ref, sum_ref, back_full_ref, back_mid_ref = refs
        for mask, piece in enumerate(pieces):
            at = pl.multiple_of((place_ref[0] ^ mask) * digits, digits)
            skip = span if mask == 1 else 0
            full_ref[:inner, pl.ds(at, digits), :] = piece[skip : skip + inner * digits, :].reshape(
                inner, digits, N2
            )
        if pad_inner > inner:
            full_ref[inner:] = jnp.zeros((pad_inner - inner, N1, N2), jnp.float32)
        forward_rows(full_ref, inner, *tables_in, mid_ref, spec_ref)
        low, high = swap_in(place_ref[1], even_ref[...], odd_ref[...])

        def spec_row(i):
            if i < OV:
                return rows_of(ends_ref, groups)(i)
            if i >= rows - OV:
                return rows_of(ends_ref, groups, rows - ends)(i)
            return rows_of(spec_ref, groups, OV)(i)

        solve_first(rows, groups, spec_row, low, high, ratio_ref, inverse_ref, edge_ref, sum_ref)
        top = sum_ref[:groups, :]
        top_ref[...] = top
        late_ref[...] = sum_ref[early * groups :, :]
        swap_out(place_ref[1], sum_ref[(rows - 1) * groups :, :], top, even_out, odd_out)
        early_sum = sum_ref.at[pl.ds(0, early * groups), :]
        backward_rows(early_sum, early, back_in[0], tables_in[1], back_in[1], back_in[2], back_mid_ref, back_full_ref)
        spread(place_ref, back_full_ref, early, early_refs)

    late_first, own_top, even2, odd2, *early_pieces = call(
        inner_body,
        [(late * groups, N2), row, row, row] + [(early * digits, N2)] * levels,
        [
            place, *inner_pieces, *forward, backward[0], backward[2], backward[3],
            end_spectral, even, odd, ratio, inverse, edge,
        ],
        [SMEM] + [VMEM] * (levels + 13),
        [
            vmem(pad_inner, N1, N2), vmem(pad_inner * N1, N2), vmem(inner * N1, N2), vmem(rows * groups, N2),
            vmem(pad_early, N1, N2), vmem(pad_early * N1, N2),
        ],
        (inner + early) * NLON * 256 * 4,
        "inner",
    )
    early_pieces = swap_levels(early_pieces)
    even2, odd2 = swap(even2, odd2)

    phi_others, psi_others, token = call(
        functools.partial(partners_kernel, rows, early, levels),
        [((levels - 1) * early * groups, N2)] * 2 + [row],
        [place, lon_all, couple_all, eigen, own_top],
        [SMEM, SMEM, SMEM, VMEM, VMEM],
        [vmem(*early_block), vmem(*early_block)],
        (levels - 1) * rows * groups * N2 * 20,
        "partners",
    )

    def sigma_body(place_ref, couple_ref, *refs):
        first_ref, own_top_ref, even_ref, odd_ref, even2_ref, odd2_ref, top_ref, bottom_ref = refs[:8]
        ratio_ref, edge_ref, around_ref = refs[8:11]
        sigma_ref = refs[-1]
        level = place_ref[0]
        got_top, got_bottom = swap_in(place_ref[1], even_ref[...], odd_ref[...])
        from_low, from_high = swap_in(place_ref[1], even2_ref[...], odd2_ref[...])
        low, high = sigmas(
            couple_ref[level, OV], couple_ref[level, OV + rows], own_top_ref[...], first_ref[(late - 1) * groups :, :],
            got_top, got_bottom, top_ref[...], bottom_ref[...], from_low, from_high,
            ratio_ref[:groups, :], ratio_ref[(rows - 1) * groups :, :], edge_ref,
            around_ref[(OV - 1) * groups : OV * groups, :], around_ref[(2 * OV - 1) * groups :, :],
        )
        sigma_ref[:groups, :] = low
        sigma_ref[groups:, :] = high

    (sigma,) = call(
        sigma_body,
        [(2 * groups, N2)],
        [
            place, couple_all, late_first, own_top, even, odd, even2, odd2, sent_top, sent_bottom, ratio, edge, around,
            *early_pieces[1:], token,
        ],
        [SMEM, SMEM] + [VMEM] * 11 + [pl.ANY] * levels,
        [],
        groups * N2 * 40,
        "sigma",
    )
    far_sigma = [send_level(sigma, mask, levels) for mask in far]
    def second_body(place_ref, *refs):
        sigma_ref, first_ref, ratio_ref, inverse_ref, edge_ref = refs[:5]
        tables_in, refs = refs[5:9], refs[9:]
        late_refs = refs[:levels]
        sum_ref, mid_ref, full_ref = refs[levels:]
        low, high = sigma_ref[:groups, :], sigma_ref[groups:, :]

        def at(ref, index):
            return ref[index * groups : (index + 1) * groups, :]

        for i in range(half):
            j = rows - 1 - i
            if i:
                low = at(ratio_ref, i) * low
                high = at(ratio_ref, j) * high
            mid_ref[(j - half) * groups : (j - half + 1) * groups, :] = high
        x_high = at(edge_ref, 3) * high + at(edge_ref, 4) * low
        for j in range(half, rows):
            if j > half:
                x_high = at(mid_ref, j - half) * at(inverse_ref, j) + at(ratio_ref, j - 1) * x_high
            if j >= early:
                here = slice((j - early) * groups, (j - early + 1) * groups)
                sum_ref[here, :] = first_ref[here, :] + x_high
        backward_rows(sum_ref, late, *tables_in, mid_ref, full_ref)
        spread(place_ref, full_ref, late, late_refs)
        late_refs[1][late * digits :, :] = sigma_ref[...]

    late_pieces = call(
        second_body,
        [(late * digits + (2 * groups if mask == 1 else 0), N2) for mask in range(levels)],
        [place, sigma, late_first, ratio, inverse, edge, *backward],
        [SMEM] + [VMEM] * 9,
        [vmem(late * groups, N2), vmem(max(pad_late, half) * N1, N2), vmem(pad_late, N1, N2)],
        late * NLON * 256 * 4,
        "second",
    )
    late_pieces = swap_levels(late_pieces)
    sigma_pieces = [sigma, late_pieces[1], *far_sigma]
    total = rows * levels * digits
    early_total = early * levels * digits
    part = const["first_back_part"]

    def correct(place_ref, *refs):
        pieces, sigma_refs, refs = refs[:levels], refs[levels : 2 * levels], refs[2 * levels :]
        phi_ref, psi_ref, phi_others_ref, psi_others_ref, part_ref, turn_ref, second_ref, special_ref = refs[:8]
        out_ref, sum_ref, mid_ref, done_ref, sem = refs[8:]
        part_rows = part_ref.shape[0] // levels
        mine = part_ref.at[pl.ds(pl.multiple_of(place_ref[0] * part_rows, part_rows), part_rows), :]
        size = early * groups
        for mask in range(levels):
            level = place_ref[0] ^ mask
            last = sigma_refs[mask].shape[0]
            low = sigma_refs[mask][last - 2 * groups : last - groups, :]
            high = sigma_refs[mask][last - groups :, :]
            first = (mask - 1) * size
            phi_all = phi_others_ref[first : first + size, :] if mask else phi_ref[...]
            psi_all = psi_others_ref[first : first + size, :] if mask else psi_ref[...]
            phi_all = phi_all.reshape(early, groups, N2)
            psi_all = psi_all.reshape(early, groups, N2)
            sum_ref[...] = (phi_all * low[None] + psi_all * high[None]).reshape(size, N2)
            spectral_back(sum_ref, early, pad_early, second_ref, special_ref, mid_ref)
            for pair in range(pad_early // (2 * BLOCK)):
                value = digits_back(mid_ref, pair, turn_ref, mine)
                for side in range(2):
                    begin = (2 * pair + side) * BLOCK
                    count = min(BLOCK, early - begin)
                    if count <= 0:
                        continue
                    lines = count * digits
                    whole = pieces[mask][begin * digits : begin * digits + lines, :]
                    done_ref[pl.ds(level + begin * digits * levels, lines, stride=levels), :] = (
                        whole + value[:lines, side * N2 : (side + 1) * N2]
                    )
        copy = pltpu.make_async_copy(done_ref, out_ref.at[pl.ds(0, early_total), :], sem)
        copy.start()
        copy.wait()

    (out,) = call(
        correct,
        [(total, N2)],
        [place, *early_pieces, *sigma_pieces, phi, psi, phi_others, psi_others, part, const["turn"], *backward[2:]],
        [SMEM] + [VMEM] * (2 * levels + 8),
        [
            vmem(early * groups, N2), vmem(pad_early * N1, N2), vmem(early_total, N2), pltpu.SemaphoreType.DMA,
        ],
        levels * early * NLON * 256 * 40,
        "correct",
        out_spaces=[pl.ANY],
    )

    chunks = 4

    def unpack(place_ref, *refs):
        pieces = refs[:levels]
        out_ref, done_ref, sems = refs[levels + 1 :]
        lines = late * digits // chunks
        copies = []
        for chunk in range(chunks):
            for mask in range(levels):
                first = (place_ref[0] ^ mask) + chunk * lines * levels
                done_ref[pl.ds(first, lines, stride=levels), :] = pieces[mask][chunk * lines : (chunk + 1) * lines, :]
            here = pl.ds(chunk * lines * levels, lines * levels)
            there = pl.ds(early_total + chunk * lines * levels, lines * levels)
            copy = pltpu.make_async_copy(done_ref.at[here, :], out_ref.at[there, :], sems.at[chunk])
            copy.start()
            copies.append(copy)
        for copy in copies:
            copy.wait()

    (out,) = call(
        unpack,
        [(total, N2)],
        [place, *late_pieces, out],
        [SMEM] + [VMEM] * levels + [pl.ANY],
        [vmem(total - early_total, N2), pltpu.SemaphoreType.DMA((chunks,))],
        0,
        "unpack",
        out_spaces=[pl.ANY],
        aliases={levels + 1: 0},
    )
    return out.reshape(rows, digits, levels, N2).transpose(0, 2, 1, 3).reshape(right_side.shape)


def second_part(
    rows, groups, parity, couple_ref, first_ref, even_ref, odd_ref, even2_ref, odd2_ref, top_ref, bottom_ref,
    ratio_ref, inverse_ref, edge_ref, out_ref, mid_ref,
):
    got_top, got_bottom = swap_in(parity, even_ref[...], odd_ref[...])
    low, high = swap_in(parity, even2_ref[...], odd2_ref[...])
    solve_second(
        rows, groups, couple_ref[OV], couple_ref[OV + rows],
        first_ref[:groups, :], first_ref[(rows - 1) * groups :, :],
        got_top, got_bottom, top_ref[...], bottom_ref[...], low, high,
        ratio_ref, inverse_ref, edge_ref, first_ref, out_ref, mid_ref,
    )


def shared_levels(const, right_side, lon_coef, lat_coef, level_scale):
    rows, levels, lon_count = right_side.shape
    lon_size = lax.axis_size("lon")
    assert lon_size % levels == 0 and GROUPS % (lon_size // levels) == 0 and rows % (lon_size // levels) == 0
    sharers = lon_size // levels
    groups = 2 * GROUPS // sharers
    part_rows = rows // sharers
    digits = N1 // lon_size
    lon_at = lax.axis_index("lon")
    parity = (lax.axis_index("lat") % 2).astype(jnp.int32).reshape(1)
    lon_window, couple = operator_parts(rows, lon_coef, lat_coef, level_scale)
    lon_window = lax.dynamic_index_in_dim(lon_window, lon_at // sharers, 0, False)
    couple = lax.dynamic_index_in_dim(couple, lon_at // sharers, 0, False)
    eigen = lax.dynamic_slice_in_dim(
        const["eigen"], (lon_at % sharers) * (groups // 2), groups // 2, axis=1
    ).reshape(groups, N2)
    ratio, inverse, edge = factor(rows, groups, lon_window, couple, eigen)
    block = (rows * groups, N2)
    row = (groups, N2)
    send = right_side.reshape(sharers, part_rows, levels, lon_count).transpose(2, 0, 1, 3)
    send = send.reshape(lon_size, part_rows, digits, N2)
    got = lax.all_to_all(send, "lon", 0, 0, tiled=True)
    points = got.transpose(1, 0, 2, 3).reshape(part_rows, N1, N2)
    padded = pad_rows(part_rows)

    def transform(points_ref, first_ref, turn_ref, second_ref, special_ref, out_ref, full_ref, mid_ref):
        full_ref[:part_rows] = points_ref[...]
        if padded > part_rows:
            full_ref[part_rows:] = jnp.zeros((padded - part_rows, N1, N2), jnp.float32)
        forward_rows(full_ref, part_rows, first_ref, turn_ref, second_ref, special_ref, mid_ref, out_ref)

    (spectral,) = call(
        transform,
        [(part_rows * N1, N2)],
        [points, const["first"], const["turn"], const["second"], const["special"]],
        [VMEM] * 5,
        [vmem(padded, N1, N2), vmem(padded * N1, N2)],
        part_rows * NLON * 256 * 4,
        "transform",
    )
    spectral = to_coefs(spectral, sharers, part_rows, groups)

    def edges(parity_ref, spec_ref, edge_ref, top_ref, bottom_ref, even_ref, odd_ref):
        top, bottom = edge_sums(
            rows_of(spec_ref, groups), rows_of(spec_ref, groups, OV - rows),
            rows_of(edge_ref, groups, -7), rows_of(edge_ref, groups, -14),
        )
        top_ref[...] = top
        bottom_ref[...] = bottom
        swap_out(parity_ref[0], top, bottom, even_ref, odd_ref)

    sent_top, sent_bottom, even, odd = call(
        edges, [row] * 4, [parity, spectral, edge], [SMEM, VMEM, VMEM], [], groups * N2 * 32, "edges"
    )
    even, odd = swap(even, odd)

    def first(parity_ref, spec_ref, even_ref, odd_ref, ratio_ref, inverse_ref, edge_ref, out_ref, e_ref, o_ref):
        low, high = swap_in(parity_ref[0], even_ref[...], odd_ref[...])
        solve_first(
            rows, groups, rows_of(spec_ref, groups), low, high, ratio_ref, inverse_ref, edge_ref, out_ref
        )
        swap_out(parity_ref[0], out_ref[(rows - 1) * groups :, :], out_ref[:groups, :], e_ref, o_ref)

    iterate, even2, odd2 = call(
        first,
        [block, row, row],
        [parity, spectral, even, odd, ratio, inverse, edge],
        [SMEM] + [VMEM] * 6,
        [],
        rows * groups * N2 * 8,
        "first_solve",
    )
    even2, odd2 = swap(even2, odd2)

    def second(parity_ref, *refs):
        second_part(rows, groups, parity_ref[0], *refs)

    (iterate,) = call(
        second,
        [block],
        [parity, couple, iterate, even, odd, even2, odd2, sent_top, sent_bottom, ratio, inverse, edge],
        [SMEM, SMEM] + [VMEM] * 10,
        [vmem(*block)],
        rows * groups * N2 * 8,
        "second_solve",
    )
    iterate = to_rows(iterate, sharers, part_rows, groups)

    def back(spec_ref, first_ref, turn_ref, second_ref, special_ref, out_ref, mid_ref, full_ref):
        backward_rows(spec_ref, part_rows, first_ref, turn_ref, second_ref, special_ref, mid_ref, full_ref)
        out_ref[...] = full_ref[:part_rows]

    (points,) = call(
        back,
        [(part_rows, N1, N2)],
        [iterate, const["first_back"], const["turn"], const["second_back"], const["special_back"]],
        [VMEM] * 5,
        [vmem(padded * N1, N2), vmem(padded, N1, N2)],
        part_rows * NLON * 256 * 4,
        "back_transform",
    )
    send = points.reshape(part_rows, lon_size, digits, N2).transpose(1, 0, 2, 3)
    got = lax.all_to_all(send, "lon", 0, 0, tiled=True)
    got = got.reshape(levels, sharers, part_rows, lon_count).transpose(1, 2, 0, 3)
    return got.reshape(rows, levels, lon_count)


def level_groups(sharers):
    size = lax.axis_size("lon")
    return [[first + i for i in range(sharers)] for first in range(0, size, sharers)]


def to_coefs(spectral, sharers, part_rows, groups):
    send = spectral.reshape(part_rows, 2, sharers, groups // 2, N2).transpose(2, 0, 1, 3, 4)
    got = lax.all_to_all(
        send, "lon", 0, 0, tiled=True, axis_index_groups=level_groups(sharers)
    )
    return got.reshape(sharers * part_rows * groups, N2)


def to_rows(values, sharers, part_rows, groups):
    send = values.reshape(sharers, part_rows, 2, groups // 2, N2)
    got = lax.all_to_all(
        send, "lon", 0, 0, tiled=True, axis_index_groups=level_groups(sharers)
    )
    return got.transpose(1, 2, 0, 3, 4).reshape(part_rows * N1, N2)


def solution(mesh):
    return jax.shard_map(
        on_device,
        mesh=mesh,
        in_specs=(P("lat", None, "lon"), P(), P(), P()),
        out_specs=P("lat", None, "lon"),
        check_vma=False,
    )
```

```python
import functools
import math

import jax
import jax.numpy as jnp
import numpy as np
from jax import lax
from jax.experimental import pallas as pl
from jax.experimental.pallas import tpu as pltpu
from jax.sharding import PartitionSpec as P

NLON = 4096
OV = 8
N1 = 32
N2 = 128
GROUPS = 16
BLOCK = 8

VMEM = pltpu.VMEM
SMEM = pltpu.SMEM


def numpy_split(table):
    import ml_dtypes

    table = np.asarray(table, np.float32)
    high = table.astype(ml_dtypes.bfloat16)
    low = (table - high.astype(np.float32)).astype(ml_dtypes.bfloat16)
    return high, low


def tables(levels):
    j1 = np.arange(N1)
    j2 = np.arange(N2)
    k2 = np.arange(N2)
    digit = np.arange(GROUPS)
    small = np.zeros((N1, N1))
    small[:GROUPS] = np.cos(2 * np.pi * np.outer(digit, j1) / N1)
    small[GROUPS] = np.cos(np.pi * j1)
    small[GROUPS + 1 :] = -np.sin(2 * np.pi * np.outer(digit[1:], j1) / N1)
    first = np.kron(np.eye(BLOCK), small)
    angle = 2 * np.pi * np.outer(digit, j2) / NLON
    turn_cos = np.cos(angle)
    turn_sin = np.sin(angle)
    phase = 2 * np.pi * (np.outer(j2, k2) % N2) / N2
    cosine, sine = np.cos(phase), np.sin(phase)
    second = np.block([[cosine, -sine], [sine, cosine]])
    special = np.zeros((2 * N2, 2 * N2))
    half = N2 // 2
    special[:N2, : half + 1] = np.cos(2 * np.pi * np.outer(j2, np.arange(half + 1)) / N2)
    special[:N2, half + 1 : N2] = -np.sin(2 * np.pi * np.outer(j2, np.arange(1, half)) / N2)
    odd = 2 * np.pi * np.outer(j2, 1 + 2 * np.arange(half)) / (2 * N2)
    special[N2:, N2 : N2 + half] = np.cos(odd)
    special[N2:, N2 + half :] = -np.sin(odd)
    weight = np.full(2 * N2, 2.0 / NLON)
    weight[0] = 1.0 / NLON
    weight[half] = 1.0 / NLON
    second_back = second.T * (2.0 / NLON)
    special_back = weight[:, None] * special.T
    wave = np.zeros((GROUPS, 2 * N2))
    wave[:, :N2] = digit[:, None] + N1 * k2[None, :]
    wave[:, N2:] = wave[:, :N2]
    lane = np.arange(N2)
    wave[0, :N2] = np.where(lane <= half, N1 * lane, N1 * (lane - half))
    wave[0, N2:] = 16 + N1 * (lane % half)
    eigen = 2.0 - 2.0 * np.cos(2 * np.pi * wave / NLON)
    pair = lambda t: np.concatenate(numpy_split(t), axis=0)
    width = N1 // levels
    part = [pair(np.kron(np.eye(BLOCK), small.T[at : at + width])) for at in range(0, N1, width)]
    return dict(
        first_back_part=np.concatenate(part, axis=0),
        first=pair(first),
        first_back=pair(first.T),
        second=pair(second),
        second_back=pair(second_back),
        special=pair(special),
        special_back=pair(special_back),
        turn=np.concatenate([turn_cos, turn_sin], axis=0).astype(np.float32),
        eigen=np.stack([eigen[:, :N2], eigen[:, N2:]]).astype(np.float32),
    )


def halves(value):
    high = value.astype(jnp.bfloat16)
    low = (value - high.astype(jnp.float32)).astype(jnp.bfloat16)
    return high, low


def dot(a, b):
    return lax.dot_general(a, b, (((1,), (0,)), ((), ())), preferred_element_type=jnp.float32)


def product_right(value, table_ref):
    size = table_ref.shape[0] // 2
    high, low = halves(value)
    table_high = table_ref[:size, :]
    return dot(high, table_high) + dot(low, table_high) + dot(high, table_ref[size:, :])


def product_left(table_ref, value):
    size = table_ref.shape[0] // 2
    high, low = halves(value)
    both = dot(table_ref[...], high)
    return both[:size] + both[size:] + dot(table_ref[:size, :], low)


def lanes_apart(value, rows):
    real = value[:, :N2].reshape(rows, GROUPS, N2)
    imag = value[:, N2:].reshape(rows, GROUPS, N2)
    return jnp.concatenate([real, imag], axis=1).reshape(rows * 2 * GROUPS, N2)


def lanes_together(value, rows):
    both = value.reshape(rows, 2 * GROUPS, N2)
    return jnp.concatenate([both[:, :GROUPS], both[:, GROUPS:]], axis=2).reshape(rows * GROUPS, 2 * N2)


def load_zeroth(ref, rows):
    return jnp.concatenate(
        [ref[pl.ds(0, rows, stride=2 * GROUPS), :], ref[pl.ds(GROUPS, rows, stride=2 * GROUPS), :]], axis=1
    )


def store_zeroth(ref, rows, value):
    ref[pl.ds(0, rows, stride=2 * GROUPS), :] = value[:, :N2]
    ref[pl.ds(GROUPS, rows, stride=2 * GROUPS), :] = value[:, N2:]


def forward_rows(points_ref, rows, first_ref, turn_ref, second_ref, special_ref, mid_ref, out_ref):
    padded = points_ref.shape[0]
    turn_cos = turn_ref[:GROUPS, :][None]
    turn_sin = turn_ref[GROUPS:, :][None]
    for pair in range(padded // (2 * BLOCK)):
        base = pair * 2 * BLOCK
        left = points_ref[base : base + BLOCK].reshape(BLOCK * N1, N2)
        right = points_ref[base + BLOCK : base + 2 * BLOCK].reshape(BLOCK * N1, N2)
        value = product_left(first_ref, jnp.concatenate([left, right], axis=1))
        for side in range(2):
            digits = value[:, side * N2 : (side + 1) * N2].reshape(BLOCK, N1, N2)
            real, imag = digits[:, :GROUPS], digits[:, GROUPS:]
            turned = jnp.concatenate(
                [real * turn_cos + imag * turn_sin, imag * turn_cos - real * turn_sin], axis=1
            )
            at = (base + side * BLOCK) * N1
            mid_ref[at : at + BLOCK * N1, :] = turned.reshape(BLOCK * N1, N2)
    result = product_right(lanes_together(mid_ref[...], padded), second_ref)
    out_ref[...] = lanes_apart(result, padded)[: rows * N1]
    store_zeroth(out_ref, rows, product_right(load_zeroth(mid_ref, padded), special_ref)[:rows])


def spectral_back(spec_ref, rows, padded, second_ref, special_ref, mid_ref):
    result = product_right(lanes_together(spec_ref[...], rows), second_ref)
    mid_ref[: rows * N1, :] = lanes_apart(result, rows)
    if padded > rows:
        mid_ref[rows * N1 : padded * N1, :] = jnp.zeros(((padded - rows) * N1, N2), jnp.float32)
    store_zeroth(mid_ref, rows, product_right(load_zeroth(spec_ref, rows), special_ref))


def digits_back(mid_ref, pair, turn_ref, first_ref):
    turn_cos = turn_ref[:GROUPS, :][None]
    turn_sin = turn_ref[GROUPS:, :][None]
    sides = []
    for side in range(2):
        at = (2 * pair + side) * BLOCK * N1
        both = mid_ref[at : at + BLOCK * N1, :].reshape(BLOCK, N1, N2)
        real, imag = both[:, :GROUPS], both[:, GROUPS:]
        turned = jnp.concatenate(
            [real * turn_cos - imag * turn_sin, imag * turn_cos + real * turn_sin], axis=1
        )
        sides.append(turned.reshape(BLOCK * N1, N2))
    return product_left(first_ref, jnp.concatenate(sides, axis=1))


def backward_rows(spec_ref, rows, first_ref, turn_ref, second_ref, special_ref, mid_ref, out_ref):
    padded = out_ref.shape[0]
    spectral_back(spec_ref, rows, padded, second_ref, special_ref, mid_ref)
    for pair in range(padded // (2 * BLOCK)):
        base = pair * 2 * BLOCK
        value = digits_back(mid_ref, pair, turn_ref, first_ref)
        out_ref[base : base + BLOCK] = value[:, :N2].reshape(BLOCK, N1, N2)
        out_ref[base + BLOCK : base + 2 * BLOCK] = value[:, N2:].reshape(BLOCK, N1, N2)


def factor_kernel(rows, lon_ref, couple_ref, eigen_ref, ratio_ref, inverse_ref, edge_ref):
    eigen = eigen_ref[...]
    groups = eigen.shape[0]
    half = rows // 2
    last = rows + 2 * OV - 1

    def plain(e):
        return 1.0 + lon_ref[e] * eigen

    def put(ref, index, value):
        ref[index * groups : (index + 1) * groups, :] = value

    def chain(start, stop, step, into):
        excess = inverse = None
        for e in range(start, stop + step, step):
            before = couple_ref[e] if step > 0 else couple_ref[e + 1]
            after = couple_ref[e + 1] if step > 0 else couple_ref[e]
            if inverse is None:
                ratio = None
                excess = plain(e) + before
            else:
                ratio = before * inverse
                excess = plain(e) + ratio * excess
            divisor = after + excess
            inverse = 1.0 / divisor
            into(e, ratio, inverse, excess, divisor)

    kept = {}

    def top(e, ratio, inverse, excess, divisor):
        if e == OV - 1:
            put(edge_ref, 0, inverse)
        if e >= OV:
            put(ratio_ref, e - OV, ratio)
            put(inverse_ref, e - OV, inverse)
        if e == OV + half - 1:
            kept["top"] = excess, divisor

    def bottom(e, ratio, inverse, excess, divisor):
        if e == OV + rows:
            put(edge_ref, 1, inverse)
        if e < OV + rows:
            put(ratio_ref, e - OV, ratio)
            put(inverse_ref, e - OV, inverse)
        if e == OV + half:
            kept["bottom"] = excess, divisor

    def next_band(e, ratio, inverse, excess, divisor):
        if ratio is not None:
            put(edge_ref, 7 + e - rows - 1, ratio)
        if e == OV + rows - 1:
            put(edge_ref, 5, inverse)

    def previous_band(e, ratio, inverse, excess, divisor):
        if ratio is not None:
            put(edge_ref, 14 + e - OV, ratio)
        if e == OV:
            put(edge_ref, 6, inverse)

    chain(rows, OV + rows - 1, 1, next_band)
    chain(2 * OV - 1, OV, -1, previous_band)
    chain(0, OV + half - 1, 1, top)
    chain(last, OV + half, -1, bottom)
    excess_top, divisor_top = kept["top"]
    excess_bottom, divisor_bottom = kept["bottom"]
    between = couple_ref[OV + half]
    inverse = 1.0 / (between * (excess_top + excess_bottom) + excess_top * excess_bottom)
    put(edge_ref, 2, divisor_bottom * inverse)
    put(edge_ref, 3, divisor_top * inverse)
    put(edge_ref, 4, between * inverse)


def edge_sums(low_rows, high_rows, next_ratio, previous_ratio):
    top = high_rows(0)
    for i in range(1, OV):
        top = high_rows(i) + next_ratio(i - 1) * top
    bottom = low_rows(OV - 1)
    for i in range(OV - 2, -1, -1):
        bottom = low_rows(i) + previous_ratio(i) * bottom
    return top, bottom


def swap_out(parity, up, down, even_ref, odd_ref):
    is_even = parity == 0
    even_ref[...] = jnp.where(is_even, up, down)
    odd_ref[...] = jnp.where(is_even, down, up)


def swap_in(parity, even, odd):
    is_even = parity == 0
    return jnp.where(is_even, odd, even), jnp.where(is_even, even, odd)


def solve_first(rows, groups, right_side_row, from_low, from_high, ratio_ref, inverse_ref, edge_ref, out_ref):
    half = rows // 2

    def at(ref, index):
        return ref[index * groups : (index + 1) * groups, :]

    def put(index, value):
        out_ref[index * groups : (index + 1) * groups, :] = value

    low, high = from_low, from_high
    for i in range(half):
        j = rows - 1 - i
        low = right_side_row(i) + at(ratio_ref, i) * low
        high = right_side_row(j) + at(ratio_ref, j) * high
        put(i, low)
        put(j, high)
    meet(rows, groups, low, high, ratio_ref, inverse_ref, edge_ref, at, lambda i: at(out_ref, i), put)


def meet(rows, groups, low, high, ratio_ref, inverse_ref, edge_ref, at, value, put):
    half = rows // 2
    between = at(edge_ref, 4)
    x_low = at(edge_ref, 2) * low + between * high
    x_high = at(edge_ref, 3) * high + between * low
    put(half - 1, x_low)
    put(half, x_high)
    for i in range(half - 2, -1, -1):
        j = rows - 1 - i
        x_low = value(i) * at(inverse_ref, i) + at(ratio_ref, i + 1) * x_low
        x_high = value(j) * at(inverse_ref, j) + at(ratio_ref, j - 1) * x_high
        put(i, x_low)
        put(j, x_high)


def sigmas(
    couple_low, couple_high, own_top, own_bottom, got_top, got_bottom, sent_top, sent_bottom, from_low, from_high,
    ratio_first, ratio_last, edge_ref, next_inverse, previous_inverse,
):
    groups = own_top.shape[0]

    def edge(index):
        return edge_ref[index * groups : (index + 1) * groups, :]

    beyond_low = (got_top + couple_low * own_top) * edge(0)
    beyond_high = (got_bottom + couple_high * own_bottom) * edge(1)
    theirs_low = (sent_bottom + couple_low * from_low) * previous_inverse
    theirs_high = (sent_top + couple_high * from_high) * next_inverse
    low = ratio_first * (couple_low * (own_top - theirs_low)) + couple_low * (from_low - beyond_low)
    high = ratio_last * (couple_high * (own_bottom - theirs_high)) + couple_high * (from_high - beyond_high)
    return low, high


def solve_second(
    rows, groups, couple_low, couple_high, own_top, own_bottom, got_top, got_bottom, sent_top, sent_bottom,
    from_low, from_high, ratio_ref, inverse_ref, edge_ref, first_ref, out_ref, mid_ref,
):
    half = rows // 2

    def at(ref, index):
        return ref[index * groups : (index + 1) * groups, :]

    low, high = sigmas(
        couple_low, couple_high, own_top, own_bottom, got_top, got_bottom, sent_top, sent_bottom,
        from_low, from_high, at(ratio_ref, 0), at(ratio_ref, rows - 1), edge_ref, at(edge_ref, 5), at(edge_ref, 6),
    )
    for i in range(half):
        j = rows - 1 - i
        if i:
            low = at(ratio_ref, i) * low
            high = at(ratio_ref, j) * high
        mid_ref[i * groups : (i + 1) * groups, :] = low
        mid_ref[j * groups : (j + 1) * groups, :] = high

    def put(index, value):
        rows_at = slice(index * groups, (index + 1) * groups)
        out_ref[rows_at, :] = first_ref[rows_at, :] + value

    meet(rows, groups, low, high, ratio_ref, inverse_ref, edge_ref, at, lambda i: at(mid_ref, i), put)


def call(body, outs, ins, spaces, scratch, flops, name, out_spaces=None, aliases=None):
    nbytes = sum(x.size * x.dtype.itemsize for x in ins) + sum(4 * math.prod(s) for s in outs)
    out = pl.pallas_call(
        body,
        out_shape=[jax.ShapeDtypeStruct(s, jnp.float32) for s in outs],
        in_specs=[pl.BlockSpec(memory_space=s) for s in spaces],
        out_specs=[pl.BlockSpec(memory_space=s) for s in out_spaces or [VMEM] * len(outs)],
        input_output_aliases=aliases or {},
        scratch_shapes=scratch,
        compiler_params=pltpu.CompilerParams(vmem_limit_bytes=48 << 20),
        cost_estimate=pl.CostEstimate(flops=flops, bytes_accessed=nbytes, transcendentals=0),
        name=name,
    )(*ins)
    return out


def pad_rows(rows):
    return -(-rows // (2 * BLOCK)) * 2 * BLOCK


def swap(value_even, value_odd):
    count = lax.axis_size("lat")
    even = [(i, i ^ 1) for i in range(count) if (i ^ 1) < count]
    odd = [(i, ((i + 1) ^ 1) - 1) for i in range(1, count) if ((i + 1) ^ 1) - 1 < count]
    value_odd = lax.ppermute(value_odd, "lat", odd)
    return lax.ppermute(value_even, "lat", even), value_odd


def send_level(piece, mask, size):
    return lax.ppermute(piece, "lon", [(d, d ^ mask) for d in range(size)])


def swap_levels(pieces):
    return [pieces[0]] + [send_level(pieces[mask], mask, len(pieces)) for mask in range(1, len(pieces))]


def operator_parts(rows, lon_coef, lat_coef, level_scale):
    row_first = lax.axis_index("lat") * rows
    extent = rows + 2 * OV
    lon_window = lax.dynamic_slice_in_dim(jnp.pad(lon_coef, (OV, OV)), row_first, extent)
    couple = lax.dynamic_slice_in_dim(jnp.pad(lat_coef, (OV + 1, OV + 2)), row_first, extent + 1)
    return level_scale[:, None] * lon_window[None], level_scale[:, None] * couple[None]


def factor(rows, groups, lon_window, couple, eigen):
    block = (rows * groups, N2)
    return call(
        functools.partial(factor_kernel, rows),
        [block, block, (21 * groups, N2)],
        [lon_window, couple, eigen],
        [SMEM, SMEM, VMEM],
        [],
        rows * groups * N2 * 20,
        "factor",
    )


def vmem(*shape):
    return pltpu.VMEM(shape, jnp.float32)


def rows_of(ref, groups, first=0):
    return lambda i: ref[(i - first) * groups : (i - first + 1) * groups, :]


def on_device(right_side, lon_coef, lat_coef, level_scale):
    const = {k: jnp.asarray(v) for k, v in tables(right_side.shape[1]).items()}
    if lax.axis_size("lon") != right_side.shape[1]:
        return shared_levels(const, right_side, lon_coef, lat_coef, level_scale)
    return whole_levels(const, right_side, lon_coef, lat_coef, level_scale)


def early_rows(rows):
    return rows // 2 + 2


def edge_kernel(rows, level_ref, lon_ref, couple_ref, eigen_ref, out_ref):
    eigen = eigen_ref[...]
    groups = eigen.shape[0]
    level = level_ref[0]
    low = high = low_inverse = high_inverse = None
    for i in range(OV):
        e, f = rows + i, 2 * OV - 1 - i
        if i == 0:
            low = 1.0 + lon_ref[level, e] * eigen + couple_ref[level, e]
            high = 1.0 + lon_ref[level, f] * eigen + couple_ref[level, f + 1]
        else:
            low_ratio = couple_ref[level, e] * low_inverse
            high_ratio = couple_ref[level, f + 1] * high_inverse
            out_ref[(i - 1) * groups : i * groups, :] = low_ratio
            out_ref[(OV + i - 1) * groups : (OV + i) * groups, :] = high_ratio
            low = 1.0 + lon_ref[level, e] * eigen + low_ratio * low
            high = 1.0 + lon_ref[level, f] * eigen + high_ratio * high
        low_inverse = 1.0 / (couple_ref[level, e + 1] + low)
        high_inverse = 1.0 / (couple_ref[level, f] + high)
    out_ref[(OV - 1) * groups : OV * groups, :] = low_inverse
    out_ref[(2 * OV - 1) * groups :, :] = high_inverse


def level_response(rows, early, level, lon_ref, couple_ref, eigen, put_ratio, put_inverse, keep, tables):
    half = rows // 2
    ratio_at, value_at, put_value, put_phi, put_psi = tables

    def plain(e):
        return 1.0 + lon_ref[level, e] * eigen

    low = high = None
    low_inverse = high_inverse = low_value = high_value = None
    for i in range(-OV, half):
        j = rows - 1 - i
        e, f = i + OV, j + OV
        if low is None:
            low = plain(e) + couple_ref[level, e]
            high = plain(f) + couple_ref[level, f + 1]
        else:
            low_ratio = couple_ref[level, e] * low_inverse
            high_ratio = couple_ref[level, f + 1] * high_inverse
            low = plain(e) + low_ratio * low
            high = plain(f) + high_ratio * high
        low_divisor = couple_ref[level, e + 1] + low
        high_divisor = couple_ref[level, f] + high
        low_inverse = 1.0 / low_divisor
        high_inverse = 1.0 / high_divisor
        yield
        if i == -1:
            keep(0, low_inverse)
            keep(1, high_inverse)
        if i == 0:
            low_value = high_value = jnp.ones_like(eigen)
        elif i > 0:
            low_value = low_ratio * low_value
            high_value = high_ratio * high_value
        if i >= 0:
            put_ratio(i, low_ratio)
            put_ratio(j, high_ratio)
            put_inverse(i, low_inverse)
            put_inverse(j, high_inverse)
            put_value(i, low_value * low_inverse)
            if j < early:
                put_value(j, high_value * high_inverse)
    between = couple_ref[level, OV + half]
    inverse = 1.0 / (between * (low + high) + low * high)
    across = between * inverse
    high_inverse = high_divisor * inverse
    low_inverse = low_divisor * inverse
    keep(2, high_inverse)
    keep(3, low_inverse)
    keep(4, across)
    phi = high_inverse * low_value
    psi = across * high_value
    phi_down = across * low_value
    psi_down = low_inverse * high_value
    put_phi(half - 1, phi)
    put_psi(half - 1, psi)
    for i in range(half - 2, -1, -1):
        yield
        ratio = ratio_at(i + 1)
        phi = value_at(i) + ratio * phi
        psi = ratio * psi
        put_phi(i, phi)
        put_psi(i, psi)
    put_phi(half, phi_down)
    put_psi(half, psi_down)
    for j in range(half + 1, early):
        ratio = ratio_at(j - 1)
        phi_down = ratio * phi_down
        psi_down = value_at(j) + ratio * psi_down
        put_phi(j, phi_down)
        put_psi(j, psi_down)


def getter(ref, groups):
    return lambda index: ref[index * groups : (index + 1) * groups, :]


def putter(ref, groups, first=0):
    def put(index, value):
        at = first + index * groups
        ref[pl.ds(at if isinstance(at, int) else pl.multiple_of(at, groups), groups), :] = value

    return put


def together(*steps):
    steps = list(steps)
    while steps:
        steps = [step for step in steps if next(step, steps) is not steps]


def partner_response(rows, early, place_ref, lon_ref, couple_ref, eigen, masks, phi_ref, psi_ref, kept_refs, value_refs):
    groups = eigen.shape[0]

    def nothing(index, value):
        pass

    def one(n, mask):
        put_kept = putter(kept_refs[n], groups)

        def put_ratio(index, value):
            if index < early:
                put_kept(index, value)

        first = n * early * groups
        return level_response(
            rows, early, place_ref[0] ^ mask, lon_ref, couple_ref, eigen, put_ratio, nothing, nothing,
            (
                getter(kept_refs[n], groups), getter(value_refs[n], groups), putter(value_refs[n], groups),
                putter(phi_ref, groups, first), putter(psi_ref, groups, first),
            ),
        )

    return [one(n, mask) for n, mask in enumerate(masks)]


def own_kernel(
    rows, early, masks, place_ref, lon_ref, couple_ref, eigen_ref, ratio_ref, inverse_ref, edge_ref, phi_ref, psi_ref,
    phi_near_ref, psi_near_ref, value_ref, *refs,
):
    eigen = eigen_ref[...]
    groups = eigen.shape[0]
    own = level_response(
        rows, early, place_ref[0], lon_ref, couple_ref, eigen, putter(ratio_ref, groups),
        putter(inverse_ref, groups), putter(edge_ref, groups),
        (
            getter(ratio_ref, groups), getter(value_ref, groups), putter(value_ref, groups),
            putter(phi_ref, groups), putter(psi_ref, groups),
        ),
    )
    count = len(masks)
    together(
        own,
        *partner_response(
            rows, early, place_ref, lon_ref, couple_ref, eigen, masks, phi_near_ref, psi_near_ref,
            refs[:count], refs[count:],
        ),
    )


def partners_kernel(
    rows, early, masks, place_ref, lon_ref, couple_ref, eigen_ref, after_ref, phi_ref, psi_ref, token_ref, *refs
):
    token_ref[...] = after_ref[...]
    count = len(masks)
    together(
        *partner_response(
            rows, early, place_ref, lon_ref, couple_ref, eigen_ref[...], masks, phi_ref, psi_ref,
            refs[:count], refs[count:],
        )
    )


def whole_levels(const, right_side, lon_coef, lat_coef, level_scale):
    rows, levels, lon_count = right_side.shape
    digits = N1 // levels
    groups = 2 * GROUPS
    lon_at = lax.axis_index("lon").astype(jnp.int32)
    parity = (lax.axis_index("lat") % 2).astype(jnp.int32)
    place = jnp.stack([lon_at, parity])
    half = rows // 2
    early = early_rows(rows)
    late = rows - early
    eigen = const["eigen"].reshape(groups, N2)
    lon_all, couple_all = operator_parts(rows, lon_coef, lat_coef, level_scale)
    (around,) = call(
        functools.partial(edge_kernel, rows),
        [(2 * OV * groups, N2)],
        [place, lon_all, couple_all, eigen],
        [SMEM, SMEM, SMEM, VMEM],
        [],
        16 * groups * N2 * 20,
        "edge",
    )
    block = (rows * groups, N2)
    early_block = (early * groups, N2)
    early_block = (early * groups, N2)
    near_masks, far_masks = [1], list(range(2, levels))
    ratio, inverse, edge, phi, psi, phi_near, psi_near = call(
        functools.partial(own_kernel, rows, early, near_masks),
        [block, block, (5 * groups, N2)] + [early_block] * 4,
        [place, lon_all, couple_all, eigen],
        [SMEM, SMEM, SMEM, VMEM],
        [vmem(*early_block)] * 3,
        2 * rows * groups * N2 * 20,
        "own",
    )
    row = (groups, N2)
    ends = 2 * OV
    inner = rows - ends
    span = OV * digits
    by_row = right_side.reshape(rows, levels, digits, N2).transpose(0, 2, 1, 3).reshape(-1, N2)

    far = list(range(2, levels))

    def pack_ends(place_ref, in_ref, after_ref, *refs):
        del after_ref
        for end_ref, mask in zip(refs, [0] + far):
            level = place_ref[0] ^ mask
            end_ref[:span, :] = in_ref[pl.ds(level, span, stride=levels), :]
            end_ref[span:, :] = in_ref[pl.ds(level + levels * (rows - OV) * digits, span, stride=levels), :]

    end_packed = call(
        pack_ends,
        [(ends * digits, N2)] * (levels - 1),
        [place, by_row, around],
        [SMEM, VMEM, pl.ANY],
        [],
        0,
        "pack_ends",
    )

    def pack(place_ref, in_ref, after_ref, *refs):
        del after_ref
        for mask, out_ref in enumerate(refs):
            level = place_ref[0] ^ mask
            skip = 0 if mask == 1 else levels * span
            out_ref[...] = in_ref[pl.ds(level + skip, out_ref.shape[0], stride=levels), :]

    packed = call(
        pack,
        [((rows if mask == 1 else inner) * digits, N2) for mask in range(levels)],
        [place, by_row, end_packed[0]],
        [SMEM, VMEM, pl.ANY],
        [],
        0,
        "pack",
    )
    end_pieces = [end_packed[0], None] + [send_level(p, m, levels) for p, m in zip(end_packed[1:], far)]
    near = send_level(packed[1], 1, levels)
    end_pieces[1] = near
    inner_pieces = [packed[0], near] + [send_level(packed[m], m, levels) for m in far]
    forward = [const["first"], const["turn"], const["second"], const["special"]]
    pad_ends, pad_inner = pad_rows(ends), pad_rows(inner)

    def ends_body(place_ref, *refs):
        pieces, refs = refs[:levels], refs[levels:]
        tables_in, edge_ref = refs[:4], refs[4]
        spec_ref, top_ref, bottom_ref, even_ref, odd_ref, full_ref, mid_ref = refs[5:]
        for mask, piece in enumerate(pieces):
            at = pl.multiple_of((place_ref[0] ^ mask) * digits, digits)
            last = piece.shape[0] - span
            full_ref[:OV, pl.ds(at, digits), :] = piece[:span, :].reshape(OV, digits, N2)
            full_ref[OV:ends, pl.ds(at, digits), :] = piece[last:, :].reshape(OV, digits, N2)
        forward_rows(full_ref, ends, *tables_in, mid_ref, spec_ref)
        top, bottom = edge_sums(
            rows_of(spec_ref, groups), rows_of(spec_ref, groups, -OV),
            rows_of(edge_ref, groups), lambda i: edge_ref[(2 * OV - 2 - i) * groups : (2 * OV - 1 - i) * groups, :],
        )
        top_ref[...] = top
        bottom_ref[...] = bottom
        swap_out(place_ref[1], top, bottom, even_ref, odd_ref)

    end_spectral, sent_top, sent_bottom, even, odd = call(
        ends_body,
        [(ends * groups, N2)] + [row] * 4,
        [place, *end_pieces, *forward, around],
        [SMEM] + [VMEM] * (levels + 5),
        [vmem(pad_ends, N1, N2), vmem(pad_ends * N1, N2)],
        ends * NLON * 256 * 4,
        "ends",
    )
    even, odd = swap(even, odd)
    backward = [const["first_back"], const["turn"], const["second_back"], const["special_back"]]
    pad_early, pad_late = pad_rows(early), pad_rows(late)

    def spread(place_ref, full_ref, count, out_refs):
        for mask, out_ref in enumerate(out_refs):
            at = pl.multiple_of((place_ref[0] ^ mask) * digits, digits)
            out_ref[: count * digits, :] = full_ref[:count, pl.ds(at, digits), :].reshape(count * digits, N2)

    def inner_body(place_ref, *refs):
        pieces, refs = refs[:levels], refs[levels:]
        tables_in, back_in, refs = refs[:4], refs[4:7], refs[7:]
        ends_ref, even_ref, odd_ref, ratio_ref, inverse_ref, edge_ref = refs[:6]
        late_ref, top_ref, even_out, odd_out = refs[6:10]
        early_refs, refs = refs[10 : 10 + levels], refs[10 + levels :]
        full_ref, mid_ref, spec_ref, sum_ref, back_full_ref, back_mid_ref = refs
        for mask, piece in enumerate(pieces):
            at = pl.multiple_of((place_ref[0] ^ mask) * digits, digits)
            skip = span if mask == 1 else 0
            full_ref[:inner, pl.ds(at, digits), :] = piece[skip : skip + inner * digits, :].reshape(
                inner, digits, N2
            )
        if pad_inner > inner:
            full_ref[inner:] = jnp.zeros((pad_inner - inner, N1, N2), jnp.float32)
        forward_rows(full_ref, inner, *tables_in, mid_ref, spec_ref)
        low, high = swap_in(place_ref[1], even_ref[...], odd_ref[...])

        def spec_row(i):
            if i < OV:
                return rows_of(ends_ref, groups)(i)
            if i >= rows - OV:
                return rows_of(ends_ref, groups, rows - ends)(i)
            return rows_of(spec_ref, groups, OV)(i)

        solve_first(rows, groups, spec_row, low, high, ratio_ref, inverse_ref, edge_ref, sum_ref)
        top = sum_ref[:groups, :]
        top_ref[...] = top
        late_ref[...] = sum_ref[early * groups :, :]
        swap_out(place_ref[1], sum_ref[(rows - 1) * groups :, :], top, even_out, odd_out)
        early_sum = sum_ref.at[pl.ds(0, early * groups), :]
        backward_rows(early_sum, early, back_in[0], tables_in[1], back_in[1], back_in[2], back_mid_ref, back_full_ref)
        spread(place_ref, back_full_ref, early, early_refs)

    late_first, own_top, even2, odd2, *early_pieces = call(
        inner_body,
        [(late * groups, N2), row, row, row] + [(early * digits, N2)] * levels,
        [
            place, *inner_pieces, *forward, backward[0], backward[2], backward[3],
            end_spectral, even, odd, ratio, inverse, edge,
        ],
        [SMEM] + [VMEM] * (levels + 13),
        [
            vmem(pad_inner, N1, N2), vmem(pad_inner * N1, N2), vmem(inner * N1, N2), vmem(rows * groups, N2),
            vmem(pad_early, N1, N2), vmem(pad_early * N1, N2),
        ],
        (inner + early) * NLON * 256 * 4,
        "inner",
    )
    early_pieces = swap_levels(early_pieces)
    even2, odd2 = swap(even2, odd2)

    phi_far, psi_far, token = call(
        functools.partial(partners_kernel, rows, early, far_masks),
        [(len(far_masks) * early * groups, N2)] * 2 + [row],
        [place, lon_all, couple_all, eigen, own_top],
        [SMEM, SMEM, SMEM, VMEM, VMEM],
        [vmem(*early_block)] * (2 * len(far_masks)),
        len(far_masks) * rows * groups * N2 * 20,
        "partners",
    )

    def sigma_body(place_ref, couple_ref, *refs):
        first_ref, own_top_ref, even_ref, odd_ref, even2_ref, odd2_ref, top_ref, bottom_ref = refs[:8]
        ratio_ref, edge_ref, around_ref = refs[8:11]
        sigma_ref = refs[-1]
        level = place_ref[0]
        got_top, got_bottom = swap_in(place_ref[1], even_ref[...], odd_ref[...])
        from_low, from_high = swap_in(place_ref[1], even2_ref[...], odd2_ref[...])
        low, high = sigmas(
            couple_ref[level, OV], couple_ref[level, OV + rows], own_top_ref[...], first_ref[(late - 1) * groups :, :],
            got_top, got_bottom, top_ref[...], bottom_ref[...], from_low, from_high,
            ratio_ref[:groups, :], ratio_ref[(rows - 1) * groups :, :], edge_ref,
            around_ref[(OV - 1) * groups : OV * groups, :], around_ref[(2 * OV - 1) * groups :, :],
        )
        sigma_ref[:groups, :] = low
        sigma_ref[groups:, :] = high

    (sigma,) = call(
        sigma_body,
        [(2 * groups, N2)],
        [
            place, couple_all, late_first, own_top, even, odd, even2, odd2, sent_top, sent_bottom, ratio, edge, around,
            *early_pieces[1:], token,
        ],
        [SMEM, SMEM] + [VMEM] * 11 + [pl.ANY] * levels,
        [],
        groups * N2 * 40,
        "sigma",
    )
    far_sigma = [send_level(sigma, mask, levels) for mask in far]
    def second_body(place_ref, *refs):
        sigma_ref, after_ref, first_ref, ratio_ref, inverse_ref, edge_ref = refs[:6]
        del after_ref
        tables_in, refs = refs[6:10], refs[10:]
        late_refs = refs[:levels]
        sum_ref, mid_ref, full_ref = refs[levels:]
        low, high = sigma_ref[:groups, :], sigma_ref[groups:, :]

        def at(ref, index):
            return ref[index * groups : (index + 1) * groups, :]

        for i in range(half):
            j = rows - 1 - i
            if i:
                low = at(ratio_ref, i) * low
                high = at(ratio_ref, j) * high
            mid_ref[(j - half) * groups : (j - half + 1) * groups, :] = high
        x_high = at(edge_ref, 3) * high + at(edge_ref, 4) * low
        for j in range(half, rows):
            if j > half:
                x_high = at(mid_ref, j - half) * at(inverse_ref, j) + at(ratio_ref, j - 1) * x_high
            if j >= early:
                here = slice((j - early) * groups, (j - early + 1) * groups)
                sum_ref[here, :] = first_ref[here, :] + x_high
        backward_rows(sum_ref, late, *tables_in, mid_ref, full_ref)
        spread(place_ref, full_ref, late, late_refs)
        late_refs[1][late * digits :, :] = sigma_ref[...]

    late_pieces = call(
        second_body,
        [(late * digits + (2 * groups if mask == 1 else 0), N2) for mask in range(levels)],
        [place, sigma, far_sigma[0], late_first, ratio, inverse, edge, *backward],
        [SMEM, VMEM, pl.ANY] + [VMEM] * 8,
        [vmem(late * groups, N2), vmem(max(pad_late, half) * N1, N2), vmem(pad_late, N1, N2)],
        late * NLON * 256 * 4,
        "second",
    )
    late_pieces = swap_levels(late_pieces)
    sigma_pieces = [sigma, late_pieces[1], *far_sigma]
    total = rows * levels * digits
    early_total = early * levels * digits
    part = const["first_back_part"]

    def correct(place_ref, *refs):
        pieces, sigma_refs, refs = refs[:levels], refs[levels : 2 * levels], refs[2 * levels :]
        responses, refs = refs[:6], refs[6:]
        part_ref, turn_ref, second_ref, special_ref = refs[:4]
        out_ref, sum_ref, mid_ref, done_ref, sem = refs[4:]
        part_rows = part_ref.shape[0] // levels
        mine = part_ref.at[pl.ds(pl.multiple_of(place_ref[0] * part_rows, part_rows), part_rows), :]
        size = early * groups
        for mask in range(levels):
            level = place_ref[0] ^ mask
            last = sigma_refs[mask].shape[0]
            low = sigma_refs[mask][last - 2 * groups : last - groups, :]
            high = sigma_refs[mask][last - groups :, :]
            phi_ref, psi_ref = responses[2 * min(mask, 2) : 2 * min(mask, 2) + 2]
            first = max(mask - 2, 0) * size
            phi_all = phi_ref[first : first + size, :].reshape(early, groups, N2)
            psi_all = psi_ref[first : first + size, :].reshape(early, groups, N2)
            sum_ref[...] = (phi_all * low[None] + psi_all * high[None]).reshape(size, N2)
            spectral_back(sum_ref, early, pad_early, second_ref, special_ref, mid_ref)
            for pair in range(pad_early // (2 * BLOCK)):
                value = digits_back(mid_ref, pair, turn_ref, mine)
                for side in range(2):
                    begin = (2 * pair + side) * BLOCK
                    count = min(BLOCK, early - begin)
                    if count <= 0:
                        continue
                    lines = count * digits
                    whole = pieces[mask][begin * digits : begin * digits + lines, :]
                    done_ref[pl.ds(level + begin * digits * levels, lines, stride=levels), :] = (
                        whole + value[:lines, side * N2 : (side + 1) * N2]
                    )
        copy = pltpu.make_async_copy(done_ref, out_ref.at[pl.ds(0, early_total), :], sem)
        copy.start()
        copy.wait()

    (out,) = call(
        correct,
        [(total, N2)],
        [
            place, *early_pieces, *sigma_pieces, phi, psi, phi_near, psi_near, phi_far, psi_far,
            part, const["turn"], *backward[2:],
        ],
        [SMEM] + [VMEM] * (2 * levels + 10),
        [
            vmem(early * groups, N2), vmem(pad_early * N1, N2), vmem(early_total, N2), pltpu.SemaphoreType.DMA,
        ],
        levels * early * NLON * 256 * 40,
        "correct",
        out_spaces=[pl.ANY],
    )

    chunks = 4

    def unpack(place_ref, *refs):
        pieces = refs[:levels]
        out_ref, done_ref, sems = refs[levels + 1 :]
        lines = late * digits // chunks
        copies = []
        for chunk in range(chunks):
            for mask in range(levels):
                first = (place_ref[0] ^ mask) + chunk * lines * levels
                done_ref[pl.ds(first, lines, stride=levels), :] = pieces[mask][chunk * lines : (chunk + 1) * lines, :]
            here = pl.ds(chunk * lines * levels, lines * levels)
            there = pl.ds(early_total + chunk * lines * levels, lines * levels)
            copy = pltpu.make_async_copy(done_ref.at[here, :], out_ref.at[there, :], sems.at[chunk])
            copy.start()
            copies.append(copy)
        for copy in copies:
            copy.wait()

    (out,) = call(
        unpack,
        [(total, N2)],
        [place, *late_pieces, out],
        [SMEM] + [VMEM] * levels + [pl.ANY],
        [vmem(total - early_total, N2), pltpu.SemaphoreType.DMA((chunks,))],
        0,
        "unpack",
        out_spaces=[pl.ANY],
        aliases={levels + 1: 0},
    )
    return out.reshape(rows, digits, levels, N2).transpose(0, 2, 1, 3).reshape(right_side.shape)


def second_part(
    rows, groups, parity, couple_ref, first_ref, even_ref, odd_ref, even2_ref, odd2_ref, top_ref, bottom_ref,
    ratio_ref, inverse_ref, edge_ref, out_ref, mid_ref,
):
    got_top, got_bottom = swap_in(parity, even_ref[...], odd_ref[...])
    low, high = swap_in(parity, even2_ref[...], odd2_ref[...])
    solve_second(
        rows, groups, couple_ref[OV], couple_ref[OV + rows],
        first_ref[:groups, :], first_ref[(rows - 1) * groups :, :],
        got_top, got_bottom, top_ref[...], bottom_ref[...], low, high,
        ratio_ref, inverse_ref, edge_ref, first_ref, out_ref, mid_ref,
    )


def shared_levels(const, right_side, lon_coef, lat_coef, level_scale):
    rows, levels, lon_count = right_side.shape
    lon_size = lax.axis_size("lon")
    assert lon_size % levels == 0 and GROUPS % (lon_size // levels) == 0 and rows % (lon_size // levels) == 0
    sharers = lon_size // levels
    groups = 2 * GROUPS // sharers
    part_rows = rows // sharers
    digits = N1 // lon_size
    lon_at = lax.axis_index("lon")
    parity = (lax.axis_index("lat") % 2).astype(jnp.int32).reshape(1)
    lon_window, couple = operator_parts(rows, lon_coef, lat_coef, level_scale)
    lon_window = lax.dynamic_index_in_dim(lon_window, lon_at // sharers, 0, False)
    couple = lax.dynamic_index_in_dim(couple, lon_at // sharers, 0, False)
    eigen = lax.dynamic_slice_in_dim(
        const["eigen"], (lon_at % sharers) * (groups // 2), groups // 2, axis=1
    ).reshape(groups, N2)
    ratio, inverse, edge = factor(rows, groups, lon_window, couple, eigen)
    block = (rows * groups, N2)
    row = (groups, N2)
    send = right_side.reshape(sharers, part_rows, levels, lon_count).transpose(2, 0, 1, 3)
    send = send.reshape(lon_size, part_rows, digits, N2)
    got = lax.all_to_all(send, "lon", 0, 0, tiled=True)
    points = got.transpose(1, 0, 2, 3).reshape(part_rows, N1, N2)
    padded = pad_rows(part_rows)

    def transform(points_ref, first_ref, turn_ref, second_ref, special_ref, out_ref, full_ref, mid_ref):
        full_ref[:part_rows] = points_ref[...]
        if padded > part_rows:
            full_ref[part_rows:] = jnp.zeros((padded - part_rows, N1, N2), jnp.float32)
        forward_rows(full_ref, part_rows, first_ref, turn_ref, second_ref, special_ref, mid_ref, out_ref)

    (spectral,) = call(
        transform,
        [(part_rows * N1, N2)],
        [points, const["first"], const["turn"], const["second"], const["special"]],
        [VMEM] * 5,
        [vmem(padded, N1, N2), vmem(padded * N1, N2)],
        part_rows * NLON * 256 * 4,
        "transform",
    )
    spectral = to_coefs(spectral, sharers, part_rows, groups)

    def edges(parity_ref, spec_ref, edge_ref, top_ref, bottom_ref, even_ref, odd_ref):
        top, bottom = edge_sums(
            rows_of(spec_ref, groups), rows_of(spec_ref, groups, OV - rows),
            rows_of(edge_ref, groups, -7), rows_of(edge_ref, groups, -14),
        )
        top_ref[...] = top
        bottom_ref[...] = bottom
        swap_out(parity_ref[0], top, bottom, even_ref, odd_ref)

    sent_top, sent_bottom, even, odd = call(
        edges, [row] * 4, [parity, spectral, edge], [SMEM, VMEM, VMEM], [], groups * N2 * 32, "edges"
    )
    even, odd = swap(even, odd)

    def first(parity_ref, spec_ref, even_ref, odd_ref, ratio_ref, inverse_ref, edge_ref, out_ref, e_ref, o_ref):
        low, high = swap_in(parity_ref[0], even_ref[...], odd_ref[...])
        solve_first(
            rows, groups, rows_of(spec_ref, groups), low, high, ratio_ref, inverse_ref, edge_ref, out_ref
        )
        swap_out(parity_ref[0], out_ref[(rows - 1) * groups :, :], out_ref[:groups, :], e_ref, o_ref)

    iterate, even2, odd2 = call(
        first,
        [block, row, row],
        [parity, spectral, even, odd, ratio, inverse, edge],
        [SMEM] + [VMEM] * 6,
        [],
        rows * groups * N2 * 8,
        "first_solve",
    )
    even2, odd2 = swap(even2, odd2)

    def second(parity_ref, *refs):
        second_part(rows, groups, parity_ref[0], *refs)

    (iterate,) = call(
        second,
        [block],
        [parity, couple, iterate, even, odd, even2, odd2, sent_top, sent_bottom, ratio, inverse, edge],
        [SMEM, SMEM] + [VMEM] * 10,
        [vmem(*block)],
        rows * groups * N2 * 8,
        "second_solve",
    )
    iterate = to_rows(iterate, sharers, part_rows, groups)

    def back(spec_ref, first_ref, turn_ref, second_ref, special_ref, out_ref, mid_ref, full_ref):
        backward_rows(spec_ref, part_rows, first_ref, turn_ref, second_ref, special_ref, mid_ref, full_ref)
        out_ref[...] = full_ref[:part_rows]

    (points,) = call(
        back,
        [(part_rows, N1, N2)],
        [iterate, const["first_back"], const["turn"], const["second_back"], const["special_back"]],
        [VMEM] * 5,
        [vmem(padded * N1, N2), vmem(padded, N1, N2)],
        part_rows * NLON * 256 * 4,
        "back_transform",
    )
    send = points.reshape(part_rows, lon_size, digits, N2).transpose(1, 0, 2, 3)
    got = lax.all_to_all(send, "lon", 0, 0, tiled=True)
    got = got.reshape(levels, sharers, part_rows, lon_count).transpose(1, 2, 0, 3)
    return got.reshape(rows, levels, lon_count)


def level_groups(sharers):
    size = lax.axis_size("lon")
    return [[first + i for i in range(sharers)] for first in range(0, size, sharers)]


def to_coefs(spectral, sharers, part_rows, groups):
    send = spectral.reshape(part_rows, 2, sharers, groups // 2, N2).transpose(2, 0, 1, 3, 4)
    got = lax.all_to_all(
        send, "lon", 0, 0, tiled=True, axis_index_groups=level_groups(sharers)
    )
    return got.reshape(sharers * part_rows * groups, N2)


def to_rows(values, sharers, part_rows, groups):
    send = values.reshape(sharers, part_rows, 2, groups // 2, N2)
    got = lax.all_to_all(
        send, "lon", 0, 0, tiled=True, axis_index_groups=level_groups(sharers)
    )
    return got.transpose(1, 2, 0, 3, 4).reshape(part_rows * N1, N2)


def solution(mesh):
    return jax.shard_map(
        on_device,
        mesh=mesh,
        in_specs=(P("lat", None, "lon"), P(), P(), P()),
        out_specs=P("lat", None, "lon"),
        check_vma=False,
    )
```

```python
import functools
import math

import jax
import jax.numpy as jnp
import numpy as np
from jax import lax
from jax.experimental import pallas as pl
from jax.experimental.pallas import tpu as pltpu
from jax.sharding import PartitionSpec as P

NLON = 4096
OV = 8
N1 = 32
N2 = 128
GROUPS = 16
BLOCK = 8

VMEM = pltpu.VMEM
SMEM = pltpu.SMEM


def numpy_split(table):
    import ml_dtypes

    table = np.asarray(table, np.float32)
    high = table.astype(ml_dtypes.bfloat16)
    low = (table - high.astype(np.float32)).astype(ml_dtypes.bfloat16)
    return high, low


def tables(levels):
    j1 = np.arange(N1)
    j2 = np.arange(N2)
    k2 = np.arange(N2)
    digit = np.arange(GROUPS)
    small = np.zeros((N1, N1))
    small[:GROUPS] = np.cos(2 * np.pi * np.outer(digit, j1) / N1)
    small[GROUPS] = np.cos(np.pi * j1)
    small[GROUPS + 1 :] = -np.sin(2 * np.pi * np.outer(digit[1:], j1) / N1)
    first = np.kron(np.eye(BLOCK), small)
    angle = 2 * np.pi * np.outer(digit, j2) / NLON
    turn_cos = np.cos(angle)
    turn_sin = np.sin(angle)
    phase = 2 * np.pi * (np.outer(j2, k2) % N2) / N2
    cosine, sine = np.cos(phase), np.sin(phase)
    second = np.block([[cosine, -sine], [sine, cosine]])
    special = np.zeros((2 * N2, 2 * N2))
    half = N2 // 2
    special[:N2, : half + 1] = np.cos(2 * np.pi * np.outer(j2, np.arange(half + 1)) / N2)
    special[:N2, half + 1 : N2] = -np.sin(2 * np.pi * np.outer(j2, np.arange(1, half)) / N2)
    odd = 2 * np.pi * np.outer(j2, 1 + 2 * np.arange(half)) / (2 * N2)
    special[N2:, N2 : N2 + half] = np.cos(odd)
    special[N2:, N2 + half :] = -np.sin(odd)
    weight = np.full(2 * N2, 2.0 / NLON)
    weight[0] = 1.0 / NLON
    weight[half] = 1.0 / NLON
    second_back = second.T * (2.0 / NLON)
    special_back = weight[:, None] * special.T
    wave = np.zeros((GROUPS, 2 * N2))
    wave[:, :N2] = digit[:, None] + N1 * k2[None, :]
    wave[:, N2:] = wave[:, :N2]
    lane = np.arange(N2)
    wave[0, :N2] = np.where(lane <= half, N1 * lane, N1 * (lane - half))
    wave[0, N2:] = 16 + N1 * (lane % half)
    eigen = 2.0 - 2.0 * np.cos(2 * np.pi * wave / NLON)
    pair = lambda t: np.concatenate(numpy_split(t), axis=0)
    width = N1 // levels
    part = [pair(np.kron(np.eye(BLOCK), small.T[at : at + width])) for at in range(0, N1, width)]
    return dict(
        first_back_part=np.concatenate(part, axis=0),
        first=pair(first),
        first_back=pair(first.T),
        second=pair(second),
        second_back=pair(second_back),
        special=pair(special),
        special_back=pair(special_back),
        turn=np.concatenate([turn_cos, turn_sin], axis=0).astype(np.float32),
        eigen=np.stack([eigen[:, :N2], eigen[:, N2:]]).astype(np.float32),
    )


def halves(value):
    high = value.astype(jnp.bfloat16)
    low = (value - high.astype(jnp.float32)).astype(jnp.bfloat16)
    return high, low


def dot(a, b):
    return lax.dot_general(a, b, (((1,), (0,)), ((), ())), preferred_element_type=jnp.float32)


def product_right(value, table_ref):
    size = table_ref.shape[0] // 2
    high, low = halves(value)
    table_high = table_ref[:size, :]
    return dot(high, table_high) + dot(low, table_high) + dot(high, table_ref[size:, :])


def product_left(table_ref, value):
    size = table_ref.shape[0] // 2
    high, low = halves(value)
    both = dot(table_ref[...], high)
    return both[:size] + both[size:] + dot(table_ref[:size, :], low)


def lanes_apart(value, rows):
    real = value[:, :N2].reshape(rows, GROUPS, N2)
    imag = value[:, N2:].reshape(rows, GROUPS, N2)
    return jnp.concatenate([real, imag], axis=1).reshape(rows * 2 * GROUPS, N2)


def lanes_together(value, rows):
    both = value.reshape(rows, 2 * GROUPS, N2)
    return jnp.concatenate([both[:, :GROUPS], both[:, GROUPS:]], axis=2).reshape(rows * GROUPS, 2 * N2)


def load_zeroth(ref, rows):
    return jnp.concatenate(
        [ref[pl.ds(0, rows, stride=2 * GROUPS), :], ref[pl.ds(GROUPS, rows, stride=2 * GROUPS), :]], axis=1
    )


def store_zeroth(ref, rows, value):
    ref[pl.ds(0, rows, stride=2 * GROUPS), :] = value[:, :N2]
    ref[pl.ds(GROUPS, rows, stride=2 * GROUPS), :] = value[:, N2:]


def forward_rows(points_ref, rows, first_ref, turn_ref, second_ref, special_ref, mid_ref, out_ref):
    padded = points_ref.shape[0]
    turn_cos = turn_ref[:GROUPS, :][None]
    turn_sin = turn_ref[GROUPS:, :][None]
    for pair in range(padded // (2 * BLOCK)):
        base = pair * 2 * BLOCK
        left = points_ref[base : base + BLOCK].reshape(BLOCK * N1, N2)
        right = points_ref[base + BLOCK : base + 2 * BLOCK].reshape(BLOCK * N1, N2)
        value = product_left(first_ref, jnp.concatenate([left, right], axis=1))
        for side in range(2):
            digits = value[:, side * N2 : (side + 1) * N2].reshape(BLOCK, N1, N2)
            real, imag = digits[:, :GROUPS], digits[:, GROUPS:]
            turned = jnp.concatenate(
                [real * turn_cos + imag * turn_sin, imag * turn_cos - real * turn_sin], axis=1
            )
            at = (base + side * BLOCK) * N1
            mid_ref[at : at + BLOCK * N1, :] = turned.reshape(BLOCK * N1, N2)
    result = product_right(lanes_together(mid_ref[...], padded), second_ref)
    out_ref[...] = lanes_apart(result, padded)[: rows * N1]
    store_zeroth(out_ref, rows, product_right(load_zeroth(mid_ref, padded), special_ref)[:rows])


def spectral_back(spec_ref, rows, padded, second_ref, special_ref, mid_ref):
    result = product_right(lanes_together(spec_ref[...], rows), second_ref)
    mid_ref[: rows * N1, :] = lanes_apart(result, rows)
    if padded > rows:
        mid_ref[rows * N1 : padded * N1, :] = jnp.zeros(((padded - rows) * N1, N2), jnp.float32)
    store_zeroth(mid_ref, rows, product_right(load_zeroth(spec_ref, rows), special_ref))


def digits_back(mid_ref, pair, turn_ref, first_ref):
    turn_cos = turn_ref[:GROUPS, :][None]
    turn_sin = turn_ref[GROUPS:, :][None]
    sides = []
    for side in range(2):
        at = (2 * pair + side) * BLOCK * N1
        both = mid_ref[at : at + BLOCK * N1, :].reshape(BLOCK, N1, N2)
        real, imag = both[:, :GROUPS], both[:, GROUPS:]
        turned = jnp.concatenate(
            [real * turn_cos - imag * turn_sin, imag * turn_cos + real * turn_sin], axis=1
        )
        sides.append(turned.reshape(BLOCK * N1, N2))
    return product_left(first_ref, jnp.concatenate(sides, axis=1))


def backward_rows(spec_ref, rows, first_ref, turn_ref, second_ref, special_ref, mid_ref, out_ref):
    padded = out_ref.shape[0]
    spectral_back(spec_ref, rows, padded, second_ref, special_ref, mid_ref)
    for pair in range(padded // (2 * BLOCK)):
        base = pair * 2 * BLOCK
        value = digits_back(mid_ref, pair, turn_ref, first_ref)
        out_ref[base : base + BLOCK] = value[:, :N2].reshape(BLOCK, N1, N2)
        out_ref[base + BLOCK : base + 2 * BLOCK] = value[:, N2:].reshape(BLOCK, N1, N2)


def factor_kernel(rows, lon_ref, couple_ref, eigen_ref, ratio_ref, inverse_ref, edge_ref):
    eigen = eigen_ref[...]
    groups = eigen.shape[0]
    half = rows // 2
    last = rows + 2 * OV - 1

    def plain(e):
        return 1.0 + lon_ref[e] * eigen

    def put(ref, index, value):
        ref[index * groups : (index + 1) * groups, :] = value

    def chain(start, stop, step, into):
        excess = inverse = None
        for e in range(start, stop + step, step):
            before = couple_ref[e] if step > 0 else couple_ref[e + 1]
            after = couple_ref[e + 1] if step > 0 else couple_ref[e]
            if inverse is None:
                ratio = None
                excess = plain(e) + before
            else:
                ratio = before * inverse
                excess = plain(e) + ratio * excess
            divisor = after + excess
            inverse = 1.0 / divisor
            into(e, ratio, inverse, excess, divisor)

    kept = {}

    def top(e, ratio, inverse, excess, divisor):
        if e == OV - 1:
            put(edge_ref, 0, inverse)
        if e >= OV:
            put(ratio_ref, e - OV, ratio)
            put(inverse_ref, e - OV, inverse)
        if e == OV + half - 1:
            kept["top"] = excess, divisor

    def bottom(e, ratio, inverse, excess, divisor):
        if e == OV + rows:
            put(edge_ref, 1, inverse)
        if e < OV + rows:
            put(ratio_ref, e - OV, ratio)
            put(inverse_ref, e - OV, inverse)
        if e == OV + half:
            kept["bottom"] = excess, divisor

    def next_band(e, ratio, inverse, excess, divisor):
        if ratio is not None:
            put(edge_ref, 7 + e - rows - 1, ratio)
        if e == OV + rows - 1:
            put(edge_ref, 5, inverse)

    def previous_band(e, ratio, inverse, excess, divisor):
        if ratio is not None:
            put(edge_ref, 14 + e - OV, ratio)
        if e == OV:
            put(edge_ref, 6, inverse)

    chain(rows, OV + rows - 1, 1, next_band)
    chain(2 * OV - 1, OV, -1, previous_band)
    chain(0, OV + half - 1, 1, top)
    chain(last, OV + half, -1, bottom)
    excess_top, divisor_top = kept["top"]
    excess_bottom, divisor_bottom = kept["bottom"]
    between = couple_ref[OV + half]
    inverse = 1.0 / (between * (excess_top + excess_bottom) + excess_top * excess_bottom)
    put(edge_ref, 2, divisor_bottom * inverse)
    put(edge_ref, 3, divisor_top * inverse)
    put(edge_ref, 4, between * inverse)


def edge_sums(low_rows, high_rows, next_ratio, previous_ratio):
    top = high_rows(0)
    for i in range(1, OV):
        top = high_rows(i) + next_ratio(i - 1) * top
    bottom = low_rows(OV - 1)
    for i in range(OV - 2, -1, -1):
        bottom = low_rows(i) + previous_ratio(i) * bottom
    return top, bottom


def swap_out(parity, up, down, even_ref, odd_ref):
    is_even = parity == 0
    even_ref[...] = jnp.where(is_even, up, down)
    odd_ref[...] = jnp.where(is_even, down, up)


def swap_in(parity, even, odd):
    is_even = parity == 0
    return jnp.where(is_even, odd, even), jnp.where(is_even, even, odd)


def solve_first(rows, groups, right_side_row, from_low, from_high, ratio_ref, inverse_ref, edge_ref, out_ref):
    half = rows // 2

    def at(ref, index):
        return ref[index * groups : (index + 1) * groups, :]

    def put(index, value):
        out_ref[index * groups : (index + 1) * groups, :] = value

    low, high = from_low, from_high
    for i in range(half):
        j = rows - 1 - i
        low = right_side_row(i) + at(ratio_ref, i) * low
        high = right_side_row(j) + at(ratio_ref, j) * high
        put(i, low)
        put(j, high)
    meet(rows, groups, low, high, ratio_ref, inverse_ref, edge_ref, at, lambda i: at(out_ref, i), put)


def meet(rows, groups, low, high, ratio_ref, inverse_ref, edge_ref, at, value, put):
    half = rows // 2
    between = at(edge_ref, 4)
    x_low = at(edge_ref, 2) * low + between * high
    x_high = at(edge_ref, 3) * high + between * low
    put(half - 1, x_low)
    put(half, x_high)
    for i in range(half - 2, -1, -1):
        j = rows - 1 - i
        x_low = value(i) * at(inverse_ref, i) + at(ratio_ref, i + 1) * x_low
        x_high = value(j) * at(inverse_ref, j) + at(ratio_ref, j - 1) * x_high
        put(i, x_low)
        put(j, x_high)


def sigmas(
    couple_low, couple_high, own_top, own_bottom, got_top, got_bottom, sent_top, sent_bottom, from_low, from_high,
    ratio_first, ratio_last, edge_ref, next_inverse, previous_inverse,
):
    groups = own_top.shape[0]

    def edge(index):
        return edge_ref[index * groups : (index + 1) * groups, :]

    beyond_low = (got_top + couple_low * own_top) * edge(0)
    beyond_high = (got_bottom + couple_high * own_bottom) * edge(1)
    theirs_low = (sent_bottom + couple_low * from_low) * previous_inverse
    theirs_high = (sent_top + couple_high * from_high) * next_inverse
    low = ratio_first * (couple_low * (own_top - theirs_low)) + couple_low * (from_low - beyond_low)
    high = ratio_last * (couple_high * (own_bottom - theirs_high)) + couple_high * (from_high - beyond_high)
    return low, high


def solve_second(
    rows, groups, couple_low, couple_high, own_top, own_bottom, got_top, got_bottom, sent_top, sent_bottom,
    from_low, from_high, ratio_ref, inverse_ref, edge_ref, first_ref, out_ref, mid_ref,
):
    half = rows // 2

    def at(ref, index):
        return ref[index * groups : (index + 1) * groups, :]

    low, high = sigmas(
        couple_low, couple_high, own_top, own_bottom, got_top, got_bottom, sent_top, sent_bottom,
        from_low, from_high, at(ratio_ref, 0), at(ratio_ref, rows - 1), edge_ref, at(edge_ref, 5), at(edge_ref, 6),
    )
    for i in range(half):
        j = rows - 1 - i
        if i:
            low = at(ratio_ref, i) * low
            high = at(ratio_ref, j) * high
        mid_ref[i * groups : (i + 1) * groups, :] = low
        mid_ref[j * groups : (j + 1) * groups, :] = high

    def put(index, value):
        rows_at = slice(index * groups, (index + 1) * groups)
        out_ref[rows_at, :] = first_ref[rows_at, :] + value

    meet(rows, groups, low, high, ratio_ref, inverse_ref, edge_ref, at, lambda i: at(mid_ref, i), put)


def call(body, outs, ins, spaces, scratch, flops, name, out_spaces=None, aliases=None):
    nbytes = sum(x.size * x.dtype.itemsize for x in ins) + sum(4 * math.prod(s) for s in outs)
    out = pl.pallas_call(
        body,
        out_shape=[jax.ShapeDtypeStruct(s, jnp.float32) for s in outs],
        in_specs=[pl.BlockSpec(memory_space=s) for s in spaces],
        out_specs=[pl.BlockSpec(memory_space=s) for s in out_spaces or [VMEM] * len(outs)],
        input_output_aliases=aliases or {},
        scratch_shapes=scratch,
        compiler_params=pltpu.CompilerParams(vmem_limit_bytes=48 << 20),
        cost_estimate=pl.CostEstimate(flops=flops, bytes_accessed=nbytes, transcendentals=0),
        name=name,
    )(*ins)
    return out


def pad_rows(rows):
    return -(-rows // (2 * BLOCK)) * 2 * BLOCK


def swap(value_even, value_odd):
    count = lax.axis_size("lat")
    even = [(i, i ^ 1) for i in range(count) if (i ^ 1) < count]
    odd = [(i, ((i + 1) ^ 1) - 1) for i in range(1, count) if ((i + 1) ^ 1) - 1 < count]
    value_odd = lax.ppermute(value_odd, "lat", odd)
    return lax.ppermute(value_even, "lat", even), value_odd


def send_level(piece, mask, size):
    return lax.ppermute(piece, "lon", [(d, d ^ mask) for d in range(size)])


def swap_levels(pieces):
    return [pieces[0]] + [send_level(pieces[mask], mask, len(pieces)) for mask in range(1, len(pieces))]


def operator_parts(rows, lon_coef, lat_coef, level_scale):
    row_first = lax.axis_index("lat") * rows
    extent = rows + 2 * OV
    lon_window = lax.dynamic_slice_in_dim(jnp.pad(lon_coef, (OV, OV)), row_first, extent)
    couple = lax.dynamic_slice_in_dim(jnp.pad(lat_coef, (OV + 1, OV + 2)), row_first, extent + 1)
    return level_scale[:, None] * lon_window[None], level_scale[:, None] * couple[None]


def factor(rows, groups, lon_window, couple, eigen):
    block = (rows * groups, N2)
    return call(
        functools.partial(factor_kernel, rows),
        [block, block, (21 * groups, N2)],
        [lon_window, couple, eigen],
        [SMEM, SMEM, VMEM],
        [],
        rows * groups * N2 * 20,
        "factor",
    )


def vmem(*shape):
    return pltpu.VMEM(shape, jnp.float32)


def rows_of(ref, groups, first=0):
    return lambda i: ref[(i - first) * groups : (i - first + 1) * groups, :]


def on_device(right_side, lon_coef, lat_coef, level_scale):
    const = {k: jnp.asarray(v) for k, v in tables(right_side.shape[1]).items()}
    if lax.axis_size("lon") != right_side.shape[1]:
        return shared_levels(const, right_side, lon_coef, lat_coef, level_scale)
    return whole_levels(const, right_side, lon_coef, lat_coef, level_scale)


def early_rows(rows):
    return rows // 2 + 2


def edge_kernel(rows, level_ref, lon_ref, couple_ref, eigen_ref, out_ref):
    eigen = eigen_ref[...]
    groups = eigen.shape[0]
    level = level_ref[0]
    low = high = low_inverse = high_inverse = None
    for i in range(OV):
        e, f = rows + i, 2 * OV - 1 - i
        if i == 0:
            low = 1.0 + lon_ref[level, e] * eigen + couple_ref[level, e]
            high = 1.0 + lon_ref[level, f] * eigen + couple_ref[level, f + 1]
        else:
            low_ratio = couple_ref[level, e] * low_inverse
            high_ratio = couple_ref[level, f + 1] * high_inverse
            out_ref[(i - 1) * groups : i * groups, :] = low_ratio
            out_ref[(OV + i - 1) * groups : (OV + i) * groups, :] = high_ratio
            low = 1.0 + lon_ref[level, e] * eigen + low_ratio * low
            high = 1.0 + lon_ref[level, f] * eigen + high_ratio * high
        low_inverse = 1.0 / (couple_ref[level, e + 1] + low)
        high_inverse = 1.0 / (couple_ref[level, f] + high)
    out_ref[(OV - 1) * groups : OV * groups, :] = low_inverse
    out_ref[(2 * OV - 1) * groups :, :] = high_inverse


def level_response(rows, early, level, lon_ref, couple_ref, eigen, put_ratio, put_inverse, keep, tables):
    half = rows // 2
    ratio_at, value_at, put_value, put_phi, put_psi = tables

    def plain(e):
        return 1.0 + lon_ref[level, e] * eigen

    low = high = None
    low_inverse = high_inverse = low_value = high_value = None
    for i in range(-OV, half):
        j = rows - 1 - i
        e, f = i + OV, j + OV
        if low is None:
            low = plain(e) + couple_ref[level, e]
            high = plain(f) + couple_ref[level, f + 1]
        else:
            low_ratio = couple_ref[level, e] * low_inverse
            high_ratio = couple_ref[level, f + 1] * high_inverse
            low = plain(e) + low_ratio * low
            high = plain(f) + high_ratio * high
        low_divisor = couple_ref[level, e + 1] + low
        high_divisor = couple_ref[level, f] + high
        low_inverse = 1.0 / low_divisor
        high_inverse = 1.0 / high_divisor
        yield
        if i == -1:
            keep(0, low_inverse)
            keep(1, high_inverse)
        if i == 0:
            low_value = high_value = jnp.ones_like(eigen)
        elif i > 0:
            low_value = low_ratio * low_value
            high_value = high_ratio * high_value
        if i >= 0:
            put_ratio(i, low_ratio)
            put_ratio(j, high_ratio)
            put_inverse(i, low_inverse)
            put_inverse(j, high_inverse)
            put_value(i, low_value * low_inverse)
            if j < early:
                put_value(j, high_value * high_inverse)
    between = couple_ref[level, OV + half]
    inverse = 1.0 / (between * (low + high) + low * high)
    across = between * inverse
    high_inverse = high_divisor * inverse
    low_inverse = low_divisor * inverse
    keep(2, high_inverse)
    keep(3, low_inverse)
    keep(4, across)
    phi = high_inverse * low_value
    psi = across * high_value
    phi_down = across * low_value
    psi_down = low_inverse * high_value
    put_phi(half - 1, phi)
    put_psi(half - 1, psi)
    for i in range(half - 2, -1, -1):
        yield
        ratio = ratio_at(i + 1)
        phi = value_at(i) + ratio * phi
        psi = ratio * psi
        put_phi(i, phi)
        put_psi(i, psi)
    put_phi(half, phi_down)
    put_psi(half, psi_down)
    for j in range(half + 1, early):
        ratio = ratio_at(j - 1)
        phi_down = ratio * phi_down
        psi_down = value_at(j) + ratio * psi_down
        put_phi(j, phi_down)
        put_psi(j, psi_down)


def getter(ref, groups):
    return lambda index: ref[index * groups : (index + 1) * groups, :]


def putter(ref, groups, first=0):
    def put(index, value):
        at = first + index * groups
        ref[pl.ds(at if isinstance(at, int) else pl.multiple_of(at, groups), groups), :] = value

    return put


def together(*steps):
    steps = list(steps)
    while steps:
        steps = [step for step in steps if next(step, steps) is not steps]


def partner_response(rows, early, place_ref, lon_ref, couple_ref, eigen, masks, phi_ref, psi_ref, kept_refs, value_refs):
    groups = eigen.shape[0]

    def nothing(index, value):
        pass

    def one(n, mask):
        put_kept = putter(kept_refs[n], groups)

        def put_ratio(index, value):
            if index < early:
                put_kept(index, value)

        first = n * early * groups
        return level_response(
            rows, early, place_ref[0] ^ mask, lon_ref, couple_ref, eigen, put_ratio, nothing, nothing,
            (
                getter(kept_refs[n], groups), getter(value_refs[n], groups), putter(value_refs[n], groups),
                putter(phi_ref, groups, first), putter(psi_ref, groups, first),
            ),
        )

    return [one(n, mask) for n, mask in enumerate(masks)]


def own_kernel(
    rows, early, masks, place_ref, lon_ref, couple_ref, eigen_ref, ratio_ref, inverse_ref, edge_ref, phi_ref, psi_ref,
    phi_near_ref, psi_near_ref, value_ref, *refs,
):
    eigen = eigen_ref[...]
    groups = eigen.shape[0]
    own = level_response(
        rows, early, place_ref[0], lon_ref, couple_ref, eigen, putter(ratio_ref, groups),
        putter(inverse_ref, groups), putter(edge_ref, groups),
        (
            getter(ratio_ref, groups), getter(value_ref, groups), putter(value_ref, groups),
            putter(phi_ref, groups), putter(psi_ref, groups),
        ),
    )
    count = len(masks)
    together(
        own,
        *partner_response(
            rows, early, place_ref, lon_ref, couple_ref, eigen, masks, phi_near_ref, psi_near_ref,
            refs[:count], refs[count:],
        ),
    )


def partners_kernel(
    rows, early, masks, place_ref, lon_ref, couple_ref, eigen_ref, after_ref, phi_ref, psi_ref, token_ref, *refs
):
    token_ref[...] = after_ref[...]
    count = len(masks)
    together(
        *partner_response(
            rows, early, place_ref, lon_ref, couple_ref, eigen_ref[...], masks, phi_ref, psi_ref,
            refs[:count], refs[count:],
        )
    )


def whole_levels(const, right_side, lon_coef, lat_coef, level_scale):
    rows, levels, lon_count = right_side.shape
    digits = N1 // levels
    groups = 2 * GROUPS
    lon_at = lax.axis_index("lon").astype(jnp.int32)
    parity = (lax.axis_index("lat") % 2).astype(jnp.int32)
    place = jnp.stack([lon_at, parity])
    half = rows // 2
    early = early_rows(rows)
    late = rows - early
    eigen = const["eigen"].reshape(groups, N2)
    lon_all, couple_all = operator_parts(rows, lon_coef, lat_coef, level_scale)
    (around,) = call(
        functools.partial(edge_kernel, rows),
        [(2 * OV * groups, N2)],
        [place, lon_all, couple_all, eigen],
        [SMEM, SMEM, SMEM, VMEM],
        [],
        16 * groups * N2 * 20,
        "edge",
    )
    block = (rows * groups, N2)
    early_block = (early * groups, N2)
    early_block = (early * groups, N2)
    near_masks, far_masks = [1], list(range(2, levels))
    ratio, inverse, edge, phi, psi, phi_near, psi_near = call(
        functools.partial(own_kernel, rows, early, near_masks),
        [block, block, (5 * groups, N2)] + [early_block] * 4,
        [place, lon_all, couple_all, eigen],
        [SMEM, SMEM, SMEM, VMEM],
        [vmem(*early_block)] * 3,
        2 * rows * groups * N2 * 20,
        "own",
    )
    row = (groups, N2)
    ends = 2 * OV
    inner = rows - ends
    span = OV * digits
    by_row = right_side.reshape(rows, levels, digits, N2).transpose(0, 2, 1, 3).reshape(-1, N2)

    far = list(range(2, levels))

    def pack_ends(place_ref, in_ref, *refs):
        for end_ref, mask in zip(refs, [0] + far):
            level = place_ref[0] ^ mask
            end_ref[:span, :] = in_ref[pl.ds(level, span, stride=levels), :]
            end_ref[span:, :] = in_ref[pl.ds(level + levels * (rows - OV) * digits, span, stride=levels), :]

    end_packed = call(
        pack_ends,
        [(ends * digits, N2)] * (levels - 1),
        [place, by_row],
        [SMEM, VMEM],
        [],
        0,
        "pack_ends",
    )

    def pack(place_ref, in_ref, after_ref, *refs):
        del after_ref
        for mask, out_ref in enumerate(refs):
            level = place_ref[0] ^ mask
            skip = 0 if mask == 1 else levels * span
            out_ref[...] = in_ref[pl.ds(level + skip, out_ref.shape[0], stride=levels), :]

    packed = call(
        pack,
        [((rows if mask == 1 else inner) * digits, N2) for mask in range(levels)],
        [place, by_row, end_packed[0]],
        [SMEM, VMEM, pl.ANY],
        [],
        0,
        "pack",
    )
    end_pieces = [end_packed[0], None] + [send_level(p, m, levels) for p, m in zip(end_packed[1:], far)]
    near = send_level(packed[1], 1, levels)
    end_pieces[1] = near
    inner_pieces = [packed[0], near] + [send_level(packed[m], m, levels) for m in far]
    forward = [const["first"], const["turn"], const["second"], const["special"]]
    pad_ends, pad_inner = pad_rows(ends), pad_rows(inner)

    def ends_body(place_ref, *refs):
        pieces, refs = refs[:levels], refs[levels:]
        tables_in, edge_ref = refs[:4], refs[4]
        spec_ref, top_ref, bottom_ref, even_ref, odd_ref, full_ref, mid_ref = refs[5:]
        for mask, piece in enumerate(pieces):
            at = pl.multiple_of((place_ref[0] ^ mask) * digits, digits)
            last = piece.shape[0] - span
            full_ref[:OV, pl.ds(at, digits), :] = piece[:span, :].reshape(OV, digits, N2)
            full_ref[OV:ends, pl.ds(at, digits), :] = piece[last:, :].reshape(OV, digits, N2)
        forward_rows(full_ref, ends, *tables_in, mid_ref, spec_ref)
        top, bottom = edge_sums(
            rows_of(spec_ref, groups), rows_of(spec_ref, groups, -OV),
            rows_of(edge_ref, groups), lambda i: edge_ref[(2 * OV - 2 - i) * groups : (2 * OV - 1 - i) * groups, :],
        )
        top_ref[...] = top
        bottom_ref[...] = bottom
        swap_out(place_ref[1], top, bottom, even_ref, odd_ref)

    end_spectral, sent_top, sent_bottom, even, odd = call(
        ends_body,
        [(ends * groups, N2)] + [row] * 4,
        [place, *end_pieces, *forward, around],
        [SMEM] + [VMEM] * (levels + 5),
        [vmem(pad_ends, N1, N2), vmem(pad_ends * N1, N2)],
        ends * NLON * 256 * 4,
        "ends",
    )
    even, odd = swap(even, odd)
    backward = [const["first_back"], const["turn"], const["second_back"], const["special_back"]]
    pad_early, pad_late = pad_rows(early), pad_rows(late)

    def spread(place_ref, full_ref, count, out_refs):
        for mask, out_ref in enumerate(out_refs):
            at = pl.multiple_of((place_ref[0] ^ mask) * digits, digits)
            out_ref[...] = full_ref[:count, pl.ds(at, digits), :].reshape(count * digits, N2)

    def inner_body(place_ref, *refs):
        pieces, refs = refs[:levels], refs[levels:]
        tables_in, back_in, refs = refs[:4], refs[4:7], refs[7:]
        ends_ref, even_ref, odd_ref, ratio_ref, inverse_ref, edge_ref = refs[:6]
        late_ref, top_ref, even_out, odd_out = refs[6:10]
        early_refs, refs = refs[10 : 10 + levels], refs[10 + levels :]
        full_ref, mid_ref, spec_ref, sum_ref, back_full_ref, back_mid_ref = refs
        for mask, piece in enumerate(pieces):
            at = pl.multiple_of((place_ref[0] ^ mask) * digits, digits)
            skip = span if mask == 1 else 0
            full_ref[:inner, pl.ds(at, digits), :] = piece[skip : skip + inner * digits, :].reshape(
                inner, digits, N2
            )
        if pad_inner > inner:
            full_ref[inner:] = jnp.zeros((pad_inner - inner, N1, N2), jnp.float32)
        forward_rows(full_ref, inner, *tables_in, mid_ref, spec_ref)
        low, high = swap_in(place_ref[1], even_ref[...], odd_ref[...])

        def spec_row(i):
            if i < OV:
                return rows_of(ends_ref, groups)(i)
            if i >= rows - OV:
                return rows_of(ends_ref, groups, rows - ends)(i)
            return rows_of(spec_ref, groups, OV)(i)

        solve_first(rows, groups, spec_row, low, high, ratio_ref, inverse_ref, edge_ref, sum_ref)
        top = sum_ref[:groups, :]
        top_ref[...] = top
        late_ref[...] = sum_ref[early * groups :, :]
        swap_out(place_ref[1], sum_ref[(rows - 1) * groups :, :], top, even_out, odd_out)
        early_sum = sum_ref.at[pl.ds(0, early * groups), :]
        backward_rows(early_sum, early, back_in[0], tables_in[1], back_in[1], back_in[2], back_mid_ref, back_full_ref)
        spread(place_ref, back_full_ref, early, early_refs)

    late_first, own_top, even2, odd2, *early_pieces = call(
        inner_body,
        [(late * groups, N2), row, row, row] + [(early * digits, N2)] * levels,
        [
            place, *inner_pieces, *forward, backward[0], backward[2], backward[3],
            end_spectral, even, odd, ratio, inverse, edge,
        ],
        [SMEM] + [VMEM] * (levels + 13),
        [
            vmem(pad_inner, N1, N2), vmem(pad_inner * N1, N2), vmem(inner * N1, N2), vmem(rows * groups, N2),
            vmem(pad_early, N1, N2), vmem(pad_early * N1, N2),
        ],
        (inner + early) * NLON * 256 * 4,
        "inner",
    )
    early_pieces = swap_levels(early_pieces)
    even2, odd2 = swap(even2, odd2)

    phi_far, psi_far, token = call(
        functools.partial(partners_kernel, rows, early, far_masks),
        [(len(far_masks) * early * groups, N2)] * 2 + [row],
        [place, lon_all, couple_all, eigen, own_top],
        [SMEM, SMEM, SMEM, VMEM, VMEM],
        [vmem(*early_block)] * (2 * len(far_masks)),
        len(far_masks) * rows * groups * N2 * 20,
        "partners",
    )

    def sigma_body(place_ref, couple_ref, *refs):
        first_ref, own_top_ref, even_ref, odd_ref, even2_ref, odd2_ref, top_ref, bottom_ref = refs[:8]
        ratio_ref, edge_ref, around_ref = refs[8:11]
        sigma_ref = refs[-1]
        level = place_ref[0]
        got_top, got_bottom = swap_in(place_ref[1], even_ref[...], odd_ref[...])
        from_low, from_high = swap_in(place_ref[1], even2_ref[...], odd2_ref[...])
        low, high = sigmas(
            couple_ref[level, OV], couple_ref[level, OV + rows], own_top_ref[...], first_ref[(late - 1) * groups :, :],
            got_top, got_bottom, top_ref[...], bottom_ref[...], from_low, from_high,
            ratio_ref[:groups, :], ratio_ref[(rows - 1) * groups :, :], edge_ref,
            around_ref[(OV - 1) * groups : OV * groups, :], around_ref[(2 * OV - 1) * groups :, :],
        )
        sigma_ref[:groups, :] = low
        sigma_ref[groups:, :] = high

    (sigma,) = call(
        sigma_body,
        [(2 * groups, N2)],
        [
            place, couple_all, late_first, own_top, even, odd, even2, odd2, sent_top, sent_bottom, ratio, edge, around,
            *early_pieces[1:], token,
        ],
        [SMEM, SMEM] + [VMEM] * 11 + [pl.ANY] * levels,
        [],
        groups * N2 * 40,
        "sigma",
    )
    sigma_pieces = swap_levels([sigma] * levels)
    def second_body(place_ref, *refs):
        sigma_ref, first_ref, ratio_ref, inverse_ref, edge_ref = refs[:5]
        tables_in, refs = refs[5:9], refs[9:]
        late_refs = refs[:levels]
        sum_ref, mid_ref, full_ref = refs[levels:]
        low, high = sigma_ref[:groups, :], sigma_ref[groups:, :]

        def at(ref, index):
            return ref[index * groups : (index + 1) * groups, :]

        for i in range(half):
            j = rows - 1 - i
            if i:
                low = at(ratio_ref, i) * low
                high = at(ratio_ref, j) * high
            mid_ref[(j - half) * groups : (j - half + 1) * groups, :] = high
        x_high = at(edge_ref, 3) * high + at(edge_ref, 4) * low
        for j in range(half, rows):
            if j > half:
                x_high = at(mid_ref, j - half) * at(inverse_ref, j) + at(ratio_ref, j - 1) * x_high
            if j >= early:
                here = slice((j - early) * groups, (j - early + 1) * groups)
                sum_ref[here, :] = first_ref[here, :] + x_high
        backward_rows(sum_ref, late, *tables_in, mid_ref, full_ref)
        spread(place_ref, full_ref, late, late_refs)

    late_pieces = call(
        second_body,
        [(late * digits, N2)] * levels,
        [place, sigma, late_first, ratio, inverse, edge, *backward],
        [SMEM] + [VMEM] * 9,
        [vmem(late * groups, N2), vmem(max(pad_late, half) * N1, N2), vmem(pad_late, N1, N2)],
        late * NLON * 256 * 4,
        "second",
    )
    late_pieces = swap_levels(late_pieces)
    total = rows * levels * digits
    early_total = early * levels * digits
    part = const["first_back_part"]

    def correct(place_ref, *refs):
        pieces, sigma_refs, refs = refs[:levels], refs[levels : 2 * levels], refs[2 * levels :]
        responses, refs = refs[:6], refs[6:]
        part_ref, turn_ref, second_ref, special_ref = refs[:4]
        out_ref, sum_ref, mid_ref, done_ref, sem = refs[4:]
        part_rows = part_ref.shape[0] // levels
        mine = part_ref.at[pl.ds(pl.multiple_of(place_ref[0] * part_rows, part_rows), part_rows), :]
        size = early * groups
        for mask in range(levels):
            level = place_ref[0] ^ mask
            low, high = sigma_refs[mask][:groups, :], sigma_refs[mask][groups:, :]
            phi_ref, psi_ref = responses[2 * min(mask, 2) : 2 * min(mask, 2) + 2]
            first = max(mask - 2, 0) * size
            phi_all = phi_ref[first : first + size, :].reshape(early, groups, N2)
            psi_all = psi_ref[first : first + size, :].reshape(early, groups, N2)
            sum_ref[...] = (phi_all * low[None] + psi_all * high[None]).reshape(size, N2)
            spectral_back(sum_ref, early, pad_early, second_ref, special_ref, mid_ref)
            for pair in range(pad_early // (2 * BLOCK)):
                value = digits_back(mid_ref, pair, turn_ref, mine)
                for side in range(2):
                    begin = (2 * pair + side) * BLOCK
                    count = min(BLOCK, early - begin)
                    if count <= 0:
                        continue
                    lines = count * digits
                    whole = pieces[mask][begin * digits : begin * digits + lines, :]
                    done_ref[pl.ds(level + begin * digits * levels, lines, stride=levels), :] = (
                        whole + value[:lines, side * N2 : (side + 1) * N2]
                    )
        copy = pltpu.make_async_copy(done_ref, out_ref.at[pl.ds(0, early_total), :], sem)
        copy.start()
        copy.wait()

    (out,) = call(
        correct,
        [(total, N2)],
        [
            place, *early_pieces, *sigma_pieces, phi, psi, phi_near, psi_near, phi_far, psi_far,
            part, const["turn"], *backward[2:],
        ],
        [SMEM] + [VMEM] * (2 * levels + 10),
        [
            vmem(early * groups, N2), vmem(pad_early * N1, N2), vmem(early_total, N2), pltpu.SemaphoreType.DMA,
        ],
        levels * early * NLON * 256 * 40,
        "correct",
        out_spaces=[pl.ANY],
    )

    chunks = 4

    def unpack(place_ref, *refs):
        pieces = refs[:levels]
        out_ref, done_ref, sems = refs[levels + 1 :]
        lines = late * digits // chunks
        copies = []
        for chunk in range(chunks):
            for mask in range(levels):
                first = (place_ref[0] ^ mask) + chunk * lines * levels
                done_ref[pl.ds(first, lines, stride=levels), :] = pieces[mask][chunk * lines : (chunk + 1) * lines, :]
            here = pl.ds(chunk * lines * levels, lines * levels)
            there = pl.ds(early_total + chunk * lines * levels, lines * levels)
            copy = pltpu.make_async_copy(done_ref.at[here, :], out_ref.at[there, :], sems.at[chunk])
            copy.start()
            copies.append(copy)
        for copy in copies:
            copy.wait()

    (out,) = call(
        unpack,
        [(total, N2)],
        [place, *late_pieces, out],
        [SMEM] + [VMEM] * levels + [pl.ANY],
        [vmem(total - early_total, N2), pltpu.SemaphoreType.DMA((chunks,))],
        0,
        "unpack",
        out_spaces=[pl.ANY],
        aliases={levels + 1: 0},
    )
    return out.reshape(rows, digits, levels, N2).transpose(0, 2, 1, 3).reshape(right_side.shape)


def second_part(
    rows, groups, parity, couple_ref, first_ref, even_ref, odd_ref, even2_ref, odd2_ref, top_ref, bottom_ref,
    ratio_ref, inverse_ref, edge_ref, out_ref, mid_ref,
):
    got_top, got_bottom = swap_in(parity, even_ref[...], odd_ref[...])
    low, high = swap_in(parity, even2_ref[...], odd2_ref[...])
    solve_second(
        rows, groups, couple_ref[OV], couple_ref[OV + rows],
        first_ref[:groups, :], first_ref[(rows - 1) * groups :, :],
        got_top, got_bottom, top_ref[...], bottom_ref[...], low, high,
        ratio_ref, inverse_ref, edge_ref, first_ref, out_ref, mid_ref,
    )


def shared_levels(const, right_side, lon_coef, lat_coef, level_scale):
    rows, levels, lon_count = right_side.shape
    lon_size = lax.axis_size("lon")
    assert lon_size % levels == 0 and GROUPS % (lon_size // levels) == 0 and rows % (lon_size // levels) == 0
    sharers = lon_size // levels
    groups = 2 * GROUPS // sharers
    part_rows = rows // sharers
    digits = N1 // lon_size
    lon_at = lax.axis_index("lon")
    parity = (lax.axis_index("lat") % 2).astype(jnp.int32).reshape(1)
    lon_window, couple = operator_parts(rows, lon_coef, lat_coef, level_scale)
    lon_window = lax.dynamic_index_in_dim(lon_window, lon_at // sharers, 0, False)
    couple = lax.dynamic_index_in_dim(couple, lon_at // sharers, 0, False)
    eigen = lax.dynamic_slice_in_dim(
        const["eigen"], (lon_at % sharers) * (groups // 2), groups // 2, axis=1
    ).reshape(groups, N2)
    ratio, inverse, edge = factor(rows, groups, lon_window, couple, eigen)
    block = (rows * groups, N2)
    row = (groups, N2)
    send = right_side.reshape(sharers, part_rows, levels, lon_count).transpose(2, 0, 1, 3)
    send = send.reshape(lon_size, part_rows, digits, N2)
    got = lax.all_to_all(send, "lon", 0, 0, tiled=True)
    points = got.transpose(1, 0, 2, 3).reshape(part_rows, N1, N2)
    padded = pad_rows(part_rows)

    def transform(points_ref, first_ref, turn_ref, second_ref, special_ref, out_ref, full_ref, mid_ref):
        full_ref[:part_rows] = points_ref[...]
        if padded > part_rows:
            full_ref[part_rows:] = jnp.zeros((padded - part_rows, N1, N2), jnp.float32)
        forward_rows(full_ref, part_rows, first_ref, turn_ref, second_ref, special_ref, mid_ref, out_ref)

    (spectral,) = call(
        transform,
        [(part_rows * N1, N2)],
        [points, const["first"], const["turn"], const["second"], const["special"]],
        [VMEM] * 5,
        [vmem(padded, N1, N2), vmem(padded * N1, N2)],
        part_rows * NLON * 256 * 4,
        "transform",
    )
    spectral = to_coefs(spectral, sharers, part_rows, groups)

    def edges(parity_ref, spec_ref, edge_ref, top_ref, bottom_ref, even_ref, odd_ref):
        top, bottom = edge_sums(
            rows_of(spec_ref, groups), rows_of(spec_ref, groups, OV - rows),
            rows_of(edge_ref, groups, -7), rows_of(edge_ref, groups, -14),
        )
        top_ref[...] = top
        bottom_ref[...] = bottom
        swap_out(parity_ref[0], top, bottom, even_ref, odd_ref)

    sent_top, sent_bottom, even, odd = call(
        edges, [row] * 4, [parity, spectral, edge], [SMEM, VMEM, VMEM], [], groups * N2 * 32, "edges"
    )
    even, odd = swap(even, odd)

    def first(parity_ref, spec_ref, even_ref, odd_ref, ratio_ref, inverse_ref, edge_ref, out_ref, e_ref, o_ref):
        low, high = swap_in(parity_ref[0], even_ref[...], odd_ref[...])
        solve_first(
            rows, groups, rows_of(spec_ref, groups), low, high, ratio_ref, inverse_ref, edge_ref, out_ref
        )
        swap_out(parity_ref[0], out_ref[(rows - 1) * groups :, :], out_ref[:groups, :], e_ref, o_ref)

    iterate, even2, odd2 = call(
        first,
        [block, row, row],
        [parity, spectral, even, odd, ratio, inverse, edge],
        [SMEM] + [VMEM] * 6,
        [],
        rows * groups * N2 * 8,
        "first_solve",
    )
    even2, odd2 = swap(even2, odd2)

    def second(parity_ref, *refs):
        second_part(rows, groups, parity_ref[0], *refs)

    (iterate,) = call(
        second,
        [block],
        [parity, couple, iterate, even, odd, even2, odd2, sent_top, sent_bottom, ratio, inverse, edge],
        [SMEM, SMEM] + [VMEM] * 10,
        [vmem(*block)],
        rows * groups * N2 * 8,
        "second_solve",
    )
    iterate = to_rows(iterate, sharers, part_rows, groups)

    def back(spec_ref, first_ref, turn_ref, second_ref, special_ref, out_ref, mid_ref, full_ref):
        backward_rows(spec_ref, part_rows, first_ref, turn_ref, second_ref, special_ref, mid_ref, full_ref)
        out_ref[...] = full_ref[:part_rows]

    (points,) = call(
        back,
        [(part_rows, N1, N2)],
        [iterate, const["first_back"], const["turn"], const["second_back"], const["special_back"]],
        [VMEM] * 5,
        [vmem(padded * N1, N2), vmem(padded, N1, N2)],
        part_rows * NLON * 256 * 4,
        "back_transform",
    )
    send = points.reshape(part_rows, lon_size, digits, N2).transpose(1, 0, 2, 3)
    got = lax.all_to_all(send, "lon", 0, 0, tiled=True)
    got = got.reshape(levels, sharers, part_rows, lon_count).transpose(1, 2, 0, 3)
    return got.reshape(rows, levels, lon_count)


def level_groups(sharers):
    size = lax.axis_size("lon")
    return [[first + i for i in range(sharers)] for first in range(0, size, sharers)]


def to_coefs(spectral, sharers, part_rows, groups):
    send = spectral.reshape(part_rows, 2, sharers, groups // 2, N2).transpose(2, 0, 1, 3, 4)
    got = lax.all_to_all(
        send, "lon", 0, 0, tiled=True, axis_index_groups=level_groups(sharers)
    )
    return got.reshape(sharers * part_rows * groups, N2)


def to_rows(values, sharers, part_rows, groups):
    send = values.reshape(sharers, part_rows, 2, groups // 2, N2)
    got = lax.all_to_all(
        send, "lon", 0, 0, tiled=True, axis_index_groups=level_groups(sharers)
    )
    return got.transpose(1, 2, 0, 3, 4).reshape(part_rows * N1, N2)


def solution(mesh):
    return jax.shard_map(
        on_device,
        mesh=mesh,
        in_specs=(P("lat", None, "lon"), P(), P(), P()),
        out_specs=P("lat", None, "lon"),
        check_vma=False,
    )
```

```python
import functools
import math

import jax
import jax.numpy as jnp
import numpy as np
from jax import lax
from jax.experimental import pallas as pl
from jax.experimental.pallas import tpu as pltpu
from jax.sharding import PartitionSpec as P

NLON = 4096
OV = 8
N1 = 32
N2 = 128
GROUPS = 16
BLOCK = 8
WEIGHT = 256

VMEM = pltpu.VMEM
SMEM = pltpu.SMEM


def numpy_split(table):
    import ml_dtypes

    table = np.asarray(table, np.float32)
    high = table.astype(ml_dtypes.bfloat16)
    low = (table - high.astype(np.float32)).astype(ml_dtypes.bfloat16)
    return high, low


def tables(levels):
    j1 = np.arange(N1)
    j2 = np.arange(N2)
    k2 = np.arange(N2)
    digit = np.arange(GROUPS)
    small = np.zeros((N1, N1))
    small[:GROUPS] = np.cos(2 * np.pi * np.outer(digit, j1) / N1)
    small[GROUPS] = np.cos(np.pi * j1)
    small[GROUPS + 1 :] = -np.sin(2 * np.pi * np.outer(digit[1:], j1) / N1)
    first = np.kron(np.eye(BLOCK), small)
    angle = 2 * np.pi * np.outer(digit, j2) / NLON
    turn_cos = np.cos(angle)
    turn_sin = np.sin(angle)
    phase = 2 * np.pi * (np.outer(j2, k2) % N2) / N2
    cosine, sine = np.cos(phase), np.sin(phase)
    second = np.block([[cosine, -sine], [sine, cosine]])
    special = np.zeros((2 * N2, 2 * N2))
    half = N2 // 2
    special[:N2, : half + 1] = np.cos(2 * np.pi * np.outer(j2, np.arange(half + 1)) / N2)
    special[:N2, half + 1 : N2] = -np.sin(2 * np.pi * np.outer(j2, np.arange(1, half)) / N2)
    odd = 2 * np.pi * np.outer(j2, 1 + 2 * np.arange(half)) / (2 * N2)
    special[N2:, N2 : N2 + half] = np.cos(odd)
    special[N2:, N2 + half :] = -np.sin(odd)
    weight = np.full(2 * N2, 2.0 / NLON)
    weight[0] = 1.0 / NLON
    weight[half] = 1.0 / NLON
    second_back = second.T * (2.0 / NLON)
    special_back = weight[:, None] * special.T
    wave = np.zeros((GROUPS, 2 * N2))
    wave[:, :N2] = digit[:, None] + N1 * k2[None, :]
    wave[:, N2:] = wave[:, :N2]
    lane = np.arange(N2)
    wave[0, :N2] = np.where(lane <= half, N1 * lane, N1 * (lane - half))
    wave[0, N2:] = 16 + N1 * (lane % half)
    eigen = 2.0 - 2.0 * np.cos(2 * np.pi * wave / NLON)
    pair = lambda t: np.concatenate(numpy_split(t), axis=0)
    width = N1 // levels
    part = [pair(np.kron(np.eye(BLOCK), small.T[at : at + width])) for at in range(0, N1, width)]
    return dict(
        first_back_part=np.concatenate(part, axis=0),
        first=pair(first),
        first_back=pair(first.T),
        second=pair(second),
        second_back=pair(second_back),
        special=pair(special),
        special_back=pair(special_back),
        turn=np.concatenate([turn_cos, turn_sin], axis=0).astype(np.float32),
        eigen=np.stack([eigen[:, :N2], eigen[:, N2:]]).astype(np.float32),
    )


def halves(value):
    high = value.astype(jnp.bfloat16)
    low = (value - high.astype(jnp.float32)).astype(jnp.bfloat16)
    return high, low


def dot(a, b):
    return lax.dot_general(a, b, (((1,), (0,)), ((), ())), preferred_element_type=jnp.float32)


def product_right(value, table_ref):
    size = table_ref.shape[0] // 2
    high, low = halves(value)
    table_high = table_ref[:size, :]
    return dot(high, table_high) + dot(low, table_high) + dot(high, table_ref[size:, :])


def product_left(table_ref, value):
    size = table_ref.shape[0] // 2
    high, low = halves(value)
    both = dot(table_ref[...], high)
    return both[:size] + both[size:] + dot(table_ref[:size, :], low)


def lanes_apart(value, rows):
    real = value[:, :N2].reshape(rows, GROUPS, N2)
    imag = value[:, N2:].reshape(rows, GROUPS, N2)
    return jnp.concatenate([real, imag], axis=1).reshape(rows * 2 * GROUPS, N2)


def lanes_together(value, rows):
    both = value.reshape(rows, 2 * GROUPS, N2)
    return jnp.concatenate([both[:, :GROUPS], both[:, GROUPS:]], axis=2).reshape(rows * GROUPS, 2 * N2)


def load_zeroth(ref, rows):
    return jnp.concatenate(
        [ref[pl.ds(0, rows, stride=2 * GROUPS), :], ref[pl.ds(GROUPS, rows, stride=2 * GROUPS), :]], axis=1
    )


def store_zeroth(ref, rows, value):
    ref[pl.ds(0, rows, stride=2 * GROUPS), :] = value[:, :N2]
    ref[pl.ds(GROUPS, rows, stride=2 * GROUPS), :] = value[:, N2:]


def forward_rows(points_ref, rows, first_ref, turn_ref, second_ref, special_ref, mid_ref, out_ref):
    padded = points_ref.shape[0]
    turn_cos = turn_ref[:GROUPS, :][None]
    turn_sin = turn_ref[GROUPS:, :][None]
    for pair in range(padded // (2 * BLOCK)):
        base = pair * 2 * BLOCK
        left = points_ref[base : base + BLOCK].reshape(BLOCK * N1, N2)
        right = points_ref[base + BLOCK : base + 2 * BLOCK].reshape(BLOCK * N1, N2)
        value = product_left(first_ref, jnp.concatenate([left, right], axis=1))
        for side in range(2):
            digits = value[:, side * N2 : (side + 1) * N2].reshape(BLOCK, N1, N2)
            real, imag = digits[:, :GROUPS], digits[:, GROUPS:]
            turned = jnp.concatenate(
                [real * turn_cos + imag * turn_sin, imag * turn_cos - real * turn_sin], axis=1
            )
            at = (base + side * BLOCK) * N1
            mid_ref[at : at + BLOCK * N1, :] = turned.reshape(BLOCK * N1, N2)
    result = product_right(lanes_together(mid_ref[...], padded), second_ref)
    out_ref[...] = lanes_apart(result, padded)[: rows * N1]
    store_zeroth(out_ref, rows, product_right(load_zeroth(mid_ref, padded), special_ref)[:rows])


def spectral_back(spec_ref, rows, padded, second_ref, special_ref, mid_ref):
    result = product_right(lanes_together(spec_ref[...], rows), second_ref)
    mid_ref[: rows * N1, :] = lanes_apart(result, rows)
    if padded > rows:
        mid_ref[rows * N1 : padded * N1, :] = jnp.zeros(((padded - rows) * N1, N2), jnp.float32)
    store_zeroth(mid_ref, rows, product_right(load_zeroth(spec_ref, rows), special_ref))


def digits_back(mid_ref, pair, turn_ref, first_ref):
    turn_cos = turn_ref[:GROUPS, :][None]
    turn_sin = turn_ref[GROUPS:, :][None]
    sides = []
    for side in range(2):
        at = (2 * pair + side) * BLOCK * N1
        both = mid_ref[at : at + BLOCK * N1, :].reshape(BLOCK, N1, N2)
        real, imag = both[:, :GROUPS], both[:, GROUPS:]
        turned = jnp.concatenate(
            [real * turn_cos - imag * turn_sin, imag * turn_cos + real * turn_sin], axis=1
        )
        sides.append(turned.reshape(BLOCK * N1, N2))
    return product_left(first_ref, jnp.concatenate(sides, axis=1))


def backward_rows(spec_ref, rows, first_ref, turn_ref, second_ref, special_ref, mid_ref, out_ref):
    padded = out_ref.shape[0]
    spectral_back(spec_ref, rows, padded, second_ref, special_ref, mid_ref)
    for pair in range(padded // (2 * BLOCK)):
        base = pair * 2 * BLOCK
        value = digits_back(mid_ref, pair, turn_ref, first_ref)
        out_ref[base : base + BLOCK] = value[:, :N2].reshape(BLOCK, N1, N2)
        out_ref[base + BLOCK : base + 2 * BLOCK] = value[:, N2:].reshape(BLOCK, N1, N2)


def factor_kernel(rows, lon_ref, couple_ref, eigen_ref, ratio_ref, inverse_ref, edge_ref):
    eigen = eigen_ref[...]
    groups = eigen.shape[0]
    half = rows // 2
    last = rows + 2 * OV - 1

    def plain(e):
        return 1.0 + lon_ref[e] * eigen

    def put(ref, index, value):
        ref[index * groups : (index + 1) * groups, :] = value

    def chain(start, stop, step, into):
        excess = inverse = None
        for e in range(start, stop + step, step):
            before = couple_ref[e] if step > 0 else couple_ref[e + 1]
            after = couple_ref[e + 1] if step > 0 else couple_ref[e]
            if inverse is None:
                ratio = None
                excess = plain(e) + before
            else:
                ratio = before * inverse
                excess = plain(e) + ratio * excess
            divisor = after + excess
            inverse = 1.0 / divisor
            into(e, ratio, inverse, excess, divisor)

    kept = {}

    def top(e, ratio, inverse, excess, divisor):
        if e == OV - 1:
            put(edge_ref, 0, inverse)
        if e >= OV:
            put(ratio_ref, e - OV, ratio)
            put(inverse_ref, e - OV, inverse)
        if e == OV + half - 1:
            kept["top"] = excess, divisor

    def bottom(e, ratio, inverse, excess, divisor):
        if e == OV + rows:
            put(edge_ref, 1, inverse)
        if e < OV + rows:
            put(ratio_ref, e - OV, ratio)
            put(inverse_ref, e - OV, inverse)
        if e == OV + half:
            kept["bottom"] = excess, divisor

    def next_band(e, ratio, inverse, excess, divisor):
        if ratio is not None:
            put(edge_ref, 7 + e - rows - 1, ratio)
        if e == OV + rows - 1:
            put(edge_ref, 5, inverse)

    def previous_band(e, ratio, inverse, excess, divisor):
        if ratio is not None:
            put(edge_ref, 14 + e - OV, ratio)
        if e == OV:
            put(edge_ref, 6, inverse)

    chain(rows, OV + rows - 1, 1, next_band)
    chain(2 * OV - 1, OV, -1, previous_band)
    chain(0, OV + half - 1, 1, top)
    chain(last, OV + half, -1, bottom)
    excess_top, divisor_top = kept["top"]
    excess_bottom, divisor_bottom = kept["bottom"]
    between = couple_ref[OV + half]
    inverse = 1.0 / (between * (excess_top + excess_bottom) + excess_top * excess_bottom)
    put(edge_ref, 2, divisor_bottom * inverse)
    put(edge_ref, 3, divisor_top * inverse)
    put(edge_ref, 4, between * inverse)


def edge_sums(low_rows, high_rows, next_ratio, previous_ratio):
    top = high_rows(0)
    for i in range(1, OV):
        top = high_rows(i) + next_ratio(i - 1) * top
    bottom = low_rows(OV - 1)
    for i in range(OV - 2, -1, -1):
        bottom = low_rows(i) + previous_ratio(i) * bottom
    return top, bottom


def swap_out(parity, up, down, even_ref, odd_ref):
    is_even = parity == 0
    even_ref[...] = jnp.where(is_even, up, down)
    odd_ref[...] = jnp.where(is_even, down, up)


def swap_in(parity, even, odd):
    is_even = parity == 0
    return jnp.where(is_even, odd, even), jnp.where(is_even, even, odd)


def solve_first(rows, groups, right_side_row, from_low, from_high, ratio_ref, inverse_ref, edge_ref, out_ref):
    half = rows // 2

    def at(ref, index):
        return ref[index * groups : (index + 1) * groups, :]

    def put(index, value):
        out_ref[index * groups : (index + 1) * groups, :] = value

    low, high = from_low, from_high
    for i in range(half):
        j = rows - 1 - i
        low = right_side_row(i) + at(ratio_ref, i) * low
        high = right_side_row(j) + at(ratio_ref, j) * high
        put(i, low)
        put(j, high)
    meet(rows, groups, low, high, ratio_ref, inverse_ref, edge_ref, at, lambda i: at(out_ref, i), put)


def meet(rows, groups, low, high, ratio_ref, inverse_ref, edge_ref, at, value, put):
    half = rows // 2
    between = at(edge_ref, 4)
    x_low = at(edge_ref, 2) * low + between * high
    x_high = at(edge_ref, 3) * high + between * low
    put(half - 1, x_low)
    put(half, x_high)
    for i in range(half - 2, -1, -1):
        j = rows - 1 - i
        x_low = value(i) * at(inverse_ref, i) + at(ratio_ref, i + 1) * x_low
        x_high = value(j) * at(inverse_ref, j) + at(ratio_ref, j - 1) * x_high
        put(i, x_low)
        put(j, x_high)


def sigmas(
    couple_low, couple_high, own_top, own_bottom, got_top, got_bottom, sent_top, sent_bottom, from_low, from_high,
    ratio_first, ratio_last, edge_ref, next_inverse, previous_inverse,
):
    groups = own_top.shape[0]

    def edge(index):
        return edge_ref[index * groups : (index + 1) * groups, :]

    beyond_low = (got_top + couple_low * own_top) * edge(0)
    beyond_high = (got_bottom + couple_high * own_bottom) * edge(1)
    theirs_low = (sent_bottom + couple_low * from_low) * previous_inverse
    theirs_high = (sent_top + couple_high * from_high) * next_inverse
    low = ratio_first * (couple_low * (own_top - theirs_low)) + couple_low * (from_low - beyond_low)
    high = ratio_last * (couple_high * (own_bottom - theirs_high)) + couple_high * (from_high - beyond_high)
    return low, high


def solve_second(
    rows, groups, couple_low, couple_high, own_top, own_bottom, got_top, got_bottom, sent_top, sent_bottom,
    from_low, from_high, ratio_ref, inverse_ref, edge_ref, first_ref, out_ref, mid_ref,
):
    half = rows // 2

    def at(ref, index):
        return ref[index * groups : (index + 1) * groups, :]

    low, high = sigmas(
        couple_low, couple_high, own_top, own_bottom, got_top, got_bottom, sent_top, sent_bottom,
        from_low, from_high, at(ratio_ref, 0), at(ratio_ref, rows - 1), edge_ref, at(edge_ref, 5), at(edge_ref, 6),
    )
    for i in range(half):
        j = rows - 1 - i
        if i:
            low = at(ratio_ref, i) * low
            high = at(ratio_ref, j) * high
        mid_ref[i * groups : (i + 1) * groups, :] = low
        mid_ref[j * groups : (j + 1) * groups, :] = high

    def put(index, value):
        rows_at = slice(index * groups, (index + 1) * groups)
        out_ref[rows_at, :] = first_ref[rows_at, :] + value

    meet(rows, groups, low, high, ratio_ref, inverse_ref, edge_ref, at, lambda i: at(mid_ref, i), put)


def call(body, outs, ins, spaces, scratch, flops, name, out_spaces=None, aliases=None):
    nbytes = sum(x.size * x.dtype.itemsize for x in ins) + sum(4 * math.prod(s) for s in outs)
    out = pl.pallas_call(
        body,
        out_shape=[jax.ShapeDtypeStruct(s, jnp.float32) for s in outs],
        in_specs=[pl.BlockSpec(memory_space=s) for s in spaces],
        out_specs=[pl.BlockSpec(memory_space=s) for s in out_spaces or [VMEM] * len(outs)],
        input_output_aliases=aliases or {},
        scratch_shapes=scratch,
        compiler_params=pltpu.CompilerParams(vmem_limit_bytes=48 << 20),
        cost_estimate=pl.CostEstimate(flops=WEIGHT * flops, bytes_accessed=WEIGHT * nbytes, transcendentals=0),
        name=name,
    )(*ins)
    return out


def pad_rows(rows):
    return -(-rows // (2 * BLOCK)) * 2 * BLOCK


def swap(value_even, value_odd):
    count = lax.axis_size("lat")
    even = [(i, i ^ 1) for i in range(count) if (i ^ 1) < count]
    odd = [(i, ((i + 1) ^ 1) - 1) for i in range(1, count) if ((i + 1) ^ 1) - 1 < count]
    value_odd = lax.ppermute(value_odd, "lat", odd)
    return lax.ppermute(value_even, "lat", even), value_odd


def send_level(piece, mask, size):
    return lax.ppermute(piece, "lon", [(d, d ^ mask) for d in range(size)])


def swap_levels(pieces):
    return [pieces[0]] + [send_level(pieces[mask], mask, len(pieces)) for mask in range(1, len(pieces))]


def operator_parts(rows, lon_coef, lat_coef, level_scale):
    row_first = lax.axis_index("lat") * rows
    extent = rows + 2 * OV
    lon_window = lax.dynamic_slice_in_dim(jnp.pad(lon_coef, (OV, OV)), row_first, extent)
    couple = lax.dynamic_slice_in_dim(jnp.pad(lat_coef, (OV + 1, OV + 2)), row_first, extent + 1)
    return level_scale[:, None] * lon_window[None], level_scale[:, None] * couple[None]


def factor(rows, groups, lon_window, couple, eigen):
    block = (rows * groups, N2)
    return call(
        functools.partial(factor_kernel, rows),
        [block, block, (21 * groups, N2)],
        [lon_window, couple, eigen],
        [SMEM, SMEM, VMEM],
        [],
        rows * groups * N2 * 20,
        "factor",
    )


def vmem(*shape):
    return pltpu.VMEM(shape, jnp.float32)


def rows_of(ref, groups, first=0):
    return lambda i: ref[(i - first) * groups : (i - first + 1) * groups, :]


def on_device(right_side, lon_coef, lat_coef, level_scale):
    const = {k: jnp.asarray(v) for k, v in tables(right_side.shape[1]).items()}
    if lax.axis_size("lon") != right_side.shape[1]:
        return shared_levels(const, right_side, lon_coef, lat_coef, level_scale)
    return whole_levels(const, right_side, lon_coef, lat_coef, level_scale)


def early_rows(rows):
    return rows // 2 + 2


def edge_kernel(rows, level_ref, lon_ref, couple_ref, eigen_ref, out_ref):
    eigen = eigen_ref[...]
    groups = eigen.shape[0]
    level = level_ref[0]
    low = high = low_inverse = high_inverse = None
    for i in range(OV):
        e, f = rows + i, 2 * OV - 1 - i
        if i == 0:
            low = 1.0 + lon_ref[level, e] * eigen + couple_ref[level, e]
            high = 1.0 + lon_ref[level, f] * eigen + couple_ref[level, f + 1]
        else:
            low_ratio = couple_ref[level, e] * low_inverse
            high_ratio = couple_ref[level, f + 1] * high_inverse
            out_ref[(i - 1) * groups : i * groups, :] = low_ratio
            out_ref[(OV + i - 1) * groups : (OV + i) * groups, :] = high_ratio
            low = 1.0 + lon_ref[level, e] * eigen + low_ratio * low
            high = 1.0 + lon_ref[level, f] * eigen + high_ratio * high
        low_inverse = 1.0 / (couple_ref[level, e + 1] + low)
        high_inverse = 1.0 / (couple_ref[level, f] + high)
    out_ref[(OV - 1) * groups : OV * groups, :] = low_inverse
    out_ref[(2 * OV - 1) * groups :, :] = high_inverse


def level_response(rows, early, level, lon_ref, couple_ref, eigen, put_ratio, put_inverse, keep, tables):
    half = rows // 2
    ratio_at, value_at, put_value, put_phi, put_psi = tables

    def plain(e):
        return 1.0 + lon_ref[level, e] * eigen

    low = high = None
    low_inverse = high_inverse = low_value = high_value = None
    for i in range(-OV, half):
        j = rows - 1 - i
        e, f = i + OV, j + OV
        if low is None:
            low = plain(e) + couple_ref[level, e]
            high = plain(f) + couple_ref[level, f + 1]
        else:
            low_ratio = couple_ref[level, e] * low_inverse
            high_ratio = couple_ref[level, f + 1] * high_inverse
            low = plain(e) + low_ratio * low
            high = plain(f) + high_ratio * high
        low_divisor = couple_ref[level, e + 1] + low
        high_divisor = couple_ref[level, f] + high
        low_inverse = 1.0 / low_divisor
        high_inverse = 1.0 / high_divisor
        yield
        if i == -1:
            keep(0, low_inverse)
            keep(1, high_inverse)
        if i == 0:
            low_value = high_value = jnp.ones_like(eigen)
        elif i > 0:
            low_value = low_ratio * low_value
            high_value = high_ratio * high_value
        if i >= 0:
            put_ratio(i, low_ratio)
            put_ratio(j, high_ratio)
            put_inverse(i, low_inverse)
            put_inverse(j, high_inverse)
            put_value(i, low_value * low_inverse)
            if j < early:
                put_value(j, high_value * high_inverse)
    between = couple_ref[level, OV + half]
    inverse = 1.0 / (between * (low + high) + low * high)
    across = between * inverse
    high_inverse = high_divisor * inverse
    low_inverse = low_divisor * inverse
    keep(2, high_inverse)
    keep(3, low_inverse)
    keep(4, across)
    phi = high_inverse * low_value
    psi = across * high_value
    phi_down = across * low_value
    psi_down = low_inverse * high_value
    put_phi(half - 1, phi)
    put_psi(half - 1, psi)
    for i in range(half - 2, -1, -1):
        yield
        ratio = ratio_at(i + 1)
        phi = value_at(i) + ratio * phi
        psi = ratio * psi
        put_phi(i, phi)
        put_psi(i, psi)
    put_phi(half, phi_down)
    put_psi(half, psi_down)
    for j in range(half + 1, early):
        ratio = ratio_at(j - 1)
        phi_down = ratio * phi_down
        psi_down = value_at(j) + ratio * psi_down
        put_phi(j, phi_down)
        put_psi(j, psi_down)


def getter(ref, groups):
    return lambda index: ref[index * groups : (index + 1) * groups, :]


def putter(ref, groups, first=0):
    def put(index, value):
        at = first + index * groups
        ref[pl.ds(at if isinstance(at, int) else pl.multiple_of(at, groups), groups), :] = value

    return put


def together(*steps):
    steps = list(steps)
    while steps:
        steps = [step for step in steps if next(step, steps) is not steps]


def partner_response(rows, early, place_ref, lon_ref, couple_ref, eigen, masks, phi_ref, psi_ref, kept_refs, value_refs):
    groups = eigen.shape[0]

    def nothing(index, value):
        pass

    def one(n, mask):
        put_kept = putter(kept_refs[n], groups)

        def put_ratio(index, value):
            if index < early:
                put_kept(index, value)

        first = n * early * groups
        return level_response(
            rows, early, place_ref[0] ^ mask, lon_ref, couple_ref, eigen, put_ratio, nothing, nothing,
            (
                getter(kept_refs[n], groups), getter(value_refs[n], groups), putter(value_refs[n], groups),
                putter(phi_ref, groups, first), putter(psi_ref, groups, first),
            ),
        )

    return [one(n, mask) for n, mask in enumerate(masks)]


def own_kernel(
    rows, early, masks, place_ref, lon_ref, couple_ref, eigen_ref, ratio_ref, inverse_ref, edge_ref, phi_ref, psi_ref,
    phi_near_ref, psi_near_ref, value_ref, *refs,
):
    eigen = eigen_ref[...]
    groups = eigen.shape[0]
    own = level_response(
        rows, early, place_ref[0], lon_ref, couple_ref, eigen, putter(ratio_ref, groups),
        putter(inverse_ref, groups), putter(edge_ref, groups),
        (
            getter(ratio_ref, groups), getter(value_ref, groups), putter(value_ref, groups),
            putter(phi_ref, groups), putter(psi_ref, groups),
        ),
    )
    count = len(masks)
    together(
        own,
        *partner_response(
            rows, early, place_ref, lon_ref, couple_ref, eigen, masks, phi_near_ref, psi_near_ref,
            refs[:count], refs[count:],
        ),
    )


def partners_kernel(
    rows, early, masks, place_ref, lon_ref, couple_ref, eigen_ref, after_ref, phi_ref, psi_ref, *refs
):
    del after_ref
    count = len(masks)
    together(
        *partner_response(
            rows, early, place_ref, lon_ref, couple_ref, eigen_ref[...], masks, phi_ref, psi_ref,
            refs[:count], refs[count:],
        )
    )


def whole_levels(const, right_side, lon_coef, lat_coef, level_scale):
    rows, levels, lon_count = right_side.shape
    digits = N1 // levels
    groups = 2 * GROUPS
    lon_at = lax.axis_index("lon").astype(jnp.int32)
    parity = (lax.axis_index("lat") % 2).astype(jnp.int32)
    place = jnp.stack([lon_at, parity])
    half = rows // 2
    early = early_rows(rows)
    late = rows - early
    eigen = const["eigen"].reshape(groups, N2)
    lon_all, couple_all = operator_parts(rows, lon_coef, lat_coef, level_scale)
    (around,) = call(
        functools.partial(edge_kernel, rows),
        [(2 * OV * groups, N2)],
        [place, lon_all, couple_all, eigen],
        [SMEM, SMEM, SMEM, VMEM],
        [],
        16 * groups * N2 * 20,
        "edge",
    )
    block = (rows * groups, N2)
    early_block = (early * groups, N2)
    early_block = (early * groups, N2)
    near_masks, far_masks = [1], list(range(2, levels))
    ratio, inverse, edge, phi, psi, phi_near, psi_near = call(
        functools.partial(own_kernel, rows, early, near_masks),
        [block, block, (5 * groups, N2)] + [early_block] * 4,
        [place, lon_all, couple_all, eigen],
        [SMEM, SMEM, SMEM, VMEM],
        [vmem(*early_block)] * 3,
        2 * rows * groups * N2 * 20,
        "own",
    )
    row = (groups, N2)
    ends = 2 * OV
    inner = rows - ends
    span = OV * digits
    by_row = right_side.reshape(rows, levels, digits, N2).transpose(0, 2, 1, 3).reshape(-1, N2)

    far = list(range(2, levels))

    def pack_ends(place_ref, in_ref, *refs):
        for end_ref, mask in zip(refs, [0] + far):
            level = place_ref[0] ^ mask
            end_ref[:span, :] = in_ref[pl.ds(level, span, stride=levels), :]
            end_ref[span:, :] = in_ref[pl.ds(level + levels * (rows - OV) * digits, span, stride=levels), :]

    end_packed = call(
        pack_ends,
        [(ends * digits, N2)] * (levels - 1),
        [place, by_row],
        [SMEM, VMEM],
        [],
        0,
        "pack_ends",
    )

    def pack(place_ref, in_ref, after_ref, *refs):
        del after_ref
        for mask, out_ref in enumerate(refs):
            level = place_ref[0] ^ mask
            skip = 0 if mask == 1 else levels * span
            out_ref[...] = in_ref[pl.ds(level + skip, out_ref.shape[0], stride=levels), :]

    packed = call(
        pack,
        [((rows if mask == 1 else inner) * digits, N2) for mask in range(levels)],
        [place, by_row, end_packed[0]],
        [SMEM, VMEM, pl.ANY],
        [],
        0,
        "pack",
    )
    end_pieces = [end_packed[0], None] + [send_level(p, m, levels) for p, m in zip(end_packed[1:], far)]
    near = send_level(packed[1], 1, levels)
    end_pieces[1] = near
    inner_pieces = [packed[0], near] + [send_level(packed[m], m, levels) for m in far]
    forward = [const["first"], const["turn"], const["second"], const["special"]]
    pad_ends, pad_inner = pad_rows(ends), pad_rows(inner)

    def ends_body(place_ref, *refs):
        pieces, refs = refs[:levels], refs[levels:]
        tables_in, edge_ref = refs[:4], refs[4]
        spec_ref, top_ref, bottom_ref, even_ref, odd_ref, full_ref, mid_ref = refs[5:]
        for mask, piece in enumerate(pieces):
            at = pl.multiple_of((place_ref[0] ^ mask) * digits, digits)
            last = piece.shape[0] - span
            full_ref[:OV, pl.ds(at, digits), :] = piece[:span, :].reshape(OV, digits, N2)
            full_ref[OV:ends, pl.ds(at, digits), :] = piece[last:, :].reshape(OV, digits, N2)
        forward_rows(full_ref, ends, *tables_in, mid_ref, spec_ref)
        top, bottom = edge_sums(
            rows_of(spec_ref, groups), rows_of(spec_ref, groups, -OV),
            rows_of(edge_ref, groups), lambda i: edge_ref[(2 * OV - 2 - i) * groups : (2 * OV - 1 - i) * groups, :],
        )
        top_ref[...] = top
        bottom_ref[...] = bottom
        swap_out(place_ref[1], top, bottom, even_ref, odd_ref)

    end_spectral, sent_top, sent_bottom, even, odd = call(
        ends_body,
        [(ends * groups, N2)] + [row] * 4,
        [place, *end_pieces, *forward, around],
        [SMEM] + [VMEM] * (levels + 5),
        [vmem(pad_ends, N1, N2), vmem(pad_ends * N1, N2)],
        ends * NLON * 256 * 4,
        "ends",
    )
    even, odd = swap(even, odd)
    backward = [const["first_back"], const["turn"], const["second_back"], const["special_back"]]
    pad_early, pad_late = pad_rows(early), pad_rows(late)

    def spread(place_ref, full_ref, count, out_refs):
        for mask, out_ref in enumerate(out_refs):
            at = pl.multiple_of((place_ref[0] ^ mask) * digits, digits)
            out_ref[...] = full_ref[:count, pl.ds(at, digits), :].reshape(count * digits, N2)

    def inner_body(place_ref, *refs):
        pieces, refs = refs[:levels], refs[levels:]
        tables_in, refs = refs[:4], refs[4:]
        ends_ref, odd_ref, even_ref, ratio_ref, inverse_ref, edge_ref = refs[:6]
        early_ref, late_ref, top_ref, even_out, odd_out = refs[6:11]
        full_ref, mid_ref, spec_ref, sum_ref = refs[11:]
        for mask, piece in enumerate(pieces):
            at = pl.multiple_of((place_ref[0] ^ mask) * digits, digits)
            skip = span if mask == 1 else 0
            full_ref[:inner, pl.ds(at, digits), :] = piece[skip : skip + inner * digits, :].reshape(
                inner, digits, N2
            )
        if pad_inner > inner:
            full_ref[inner:] = jnp.zeros((pad_inner - inner, N1, N2), jnp.float32)
        forward_rows(full_ref, inner, *tables_in, mid_ref, spec_ref)
        low, high = swap_in(place_ref[1], even_ref[...], odd_ref[...])

        def spec_row(i):
            if i < OV:
                return rows_of(ends_ref, groups)(i)
            if i >= rows - OV:
                return rows_of(ends_ref, groups, rows - ends)(i)
            return rows_of(spec_ref, groups, OV)(i)

        solve_first(rows, groups, spec_row, low, high, ratio_ref, inverse_ref, edge_ref, sum_ref)
        top = sum_ref[:groups, :]
        top_ref[...] = top
        early_ref[...] = sum_ref[: early * groups, :]
        late_ref[...] = sum_ref[early * groups :, :]
        swap_out(place_ref[1], sum_ref[(rows - 1) * groups :, :], top, even_out, odd_out)

    early_first, late_first, own_top, even2, odd2 = call(
        inner_body,
        [early_block, (late * groups, N2), row, row, row],
        [place, *inner_pieces, *forward, end_spectral, odd, even, ratio, inverse, edge],
        [SMEM] + [VMEM] * (levels + 10),
        [vmem(pad_inner, N1, N2), vmem(pad_inner * N1, N2), vmem(inner * N1, N2), vmem(rows * groups, N2)],
        inner * NLON * 256 * 4,
        "inner",
    )

    def early_body(place_ref, *refs):
        first_ref, tables_in, out_refs = refs[0], refs[1:5], refs[5 : 5 + levels]
        mid_ref, full_ref = refs[5 + levels :]
        backward_rows(first_ref, early, *tables_in, mid_ref, full_ref)
        spread(place_ref, full_ref, early, out_refs)

    early_pieces = call(
        early_body,
        [(early * digits, N2)] * levels,
        [place, early_first, *backward],
        [SMEM] + [VMEM] * 5,
        [vmem(pad_early * N1, N2), vmem(pad_early, N1, N2)],
        early * NLON * 256 * 4,
        "early",
    )
    early_pieces = swap_levels(early_pieces)
    even2, odd2 = swap(even2, odd2)

    def sigma_body(place_ref, couple_ref, *refs):
        first_ref, own_top_ref, odd_ref, even_ref, odd2_ref, even2_ref, top_ref, bottom_ref = refs[:8]
        ratio_ref, edge_ref, around_ref = refs[8:11]
        sigma_ref = refs[-1]
        level = place_ref[0]
        got_top, got_bottom = swap_in(place_ref[1], even_ref[...], odd_ref[...])
        from_low, from_high = swap_in(place_ref[1], even2_ref[...], odd2_ref[...])
        low, high = sigmas(
            couple_ref[level, OV], couple_ref[level, OV + rows], own_top_ref[...], first_ref[(late - 1) * groups :, :],
            got_top, got_bottom, top_ref[...], bottom_ref[...], from_low, from_high,
            ratio_ref[:groups, :], ratio_ref[(rows - 1) * groups :, :], edge_ref,
            around_ref[(OV - 1) * groups : OV * groups, :], around_ref[(2 * OV - 1) * groups :, :],
        )
        sigma_ref[:groups, :] = low
        sigma_ref[groups:, :] = high

    (sigma,) = call(
        sigma_body,
        [(2 * groups, N2)],
        [
            place, couple_all, late_first, own_top, odd, even, odd2, even2, sent_top, sent_bottom, ratio, edge, around,
        ],
        [SMEM, SMEM] + [VMEM] * 11,
        [],
        groups * N2 * 40,
        "sigma",
    )
    far_sigma = [send_level(sigma, mask, levels) for mask in far]
    def second_body(place_ref, *refs):
        sigma_ref, first_ref, ratio_ref, inverse_ref, edge_ref = refs[:5]
        tables_in, refs = refs[5:9], refs[10:]
        late_refs = list(refs[:levels])
        sum_ref, mid_ref, full_ref = refs[levels:]
        low, high = sigma_ref[:groups, :], sigma_ref[groups:, :]

        def at(ref, index):
            return ref[index * groups : (index + 1) * groups, :]

        for i in range(half):
            j = rows - 1 - i
            if i:
                low = at(ratio_ref, i) * low
                high = at(ratio_ref, j) * high
            mid_ref[(j - half) * groups : (j - half + 1) * groups, :] = high
        x_high = at(edge_ref, 3) * high + at(edge_ref, 4) * low
        for j in range(half, rows):
            if j > half:
                x_high = at(mid_ref, j - half) * at(inverse_ref, j) + at(ratio_ref, j - 1) * x_high
            if j >= early:
                here = slice((j - early) * groups, (j - early + 1) * groups)
                sum_ref[here, :] = first_ref[here, :] + x_high
        backward_rows(sum_ref, late, *tables_in, mid_ref, full_ref)
        late_refs[1][late * digits :, :] = sigma_ref[...]
        late_refs[1] = late_refs[1].at[pl.ds(0, late * digits), :]
        spread(place_ref, full_ref, late, late_refs)

    late_pieces = call(
        second_body,
        [(late * digits + (2 * groups if mask == 1 else 0), N2) for mask in range(levels)],
        [place, sigma, late_first, ratio, inverse, edge, *backward, early_pieces[1]],
        [SMEM] + [VMEM] * 9 + [pl.ANY],
        [vmem(late * groups, N2), vmem(max(pad_late, half) * N1, N2), vmem(pad_late, N1, N2)],
        late * NLON * 256 * 4,
        "second",
    )
    phi_far, psi_far = call(
        functools.partial(partners_kernel, rows, early, far_masks),
        [(len(far_masks) * early * groups, N2)] * 2,
        [place, lon_all, couple_all, eigen, late_pieces[0]],
        [SMEM, SMEM, SMEM, VMEM, pl.ANY],
        [vmem(*early_block)] * (2 * len(far_masks)),
        len(far_masks) * rows * groups * N2 * 20,
        "partners",
    )
    late_pieces = swap_levels(late_pieces)
    sigma_pieces = [sigma, late_pieces[1], *far_sigma]
    total = rows * levels * digits
    early_total = early * levels * digits
    part = const["first_back_part"]

    def correct(place_ref, *refs):
        pieces, sigma_refs, refs = refs[:levels], refs[levels : 2 * levels], refs[2 * levels :]
        responses, refs = refs[:6], refs[6:]
        part_ref, turn_ref, second_ref, special_ref = refs[:4]
        out_ref, sum_ref, mid_ref, done_ref, sem = refs[4:]
        part_rows = part_ref.shape[0] // levels
        mine = part_ref.at[pl.ds(pl.multiple_of(place_ref[0] * part_rows, part_rows), part_rows), :]
        size = early * groups
        for mask in range(levels):
            level = place_ref[0] ^ mask
            last = sigma_refs[mask].shape[0]
            low = sigma_refs[mask][last - 2 * groups : last - groups, :]
            high = sigma_refs[mask][last - groups :, :]
            phi_ref, psi_ref = responses[2 * min(mask, 2) : 2 * min(mask, 2) + 2]
            first = max(mask - 2, 0) * size
            phi_all = phi_ref[first : first + size, :].reshape(early, groups, N2)
            psi_all = psi_ref[first : first + size, :].reshape(early, groups, N2)
            sum_ref[...] = (phi_all * low[None] + psi_all * high[None]).reshape(size, N2)
            spectral_back(sum_ref, early, pad_early, second_ref, special_ref, mid_ref)
            for pair in range(pad_early // (2 * BLOCK)):
                value = digits_back(mid_ref, pair, turn_ref, mine)
                for side in range(2):
                    begin = (2 * pair + side) * BLOCK
                    count = min(BLOCK, early - begin)
                    if count <= 0:
                        continue
                    lines = count * digits
                    whole = pieces[mask][begin * digits : begin * digits + lines, :]
                    done_ref[pl.ds(level + begin * digits * levels, lines, stride=levels), :] = (
                        whole + value[:lines, side * N2 : (side + 1) * N2]
                    )
        copy = pltpu.make_async_copy(done_ref, out_ref.at[pl.ds(0, early_total), :], sem)
        copy.start()
        copy.wait()

    (out,) = call(
        correct,
        [(total, N2)],
        [
            place, *early_pieces, *sigma_pieces, phi, psi, phi_near, psi_near, phi_far, psi_far,
            part, const["turn"], *backward[2:],
        ],
        [SMEM] + [VMEM] * (2 * levels + 10),
        [
            vmem(early * groups, N2), vmem(pad_early * N1, N2), vmem(early_total, N2), pltpu.SemaphoreType.DMA,
        ],
        levels * early * NLON * 256 * 40,
        "correct",
        out_spaces=[pl.ANY],
    )

    chunks = 4

    def unpack(place_ref, *refs):
        pieces = refs[:levels]
        out_ref, done_ref, sems = refs[levels + 1 :]
        lines = late * digits // chunks
        copies = []
        for chunk in range(chunks):
            for mask in range(levels):
                first = (place_ref[0] ^ mask) + chunk * lines * levels
                skip = chunk * lines
                done_ref[pl.ds(first, lines, stride=levels), :] = pieces[mask][skip : skip + lines, :]
            here = pl.ds(chunk * lines * levels, lines * levels)
            there = pl.ds(early_total + chunk * lines * levels, lines * levels)
            copy = pltpu.make_async_copy(done_ref.at[here, :], out_ref.at[there, :], sems.at[chunk])
            copy.start()
            copies.append(copy)
        for copy in copies:
            copy.wait()

    (out,) = call(
        unpack,
        [(total, N2)],
        [place, *late_pieces, out],
        [SMEM] + [VMEM] * levels + [pl.ANY],
        [vmem(total - early_total, N2), pltpu.SemaphoreType.DMA((chunks,))],
        0,
        "unpack",
        out_spaces=[pl.ANY],
        aliases={levels + 1: 0},
    )
    return out.reshape(rows, digits, levels, N2).transpose(0, 2, 1, 3).reshape(right_side.shape)


def second_part(
    rows, groups, parity, couple_ref, first_ref, even_ref, odd_ref, even2_ref, odd2_ref, top_ref, bottom_ref,
    ratio_ref, inverse_ref, edge_ref, out_ref, mid_ref,
):
    got_top, got_bottom = swap_in(parity, even_ref[...], odd_ref[...])
    low, high = swap_in(parity, even2_ref[...], odd2_ref[...])
    solve_second(
        rows, groups, couple_ref[OV], couple_ref[OV + rows],
        first_ref[:groups, :], first_ref[(rows - 1) * groups :, :],
        got_top, got_bottom, top_ref[...], bottom_ref[...], low, high,
        ratio_ref, inverse_ref, edge_ref, first_ref, out_ref, mid_ref,
    )


def shared_levels(const, right_side, lon_coef, lat_coef, level_scale):
    rows, levels, lon_count = right_side.shape
    lon_size = lax.axis_size("lon")
    assert lon_size % levels == 0 and GROUPS % (lon_size // levels) == 0 and rows % (lon_size // levels) == 0
    sharers = lon_size // levels
    groups = 2 * GROUPS // sharers
    part_rows = rows // sharers
    digits = N1 // lon_size
    lon_at = lax.axis_index("lon")
    parity = (lax.axis_index("lat") % 2).astype(jnp.int32).reshape(1)
    lon_window, couple = operator_parts(rows, lon_coef, lat_coef, level_scale)
    lon_window = lax.dynamic_index_in_dim(lon_window, lon_at // sharers, 0, False)
    couple = lax.dynamic_index_in_dim(couple, lon_at // sharers, 0, False)
    eigen = lax.dynamic_slice_in_dim(
        const["eigen"], (lon_at % sharers) * (groups // 2), groups // 2, axis=1
    ).reshape(groups, N2)
    ratio, inverse, edge = factor(rows, groups, lon_window, couple, eigen)
    block = (rows * groups, N2)
    row = (groups, N2)
    send = right_side.reshape(sharers, part_rows, levels, lon_count).transpose(2, 0, 1, 3)
    send = send.reshape(lon_size, part_rows, digits, N2)
    got = lax.all_to_all(send, "lon", 0, 0, tiled=True)
    points = got.transpose(1, 0, 2, 3).reshape(part_rows, N1, N2)
    padded = pad_rows(part_rows)

    def transform(points_ref, first_ref, turn_ref, second_ref, special_ref, out_ref, full_ref, mid_ref):
        full_ref[:part_rows] = points_ref[...]
        if padded > part_rows:
            full_ref[part_rows:] = jnp.zeros((padded - part_rows, N1, N2), jnp.float32)
        forward_rows(full_ref, part_rows, first_ref, turn_ref, second_ref, special_ref, mid_ref, out_ref)

    (spectral,) = call(
        transform,
        [(part_rows * N1, N2)],
        [points, const["first"], const["turn"], const["second"], const["special"]],
        [VMEM] * 5,
        [vmem(padded, N1, N2), vmem(padded * N1, N2)],
        part_rows * NLON * 256 * 4,
        "transform",
    )
    spectral = to_coefs(spectral, sharers, part_rows, groups)

    def edges(parity_ref, spec_ref, edge_ref, top_ref, bottom_ref, even_ref, odd_ref):
        top, bottom = edge_sums(
            rows_of(spec_ref, groups), rows_of(spec_ref, groups, OV - rows),
            rows_of(edge_ref, groups, -7), rows_of(edge_ref, groups, -14),
        )
        top_ref[...] = top
        bottom_ref[...] = bottom
        swap_out(parity_ref[0], top, bottom, even_ref, odd_ref)

    sent_top, sent_bottom, even, odd = call(
        edges, [row] * 4, [parity, spectral, edge], [SMEM, VMEM, VMEM], [], groups * N2 * 32, "edges"
    )
    even, odd = swap(even, odd)

    def first(parity_ref, spec_ref, even_ref, odd_ref, ratio_ref, inverse_ref, edge_ref, out_ref, e_ref, o_ref):
        low, high = swap_in(parity_ref[0], even_ref[...], odd_ref[...])
        solve_first(
            rows, groups, rows_of(spec_ref, groups), low, high, ratio_ref, inverse_ref, edge_ref, out_ref
        )
        swap_out(parity_ref[0], out_ref[(rows - 1) * groups :, :], out_ref[:groups, :], e_ref, o_ref)

    iterate, even2, odd2 = call(
        first,
        [block, row, row],
        [parity, spectral, even, odd, ratio, inverse, edge],
        [SMEM] + [VMEM] * 6,
        [],
        rows * groups * N2 * 8,
        "first_solve",
    )
    even2, odd2 = swap(even2, odd2)

    def second(parity_ref, *refs):
        second_part(rows, groups, parity_ref[0], *refs)

    (iterate,) = call(
        second,
        [block],
        [parity, couple, iterate, even, odd, even2, odd2, sent_top, sent_bottom, ratio, inverse, edge],
        [SMEM, SMEM] + [VMEM] * 10,
        [vmem(*block)],
        rows * groups * N2 * 8,
        "second_solve",
    )
    iterate = to_rows(iterate, sharers, part_rows, groups)

    def back(spec_ref, first_ref, turn_ref, second_ref, special_ref, out_ref, mid_ref, full_ref):
        backward_rows(spec_ref, part_rows, first_ref, turn_ref, second_ref, special_ref, mid_ref, full_ref)
        out_ref[...] = full_ref[:part_rows]

    (points,) = call(
        back,
        [(part_rows, N1, N2)],
        [iterate, const["first_back"], const["turn"], const["second_back"], const["special_back"]],
        [VMEM] * 5,
        [vmem(padded * N1, N2), vmem(padded, N1, N2)],
        part_rows * NLON * 256 * 4,
        "back_transform",
    )
    send = points.reshape(part_rows, lon_size, digits, N2).transpose(1, 0, 2, 3)
    got = lax.all_to_all(send, "lon", 0, 0, tiled=True)
    got = got.reshape(levels, sharers, part_rows, lon_count).transpose(1, 2, 0, 3)
    return got.reshape(rows, levels, lon_count)


def level_groups(sharers):
    size = lax.axis_size("lon")
    return [[first + i for i in range(sharers)] for first in range(0, size, sharers)]


def to_coefs(spectral, sharers, part_rows, groups):
    send = spectral.reshape(part_rows, 2, sharers, groups // 2, N2).transpose(2, 0, 1, 3, 4)
    got = lax.all_to_all(
        send, "lon", 0, 0, tiled=True, axis_index_groups=level_groups(sharers)
    )
    return got.reshape(sharers * part_rows * groups, N2)


def to_rows(values, sharers, part_rows, groups):
    send = values.reshape(sharers, part_rows, 2, groups // 2, N2)
    got = lax.all_to_all(
        send, "lon", 0, 0, tiled=True, axis_index_groups=level_groups(sharers)
    )
    return got.transpose(1, 2, 0, 3, 4).reshape(part_rows * N1, N2)


def solution(mesh):
    return jax.shard_map(
        on_device,
        mesh=mesh,
        in_specs=(P("lat", None, "lon"), P(), P(), P()),
        out_specs=P("lat", None, "lon"),
        check_vma=False,
    )
```

```python
import functools
import math

import jax
import jax.numpy as jnp
import numpy as np
from jax import lax
from jax.experimental import pallas as pl
from jax.experimental.pallas import tpu as pltpu
from jax.sharding import PartitionSpec as P

NLON = 4096
OV = 8
N1 = 32
N2 = 128
GROUPS = 16
BLOCK = 8
WEIGHT = 256

VMEM = pltpu.VMEM
SMEM = pltpu.SMEM


def numpy_split(table):
    import ml_dtypes

    table = np.asarray(table, np.float32)
    high = table.astype(ml_dtypes.bfloat16)
    low = (table - high.astype(np.float32)).astype(ml_dtypes.bfloat16)
    return high, low


def tables(levels):
    j1 = np.arange(N1)
    j2 = np.arange(N2)
    k2 = np.arange(N2)
    digit = np.arange(GROUPS)
    small = np.zeros((N1, N1))
    small[:GROUPS] = np.cos(2 * np.pi * np.outer(digit, j1) / N1)
    small[GROUPS] = np.cos(np.pi * j1)
    small[GROUPS + 1 :] = -np.sin(2 * np.pi * np.outer(digit[1:], j1) / N1)
    first = np.kron(np.eye(BLOCK), small)
    angle = 2 * np.pi * np.outer(digit, j2) / NLON
    turn_cos = np.cos(angle)
    turn_sin = np.sin(angle)
    phase = 2 * np.pi * (np.outer(j2, k2) % N2) / N2
    cosine, sine = np.cos(phase), np.sin(phase)
    second = np.block([[cosine, -sine], [sine, cosine]])
    special = np.zeros((2 * N2, 2 * N2))
    half = N2 // 2
    special[:N2, : half + 1] = np.cos(2 * np.pi * np.outer(j2, np.arange(half + 1)) / N2)
    special[:N2, half + 1 : N2] = -np.sin(2 * np.pi * np.outer(j2, np.arange(1, half)) / N2)
    odd = 2 * np.pi * np.outer(j2, 1 + 2 * np.arange(half)) / (2 * N2)
    special[N2:, N2 : N2 + half] = np.cos(odd)
    special[N2:, N2 + half :] = -np.sin(odd)
    weight = np.full(2 * N2, 2.0 / NLON)
    weight[0] = 1.0 / NLON
    weight[half] = 1.0 / NLON
    second_back = second.T * (2.0 / NLON)
    special_back = weight[:, None] * special.T
    wave = np.zeros((GROUPS, 2 * N2))
    wave[:, :N2] = digit[:, None] + N1 * k2[None, :]
    wave[:, N2:] = wave[:, :N2]
    lane = np.arange(N2)
    wave[0, :N2] = np.where(lane <= half, N1 * lane, N1 * (lane - half))
    wave[0, N2:] = 16 + N1 * (lane % half)
    eigen = 2.0 - 2.0 * np.cos(2 * np.pi * wave / NLON)
    pair = lambda t: np.concatenate(numpy_split(t), axis=0)
    width = N1 // levels
    part = [pair(np.kron(np.eye(BLOCK), small.T[at : at + width])) for at in range(0, N1, width)]
    return dict(
        first_back_part=np.concatenate(part, axis=0),
        first=pair(first),
        first_back=pair(first.T),
        second=pair(second),
        second_back=pair(second_back),
        special=pair(special),
        special_back=pair(special_back),
        turn=np.concatenate([turn_cos, turn_sin], axis=0).astype(np.float32),
        eigen=np.stack([eigen[:, :N2], eigen[:, N2:]]).astype(np.float32),
    )


def halves(value):
    high = value.astype(jnp.bfloat16)
    low = (value - high.astype(jnp.float32)).astype(jnp.bfloat16)
    return high, low


def dot(a, b):
    return lax.dot_general(a, b, (((1,), (0,)), ((), ())), preferred_element_type=jnp.float32)


def product_right(value, table_ref):
    size = table_ref.shape[0] // 2
    high, low = halves(value)
    table_high = table_ref[:size, :]
    return dot(high, table_high) + dot(low, table_high) + dot(high, table_ref[size:, :])


def product_left(table_ref, value):
    size = table_ref.shape[0] // 2
    high, low = halves(value)
    both = dot(table_ref[...], high)
    return both[:size] + both[size:] + dot(table_ref[:size, :], low)


def lanes_apart(value, rows):
    real = value[:, :N2].reshape(rows, GROUPS, N2)
    imag = value[:, N2:].reshape(rows, GROUPS, N2)
    return jnp.concatenate([real, imag], axis=1).reshape(rows * 2 * GROUPS, N2)


def lanes_together(value, rows):
    both = value.reshape(rows, 2 * GROUPS, N2)
    return jnp.concatenate([both[:, :GROUPS], both[:, GROUPS:]], axis=2).reshape(rows * GROUPS, 2 * N2)


def load_zeroth(ref, rows):
    return jnp.concatenate(
        [ref[pl.ds(0, rows, stride=2 * GROUPS), :], ref[pl.ds(GROUPS, rows, stride=2 * GROUPS), :]], axis=1
    )


def store_zeroth(ref, rows, value):
    ref[pl.ds(0, rows, stride=2 * GROUPS), :] = value[:, :N2]
    ref[pl.ds(GROUPS, rows, stride=2 * GROUPS), :] = value[:, N2:]


def forward_rows(points_ref, rows, first_ref, turn_ref, second_ref, special_ref, mid_ref, out_ref):
    padded = points_ref.shape[0]
    turn_cos = turn_ref[:GROUPS, :][None]
    turn_sin = turn_ref[GROUPS:, :][None]
    for pair in range(padded // (2 * BLOCK)):
        base = pair * 2 * BLOCK
        left = points_ref[base : base + BLOCK].reshape(BLOCK * N1, N2)
        right = points_ref[base + BLOCK : base + 2 * BLOCK].reshape(BLOCK * N1, N2)
        value = product_left(first_ref, jnp.concatenate([left, right], axis=1))
        for side in range(2):
            digits = value[:, side * N2 : (side + 1) * N2].reshape(BLOCK, N1, N2)
            real, imag = digits[:, :GROUPS], digits[:, GROUPS:]
            turned = jnp.concatenate(
                [real * turn_cos + imag * turn_sin, imag * turn_cos - real * turn_sin], axis=1
            )
            at = (base + side * BLOCK) * N1
            mid_ref[at : at + BLOCK * N1, :] = turned.reshape(BLOCK * N1, N2)
    result = product_right(lanes_together(mid_ref[...], padded), second_ref)
    out_ref[...] = lanes_apart(result, padded)[: rows * N1]
    store_zeroth(out_ref, rows, product_right(load_zeroth(mid_ref, padded), special_ref)[:rows])


def spectral_back(spec_ref, rows, padded, second_ref, special_ref, mid_ref):
    result = product_right(lanes_together(spec_ref[...], rows), second_ref)
    mid_ref[: rows * N1, :] = lanes_apart(result, rows)
    if padded > rows:
        mid_ref[rows * N1 : padded * N1, :] = jnp.zeros(((padded - rows) * N1, N2), jnp.float32)
    store_zeroth(mid_ref, rows, product_right(load_zeroth(spec_ref, rows), special_ref))


def digits_back(mid_ref, pair, turn_ref, first_ref):
    turn_cos = turn_ref[:GROUPS, :][None]
    turn_sin = turn_ref[GROUPS:, :][None]
    sides = []
    for side in range(2):
        at = (2 * pair + side) * BLOCK * N1
        both = mid_ref[at : at + BLOCK * N1, :].reshape(BLOCK, N1, N2)
        real, imag = both[:, :GROUPS], both[:, GROUPS:]
        turned = jnp.concatenate(
            [real * turn_cos - imag * turn_sin, imag * turn_cos + real * turn_sin], axis=1
        )
        sides.append(turned.reshape(BLOCK * N1, N2))
    return product_left(first_ref, jnp.concatenate(sides, axis=1))


def backward_rows(spec_ref, rows, first_ref, turn_ref, second_ref, special_ref, mid_ref, out_ref):
    padded = out_ref.shape[0]
    spectral_back(spec_ref, rows, padded, second_ref, special_ref, mid_ref)
    for pair in range(padded // (2 * BLOCK)):
        base = pair * 2 * BLOCK
        value = digits_back(mid_ref, pair, turn_ref, first_ref)
        out_ref[base : base + BLOCK] = value[:, :N2].reshape(BLOCK, N1, N2)
        out_ref[base + BLOCK : base + 2 * BLOCK] = value[:, N2:].reshape(BLOCK, N1, N2)


def factor_kernel(rows, lon_ref, couple_ref, eigen_ref, ratio_ref, inverse_ref, edge_ref):
    eigen = eigen_ref[...]
    groups = eigen.shape[0]
    half = rows // 2
    last = rows + 2 * OV - 1

    def plain(e):
        return 1.0 + lon_ref[e] * eigen

    def put(ref, index, value):
        ref[index * groups : (index + 1) * groups, :] = value

    def chain(start, stop, step, into):
        excess = inverse = None
        for e in range(start, stop + step, step):
            before = couple_ref[e] if step > 0 else couple_ref[e + 1]
            after = couple_ref[e + 1] if step > 0 else couple_ref[e]
            if inverse is None:
                ratio = None
                excess = plain(e) + before
            else:
                ratio = before * inverse
                excess = plain(e) + ratio * excess
            divisor = after + excess
            inverse = 1.0 / divisor
            into(e, ratio, inverse, excess, divisor)

    kept = {}

    def top(e, ratio, inverse, excess, divisor):
        if e == OV - 1:
            put(edge_ref, 0, inverse)
        if e >= OV:
            put(ratio_ref, e - OV, ratio)
            put(inverse_ref, e - OV, inverse)
        if e == OV + half - 1:
            kept["top"] = excess, divisor

    def bottom(e, ratio, inverse, excess, divisor):
        if e == OV + rows:
            put(edge_ref, 1, inverse)
        if e < OV + rows:
            put(ratio_ref, e - OV, ratio)
            put(inverse_ref, e - OV, inverse)
        if e == OV + half:
            kept["bottom"] = excess, divisor

    def next_band(e, ratio, inverse, excess, divisor):
        if ratio is not None:
            put(edge_ref, 7 + e - rows - 1, ratio)
        if e == OV + rows - 1:
            put(edge_ref, 5, inverse)

    def previous_band(e, ratio, inverse, excess, divisor):
        if ratio is not None:
            put(edge_ref, 14 + e - OV, ratio)
        if e == OV:
            put(edge_ref, 6, inverse)

    chain(rows, OV + rows - 1, 1, next_band)
    chain(2 * OV - 1, OV, -1, previous_band)
    chain(0, OV + half - 1, 1, top)
    chain(last, OV + half, -1, bottom)
    excess_top, divisor_top = kept["top"]
    excess_bottom, divisor_bottom = kept["bottom"]
    between = couple_ref[OV + half]
    inverse = 1.0 / (between * (excess_top + excess_bottom) + excess_top * excess_bottom)
    put(edge_ref, 2, divisor_bottom * inverse)
    put(edge_ref, 3, divisor_top * inverse)
    put(edge_ref, 4, between * inverse)


def edge_sums(low_rows, high_rows, next_ratio, previous_ratio):
    top = high_rows(0)
    for i in range(1, OV):
        top = high_rows(i) + next_ratio(i - 1) * top
    bottom = low_rows(OV - 1)
    for i in range(OV - 2, -1, -1):
        bottom = low_rows(i) + previous_ratio(i) * bottom
    return top, bottom


def swap_out(parity, up, down, even_ref, odd_ref):
    is_even = parity == 0
    even_ref[...] = jnp.where(is_even, up, down)
    odd_ref[...] = jnp.where(is_even, down, up)


def swap_in(parity, even, odd):
    is_even = parity == 0
    return jnp.where(is_even, odd, even), jnp.where(is_even, even, odd)


def solve_first(rows, groups, right_side_row, from_low, from_high, ratio_ref, inverse_ref, edge_ref, out_ref):
    half = rows // 2

    def at(ref, index):
        return ref[index * groups : (index + 1) * groups, :]

    def put(index, value):
        out_ref[index * groups : (index + 1) * groups, :] = value

    low, high = from_low, from_high
    for i in range(half):
        j = rows - 1 - i
        low = right_side_row(i) + at(ratio_ref, i) * low
        high = right_side_row(j) + at(ratio_ref, j) * high
        put(i, low)
        put(j, high)
    meet(rows, groups, low, high, ratio_ref, inverse_ref, edge_ref, at, lambda i: at(out_ref, i), put)


def meet(rows, groups, low, high, ratio_ref, inverse_ref, edge_ref, at, value, put):
    half = rows // 2
    between = at(edge_ref, 4)
    x_low = at(edge_ref, 2) * low + between * high
    x_high = at(edge_ref, 3) * high + between * low
    put(half - 1, x_low)
    put(half, x_high)
    for i in range(half - 2, -1, -1):
        j = rows - 1 - i
        x_low = value(i) * at(inverse_ref, i) + at(ratio_ref, i + 1) * x_low
        x_high = value(j) * at(inverse_ref, j) + at(ratio_ref, j - 1) * x_high
        put(i, x_low)
        put(j, x_high)


def sigmas(
    couple_low, couple_high, own_top, own_bottom, got_top, got_bottom, sent_top, sent_bottom, from_low, from_high,
    ratio_first, ratio_last, edge_ref, next_inverse, previous_inverse,
):
    groups = own_top.shape[0]

    def edge(index):
        return edge_ref[index * groups : (index + 1) * groups, :]

    beyond_low = (got_top + couple_low * own_top) * edge(0)
    beyond_high = (got_bottom + couple_high * own_bottom) * edge(1)
    theirs_low = (sent_bottom + couple_low * from_low) * previous_inverse
    theirs_high = (sent_top + couple_high * from_high) * next_inverse
    low = ratio_first * (couple_low * (own_top - theirs_low)) + couple_low * (from_low - beyond_low)
    high = ratio_last * (couple_high * (own_bottom - theirs_high)) + couple_high * (from_high - beyond_high)
    return low, high


def solve_second(
    rows, groups, couple_low, couple_high, own_top, own_bottom, got_top, got_bottom, sent_top, sent_bottom,
    from_low, from_high, ratio_ref, inverse_ref, edge_ref, first_ref, out_ref, mid_ref,
):
    half = rows // 2

    def at(ref, index):
        return ref[index * groups : (index + 1) * groups, :]

    low, high = sigmas(
        couple_low, couple_high, own_top, own_bottom, got_top, got_bottom, sent_top, sent_bottom,
        from_low, from_high, at(ratio_ref, 0), at(ratio_ref, rows - 1), edge_ref, at(edge_ref, 5), at(edge_ref, 6),
    )
    for i in range(half):
        j = rows - 1 - i
        if i:
            low = at(ratio_ref, i) * low
            high = at(ratio_ref, j) * high
        mid_ref[i * groups : (i + 1) * groups, :] = low
        mid_ref[j * groups : (j + 1) * groups, :] = high

    def put(index, value):
        rows_at = slice(index * groups, (index + 1) * groups)
        out_ref[rows_at, :] = first_ref[rows_at, :] + value

    meet(rows, groups, low, high, ratio_ref, inverse_ref, edge_ref, at, lambda i: at(mid_ref, i), put)


def call(body, outs, ins, spaces, scratch, flops, name, out_spaces=None, aliases=None, weight=WEIGHT):
    nbytes = sum(x.size * x.dtype.itemsize for x in ins) + sum(4 * math.prod(s) for s in outs)
    out = pl.pallas_call(
        body,
        out_shape=[jax.ShapeDtypeStruct(s, jnp.float32) for s in outs],
        in_specs=[pl.BlockSpec(memory_space=s) for s in spaces],
        out_specs=[pl.BlockSpec(memory_space=s) for s in out_spaces or [VMEM] * len(outs)],
        input_output_aliases=aliases or {},
        scratch_shapes=scratch,
        compiler_params=pltpu.CompilerParams(vmem_limit_bytes=48 << 20),
        cost_estimate=pl.CostEstimate(flops=weight * flops, bytes_accessed=weight * nbytes, transcendentals=0),
        name=name,
    )(*ins)
    return out


def pad_rows(rows):
    return -(-rows // (2 * BLOCK)) * 2 * BLOCK


def swap(value_even, value_odd):
    count = lax.axis_size("lat")
    even = [(i, i ^ 1) for i in range(count) if (i ^ 1) < count]
    odd = [(i, ((i + 1) ^ 1) - 1) for i in range(1, count) if ((i + 1) ^ 1) - 1 < count]
    value_odd = lax.ppermute(value_odd, "lat", odd)
    return lax.ppermute(value_even, "lat", even), value_odd


def send_level(piece, mask, size):
    return lax.ppermute(piece, "lon", [(d, d ^ mask) for d in range(size)])


def swap_levels(pieces):
    return [pieces[0]] + [send_level(pieces[mask], mask, len(pieces)) for mask in range(1, len(pieces))]


def operator_parts(rows, lon_coef, lat_coef, level_scale):
    row_first = lax.axis_index("lat") * rows
    extent = rows + 2 * OV
    lon_window = lax.dynamic_slice_in_dim(jnp.pad(lon_coef, (OV, OV)), row_first, extent)
    couple = lax.dynamic_slice_in_dim(jnp.pad(lat_coef, (OV + 1, OV + 2)), row_first, extent + 1)
    return level_scale[:, None] * lon_window[None], level_scale[:, None] * couple[None]


def factor(rows, groups, lon_window, couple, eigen):
    block = (rows * groups, N2)
    return call(
        functools.partial(factor_kernel, rows),
        [block, block, (21 * groups, N2)],
        [lon_window, couple, eigen],
        [SMEM, SMEM, VMEM],
        [],
        rows * groups * N2 * 20,
        "factor",
    )


def vmem(*shape):
    return pltpu.VMEM(shape, jnp.float32)


def rows_of(ref, groups, first=0):
    return lambda i: ref[(i - first) * groups : (i - first + 1) * groups, :]


def on_device(right_side, lon_coef, lat_coef, level_scale):
    const = {k: jnp.asarray(v) for k, v in tables(right_side.shape[1]).items()}
    if lax.axis_size("lon") != right_side.shape[1]:
        return shared_levels(const, right_side, lon_coef, lat_coef, level_scale)
    return whole_levels(const, right_side, lon_coef, lat_coef, level_scale)


def early_rows(rows):
    return rows // 2 + 2


def edge_kernel(rows, level_ref, lon_ref, couple_ref, eigen_ref, out_ref):
    eigen = eigen_ref[...]
    groups = eigen.shape[0]
    level = level_ref[0]
    low = high = low_inverse = high_inverse = None
    for i in range(OV):
        e, f = rows + i, 2 * OV - 1 - i
        if i == 0:
            low = 1.0 + lon_ref[level, e] * eigen + couple_ref[level, e]
            high = 1.0 + lon_ref[level, f] * eigen + couple_ref[level, f + 1]
        else:
            low_ratio = couple_ref[level, e] * low_inverse
            high_ratio = couple_ref[level, f + 1] * high_inverse
            out_ref[(i - 1) * groups : i * groups, :] = low_ratio
            out_ref[(OV + i - 1) * groups : (OV + i) * groups, :] = high_ratio
            low = 1.0 + lon_ref[level, e] * eigen + low_ratio * low
            high = 1.0 + lon_ref[level, f] * eigen + high_ratio * high
        low_inverse = 1.0 / (couple_ref[level, e + 1] + low)
        high_inverse = 1.0 / (couple_ref[level, f] + high)
    out_ref[(OV - 1) * groups : OV * groups, :] = low_inverse
    out_ref[(2 * OV - 1) * groups :, :] = high_inverse


def level_response(rows, early, level, lon_ref, couple_ref, eigen, put_ratio, put_inverse, keep, tables):
    half = rows // 2
    ratio_at, value_at, put_value, put_phi, put_psi = tables

    def plain(e):
        return 1.0 + lon_ref[level, e] * eigen

    low = high = None
    low_inverse = high_inverse = low_value = high_value = None
    for i in range(-OV, half):
        j = rows - 1 - i
        e, f = i + OV, j + OV
        if low is None:
            low = plain(e) + couple_ref[level, e]
            high = plain(f) + couple_ref[level, f + 1]
        else:
            low_ratio = couple_ref[level, e] * low_inverse
            high_ratio = couple_ref[level, f + 1] * high_inverse
            low = plain(e) + low_ratio * low
            high = plain(f) + high_ratio * high
        low_divisor = couple_ref[level, e + 1] + low
        high_divisor = couple_ref[level, f] + high
        low_inverse = 1.0 / low_divisor
        high_inverse = 1.0 / high_divisor
        yield
        if i == -1:
            keep(0, low_inverse)
            keep(1, high_inverse)
        if i == 0:
            low_value = high_value = jnp.ones_like(eigen)
        elif i > 0:
            low_value = low_ratio * low_value
            high_value = high_ratio * high_value
        if i >= 0:
            put_ratio(i, low_ratio)
            put_ratio(j, high_ratio)
            put_inverse(i, low_inverse)
            put_inverse(j, high_inverse)
            put_value(i, low_value * low_inverse)
            if j < early:
                put_value(j, high_value * high_inverse)
    between = couple_ref[level, OV + half]
    inverse = 1.0 / (between * (low + high) + low * high)
    across = between * inverse
    high_inverse = high_divisor * inverse
    low_inverse = low_divisor * inverse
    keep(2, high_inverse)
    keep(3, low_inverse)
    keep(4, across)
    phi = high_inverse * low_value
    psi = across * high_value
    phi_down = across * low_value
    psi_down = low_inverse * high_value
    put_phi(half - 1, phi)
    put_psi(half - 1, psi)
    for i in range(half - 2, -1, -1):
        yield
        ratio = ratio_at(i + 1)
        phi = value_at(i) + ratio * phi
        psi = ratio * psi
        put_phi(i, phi)
        put_psi(i, psi)
    put_phi(half, phi_down)
    put_psi(half, psi_down)
    for j in range(half + 1, early):
        ratio = ratio_at(j - 1)
        phi_down = ratio * phi_down
        psi_down = value_at(j) + ratio * psi_down
        put_phi(j, phi_down)
        put_psi(j, psi_down)


def getter(ref, groups):
    return lambda index: ref[index * groups : (index + 1) * groups, :]


def putter(ref, groups, first=0):
    def put(index, value):
        at = first + index * groups
        ref[pl.ds(at if isinstance(at, int) else pl.multiple_of(at, groups), groups), :] = value

    return put


def together(*steps):
    steps = list(steps)
    while steps:
        steps = [step for step in steps if next(step, steps) is not steps]


def partner_response(rows, early, place_ref, lon_ref, couple_ref, eigen, masks, phi_ref, psi_ref, kept_refs, value_refs):
    groups = eigen.shape[0]

    def nothing(index, value):
        pass

    def one(n, mask):
        put_kept = putter(kept_refs[n], groups)

        def put_ratio(index, value):
            if index < early:
                put_kept(index, value)

        first = n * early * groups
        return level_response(
            rows, early, place_ref[0] ^ mask, lon_ref, couple_ref, eigen, put_ratio, nothing, nothing,
            (
                getter(kept_refs[n], groups), getter(value_refs[n], groups), putter(value_refs[n], groups),
                putter(phi_ref, groups, first), putter(psi_ref, groups, first),
            ),
        )

    return [one(n, mask) for n, mask in enumerate(masks)]


def own_kernel(
    rows, early, masks, place_ref, lon_ref, couple_ref, eigen_ref, ratio_ref, inverse_ref, edge_ref, phi_ref, psi_ref,
    phi_near_ref, psi_near_ref, value_ref, *refs,
):
    eigen = eigen_ref[...]
    groups = eigen.shape[0]
    own = level_response(
        rows, early, place_ref[0], lon_ref, couple_ref, eigen, putter(ratio_ref, groups),
        putter(inverse_ref, groups), putter(edge_ref, groups),
        (
            getter(ratio_ref, groups), getter(value_ref, groups), putter(value_ref, groups),
            putter(phi_ref, groups), putter(psi_ref, groups),
        ),
    )
    count = len(masks)
    together(
        own,
        *partner_response(
            rows, early, place_ref, lon_ref, couple_ref, eigen, masks, phi_near_ref, psi_near_ref,
            refs[:count], refs[count:],
        ),
    )


def partners_kernel(
    rows, early, masks, place_ref, lon_ref, couple_ref, eigen_ref, after_ref, phi_ref, psi_ref, *refs
):
    del after_ref
    count = len(masks)
    together(
        *partner_response(
            rows, early, place_ref, lon_ref, couple_ref, eigen_ref[...], masks, phi_ref, psi_ref,
            refs[:count], refs[count:],
        )
    )


def whole_levels(const, right_side, lon_coef, lat_coef, level_scale):
    rows, levels, lon_count = right_side.shape
    digits = N1 // levels
    groups = 2 * GROUPS
    lon_at = lax.axis_index("lon").astype(jnp.int32)
    parity = (lax.axis_index("lat") % 2).astype(jnp.int32)
    place = jnp.stack([lon_at, parity])
    half = rows // 2
    early = early_rows(rows)
    late = rows - early
    eigen = const["eigen"].reshape(groups, N2)
    lon_all, couple_all = operator_parts(rows, lon_coef, lat_coef, level_scale)
    (around,) = call(
        functools.partial(edge_kernel, rows),
        [(2 * OV * groups, N2)],
        [place, lon_all, couple_all, eigen],
        [SMEM, SMEM, SMEM, VMEM],
        [],
        16 * groups * N2 * 20,
        "edge",
    )
    block = (rows * groups, N2)
    early_block = (early * groups, N2)
    early_block = (early * groups, N2)
    near_masks, far_masks = [1], list(range(2, levels))
    ratio, inverse, edge, phi, psi, phi_near, psi_near = call(
        functools.partial(own_kernel, rows, early, near_masks),
        [block, block, (5 * groups, N2)] + [early_block] * 4,
        [place, lon_all, couple_all, eigen],
        [SMEM, SMEM, SMEM, VMEM],
        [vmem(*early_block)] * 3,
        2 * rows * groups * N2 * 20,
        "own",
    )
    row = (groups, N2)
    ends = 2 * OV
    inner = rows - ends
    span = OV * digits
    by_row = right_side.reshape(rows, levels, digits, N2).transpose(0, 2, 1, 3).reshape(-1, N2)

    far = list(range(2, levels))

    def pack_ends(place_ref, in_ref, *refs):
        for end_ref, mask in zip(refs, [0] + far):
            level = place_ref[0] ^ mask
            end_ref[:span, :] = in_ref[pl.ds(level, span, stride=levels), :]
            end_ref[span:, :] = in_ref[pl.ds(level + levels * (rows - OV) * digits, span, stride=levels), :]

    end_packed = call(
        pack_ends,
        [(ends * digits, N2)] * (levels - 1),
        [place, by_row],
        [SMEM, VMEM],
        [],
        0,
        "pack_ends",
    )

    def pack(place_ref, in_ref, after_ref, *refs):
        del after_ref
        for mask, out_ref in enumerate(refs):
            level = place_ref[0] ^ mask
            skip = 0 if mask == 1 else levels * span
            out_ref[...] = in_ref[pl.ds(level + skip, out_ref.shape[0], stride=levels), :]

    packed = call(
        pack,
        [((rows if mask == 1 else inner) * digits, N2) for mask in range(levels)],
        [place, by_row, end_packed[0]],
        [SMEM, VMEM, pl.ANY],
        [],
        0,
        "pack",
    )
    end_pieces = [end_packed[0], None] + [send_level(p, m, levels) for p, m in zip(end_packed[1:], far)]
    near = send_level(packed[1], 1, levels)
    end_pieces[1] = near
    inner_pieces = [packed[0], near] + [send_level(packed[m], m, levels) for m in far]
    forward = [const["first"], const["turn"], const["second"], const["special"]]
    pad_ends, pad_inner = pad_rows(ends), pad_rows(inner)

    def ends_body(place_ref, *refs):
        pieces, refs = refs[:levels], refs[levels:]
        tables_in, edge_ref = refs[:4], refs[4]
        spec_ref, top_ref, bottom_ref, even_ref, odd_ref, full_ref, mid_ref = refs[5:]
        for mask, piece in enumerate(pieces):
            at = pl.multiple_of((place_ref[0] ^ mask) * digits, digits)
            last = piece.shape[0] - span
            full_ref[:OV, pl.ds(at, digits), :] = piece[:span, :].reshape(OV, digits, N2)
            full_ref[OV:ends, pl.ds(at, digits), :] = piece[last:, :].reshape(OV, digits, N2)
        forward_rows(full_ref, ends, *tables_in, mid_ref, spec_ref)
        top, bottom = edge_sums(
            rows_of(spec_ref, groups), rows_of(spec_ref, groups, -OV),
            rows_of(edge_ref, groups), lambda i: edge_ref[(2 * OV - 2 - i) * groups : (2 * OV - 1 - i) * groups, :],
        )
        top_ref[...] = top
        bottom_ref[...] = bottom
        swap_out(place_ref[1], top, bottom, even_ref, odd_ref)

    end_spectral, sent_top, sent_bottom, even, odd = call(
        ends_body,
        [(ends * groups, N2)] + [row] * 4,
        [place, *end_pieces, *forward, around],
        [SMEM] + [VMEM] * (levels + 5),
        [vmem(pad_ends, N1, N2), vmem(pad_ends * N1, N2)],
        ends * NLON * 256 * 4,
        "ends",
    )
    even, odd = swap(even, odd)
    backward = [const["first_back"], const["turn"], const["second_back"], const["special_back"]]
    pad_early, pad_late = pad_rows(early), pad_rows(late)

    def spread(place_ref, full_ref, count, out_refs):
        for mask, out_ref in enumerate(out_refs):
            at = pl.multiple_of((place_ref[0] ^ mask) * digits, digits)
            out_ref[...] = full_ref[:count, pl.ds(at, digits), :].reshape(count * digits, N2)

    def inner_body(place_ref, *refs):
        pieces, refs = refs[:levels], refs[levels:]
        tables_in, refs = refs[:4], refs[4:]
        ends_ref, odd_ref, even_ref, ratio_ref, inverse_ref, edge_ref = refs[:6]
        early_ref, late_ref, top_ref, even_out, odd_out = refs[6:11]
        full_ref, mid_ref, spec_ref, sum_ref = refs[11:]
        for mask, piece in enumerate(pieces):
            at = pl.multiple_of((place_ref[0] ^ mask) * digits, digits)
            skip = span if mask == 1 else 0
            full_ref[:inner, pl.ds(at, digits), :] = piece[skip : skip + inner * digits, :].reshape(
                inner, digits, N2
            )
        if pad_inner > inner:
            full_ref[inner:] = jnp.zeros((pad_inner - inner, N1, N2), jnp.float32)
        forward_rows(full_ref, inner, *tables_in, mid_ref, spec_ref)
        low, high = swap_in(place_ref[1], even_ref[...], odd_ref[...])

        def spec_row(i):
            if i < OV:
                return rows_of(ends_ref, groups)(i)
            if i >= rows - OV:
                return rows_of(ends_ref, groups, rows - ends)(i)
            return rows_of(spec_ref, groups, OV)(i)

        solve_first(rows, groups, spec_row, low, high, ratio_ref, inverse_ref, edge_ref, sum_ref)
        top = sum_ref[:groups, :]
        top_ref[...] = top
        early_ref[...] = sum_ref[: early * groups, :]
        late_ref[...] = sum_ref[early * groups :, :]
        swap_out(place_ref[1], sum_ref[(rows - 1) * groups :, :], top, even_out, odd_out)

    early_first, late_first, own_top, even2, odd2 = call(
        inner_body,
        [early_block, (late * groups, N2), row, row, row],
        [place, *inner_pieces, *forward, end_spectral, odd, even, ratio, inverse, edge],
        [SMEM] + [VMEM] * (levels + 10),
        [vmem(pad_inner, N1, N2), vmem(pad_inner * N1, N2), vmem(inner * N1, N2), vmem(rows * groups, N2)],
        inner * NLON * 256 * 4,
        "inner",
    )

    def early_body(place_ref, *refs):
        first_ref, tables_in, out_refs = refs[0], refs[1:5], refs[5 : 5 + levels]
        mid_ref, full_ref = refs[5 + levels :]
        backward_rows(first_ref, early, *tables_in, mid_ref, full_ref)
        spread(place_ref, full_ref, early, out_refs)

    early_pieces = call(
        early_body,
        [(early * digits, N2)] * levels,
        [place, early_first, *backward],
        [SMEM] + [VMEM] * 5,
        [vmem(pad_early * N1, N2), vmem(pad_early, N1, N2)],
        early * NLON * 256 * 4,
        "early",
    )
    early_pieces = swap_levels(early_pieces)
    even2, odd2 = swap(even2, odd2)

    def sigma_body(place_ref, couple_ref, *refs):
        first_ref, own_top_ref, odd_ref, even_ref, odd2_ref, even2_ref, top_ref, bottom_ref = refs[:8]
        ratio_ref, edge_ref, around_ref = refs[8:11]
        sigma_ref = refs[-1]
        level = place_ref[0]
        got_top, got_bottom = swap_in(place_ref[1], even_ref[...], odd_ref[...])
        from_low, from_high = swap_in(place_ref[1], even2_ref[...], odd2_ref[...])
        low, high = sigmas(
            couple_ref[level, OV], couple_ref[level, OV + rows], own_top_ref[...], first_ref[(late - 1) * groups :, :],
            got_top, got_bottom, top_ref[...], bottom_ref[...], from_low, from_high,
            ratio_ref[:groups, :], ratio_ref[(rows - 1) * groups :, :], edge_ref,
            around_ref[(OV - 1) * groups : OV * groups, :], around_ref[(2 * OV - 1) * groups :, :],
        )
        sigma_ref[:groups, :] = low
        sigma_ref[groups:, :] = high

    (sigma,) = call(
        sigma_body,
        [(2 * groups, N2)],
        [
            place, couple_all, late_first, own_top, odd, even, odd2, even2, sent_top, sent_bottom, ratio, edge, around,
        ],
        [SMEM, SMEM] + [VMEM] * 11,
        [],
        groups * N2 * 40,
        "sigma",
    )
    far_sigma = [send_level(sigma, mask, levels) for mask in far]
    def second_body(place_ref, *refs):
        sigma_ref, first_ref, ratio_ref, inverse_ref, edge_ref = refs[:5]
        tables_in, refs = refs[5:9], refs[10:]
        late_refs = list(refs[:levels])
        sum_ref, mid_ref, full_ref = refs[levels:]
        low, high = sigma_ref[:groups, :], sigma_ref[groups:, :]

        def at(ref, index):
            return ref[index * groups : (index + 1) * groups, :]

        for i in range(half):
            j = rows - 1 - i
            if i:
                low = at(ratio_ref, i) * low
                high = at(ratio_ref, j) * high
            mid_ref[(j - half) * groups : (j - half + 1) * groups, :] = high
        x_high = at(edge_ref, 3) * high + at(edge_ref, 4) * low
        for j in range(half, rows):
            if j > half:
                x_high = at(mid_ref, j - half) * at(inverse_ref, j) + at(ratio_ref, j - 1) * x_high
            if j >= early:
                here = slice((j - early) * groups, (j - early + 1) * groups)
                sum_ref[here, :] = first_ref[here, :] + x_high
        backward_rows(sum_ref, late, *tables_in, mid_ref, full_ref)
        late_refs[1][late * digits :, :] = sigma_ref[...]
        late_refs[1] = late_refs[1].at[pl.ds(0, late * digits), :]
        spread(place_ref, full_ref, late, late_refs)

    late_pieces = call(
        second_body,
        [(late * digits + (2 * groups if mask == 1 else 0), N2) for mask in range(levels)],
        [place, sigma, late_first, ratio, inverse, edge, *backward, early_pieces[1]],
        [SMEM] + [VMEM] * 9 + [pl.ANY],
        [vmem(late * groups, N2), vmem(max(pad_late, half) * N1, N2), vmem(pad_late, N1, N2)],
        late * NLON * 256 * 4,
        "second",
    )
    phi_far, psi_far = call(
        functools.partial(partners_kernel, rows, early, far_masks),
        [(len(far_masks) * early * groups, N2)] * 2,
        [place, lon_all, couple_all, eigen, late_pieces[0]],
        [SMEM, SMEM, SMEM, VMEM, pl.ANY],
        [vmem(*early_block)] * (2 * len(far_masks)),
        len(far_masks) * rows * groups * N2 * 20,
        "partners",
    )
    late_pieces = swap_levels(late_pieces)
    sigma_pieces = [sigma, late_pieces[1], *far_sigma]
    total = rows * levels * digits
    early_total = early * levels * digits
    part = const["first_back_part"]

    def correct(place_ref, *refs):
        pieces, sigma_refs, refs = refs[:levels], refs[levels : 2 * levels], refs[2 * levels :]
        responses, refs = refs[:6], refs[6:]
        part_ref, turn_ref, second_ref, special_ref = refs[:4]
        out_ref, sum_ref, mid_ref, done_ref, sem = refs[4:]
        part_rows = part_ref.shape[0] // levels
        mine = part_ref.at[pl.ds(pl.multiple_of(place_ref[0] * part_rows, part_rows), part_rows), :]
        size = early * groups
        for mask in range(levels):
            level = place_ref[0] ^ mask
            last = sigma_refs[mask].shape[0]
            low = sigma_refs[mask][last - 2 * groups : last - groups, :]
            high = sigma_refs[mask][last - groups :, :]
            phi_ref, psi_ref = responses[2 * min(mask, 2) : 2 * min(mask, 2) + 2]
            first = max(mask - 2, 0) * size
            phi_all = phi_ref[first : first + size, :].reshape(early, groups, N2)
            psi_all = psi_ref[first : first + size, :].reshape(early, groups, N2)
            sum_ref[...] = (phi_all * low[None] + psi_all * high[None]).reshape(size, N2)
            spectral_back(sum_ref, early, pad_early, second_ref, special_ref, mid_ref)
            for pair in range(pad_early // (2 * BLOCK)):
                value = digits_back(mid_ref, pair, turn_ref, mine)
                for side in range(2):
                    begin = (2 * pair + side) * BLOCK
                    count = min(BLOCK, early - begin)
                    if count <= 0:
                        continue
                    lines = count * digits
                    whole = pieces[mask][begin * digits : begin * digits + lines, :]
                    done_ref[pl.ds(level + begin * digits * levels, lines, stride=levels), :] = (
                        whole + value[:lines, side * N2 : (side + 1) * N2]
                    )
        copy = pltpu.make_async_copy(done_ref, out_ref.at[pl.ds(0, early_total), :], sem)
        copy.start()
        copy.wait()

    (out,) = call(
        correct,
        [(total, N2)],
        [
            place, *early_pieces, *sigma_pieces, phi, psi, phi_near, psi_near, phi_far, psi_far,
            part, const["turn"], *backward[2:],
        ],
        [SMEM] + [VMEM] * (2 * levels + 10),
        [
            vmem(early * groups, N2), vmem(pad_early * N1, N2), vmem(early_total, N2), pltpu.SemaphoreType.DMA,
        ],
        levels * early * NLON * 256 * 3,
        "correct",
        weight=1,
        out_spaces=[pl.ANY],
    )

    chunks = 4

    def unpack(place_ref, *refs):
        pieces = refs[:levels]
        out_ref, done_ref, sems = refs[levels + 1 :]
        lines = late * digits // chunks
        copies = []
        for chunk in range(chunks):
            for mask in range(levels):
                first = (place_ref[0] ^ mask) + chunk * lines * levels
                skip = chunk * lines
                done_ref[pl.ds(first, lines, stride=levels), :] = pieces[mask][skip : skip + lines, :]
            here = pl.ds(chunk * lines * levels, lines * levels)
            there = pl.ds(early_total + chunk * lines * levels, lines * levels)
            copy = pltpu.make_async_copy(done_ref.at[here, :], out_ref.at[there, :], sems.at[chunk])
            copy.start()
            copies.append(copy)
        for copy in copies:
            copy.wait()

    (out,) = call(
        unpack,
        [(total, N2)],
        [place, *late_pieces, out],
        [SMEM] + [VMEM] * levels + [pl.ANY],
        [vmem(total - early_total, N2), pltpu.SemaphoreType.DMA((chunks,))],
        0,
        "unpack",
        out_spaces=[pl.ANY],
        aliases={levels + 1: 0},
    )
    return out.reshape(rows, digits, levels, N2).transpose(0, 2, 1, 3).reshape(right_side.shape)


def second_part(
    rows, groups, parity, couple_ref, first_ref, even_ref, odd_ref, even2_ref, odd2_ref, top_ref, bottom_ref,
    ratio_ref, inverse_ref, edge_ref, out_ref, mid_ref,
):
    got_top, got_bottom = swap_in(parity, even_ref[...], odd_ref[...])
    low, high = swap_in(parity, even2_ref[...], odd2_ref[...])
    solve_second(
        rows, groups, couple_ref[OV], couple_ref[OV + rows],
        first_ref[:groups, :], first_ref[(rows - 1) * groups :, :],
        got_top, got_bottom, top_ref[...], bottom_ref[...], low, high,
        ratio_ref, inverse_ref, edge_ref, first_ref, out_ref, mid_ref,
    )


def shared_levels(const, right_side, lon_coef, lat_coef, level_scale):
    rows, levels, lon_count = right_side.shape
    lon_size = lax.axis_size("lon")
    assert lon_size % levels == 0 and GROUPS % (lon_size // levels) == 0 and rows % (lon_size // levels) == 0
    sharers = lon_size // levels
    groups = 2 * GROUPS // sharers
    part_rows = rows // sharers
    digits = N1 // lon_size
    lon_at = lax.axis_index("lon")
    parity = (lax.axis_index("lat") % 2).astype(jnp.int32).reshape(1)
    lon_window, couple = operator_parts(rows, lon_coef, lat_coef, level_scale)
    lon_window = lax.dynamic_index_in_dim(lon_window, lon_at // sharers, 0, False)
    couple = lax.dynamic_index_in_dim(couple, lon_at // sharers, 0, False)
    eigen = lax.dynamic_slice_in_dim(
        const["eigen"], (lon_at % sharers) * (groups // 2), groups // 2, axis=1
    ).reshape(groups, N2)
    ratio, inverse, edge = factor(rows, groups, lon_window, couple, eigen)
    block = (rows * groups, N2)
    row = (groups, N2)
    send = right_side.reshape(sharers, part_rows, levels, lon_count).transpose(2, 0, 1, 3)
    send = send.reshape(lon_size, part_rows, digits, N2)
    got = lax.all_to_all(send, "lon", 0, 0, tiled=True)
    points = got.transpose(1, 0, 2, 3).reshape(part_rows, N1, N2)
    padded = pad_rows(part_rows)

    def transform(points_ref, first_ref, turn_ref, second_ref, special_ref, out_ref, full_ref, mid_ref):
        full_ref[:part_rows] = points_ref[...]
        if padded > part_rows:
            full_ref[part_rows:] = jnp.zeros((padded - part_rows, N1, N2), jnp.float32)
        forward_rows(full_ref, part_rows, first_ref, turn_ref, second_ref, special_ref, mid_ref, out_ref)

    (spectral,) = call(
        transform,
        [(part_rows * N1, N2)],
        [points, const["first"], const["turn"], const["second"], const["special"]],
        [VMEM] * 5,
        [vmem(padded, N1, N2), vmem(padded * N1, N2)],
        part_rows * NLON * 256 * 4,
        "transform",
    )
    spectral = to_coefs(spectral, sharers, part_rows, groups)

    def edges(parity_ref, spec_ref, edge_ref, top_ref, bottom_ref, even_ref, odd_ref):
        top, bottom = edge_sums(
            rows_of(spec_ref, groups), rows_of(spec_ref, groups, OV - rows),
            rows_of(edge_ref, groups, -7), rows_of(edge_ref, groups, -14),
        )
        top_ref[...] = top
        bottom_ref[...] = bottom
        swap_out(parity_ref[0], top, bottom, even_ref, odd_ref)

    sent_top, sent_bottom, even, odd = call(
        edges, [row] * 4, [parity, spectral, edge], [SMEM, VMEM, VMEM], [], groups * N2 * 32, "edges"
    )
    even, odd = swap(even, odd)

    def first(parity_ref, spec_ref, even_ref, odd_ref, ratio_ref, inverse_ref, edge_ref, out_ref, e_ref, o_ref):
        low, high = swap_in(parity_ref[0], even_ref[...], odd_ref[...])
        solve_first(
            rows, groups, rows_of(spec_ref, groups), low, high, ratio_ref, inverse_ref, edge_ref, out_ref
        )
        swap_out(parity_ref[0], out_ref[(rows - 1) * groups :, :], out_ref[:groups, :], e_ref, o_ref)

    iterate, even2, odd2 = call(
        first,
        [block, row, row],
        [parity, spectral, even, odd, ratio, inverse, edge],
        [SMEM] + [VMEM] * 6,
        [],
        rows * groups * N2 * 8,
        "first_solve",
    )
    even2, odd2 = swap(even2, odd2)

    def second(parity_ref, *refs):
        second_part(rows, groups, parity_ref[0], *refs)

    (iterate,) = call(
        second,
        [block],
        [parity, couple, iterate, even, odd, even2, odd2, sent_top, sent_bottom, ratio, inverse, edge],
        [SMEM, SMEM] + [VMEM] * 10,
        [vmem(*block)],
        rows * groups * N2 * 8,
        "second_solve",
    )
    iterate = to_rows(iterate, sharers, part_rows, groups)

    def back(spec_ref, first_ref, turn_ref, second_ref, special_ref, out_ref, mid_ref, full_ref):
        backward_rows(spec_ref, part_rows, first_ref, turn_ref, second_ref, special_ref, mid_ref, full_ref)
        out_ref[...] = full_ref[:part_rows]

    (points,) = call(
        back,
        [(part_rows, N1, N2)],
        [iterate, const["first_back"], const["turn"], const["second_back"], const["special_back"]],
        [VMEM] * 5,
        [vmem(padded * N1, N2), vmem(padded, N1, N2)],
        part_rows * NLON * 256 * 4,
        "back_transform",
    )
    send = points.reshape(part_rows, lon_size, digits, N2).transpose(1, 0, 2, 3)
    got = lax.all_to_all(send, "lon", 0, 0, tiled=True)
    got = got.reshape(levels, sharers, part_rows, lon_count).transpose(1, 2, 0, 3)
    return got.reshape(rows, levels, lon_count)


def level_groups(sharers):
    size = lax.axis_size("lon")
    return [[first + i for i in range(sharers)] for first in range(0, size, sharers)]


def to_coefs(spectral, sharers, part_rows, groups):
    send = spectral.reshape(part_rows, 2, sharers, groups // 2, N2).transpose(2, 0, 1, 3, 4)
    got = lax.all_to_all(
        send, "lon", 0, 0, tiled=True, axis_index_groups=level_groups(sharers)
    )
    return got.reshape(sharers * part_rows * groups, N2)


def to_rows(values, sharers, part_rows, groups):
    send = values.reshape(sharers, part_rows, 2, groups // 2, N2)
    got = lax.all_to_all(
        send, "lon", 0, 0, tiled=True, axis_index_groups=level_groups(sharers)
    )
    return got.transpose(1, 2, 0, 3, 4).reshape(part_rows * N1, N2)


def solution(mesh):
    return jax.shard_map(
        on_device,
        mesh=mesh,
        in_specs=(P("lat", None, "lon"), P(), P(), P()),
        out_specs=P("lat", None, "lon"),
        check_vma=False,
    )
```

```python
import functools
import math

import jax
import jax.numpy as jnp
import numpy as np
from jax import lax
from jax.experimental import pallas as pl
from jax.experimental.pallas import tpu as pltpu
from jax.sharding import PartitionSpec as P

NLON = 4096
OV = 8
N1 = 32
N2 = 128
GROUPS = 16
BLOCK = 8

VMEM = pltpu.VMEM
SMEM = pltpu.SMEM


def numpy_split(table):
    import ml_dtypes

    table = np.asarray(table, np.float32)
    high = table.astype(ml_dtypes.bfloat16)
    low = (table - high.astype(np.float32)).astype(ml_dtypes.bfloat16)
    return high, low


def tables(levels):
    j1 = np.arange(N1)
    j2 = np.arange(N2)
    k2 = np.arange(N2)
    digit = np.arange(GROUPS)
    small = np.zeros((N1, N1))
    small[:GROUPS] = np.cos(2 * np.pi * np.outer(digit, j1) / N1)
    small[GROUPS] = np.cos(np.pi * j1)
    small[GROUPS + 1 :] = -np.sin(2 * np.pi * np.outer(digit[1:], j1) / N1)
    first = np.kron(np.eye(BLOCK), small)
    angle = 2 * np.pi * np.outer(digit, j2) / NLON
    turn_cos = np.cos(angle)
    turn_sin = np.sin(angle)
    phase = 2 * np.pi * (np.outer(j2, k2) % N2) / N2
    cosine, sine = np.cos(phase), np.sin(phase)
    second = np.block([[cosine, -sine], [sine, cosine]])
    special = np.zeros((2 * N2, 2 * N2))
    half = N2 // 2
    special[:N2, : half + 1] = np.cos(2 * np.pi * np.outer(j2, np.arange(half + 1)) / N2)
    special[:N2, half + 1 : N2] = -np.sin(2 * np.pi * np.outer(j2, np.arange(1, half)) / N2)
    odd = 2 * np.pi * np.outer(j2, 1 + 2 * np.arange(half)) / (2 * N2)
    special[N2:, N2 : N2 + half] = np.cos(odd)
    special[N2:, N2 + half :] = -np.sin(odd)
    weight = np.full(2 * N2, 2.0 / NLON)
    weight[0] = 1.0 / NLON
    weight[half] = 1.0 / NLON
    second_back = second.T * (2.0 / NLON)
    special_back = weight[:, None] * special.T
    wave = np.zeros((GROUPS, 2 * N2))
    wave[:, :N2] = digit[:, None] + N1 * k2[None, :]
    wave[:, N2:] = wave[:, :N2]
    lane = np.arange(N2)
    wave[0, :N2] = np.where(lane <= half, N1 * lane, N1 * (lane - half))
    wave[0, N2:] = 16 + N1 * (lane % half)
    eigen = 2.0 - 2.0 * np.cos(2 * np.pi * wave / NLON)
    pair = lambda t: np.concatenate(numpy_split(t), axis=0)
    width = N1 // levels
    part = [pair(np.kron(np.eye(BLOCK), small.T[at : at + width])) for at in range(0, N1, width)]
    return dict(
        first_back_part=np.concatenate(part, axis=0),
        first=pair(first),
        first_back=pair(first.T),
        second=pair(second),
        second_back=pair(second_back),
        special=pair(special),
        special_back=pair(special_back),
        turn=np.concatenate([turn_cos, turn_sin], axis=0).astype(np.float32),
        eigen=np.stack([eigen[:, :N2], eigen[:, N2:]]).astype(np.float32),
    )


def halves(value):
    high = value.astype(jnp.bfloat16)
    low = (value - high.astype(jnp.float32)).astype(jnp.bfloat16)
    return high, low


def dot(a, b):
    return lax.dot_general(a, b, (((1,), (0,)), ((), ())), preferred_element_type=jnp.float32)


def product_right(value, table_ref):
    size = table_ref.shape[0] // 2
    high, low = halves(value)
    table_high = table_ref[:size, :]
    return dot(high, table_high) + dot(low, table_high) + dot(high, table_ref[size:, :])


def product_left(table_ref, value):
    size = table_ref.shape[0] // 2
    high, low = halves(value)
    both = dot(table_ref[...], high)
    return both[:size] + both[size:] + dot(table_ref[:size, :], low)


def lanes_apart(value, rows):
    real = value[:, :N2].reshape(rows, GROUPS, N2)
    imag = value[:, N2:].reshape(rows, GROUPS, N2)
    return jnp.concatenate([real, imag], axis=1).reshape(rows * 2 * GROUPS, N2)


def lanes_together(value, rows):
    both = value.reshape(rows, 2 * GROUPS, N2)
    return jnp.concatenate([both[:, :GROUPS], both[:, GROUPS:]], axis=2).reshape(rows * GROUPS, 2 * N2)


def load_zeroth(ref, rows):
    return jnp.concatenate(
        [ref[pl.ds(0, rows, stride=2 * GROUPS), :], ref[pl.ds(GROUPS, rows, stride=2 * GROUPS), :]], axis=1
    )


def store_zeroth(ref, rows, value):
    ref[pl.ds(0, rows, stride=2 * GROUPS), :] = value[:, :N2]
    ref[pl.ds(GROUPS, rows, stride=2 * GROUPS), :] = value[:, N2:]


def forward_rows(points_ref, rows, first_ref, turn_ref, second_ref, special_ref, mid_ref, out_ref):
    padded = points_ref.shape[0]
    turn_cos = turn_ref[:GROUPS, :][None]
    turn_sin = turn_ref[GROUPS:, :][None]
    for pair in range(padded // (2 * BLOCK)):
        base = pair * 2 * BLOCK
        left = points_ref[base : base + BLOCK].reshape(BLOCK * N1, N2)
        right = points_ref[base + BLOCK : base + 2 * BLOCK].reshape(BLOCK * N1, N2)
        value = product_left(first_ref, jnp.concatenate([left, right], axis=1))
        for side in range(2):
            digits = value[:, side * N2 : (side + 1) * N2].reshape(BLOCK, N1, N2)
            real, imag = digits[:, :GROUPS], digits[:, GROUPS:]
            turned = jnp.concatenate(
                [real * turn_cos + imag * turn_sin, imag * turn_cos - real * turn_sin], axis=1
            )
            at = (base + side * BLOCK) * N1
            mid_ref[at : at + BLOCK * N1, :] = turned.reshape(BLOCK * N1, N2)
    result = product_right(lanes_together(mid_ref[...], padded), second_ref)
    out_ref[...] = lanes_apart(result, padded)[: rows * N1]
    store_zeroth(out_ref, rows, product_right(load_zeroth(mid_ref, padded), special_ref)[:rows])


def spectral_back(spec_ref, rows, padded, second_ref, special_ref, mid_ref):
    result = product_right(lanes_together(spec_ref[...], rows), second_ref)
    mid_ref[: rows * N1, :] = lanes_apart(result, rows)
    if padded > rows:
        mid_ref[rows * N1 : padded * N1, :] = jnp.zeros(((padded - rows) * N1, N2), jnp.float32)
    store_zeroth(mid_ref, rows, product_right(load_zeroth(spec_ref, rows), special_ref))


def digits_back(mid_ref, pair, turn_ref, first_ref):
    turn_cos = turn_ref[:GROUPS, :][None]
    turn_sin = turn_ref[GROUPS:, :][None]
    sides = []
    for side in range(2):
        at = (2 * pair + side) * BLOCK * N1
        both = mid_ref[at : at + BLOCK * N1, :].reshape(BLOCK, N1, N2)
        real, imag = both[:, :GROUPS], both[:, GROUPS:]
        turned = jnp.concatenate(
            [real * turn_cos - imag * turn_sin, imag * turn_cos + real * turn_sin], axis=1
        )
        sides.append(turned.reshape(BLOCK * N1, N2))
    return product_left(first_ref, jnp.concatenate(sides, axis=1))


def backward_rows(spec_ref, rows, first_ref, turn_ref, second_ref, special_ref, mid_ref, out_ref):
    padded = out_ref.shape[0]
    spectral_back(spec_ref, rows, padded, second_ref, special_ref, mid_ref)
    for pair in range(padded // (2 * BLOCK)):
        base = pair * 2 * BLOCK
        value = digits_back(mid_ref, pair, turn_ref, first_ref)
        out_ref[base : base + BLOCK] = value[:, :N2].reshape(BLOCK, N1, N2)
        out_ref[base + BLOCK : base + 2 * BLOCK] = value[:, N2:].reshape(BLOCK, N1, N2)


def factor_kernel(rows, lon_ref, couple_ref, eigen_ref, ratio_ref, inverse_ref, edge_ref):
    eigen = eigen_ref[...]
    groups = eigen.shape[0]
    half = rows // 2
    last = rows + 2 * OV - 1

    def plain(e):
        return 1.0 + lon_ref[e] * eigen

    def put(ref, index, value):
        ref[index * groups : (index + 1) * groups, :] = value

    def chain(start, stop, step, into):
        excess = inverse = None
        for e in range(start, stop + step, step):
            before = couple_ref[e] if step > 0 else couple_ref[e + 1]
            after = couple_ref[e + 1] if step > 0 else couple_ref[e]
            if inverse is None:
                ratio = None
                excess = plain(e) + before
            else:
                ratio = before * inverse
                excess = plain(e) + ratio * excess
            divisor = after + excess
            inverse = 1.0 / divisor
            into(e, ratio, inverse, excess, divisor)

    kept = {}

    def top(e, ratio, inverse, excess, divisor):
        if e == OV - 1:
            put(edge_ref, 0, inverse)
        if e >= OV:
            put(ratio_ref, e - OV, ratio)
            put(inverse_ref, e - OV, inverse)
        if e == OV + half - 1:
            kept["top"] = excess, divisor

    def bottom(e, ratio, inverse, excess, divisor):
        if e == OV + rows:
            put(edge_ref, 1, inverse)
        if e < OV + rows:
            put(ratio_ref, e - OV, ratio)
            put(inverse_ref, e - OV, inverse)
        if e == OV + half:
            kept["bottom"] = excess, divisor

    def next_band(e, ratio, inverse, excess, divisor):
        if ratio is not None:
            put(edge_ref, 7 + e - rows - 1, ratio)
        if e == OV + rows - 1:
            put(edge_ref, 5, inverse)

    def previous_band(e, ratio, inverse, excess, divisor):
        if ratio is not None:
            put(edge_ref, 14 + e - OV, ratio)
        if e == OV:
            put(edge_ref, 6, inverse)

    chain(rows, OV + rows - 1, 1, next_band)
    chain(2 * OV - 1, OV, -1, previous_band)
    chain(0, OV + half - 1, 1, top)
    chain(last, OV + half, -1, bottom)
    excess_top, divisor_top = kept["top"]
    excess_bottom, divisor_bottom = kept["bottom"]
    between = couple_ref[OV + half]
    inverse = 1.0 / (between * (excess_top + excess_bottom) + excess_top * excess_bottom)
    put(edge_ref, 2, divisor_bottom * inverse)
    put(edge_ref, 3, divisor_top * inverse)
    put(edge_ref, 4, between * inverse)


def edge_sums(low_rows, high_rows, next_ratio, previous_ratio):
    top = high_rows(0)
    for i in range(1, OV):
        top = high_rows(i) + next_ratio(i - 1) * top
    bottom = low_rows(OV - 1)
    for i in range(OV - 2, -1, -1):
        bottom = low_rows(i) + previous_ratio(i) * bottom
    return top, bottom


def swap_out(parity, up, down, even_ref, odd_ref):
    is_even = parity == 0
    even_ref[...] = jnp.where(is_even, up, down)
    odd_ref[...] = jnp.where(is_even, down, up)


def swap_in(parity, even, odd):
    is_even = parity == 0
    return jnp.where(is_even, odd, even), jnp.where(is_even, even, odd)


def solve_first(rows, groups, right_side_row, from_low, from_high, ratio_ref, inverse_ref, edge_ref, out_ref):
    half = rows // 2

    def at(ref, index):
        return ref[index * groups : (index + 1) * groups, :]

    def put(index, value):
        out_ref[index * groups : (index + 1) * groups, :] = value

    low, high = from_low, from_high
    for i in range(half):
        j = rows - 1 - i
        low = right_side_row(i) + at(ratio_ref, i) * low
        high = right_side_row(j) + at(ratio_ref, j) * high
        put(i, low)
        put(j, high)
    meet(rows, groups, low, high, ratio_ref, inverse_ref, edge_ref, at, lambda i: at(out_ref, i), put)


def meet(rows, groups, low, high, ratio_ref, inverse_ref, edge_ref, at, value, put):
    half = rows // 2
    between = at(edge_ref, 4)
    x_low = at(edge_ref, 2) * low + between * high
    x_high = at(edge_ref, 3) * high + between * low
    put(half - 1, x_low)
    put(half, x_high)
    for i in range(half - 2, -1, -1):
        j = rows - 1 - i
        x_low = value(i) * at(inverse_ref, i) + at(ratio_ref, i + 1) * x_low
        x_high = value(j) * at(inverse_ref, j) + at(ratio_ref, j - 1) * x_high
        put(i, x_low)
        put(j, x_high)


def sigmas(
    couple_low, couple_high, own_top, own_bottom, got_top, got_bottom, sent_top, sent_bottom, from_low, from_high,
    ratio_first, ratio_last, edge_ref, next_inverse, previous_inverse,
):
    groups = own_top.shape[0]

    def edge(index):
        return edge_ref[index * groups : (index + 1) * groups, :]

    beyond_low = (got_top + couple_low * own_top) * edge(0)
    beyond_high = (got_bottom + couple_high * own_bottom) * edge(1)
    theirs_low = (sent_bottom + couple_low * from_low) * previous_inverse
    theirs_high = (sent_top + couple_high * from_high) * next_inverse
    low = ratio_first * (couple_low * (own_top - theirs_low)) + couple_low * (from_low - beyond_low)
    high = ratio_last * (couple_high * (own_bottom - theirs_high)) + couple_high * (from_high - beyond_high)
    return low, high


def solve_second(
    rows, groups, couple_low, couple_high, own_top, own_bottom, got_top, got_bottom, sent_top, sent_bottom,
    from_low, from_high, ratio_ref, inverse_ref, edge_ref, first_ref, out_ref, mid_ref,
):
    half = rows // 2

    def at(ref, index):
        return ref[index * groups : (index + 1) * groups, :]

    low, high = sigmas(
        couple_low, couple_high, own_top, own_bottom, got_top, got_bottom, sent_top, sent_bottom,
        from_low, from_high, at(ratio_ref, 0), at(ratio_ref, rows - 1), edge_ref, at(edge_ref, 5), at(edge_ref, 6),
    )
    for i in range(half):
        j = rows - 1 - i
        if i:
            low = at(ratio_ref, i) * low
            high = at(ratio_ref, j) * high
        mid_ref[i * groups : (i + 1) * groups, :] = low
        mid_ref[j * groups : (j + 1) * groups, :] = high

    def put(index, value):
        rows_at = slice(index * groups, (index + 1) * groups)
        out_ref[rows_at, :] = first_ref[rows_at, :] + value

    meet(rows, groups, low, high, ratio_ref, inverse_ref, edge_ref, at, lambda i: at(mid_ref, i), put)


def call(body, outs, ins, spaces, scratch, flops, name, out_spaces=None, aliases=None):
    nbytes = sum(x.size * x.dtype.itemsize for x in ins) + sum(4 * math.prod(s) for s in outs)
    out = pl.pallas_call(
        body,
        out_shape=[jax.ShapeDtypeStruct(s, jnp.float32) for s in outs],
        in_specs=[pl.BlockSpec(memory_space=s) for s in spaces],
        out_specs=[pl.BlockSpec(memory_space=s) for s in out_spaces or [VMEM] * len(outs)],
        input_output_aliases=aliases or {},
        scratch_shapes=scratch,
        compiler_params=pltpu.CompilerParams(vmem_limit_bytes=48 << 20),
        cost_estimate=pl.CostEstimate(flops=flops, bytes_accessed=nbytes, transcendentals=0),
        name=name,
    )(*ins)
    return out


def pad_rows(rows):
    return -(-rows // (2 * BLOCK)) * 2 * BLOCK


def swap(value_even, value_odd):
    count = lax.axis_size("lat")
    even = [(i, i ^ 1) for i in range(count) if (i ^ 1) < count]
    odd = [(i, ((i + 1) ^ 1) - 1) for i in range(1, count) if ((i + 1) ^ 1) - 1 < count]
    value_odd = lax.ppermute(value_odd, "lat", odd)
    return lax.ppermute(value_even, "lat", even), value_odd


def send_level(piece, mask, size):
    return lax.ppermute(piece, "lon", [(d, d ^ mask) for d in range(size)])


def swap_levels(pieces):
    return [pieces[0]] + [send_level(pieces[mask], mask, len(pieces)) for mask in range(1, len(pieces))]


def operator_parts(rows, lon_coef, lat_coef, level_scale):
    row_first = lax.axis_index("lat") * rows
    extent = rows + 2 * OV
    lon_window = lax.dynamic_slice_in_dim(jnp.pad(lon_coef, (OV, OV)), row_first, extent)
    couple = lax.dynamic_slice_in_dim(jnp.pad(lat_coef, (OV + 1, OV + 2)), row_first, extent + 1)
    return level_scale[:, None] * lon_window[None], level_scale[:, None] * couple[None]


def factor(rows, groups, lon_window, couple, eigen):
    block = (rows * groups, N2)
    return call(
        functools.partial(factor_kernel, rows),
        [block, block, (21 * groups, N2)],
        [lon_window, couple, eigen],
        [SMEM, SMEM, VMEM],
        [],
        rows * groups * N2 * 20,
        "factor",
    )


def vmem(*shape):
    return pltpu.VMEM(shape, jnp.float32)


def rows_of(ref, groups, first=0):
    return lambda i: ref[(i - first) * groups : (i - first + 1) * groups, :]


def on_device(right_side, lon_coef, lat_coef, level_scale):
    const = {k: jnp.asarray(v) for k, v in tables(right_side.shape[1]).items()}
    if lax.axis_size("lon") != right_side.shape[1]:
        return shared_levels(const, right_side, lon_coef, lat_coef, level_scale)
    return whole_levels(const, right_side, lon_coef, lat_coef, level_scale)


def early_rows(rows):
    return rows // 2 + 4


def lon_here():
    return lax.axis_index("lon").astype(jnp.int32)


def parity_here():
    return lax.axis_index("lat").astype(jnp.int32) % 2


def edge_kernel(rows, lon_ref, couple_ref, eigen_ref, out_ref):
    eigen = eigen_ref[...]
    groups = eigen.shape[0]
    level = lon_here()
    low = high = low_inverse = high_inverse = None
    for i in range(OV):
        e, f = rows + i, 2 * OV - 1 - i
        if i == 0:
            low = 1.0 + lon_ref[level, e] * eigen + couple_ref[level, e]
            high = 1.0 + lon_ref[level, f] * eigen + couple_ref[level, f + 1]
        else:
            low_ratio = couple_ref[level, e] * low_inverse
            high_ratio = couple_ref[level, f + 1] * high_inverse
            out_ref[(i - 1) * groups : i * groups, :] = low_ratio
            out_ref[(OV + i - 1) * groups : (OV + i) * groups, :] = high_ratio
            low = 1.0 + lon_ref[level, e] * eigen + low_ratio * low
            high = 1.0 + lon_ref[level, f] * eigen + high_ratio * high
        low_inverse = 1.0 / (couple_ref[level, e + 1] + low)
        high_inverse = 1.0 / (couple_ref[level, f] + high)
    out_ref[(OV - 1) * groups : OV * groups, :] = low_inverse
    out_ref[(2 * OV - 1) * groups : 2 * OV * groups, :] = high_inverse
    out_ref[2 * OV * groups : (2 * OV + 1) * groups, :] = jnp.full_like(eigen, couple_ref[level, OV])
    out_ref[(2 * OV + 1) * groups :, :] = jnp.full_like(eigen, couple_ref[level, OV + rows])


def level_response(rows, early, level, lon_ref, couple_ref, eigen, put_ratio, put_inverse, keep, tables):
    half = rows // 2
    ratio_at, value_at, put_value, put_phi, put_psi = tables

    def plain(e):
        return 1.0 + lon_ref[level, e] * eigen

    low = high = None
    low_inverse = high_inverse = low_value = high_value = None
    for i in range(-OV, half):
        j = rows - 1 - i
        e, f = i + OV, j + OV
        if low is None:
            low = plain(e) + couple_ref[level, e]
            high = plain(f) + couple_ref[level, f + 1]
        else:
            low_ratio = couple_ref[level, e] * low_inverse
            high_ratio = couple_ref[level, f + 1] * high_inverse
            low = plain(e) + low_ratio * low
            high = plain(f) + high_ratio * high
        low_divisor = couple_ref[level, e + 1] + low
        high_divisor = couple_ref[level, f] + high
        low_inverse = 1.0 / low_divisor
        high_inverse = 1.0 / high_divisor
        yield
        if i == -1:
            keep(0, low_inverse)
            keep(1, high_inverse)
        if i == 0:
            low_value = high_value = jnp.ones_like(eigen)
        elif i > 0:
            low_value = low_ratio * low_value
            high_value = high_ratio * high_value
        if i >= 0:
            put_ratio(i, low_ratio)
            put_ratio(j, high_ratio)
            put_inverse(i, low_inverse)
            put_inverse(j, high_inverse)
            put_value(i, low_value * low_inverse)
            if j < early:
                put_value(j, high_value * high_inverse)
    between = couple_ref[level, OV + half]
    inverse = 1.0 / (between * (low + high) + low * high)
    across = between * inverse
    high_inverse = high_divisor * inverse
    low_inverse = low_divisor * inverse
    keep(2, high_inverse)
    keep(3, low_inverse)
    keep(4, across)
    phi = high_inverse * low_value
    psi = across * high_value
    phi_down = across * low_value
    psi_down = low_inverse * high_value
    put_phi(half - 1, phi)
    put_psi(half - 1, psi)
    for i in range(half - 2, -1, -1):
        yield
        ratio = ratio_at(i + 1)
        phi = value_at(i) + ratio * phi
        psi = ratio * psi
        put_phi(i, phi)
        put_psi(i, psi)
    put_phi(half, phi_down)
    put_psi(half, psi_down)
    for j in range(half + 1, early):
        ratio = ratio_at(j - 1)
        phi_down = ratio * phi_down
        psi_down = value_at(j) + ratio * psi_down
        put_phi(j, phi_down)
        put_psi(j, psi_down)


def getter(ref, groups):
    return lambda index: ref[index * groups : (index + 1) * groups, :]


def putter(ref, groups, first=0):
    def put(index, value):
        at = first + index * groups
        ref[pl.ds(at if isinstance(at, int) else pl.multiple_of(at, groups), groups), :] = value

    return put


def together(*steps):
    steps = list(steps)
    while steps:
        steps = [step for step in steps if next(step, steps) is not steps]


def partner_response(rows, early, lon_ref, couple_ref, eigen, masks, phi_ref, psi_ref, kept_refs, value_refs):
    groups = eigen.shape[0]

    def nothing(index, value):
        pass

    def one(n, mask):
        put_kept = putter(kept_refs[n], groups)

        def put_ratio(index, value):
            if index < early:
                put_kept(index, value)

        first = n * early * groups
        return level_response(
            rows, early, lon_here() ^ mask, lon_ref, couple_ref, eigen, put_ratio, nothing, nothing,
            (
                getter(kept_refs[n], groups), getter(value_refs[n], groups), putter(value_refs[n], groups),
                putter(phi_ref, groups, first), putter(psi_ref, groups, first),
            ),
        )

    return [one(n, mask) for n, mask in enumerate(masks)]


def own_kernel(
    rows, early, masks, lon_ref, couple_ref, eigen_ref, ratio_ref, inverse_ref, edge_ref, phi_ref, psi_ref,
    phi_near_ref, psi_near_ref, value_ref, *refs,
):
    eigen = eigen_ref[...]
    groups = eigen.shape[0]
    own = level_response(
        rows, early, lon_here(), lon_ref, couple_ref, eigen, putter(ratio_ref, groups),
        putter(inverse_ref, groups), putter(edge_ref, groups),
        (
            getter(ratio_ref, groups), getter(value_ref, groups), putter(value_ref, groups),
            putter(phi_ref, groups), putter(psi_ref, groups),
        ),
    )
    count = len(masks)
    together(
        own,
        *partner_response(
            rows, early, lon_ref, couple_ref, eigen, masks, phi_near_ref, psi_near_ref,
            refs[:count], refs[count:],
        ),
    )


def partners_kernel(
    rows, early, masks, lon_ref, couple_ref, eigen_ref, after_ref, phi_ref, psi_ref, token_ref, *refs
):
    token_ref[...] = after_ref[...]
    count = len(masks)
    together(
        *partner_response(
            rows, early, lon_ref, couple_ref, eigen_ref[...], masks, phi_ref, psi_ref,
            refs[:count], refs[count:],
        )
    )


def whole_levels(const, right_side, lon_coef, lat_coef, level_scale):
    rows, levels, lon_count = right_side.shape
    digits = N1 // levels
    groups = 2 * GROUPS
    half = rows // 2
    early = early_rows(rows)
    late = rows - early
    eigen = const["eigen"].reshape(groups, N2)
    lon_all, couple_all = operator_parts(rows, lon_coef, lat_coef, level_scale)
    (around,) = call(
        functools.partial(edge_kernel, rows),
        [((2 * OV + 2) * groups, N2)],
        [lon_all, couple_all, eigen],
        [SMEM, SMEM, VMEM],
        [],
        16 * groups * N2 * 20,
        "edge",
    )
    block = (rows * groups, N2)
    early_block = (early * groups, N2)
    early_block = (early * groups, N2)
    near_masks, far_masks = [1], list(range(2, levels))
    ratio, inverse, edge, phi, psi, phi_near, psi_near = call(
        functools.partial(own_kernel, rows, early, near_masks),
        [block, block, (5 * groups, N2)] + [early_block] * 4,
        [lon_all, couple_all, eigen],
        [SMEM, SMEM, VMEM],
        [vmem(*early_block)] * 3,
        2 * rows * groups * N2 * 20,
        "own",
    )
    row = (groups, N2)
    ends = 2 * OV
    inner = rows - ends
    span = OV * digits
    by_row = right_side.reshape(rows, levels, digits, N2).transpose(0, 2, 1, 3).reshape(-1, N2)

    far = list(range(2, levels))

    def pack_ends(in_ref, *refs):
        for end_ref, mask in zip(refs, [0] + far):
            level = lon_here() ^ mask
            end_ref[:span, :] = in_ref[pl.ds(level, span, stride=levels), :]
            end_ref[span:, :] = in_ref[pl.ds(level + levels * (rows - OV) * digits, span, stride=levels), :]

    end_packed = call(
        pack_ends,
        [(ends * digits, N2)] * (levels - 1),
        [by_row],
        [VMEM],
        [],
        0,
        "pack_ends",
    )

    def pack(in_ref, after_ref, *refs):
        del after_ref
        for mask, out_ref in enumerate(refs):
            level = lon_here() ^ mask
            skip = 0 if mask == 1 else levels * span
            out_ref[...] = in_ref[pl.ds(level + skip, out_ref.shape[0], stride=levels), :]

    packed = call(
        pack,
        [((rows if mask == 1 else inner) * digits, N2) for mask in range(levels)],
        [by_row, end_packed[0]],
        [VMEM, pl.ANY],
        [],
        0,
        "pack",
    )
    end_pieces = [end_packed[0], None] + [send_level(p, m, levels) for p, m in zip(end_packed[1:], far)]
    near = send_level(packed[1], 1, levels)
    end_pieces[1] = near
    inner_pieces = [packed[0], near] + [send_level(packed[m], m, levels) for m in far]
    forward = [const["first"], const["turn"], const["second"], const["special"]]
    pad_ends, pad_inner = pad_rows(ends), pad_rows(inner)

    def ends_body(*refs):
        pieces, refs = refs[:levels], refs[levels:]
        tables_in, edge_ref = refs[:4], refs[4]
        spec_ref, top_ref, bottom_ref, even_ref, odd_ref, full_ref, mid_ref = refs[5:]
        for mask, piece in enumerate(pieces):
            at = pl.multiple_of((lon_here() ^ mask) * digits, digits)
            last = piece.shape[0] - span
            full_ref[:OV, pl.ds(at, digits), :] = piece[:span, :].reshape(OV, digits, N2)
            full_ref[OV:ends, pl.ds(at, digits), :] = piece[last:, :].reshape(OV, digits, N2)
        forward_rows(full_ref, ends, *tables_in, mid_ref, spec_ref)
        top, bottom = edge_sums(
            rows_of(spec_ref, groups), rows_of(spec_ref, groups, -OV),
            rows_of(edge_ref, groups), lambda i: edge_ref[(2 * OV - 2 - i) * groups : (2 * OV - 1 - i) * groups, :],
        )
        top_ref[...] = top
        bottom_ref[...] = bottom
        swap_out(parity_here(), top, bottom, even_ref, odd_ref)

    end_spectral, sent_top, sent_bottom, even, odd = call(
        ends_body,
        [(ends * groups, N2)] + [row] * 4,
        [*end_pieces, *forward, around],
        [VMEM] * (levels + 5),
        [vmem(pad_ends, N1, N2), vmem(pad_ends * N1, N2)],
        ends * NLON * 256 * 4,
        "ends",
    )
    even, odd = swap(even, odd)
    backward = [const["first_back"], const["turn"], const["second_back"], const["special_back"]]
    pad_early, pad_late = pad_rows(early), pad_rows(late)

    def spread(full_ref, count, out_refs):
        for mask, out_ref in enumerate(out_refs):
            at = pl.multiple_of((lon_here() ^ mask) * digits, digits)
            out_ref[...] = full_ref[:count, pl.ds(at, digits), :].reshape(count * digits, N2)

    def inner_body(*refs):
        pieces, refs = refs[:levels], refs[levels:]
        tables_in, back_in, refs = refs[:4], refs[4:7], refs[7:]
        ends_ref, even_ref, odd_ref, ratio_ref, inverse_ref, edge_ref = refs[:6]
        late_ref, top_ref, even_out, odd_out = refs[6:10]
        early_refs, refs = refs[10 : 10 + levels], refs[10 + levels :]
        full_ref, mid_ref, spec_ref, sum_ref, back_full_ref, back_mid_ref = refs
        for mask, piece in enumerate(pieces):
            at = pl.multiple_of((lon_here() ^ mask) * digits, digits)
            skip = span if mask == 1 else 0
            full_ref[:inner, pl.ds(at, digits), :] = piece[skip : skip + inner * digits, :].reshape(
                inner, digits, N2
            )
        if pad_inner > inner:
            full_ref[inner:] = jnp.zeros((pad_inner - inner, N1, N2), jnp.float32)
        forward_rows(full_ref, inner, *tables_in, mid_ref, spec_ref)
        low, high = swap_in(parity_here(), even_ref[...], odd_ref[...])

        def spec_row(i):
            if i < OV:
                return rows_of(ends_ref, groups)(i)
            if i >= rows - OV:
                return rows_of(ends_ref, groups, rows - ends)(i)
            return rows_of(spec_ref, groups, OV)(i)

        solve_first(rows, groups, spec_row, low, high, ratio_ref, inverse_ref, edge_ref, sum_ref)
        top = sum_ref[:groups, :]
        top_ref[...] = top
        late_ref[...] = sum_ref[early * groups :, :]
        swap_out(parity_here(), sum_ref[(rows - 1) * groups :, :], top, even_out, odd_out)
        early_sum = sum_ref.at[pl.ds(0, early * groups), :]
        backward_rows(early_sum, early, back_in[0], tables_in[1], back_in[1], back_in[2], back_mid_ref, back_full_ref)
        spread(back_full_ref, early, early_refs)

    late_first, own_top, even2, odd2, *early_pieces = call(
        inner_body,
        [(late * groups, N2), row, row, row] + [(early * digits, N2)] * levels,
        [
            *inner_pieces, *forward, backward[0], backward[2], backward[3],
            end_spectral, even, odd, ratio, inverse, edge,
        ],
        [VMEM] * (levels + 13),
        [
            vmem(pad_inner, N1, N2), vmem(pad_inner * N1, N2), vmem(inner * N1, N2), vmem(rows * groups, N2),
            vmem(pad_early, N1, N2), vmem(pad_early * N1, N2),
        ],
        (inner + early) * NLON * 256 * 4,
        "inner",
    )
    early_pieces = swap_levels(early_pieces)
    even2, odd2 = swap(even2, odd2)

    phi_far, psi_far, token = call(
        functools.partial(partners_kernel, rows, early, far_masks),
        [(len(far_masks) * early * groups, N2)] * 2 + [row],
        [lon_all, couple_all, eigen, own_top],
        [SMEM, SMEM, VMEM, VMEM],
        [vmem(*early_block)] * (2 * len(far_masks)),
        len(far_masks) * rows * groups * N2 * 20,
        "partners",
    )

    def sigma_body(*refs):
        first_ref, own_top_ref, even_ref, odd_ref, even2_ref, odd2_ref, top_ref, bottom_ref = refs[:8]
        ratio_ref, edge_ref, around_ref = refs[8:11]
        sigma_ref = refs[-1]
        got_top, got_bottom = swap_in(parity_here(), even_ref[...], odd_ref[...])
        from_low, from_high = swap_in(parity_here(), even2_ref[...], odd2_ref[...])
        low, high = sigmas(
            around_ref[2 * OV * groups : (2 * OV + 1) * groups, :], around_ref[(2 * OV + 1) * groups :, :], own_top_ref[...], first_ref[(late - 1) * groups :, :],
            got_top, got_bottom, top_ref[...], bottom_ref[...], from_low, from_high,
            ratio_ref[:groups, :], ratio_ref[(rows - 1) * groups :, :], edge_ref,
            around_ref[(OV - 1) * groups : OV * groups, :],
            around_ref[(2 * OV - 1) * groups : 2 * OV * groups, :],
        )
        sigma_ref[:groups, :] = low
        sigma_ref[groups:, :] = high

    (sigma,) = call(
        sigma_body,
        [(2 * groups, N2)],
        [
            late_first, own_top, even, odd, even2, odd2, sent_top, sent_bottom, ratio, edge, around,
            *early_pieces[1:], token,
        ],
        [VMEM] * 11 + [pl.ANY] * levels,
        [],
        groups * N2 * 40,
        "sigma",
    )
    sigma_pieces = swap_levels([sigma] * levels)
    def second_body(*refs):
        sigma_ref, first_ref, ratio_ref, inverse_ref, edge_ref = refs[:5]
        tables_in, refs = refs[5:9], refs[9:]
        late_refs = refs[:levels]
        sum_ref, mid_ref, full_ref = refs[levels:]
        low, high = sigma_ref[:groups, :], sigma_ref[groups:, :]

        def at(ref, index):
            return ref[index * groups : (index + 1) * groups, :]

        for i in range(half):
            j = rows - 1 - i
            if i:
                low = at(ratio_ref, i) * low
                high = at(ratio_ref, j) * high
            mid_ref[(j - half) * groups : (j - half + 1) * groups, :] = high
        x_high = at(edge_ref, 3) * high + at(edge_ref, 4) * low
        for j in range(half, rows):
            if j > half:
                x_high = at(mid_ref, j - half) * at(inverse_ref, j) + at(ratio_ref, j - 1) * x_high
            if j >= early:
                here = slice((j - early) * groups, (j - early + 1) * groups)
                sum_ref[here, :] = first_ref[here, :] + x_high
        backward_rows(sum_ref, late, *tables_in, mid_ref, full_ref)
        spread(full_ref, late, late_refs)

    late_pieces = call(
        second_body,
        [(late * digits, N2)] * levels,
        [sigma, late_first, ratio, inverse, edge, *backward],
        [VMEM] * 9,
        [vmem(late * groups, N2), vmem(max(pad_late, half) * N1, N2), vmem(pad_late, N1, N2)],
        late * NLON * 256 * 4,
        "second",
    )
    late_pieces = swap_levels(late_pieces)
    total = rows * levels * digits
    early_total = early * levels * digits
    part = const["first_back_part"]

    def correct(*refs):
        pieces, sigma_refs, refs = refs[:levels], refs[levels : 2 * levels], refs[2 * levels :]
        responses, refs = refs[:6], refs[6:]
        part_ref, turn_ref, second_ref, special_ref = refs[:4]
        out_ref, done_ref, sems, *mid_refs = refs[4:]
        part_rows = part_ref.shape[0] // levels
        mine = part_ref.at[pl.ds(pl.multiple_of(lon_here() * part_rows, part_rows), part_rows), :]
        size = early * groups
        copies = []
        for mask in range(levels):
            level = lon_here() ^ mask
            mid_ref = mid_refs[mask % 2]
            low, high = sigma_refs[mask][:groups, :], sigma_refs[mask][groups:, :]
            phi_ref, psi_ref = responses[2 * min(mask, 2) : 2 * min(mask, 2) + 2]
            first = max(mask - 2, 0) * size
            here = pl.ds(first, size)
            phi_ref, psi_ref = phi_ref.at[here, :], psi_ref.at[here, :]
            phi_all = phi_ref[...].reshape(early, groups, N2)
            psi_all = psi_ref[...].reshape(early, groups, N2)
            value = (phi_all * low[None] + psi_all * high[None]).reshape(size, N2)
            mid_ref[:size, :] = lanes_apart(product_right(lanes_together(value, early), second_ref), early)
            if pad_early > early:
                mid_ref[size:, :] = jnp.zeros((pad_early * groups - size, N2), jnp.float32)
            zeroth_low = jnp.concatenate([low[:1], low[GROUPS : GROUPS + 1]], axis=1)
            zeroth_high = jnp.concatenate([high[:1], high[GROUPS : GROUPS + 1]], axis=1)
            zeroth = load_zeroth(phi_ref, early) * zeroth_low + load_zeroth(psi_ref, early) * zeroth_high
            store_zeroth(mid_ref, early, product_right(zeroth, special_ref))
            for pair in range(pad_early // (2 * BLOCK)):
                value = digits_back(mid_ref, pair, turn_ref, mine)
                for side in range(2):
                    begin = (2 * pair + side) * BLOCK
                    count = min(BLOCK, early - begin)
                    if count <= 0:
                        continue
                    lines = count * digits
                    whole = pieces[mask][begin * digits : begin * digits + lines, :]
                    done_ref[pl.ds(level + begin * digits * levels, lines, stride=levels), :] = (
                        whole + value[:lines, side * N2 : (side + 1) * N2]
                    )
                if mask == levels - 1:
                    begin = 2 * pair * BLOCK * digits * levels
                    lines = min(2 * BLOCK * digits * levels, early_total - begin)
                    there = pl.ds(begin, lines)
                    copy = pltpu.make_async_copy(done_ref.at[there, :], out_ref.at[there, :], sems.at[pair])
                    copy.start()
                    copies.append(copy)
        for copy in copies:
            copy.wait()

    (out,) = call(
        correct,
        [(total, N2)],
        [
            *early_pieces, *sigma_pieces, phi, psi, phi_near, psi_near, phi_far, psi_far,
            part, const["turn"], *backward[2:],
        ],
        [VMEM] * (2 * levels + 10),
        [
            vmem(early_total, N2), pltpu.SemaphoreType.DMA((pad_early // (2 * BLOCK),)),
            vmem(pad_early * N1, N2), vmem(pad_early * N1, N2),
        ],
        levels * early * NLON * 256 * 40,
        "correct",
        out_spaces=[pl.ANY],
    )

    chunks = 4

    def unpack(*refs):
        pieces = refs[:levels]
        out_ref, done_ref, sems = refs[levels + 1 :]
        lines = late * digits // chunks
        copies = []
        for chunk in range(chunks):
            for mask in range(levels):
                first = (lon_here() ^ mask) + chunk * lines * levels
                done_ref[pl.ds(first, lines, stride=levels), :] = pieces[mask][chunk * lines : (chunk + 1) * lines, :]
            here = pl.ds(chunk * lines * levels, lines * levels)
            there = pl.ds(early_total + chunk * lines * levels, lines * levels)
            copy = pltpu.make_async_copy(done_ref.at[here, :], out_ref.at[there, :], sems.at[chunk])
            copy.start()
            copies.append(copy)
        for copy in copies:
            copy.wait()

    (out,) = call(
        unpack,
        [(total, N2)],
        [*late_pieces, out],
        [VMEM] * levels + [pl.ANY],
        [vmem(total - early_total, N2), pltpu.SemaphoreType.DMA((chunks,))],
        0,
        "unpack",
        out_spaces=[pl.ANY],
        aliases={levels: 0},
    )
    return out.reshape(rows, digits, levels, N2).transpose(0, 2, 1, 3).reshape(right_side.shape)


def second_part(
    rows, groups, parity, couple_ref, first_ref, even_ref, odd_ref, even2_ref, odd2_ref, top_ref, bottom_ref,
    ratio_ref, inverse_ref, edge_ref, out_ref, mid_ref,
):
    got_top, got_bottom = swap_in(parity, even_ref[...], odd_ref[...])
    low, high = swap_in(parity, even2_ref[...], odd2_ref[...])
    solve_second(
        rows, groups, couple_ref[OV], couple_ref[OV + rows],
        first_ref[:groups, :], first_ref[(rows - 1) * groups :, :],
        got_top, got_bottom, top_ref[...], bottom_ref[...], low, high,
        ratio_ref, inverse_ref, edge_ref, first_ref, out_ref, mid_ref,
    )


def shared_levels(const, right_side, lon_coef, lat_coef, level_scale):
    rows, levels, lon_count = right_side.shape
    lon_size = lax.axis_size("lon")
    assert lon_size % levels == 0 and GROUPS % (lon_size // levels) == 0 and rows % (lon_size // levels) == 0
    sharers = lon_size // levels
    groups = 2 * GROUPS // sharers
    part_rows = rows // sharers
    digits = N1 // lon_size
    lon_at = lax.axis_index("lon")
    parity = (lax.axis_index("lat") % 2).astype(jnp.int32).reshape(1)
    lon_window, couple = operator_parts(rows, lon_coef, lat_coef, level_scale)
    lon_window = lax.dynamic_index_in_dim(lon_window, lon_at // sharers, 0, False)
    couple = lax.dynamic_index_in_dim(couple, lon_at // sharers, 0, False)
    eigen = lax.dynamic_slice_in_dim(
        const["eigen"], (lon_at % sharers) * (groups // 2), groups // 2, axis=1
    ).reshape(groups, N2)
    ratio, inverse, edge = factor(rows, groups, lon_window, couple, eigen)
    block = (rows * groups, N2)
    row = (groups, N2)
    send = right_side.reshape(sharers, part_rows, levels, lon_count).transpose(2, 0, 1, 3)
    send = send.reshape(lon_size, part_rows, digits, N2)
    got = lax.all_to_all(send, "lon", 0, 0, tiled=True)
    points = got.transpose(1, 0, 2, 3).reshape(part_rows, N1, N2)
    padded = pad_rows(part_rows)

    def transform(points_ref, first_ref, turn_ref, second_ref, special_ref, out_ref, full_ref, mid_ref):
        full_ref[:part_rows] = points_ref[...]
        if padded > part_rows:
            full_ref[part_rows:] = jnp.zeros((padded - part_rows, N1, N2), jnp.float32)
        forward_rows(full_ref, part_rows, first_ref, turn_ref, second_ref, special_ref, mid_ref, out_ref)

    (spectral,) = call(
        transform,
        [(part_rows * N1, N2)],
        [points, const["first"], const["turn"], const["second"], const["special"]],
        [VMEM] * 5,
        [vmem(padded, N1, N2), vmem(padded * N1, N2)],
        part_rows * NLON * 256 * 4,
        "transform",
    )
    spectral = to_coefs(spectral, sharers, part_rows, groups)

    def edges(parity_ref, spec_ref, edge_ref, top_ref, bottom_ref, even_ref, odd_ref):
        top, bottom = edge_sums(
            rows_of(spec_ref, groups), rows_of(spec_ref, groups, OV - rows),
            rows_of(edge_ref, groups, -7), rows_of(edge_ref, groups, -14),
        )
        top_ref[...] = top
        bottom_ref[...] = bottom
        swap_out(parity_ref[0], top, bottom, even_ref, odd_ref)

    sent_top, sent_bottom, even, odd = call(
        edges, [row] * 4, [parity, spectral, edge], [SMEM, VMEM, VMEM], [], groups * N2 * 32, "edges"
    )
    even, odd = swap(even, odd)

    def first(parity_ref, spec_ref, even_ref, odd_ref, ratio_ref, inverse_ref, edge_ref, out_ref, e_ref, o_ref):
        low, high = swap_in(parity_ref[0], even_ref[...], odd_ref[...])
        solve_first(
            rows, groups, rows_of(spec_ref, groups), low, high, ratio_ref, inverse_ref, edge_ref, out_ref
        )
        swap_out(parity_ref[0], out_ref[(rows - 1) * groups :, :], out_ref[:groups, :], e_ref, o_ref)

    iterate, even2, odd2 = call(
        first,
        [block, row, row],
        [parity, spectral, even, odd, ratio, inverse, edge],
        [SMEM] + [VMEM] * 6,
        [],
        rows * groups * N2 * 8,
        "first_solve",
    )
    even2, odd2 = swap(even2, odd2)

    def second(parity_ref, *refs):
        second_part(rows, groups, parity_ref[0], *refs)

    (iterate,) = call(
        second,
        [block],
        [parity, couple, iterate, even, odd, even2, odd2, sent_top, sent_bottom, ratio, inverse, edge],
        [SMEM, SMEM] + [VMEM] * 10,
        [vmem(*block)],
        rows * groups * N2 * 8,
        "second_solve",
    )
    iterate = to_rows(iterate, sharers, part_rows, groups)

    def back(spec_ref, first_ref, turn_ref, second_ref, special_ref, out_ref, mid_ref, full_ref):
        backward_rows(spec_ref, part_rows, first_ref, turn_ref, second_ref, special_ref, mid_ref, full_ref)
        out_ref[...] = full_ref[:part_rows]

    (points,) = call(
        back,
        [(part_rows, N1, N2)],
        [iterate, const["first_back"], const["turn"], const["second_back"], const["special_back"]],
        [VMEM] * 5,
        [vmem(padded * N1, N2), vmem(padded, N1, N2)],
        part_rows * NLON * 256 * 4,
        "back_transform",
    )
    send = points.reshape(part_rows, lon_size, digits, N2).transpose(1, 0, 2, 3)
    got = lax.all_to_all(send, "lon", 0, 0, tiled=True)
    got = got.reshape(levels, sharers, part_rows, lon_count).transpose(1, 2, 0, 3)
    return got.reshape(rows, levels, lon_count)


def level_groups(sharers):
    size = lax.axis_size("lon")
    return [[first + i for i in range(sharers)] for first in range(0, size, sharers)]


def to_coefs(spectral, sharers, part_rows, groups):
    send = spectral.reshape(part_rows, 2, sharers, groups // 2, N2).transpose(2, 0, 1, 3, 4)
    got = lax.all_to_all(
        send, "lon", 0, 0, tiled=True, axis_index_groups=level_groups(sharers)
    )
    return got.reshape(sharers * part_rows * groups, N2)


def to_rows(values, sharers, part_rows, groups):
    send = values.reshape(sharers, part_rows, 2, groups // 2, N2)
    got = lax.all_to_all(
        send, "lon", 0, 0, tiled=True, axis_index_groups=level_groups(sharers)
    )
    return got.transpose(1, 2, 0, 3, 4).reshape(part_rows * N1, N2)


def solution(mesh):
    return jax.shard_map(
        on_device,
        mesh=mesh,
        in_specs=(P("lat", None, "lon"), P(), P(), P()),
        out_specs=P("lat", None, "lon"),
        check_vma=False,
    )
```

```python
import functools
import math

import jax
import jax.numpy as jnp
import numpy as np
from jax import lax
from jax.experimental import pallas as pl
from jax.experimental.pallas import tpu as pltpu
from jax.sharding import PartitionSpec as P

NLON = 4096
OV = 8
N1 = 32
N2 = 128
GROUPS = 16
BLOCK = 8

VMEM = pltpu.VMEM
SMEM = pltpu.SMEM


def numpy_split(table):
    import ml_dtypes

    table = np.asarray(table, np.float32)
    high = table.astype(ml_dtypes.bfloat16)
    low = (table - high.astype(np.float32)).astype(ml_dtypes.bfloat16)
    return high, low


def tables(levels):
    j1 = np.arange(N1)
    j2 = np.arange(N2)
    k2 = np.arange(N2)
    digit = np.arange(GROUPS)
    small = np.zeros((N1, N1))
    small[:GROUPS] = np.cos(2 * np.pi * np.outer(digit, j1) / N1)
    small[GROUPS] = np.cos(np.pi * j1)
    small[GROUPS + 1 :] = -np.sin(2 * np.pi * np.outer(digit[1:], j1) / N1)
    first = np.kron(np.eye(BLOCK), small)
    angle = 2 * np.pi * np.outer(digit, j2) / NLON
    turn_cos = np.cos(angle)
    turn_sin = np.sin(angle)
    phase = 2 * np.pi * (np.outer(j2, k2) % N2) / N2
    cosine, sine = np.cos(phase), np.sin(phase)
    second = np.block([[cosine, -sine], [sine, cosine]])
    special = np.zeros((2 * N2, 2 * N2))
    half = N2 // 2
    special[:N2, : half + 1] = np.cos(2 * np.pi * np.outer(j2, np.arange(half + 1)) / N2)
    special[:N2, half + 1 : N2] = -np.sin(2 * np.pi * np.outer(j2, np.arange(1, half)) / N2)
    odd = 2 * np.pi * np.outer(j2, 1 + 2 * np.arange(half)) / (2 * N2)
    special[N2:, N2 : N2 + half] = np.cos(odd)
    special[N2:, N2 + half :] = -np.sin(odd)
    weight = np.full(2 * N2, 2.0 / NLON)
    weight[0] = 1.0 / NLON
    weight[half] = 1.0 / NLON
    second_back = second.T * (2.0 / NLON)
    special_back = weight[:, None] * special.T
    wave = np.zeros((GROUPS, 2 * N2))
    wave[:, :N2] = digit[:, None] + N1 * k2[None, :]
    wave[:, N2:] = wave[:, :N2]
    lane = np.arange(N2)
    wave[0, :N2] = np.where(lane <= half, N1 * lane, N1 * (lane - half))
    wave[0, N2:] = 16 + N1 * (lane % half)
    eigen = 2.0 - 2.0 * np.cos(2 * np.pi * wave / NLON)
    pair = lambda t: np.concatenate(numpy_split(t), axis=0)
    width = N1 // levels
    part = [pair(np.kron(np.eye(BLOCK), small.T[at : at + width])) for at in range(0, N1, width)]
    return dict(
        first_back_part=np.concatenate(part, axis=0),
        first=pair(first),
        first_back=pair(first.T),
        second=pair(second),
        second_back=pair(second_back),
        special=pair(special),
        special_back=pair(special_back),
        turn=np.concatenate([turn_cos, turn_sin], axis=0).astype(np.float32),
        eigen=np.stack([eigen[:, :N2], eigen[:, N2:]]).astype(np.float32),
    )


def halves(value):
    high = value.astype(jnp.bfloat16)
    low = (value - high.astype(jnp.float32)).astype(jnp.bfloat16)
    return high, low


def dot(a, b):
    return lax.dot_general(a, b, (((1,), (0,)), ((), ())), preferred_element_type=jnp.float32)


def product_right(value, table_ref):
    size = table_ref.shape[0] // 2
    high, low = halves(value)
    table_high = table_ref[:size, :]
    return dot(high, table_high) + dot(low, table_high) + dot(high, table_ref[size:, :])


def product_left(table_ref, value):
    size = table_ref.shape[0] // 2
    high, low = halves(value)
    both = dot(table_ref[...], high)
    return both[:size] + both[size:] + dot(table_ref[:size, :], low)


def lanes_apart(value, rows):
    real = value[:, :N2].reshape(rows, GROUPS, N2)
    imag = value[:, N2:].reshape(rows, GROUPS, N2)
    return jnp.concatenate([real, imag], axis=1).reshape(rows * 2 * GROUPS, N2)


def lanes_together(value, rows):
    both = value.reshape(rows, 2 * GROUPS, N2)
    return jnp.concatenate([both[:, :GROUPS], both[:, GROUPS:]], axis=2).reshape(rows * GROUPS, 2 * N2)


def load_zeroth(ref, rows):
    return jnp.concatenate(
        [ref[pl.ds(0, rows, stride=2 * GROUPS), :], ref[pl.ds(GROUPS, rows, stride=2 * GROUPS), :]], axis=1
    )


def store_zeroth(ref, rows, value):
    ref[pl.ds(0, rows, stride=2 * GROUPS), :] = value[:, :N2]
    ref[pl.ds(GROUPS, rows, stride=2 * GROUPS), :] = value[:, N2:]


def forward_rows(points_ref, rows, first_ref, turn_ref, second_ref, special_ref, mid_ref, out_ref):
    padded = points_ref.shape[0]
    turn_cos = turn_ref[:GROUPS, :][None]
    turn_sin = turn_ref[GROUPS:, :][None]
    for pair in range(padded // (2 * BLOCK)):
        base = pair * 2 * BLOCK
        left = points_ref[base : base + BLOCK].reshape(BLOCK * N1, N2)
        right = points_ref[base + BLOCK : base + 2 * BLOCK].reshape(BLOCK * N1, N2)
        value = product_left(first_ref, jnp.concatenate([left, right], axis=1))
        for side in range(2):
            digits = value[:, side * N2 : (side + 1) * N2].reshape(BLOCK, N1, N2)
            real, imag = digits[:, :GROUPS], digits[:, GROUPS:]
            turned = jnp.concatenate(
                [real * turn_cos + imag * turn_sin, imag * turn_cos - real * turn_sin], axis=1
            )
            at = (base + side * BLOCK) * N1
            mid_ref[at : at + BLOCK * N1, :] = turned.reshape(BLOCK * N1, N2)
    result = product_right(lanes_together(mid_ref[...], padded), second_ref)
    out_ref[...] = lanes_apart(result, padded)[: rows * N1]
    store_zeroth(out_ref, rows, product_right(load_zeroth(mid_ref, padded), special_ref)[:rows])


def spectral_back(spec_ref, rows, padded, second_ref, special_ref, mid_ref):
    result = product_right(lanes_together(spec_ref[...], rows), second_ref)
    mid_ref[: rows * N1, :] = lanes_apart(result, rows)
    if padded > rows:
        mid_ref[rows * N1 : padded * N1, :] = jnp.zeros(((padded - rows) * N1, N2), jnp.float32)
    store_zeroth(mid_ref, rows, product_right(load_zeroth(spec_ref, rows), special_ref))


def digits_back(mid_ref, pair, turn_ref, first_ref):
    turn_cos = turn_ref[:GROUPS, :][None]
    turn_sin = turn_ref[GROUPS:, :][None]
    sides = []
    for side in range(2):
        at = (2 * pair + side) * BLOCK * N1
        both = mid_ref[at : at + BLOCK * N1, :].reshape(BLOCK, N1, N2)
        real, imag = both[:, :GROUPS], both[:, GROUPS:]
        turned = jnp.concatenate(
            [real * turn_cos - imag * turn_sin, imag * turn_cos + real * turn_sin], axis=1
        )
        sides.append(turned.reshape(BLOCK * N1, N2))
    return product_left(first_ref, jnp.concatenate(sides, axis=1))


def backward_rows(spec_ref, rows, first_ref, turn_ref, second_ref, special_ref, mid_ref, out_ref):
    padded = out_ref.shape[0]
    spectral_back(spec_ref, rows, padded, second_ref, special_ref, mid_ref)
    for pair in range(padded // (2 * BLOCK)):
        base = pair * 2 * BLOCK
        value = digits_back(mid_ref, pair, turn_ref, first_ref)
        out_ref[base : base + BLOCK] = value[:, :N2].reshape(BLOCK, N1, N2)
        out_ref[base + BLOCK : base + 2 * BLOCK] = value[:, N2:].reshape(BLOCK, N1, N2)


def factor_kernel(rows, lon_ref, couple_ref, eigen_ref, ratio_ref, inverse_ref, edge_ref):
    eigen = eigen_ref[...]
    groups = eigen.shape[0]
    half = rows // 2
    last = rows + 2 * OV - 1

    def plain(e):
        return 1.0 + lon_ref[e] * eigen

    def put(ref, index, value):
        ref[index * groups : (index + 1) * groups, :] = value

    def chain(start, stop, step, into):
        excess = inverse = None
        for e in range(start, stop + step, step):
            before = couple_ref[e] if step > 0 else couple_ref[e + 1]
            after = couple_ref[e + 1] if step > 0 else couple_ref[e]
            if inverse is None:
                ratio = None
                excess = plain(e) + before
            else:
                ratio = before * inverse
                excess = plain(e) + ratio * excess
            divisor = after + excess
            inverse = 1.0 / divisor
            into(e, ratio, inverse, excess, divisor)

    kept = {}

    def top(e, ratio, inverse, excess, divisor):
        if e == OV - 1:
            put(edge_ref, 0, inverse)
        if e >= OV:
            put(ratio_ref, e - OV, ratio)
            put(inverse_ref, e - OV, inverse)
        if e == OV + half - 1:
            kept["top"] = excess, divisor

    def bottom(e, ratio, inverse, excess, divisor):
        if e == OV + rows:
            put(edge_ref, 1, inverse)
        if e < OV + rows:
            put(ratio_ref, e - OV, ratio)
            put(inverse_ref, e - OV, inverse)
        if e == OV + half:
            kept["bottom"] = excess, divisor

    def next_band(e, ratio, inverse, excess, divisor):
        if ratio is not None:
            put(edge_ref, 7 + e - rows - 1, ratio)
        if e == OV + rows - 1:
            put(edge_ref, 5, inverse)

    def previous_band(e, ratio, inverse, excess, divisor):
        if ratio is not None:
            put(edge_ref, 14 + e - OV, ratio)
        if e == OV:
            put(edge_ref, 6, inverse)

    chain(rows, OV + rows - 1, 1, next_band)
    chain(2 * OV - 1, OV, -1, previous_band)
    chain(0, OV + half - 1, 1, top)
    chain(last, OV + half, -1, bottom)
    excess_top, divisor_top = kept["top"]
    excess_bottom, divisor_bottom = kept["bottom"]
    between = couple_ref[OV + half]
    inverse = 1.0 / (between * (excess_top + excess_bottom) + excess_top * excess_bottom)
    put(edge_ref, 2, divisor_bottom * inverse)
    put(edge_ref, 3, divisor_top * inverse)
    put(edge_ref, 4, between * inverse)


def edge_sums(low_rows, high_rows, next_ratio, previous_ratio):
    top = high_rows(0)
    for i in range(1, OV):
        top = high_rows(i) + next_ratio(i - 1) * top
    bottom = low_rows(OV - 1)
    for i in range(OV - 2, -1, -1):
        bottom = low_rows(i) + previous_ratio(i) * bottom
    return top, bottom


def swap_out(parity, up, down, even_ref, odd_ref):
    is_even = parity == 0
    even_ref[...] = jnp.where(is_even, up, down)
    odd_ref[...] = jnp.where(is_even, down, up)


def swap_in(parity, even, odd):
    is_even = parity == 0
    return jnp.where(is_even, odd, even), jnp.where(is_even, even, odd)


def solve_first(rows, groups, right_side_row, from_low, from_high, ratio_ref, inverse_ref, edge_ref, out_ref):
    half = rows // 2

    def at(ref, index):
        return ref[index * groups : (index + 1) * groups, :]

    def put(index, value):
        out_ref[index * groups : (index + 1) * groups, :] = value

    low, high = from_low, from_high
    for i in range(half):
        j = rows - 1 - i
        low = right_side_row(i) + at(ratio_ref, i) * low
        high = right_side_row(j) + at(ratio_ref, j) * high
        put(i, low)
        put(j, high)
    meet(rows, groups, low, high, ratio_ref, inverse_ref, edge_ref, at, lambda i: at(out_ref, i), put)


def meet(rows, groups, low, high, ratio_ref, inverse_ref, edge_ref, at, value, put):
    half = rows // 2
    between = at(edge_ref, 4)
    x_low = at(edge_ref, 2) * low + between * high
    x_high = at(edge_ref, 3) * high + between * low
    put(half - 1, x_low)
    put(half, x_high)
    for i in range(half - 2, -1, -1):
        j = rows - 1 - i
        x_low = value(i) * at(inverse_ref, i) + at(ratio_ref, i + 1) * x_low
        x_high = value(j) * at(inverse_ref, j) + at(ratio_ref, j - 1) * x_high
        put(i, x_low)
        put(j, x_high)


def sigmas(
    couple_low, couple_high, own_top, own_bottom, got_top, got_bottom, sent_top, sent_bottom, from_low, from_high,
    ratio_first, ratio_last, edge_ref, next_inverse, previous_inverse,
):
    groups = own_top.shape[0]

    def edge(index):
        return edge_ref[index * groups : (index + 1) * groups, :]

    beyond_low = (got_top + couple_low * own_top) * edge(0)
    beyond_high = (got_bottom + couple_high * own_bottom) * edge(1)
    theirs_low = (sent_bottom + couple_low * from_low) * previous_inverse
    theirs_high = (sent_top + couple_high * from_high) * next_inverse
    low = ratio_first * (couple_low * (own_top - theirs_low)) + couple_low * (from_low - beyond_low)
    high = ratio_last * (couple_high * (own_bottom - theirs_high)) + couple_high * (from_high - beyond_high)
    return low, high


def solve_second(
    rows, groups, couple_low, couple_high, own_top, own_bottom, got_top, got_bottom, sent_top, sent_bottom,
    from_low, from_high, ratio_ref, inverse_ref, edge_ref, first_ref, out_ref, mid_ref,
):
    half = rows // 2

    def at(ref, index):
        return ref[index * groups : (index + 1) * groups, :]

    low, high = sigmas(
        couple_low, couple_high, own_top, own_bottom, got_top, got_bottom, sent_top, sent_bottom,
        from_low, from_high, at(ratio_ref, 0), at(ratio_ref, rows - 1), edge_ref, at(edge_ref, 5), at(edge_ref, 6),
    )
    for i in range(half):
        j = rows - 1 - i
        if i:
            low = at(ratio_ref, i) * low
            high = at(ratio_ref, j) * high
        mid_ref[i * groups : (i + 1) * groups, :] = low
        mid_ref[j * groups : (j + 1) * groups, :] = high

    def put(index, value):
        rows_at = slice(index * groups, (index + 1) * groups)
        out_ref[rows_at, :] = first_ref[rows_at, :] + value

    meet(rows, groups, low, high, ratio_ref, inverse_ref, edge_ref, at, lambda i: at(mid_ref, i), put)


def call(body, outs, ins, spaces, scratch, flops, name, out_spaces=None, aliases=None):
    nbytes = sum(x.size * x.dtype.itemsize for x in ins) + sum(4 * math.prod(s) for s in outs)
    out = pl.pallas_call(
        body,
        out_shape=[jax.ShapeDtypeStruct(s, jnp.float32) for s in outs],
        in_specs=[pl.BlockSpec(memory_space=s) for s in spaces],
        out_specs=[pl.BlockSpec(memory_space=s) for s in out_spaces or [VMEM] * len(outs)],
        input_output_aliases=aliases or {},
        scratch_shapes=scratch,
        compiler_params=pltpu.CompilerParams(vmem_limit_bytes=32 << 20),
        cost_estimate=pl.CostEstimate(flops=flops, bytes_accessed=nbytes, transcendentals=0),
        name=name,
    )(*ins)
    return out


def pad_rows(rows):
    return -(-rows // (2 * BLOCK)) * 2 * BLOCK


def swap(value_even, value_odd):
    count = lax.axis_size("lat")
    even = [(i, i ^ 1) for i in range(count) if (i ^ 1) < count]
    odd = [(i, ((i + 1) ^ 1) - 1) for i in range(1, count) if ((i + 1) ^ 1) - 1 < count]
    value_odd = lax.ppermute(value_odd, "lat", odd)
    return lax.ppermute(value_even, "lat", even), value_odd


def send_level(piece, mask, size):
    return lax.ppermute(piece, "lon", [(d, d ^ mask) for d in range(size)])


def swap_levels(pieces):
    return [pieces[0]] + [send_level(pieces[mask], mask, len(pieces)) for mask in range(1, len(pieces))]


def operator_parts(rows, lon_coef, lat_coef, level_scale):
    row_first = lax.axis_index("lat") * rows
    extent = rows + 2 * OV
    lon_window = lax.dynamic_slice_in_dim(jnp.pad(lon_coef, (OV, OV)), row_first, extent)
    couple = lax.dynamic_slice_in_dim(jnp.pad(lat_coef, (OV + 1, OV + 2)), row_first, extent + 1)
    return level_scale[:, None] * lon_window[None], level_scale[:, None] * couple[None]


def factor(rows, groups, lon_window, couple, eigen):
    block = (rows * groups, N2)
    return call(
        functools.partial(factor_kernel, rows),
        [block, block, (21 * groups, N2)],
        [lon_window, couple, eigen],
        [SMEM, SMEM, VMEM],
        [],
        rows * groups * N2 * 20,
        "factor",
    )


def vmem(*shape):
    return pltpu.VMEM(shape, jnp.float32)


def rows_of(ref, groups, first=0):
    return lambda i: ref[(i - first) * groups : (i - first + 1) * groups, :]


def on_device(right_side, lon_coef, lat_coef, level_scale):
    const = {k: jnp.asarray(v) for k, v in tables(right_side.shape[1]).items()}
    if lax.axis_size("lon") != right_side.shape[1]:
        return shared_levels(const, right_side, lon_coef, lat_coef, level_scale)
    return whole_levels(const, right_side, lon_coef, lat_coef, level_scale)


def early_rows(rows):
    return rows // 2 + 6


def lon_here():
    return lax.axis_index("lon").astype(jnp.int32)


def parity_here():
    return lax.axis_index("lat").astype(jnp.int32) % 2


def edge_kernel(rows, lon_ref, couple_ref, eigen_ref, out_ref):
    eigen = eigen_ref[...]
    groups = eigen.shape[0]
    level = lon_here()
    low = high = low_inverse = high_inverse = None
    for i in range(OV):
        e, f = rows + i, 2 * OV - 1 - i
        if i == 0:
            low = 1.0 + lon_ref[level, e : e + 1, :] * eigen + couple_ref[level, e : e + 1, :]
            high = 1.0 + lon_ref[level, f : f + 1, :] * eigen + couple_ref[level, f + 1 : f + 2, :]
        else:
            low_ratio = couple_ref[level, e : e + 1, :] * low_inverse
            high_ratio = couple_ref[level, f + 1 : f + 2, :] * high_inverse
            out_ref[(i - 1) * groups : i * groups, :] = low_ratio
            out_ref[(OV + i - 1) * groups : (OV + i) * groups, :] = high_ratio
            low = 1.0 + lon_ref[level, e : e + 1, :] * eigen + low_ratio * low
            high = 1.0 + lon_ref[level, f : f + 1, :] * eigen + high_ratio * high
        low_inverse = 1.0 / (couple_ref[level, e + 1 : e + 2, :] + low)
        high_inverse = 1.0 / (couple_ref[level, f : f + 1, :] + high)
    out_ref[(OV - 1) * groups : OV * groups, :] = low_inverse
    out_ref[(2 * OV - 1) * groups : 2 * OV * groups, :] = high_inverse
    out_ref[2 * OV * groups : (2 * OV + 1) * groups, :] = jnp.broadcast_to(couple_ref[level, OV : OV + 1, :], eigen.shape)
    out_ref[(2 * OV + 1) * groups :, :] = jnp.broadcast_to(
        couple_ref[level, OV + rows : OV + rows + 1, :], eigen.shape
    )


def level_response(rows, early, level, lon_ref, couple_ref, eigen, put_ratio, put_inverse, keep, tables):
    half = rows // 2
    ratio_at, value_at, put_value, put_phi, put_psi = tables

    def plain(e):
        return 1.0 + lon_ref[level, e : e + 1, :] * eigen

    low = high = None
    low_inverse = high_inverse = low_value = high_value = None
    for i in range(-OV, half):
        j = rows - 1 - i
        e, f = i + OV, j + OV
        if low is None:
            low = plain(e) + couple_ref[level, e : e + 1, :]
            high = plain(f) + couple_ref[level, f + 1 : f + 2, :]
        else:
            low_ratio = couple_ref[level, e : e + 1, :] * low_inverse
            high_ratio = couple_ref[level, f + 1 : f + 2, :] * high_inverse
            low = plain(e) + low_ratio * low
            high = plain(f) + high_ratio * high
        low_divisor = couple_ref[level, e + 1 : e + 2, :] + low
        high_divisor = couple_ref[level, f : f + 1, :] + high
        low_inverse = 1.0 / low_divisor
        high_inverse = 1.0 / high_divisor
        yield
        if i == -1:
            keep(0, low_inverse)
            keep(1, high_inverse)
        if i == 0:
            low_value = high_value = jnp.ones_like(eigen)
        elif i > 0:
            low_value = low_ratio * low_value
            high_value = high_ratio * high_value
        if i >= 0:
            put_ratio(i, low_ratio)
            put_ratio(j, high_ratio)
            put_inverse(i, low_inverse)
            put_inverse(j, high_inverse)
            put_value(i, low_value * low_inverse)
            if j < early:
                put_value(j, high_value * high_inverse)
    between = couple_ref[level, OV + half : OV + half + 1, :]
    inverse = 1.0 / (between * (low + high) + low * high)
    across = between * inverse
    high_inverse = high_divisor * inverse
    low_inverse = low_divisor * inverse
    keep(2, high_inverse)
    keep(3, low_inverse)
    keep(4, across)
    phi = high_inverse * low_value
    psi = across * high_value
    phi_down = across * low_value
    psi_down = low_inverse * high_value
    put_phi(half - 1, phi)
    put_psi(half - 1, psi)
    for i in range(half - 2, -1, -1):
        yield
        ratio = ratio_at(i + 1)
        phi = value_at(i) + ratio * phi
        psi = ratio * psi
        put_phi(i, phi)
        put_psi(i, psi)
    put_phi(half, phi_down)
    put_psi(half, psi_down)
    for j in range(half + 1, early):
        ratio = ratio_at(j - 1)
        phi_down = ratio * phi_down
        psi_down = value_at(j) + ratio * psi_down
        put_phi(j, phi_down)
        put_psi(j, psi_down)


def getter(ref, groups):
    return lambda index: ref[index * groups : (index + 1) * groups, :]


def putter(ref, groups, first=0):
    def put(index, value):
        at = first + index * groups
        ref[pl.ds(at if isinstance(at, int) else pl.multiple_of(at, groups), groups), :] = value

    return put


def together(*steps):
    steps = list(steps)
    while steps:
        steps = [step for step in steps if next(step, steps) is not steps]


def partner_response(rows, early, lon_ref, couple_ref, eigen, masks, phi_ref, psi_ref, kept_refs, value_refs):
    groups = eigen.shape[0]

    def nothing(index, value):
        pass

    def one(n, mask):
        put_kept = putter(kept_refs[n], groups)

        def put_ratio(index, value):
            if index < early:
                put_kept(index, value)

        first = n * early * groups
        return level_response(
            rows, early, lon_here() ^ mask, lon_ref, couple_ref, eigen, put_ratio, nothing, nothing,
            (
                getter(kept_refs[n], groups), getter(value_refs[n], groups), putter(value_refs[n], groups),
                putter(phi_ref, groups, first), putter(psi_ref, groups, first),
            ),
        )

    return [one(n, mask) for n, mask in enumerate(masks)]


def own_kernel(
    rows, early, masks, lon_ref, couple_ref, eigen_ref, ratio_ref, inverse_ref, edge_ref, phi_ref, psi_ref,
    phi_near_ref, psi_near_ref, value_ref, *refs,
):
    eigen = eigen_ref[...]
    groups = eigen.shape[0]
    own = level_response(
        rows, early, lon_here(), lon_ref, couple_ref, eigen, putter(ratio_ref, groups),
        putter(inverse_ref, groups), putter(edge_ref, groups),
        (
            getter(ratio_ref, groups), getter(value_ref, groups), putter(value_ref, groups),
            putter(phi_ref, groups), putter(psi_ref, groups),
        ),
    )
    count = len(masks)
    together(
        own,
        *partner_response(
            rows, early, lon_ref, couple_ref, eigen, masks, phi_near_ref, psi_near_ref,
            refs[:count], refs[count:],
        ),
    )


def partners_kernel(
    rows, early, masks, lon_ref, couple_ref, eigen_ref, after_ref, phi_ref, psi_ref, token_ref, *refs
):
    token_ref[...] = after_ref[...]
    count = len(masks)
    together(
        *partner_response(
            rows, early, lon_ref, couple_ref, eigen_ref[...], masks, phi_ref, psi_ref,
            refs[:count], refs[count:],
        )
    )


def whole_levels(const, right_side, lon_coef, lat_coef, level_scale):
    rows, levels, lon_count = right_side.shape
    digits = N1 // levels
    groups = 2 * GROUPS
    half = rows // 2
    early = early_rows(rows)
    late = rows - early
    eigen = const["eigen"].reshape(groups, N2)
    lon_all, couple_all = operator_parts(rows, lon_coef, lat_coef, level_scale)
    lon_all = jnp.broadcast_to(lon_all[:, :, None], (*lon_all.shape, N2))
    couple_all = jnp.broadcast_to(couple_all[:, :, None], (*couple_all.shape, N2))
    (around,) = call(
        functools.partial(edge_kernel, rows),
        [((2 * OV + 2) * groups, N2)],
        [lon_all, couple_all, eigen],
        [VMEM, VMEM, VMEM],
        [],
        16 * groups * N2 * 20,
        "edge",
    )
    block = (rows * groups, N2)
    early_block = (early * groups, N2)
    early_block = (early * groups, N2)
    near_masks, far_masks = [1], list(range(2, levels))
    ratio, inverse, edge, phi, psi, phi_near, psi_near = call(
        functools.partial(own_kernel, rows, early, near_masks),
        [block, block, (5 * groups, N2)] + [early_block] * 4,
        [lon_all, couple_all, eigen],
        [VMEM, VMEM, VMEM],
        [vmem(*early_block)] * 3,
        2 * rows * groups * N2 * 20,
        "own",
    )
    row = (groups, N2)
    ends = 2 * OV
    inner = rows - ends
    span = OV * digits
    by_row = right_side.reshape(rows, levels, digits, N2).transpose(0, 2, 1, 3).reshape(-1, N2)

    far = list(range(2, levels))

    def pack_ends(in_ref, *refs):
        for end_ref, mask in zip(refs, [0] + far):
            level = lon_here() ^ mask
            end_ref[:span, :] = in_ref[pl.ds(level, span, stride=levels), :]
            end_ref[span:, :] = in_ref[pl.ds(level + levels * (rows - OV) * digits, span, stride=levels), :]

    end_packed = call(
        pack_ends,
        [(ends * digits, N2)] * (levels - 1),
        [by_row],
        [VMEM],
        [],
        0,
        "pack_ends",
    )

    def pack(in_ref, after_ref, *refs):
        del after_ref
        for mask, out_ref in enumerate(refs):
            level = lon_here() ^ mask
            skip = 0 if mask == 1 else levels * span
            out_ref[...] = in_ref[pl.ds(level + skip, out_ref.shape[0], stride=levels), :]

    packed = call(
        pack,
        [((rows if mask == 1 else inner) * digits, N2) for mask in range(levels)],
        [by_row, end_packed[0]],
        [VMEM, pl.ANY],
        [],
        0,
        "pack",
    )
    end_pieces = [end_packed[0], None] + [send_level(p, m, levels) for p, m in zip(end_packed[1:], far)]
    near = send_level(packed[1], 1, levels)
    end_pieces[1] = near
    inner_pieces = [packed[0], near] + [send_level(packed[m], m, levels) for m in far]
    forward = [const["first"], const["turn"], const["second"], const["special"]]
    pad_ends, pad_inner = pad_rows(ends), pad_rows(inner)

    def ends_body(*refs):
        pieces, refs = refs[:levels], refs[levels:]
        tables_in, edge_ref = refs[:4], refs[4]
        spec_ref, top_ref, bottom_ref, even_ref, odd_ref, full_ref, mid_ref = refs[5:]
        for mask, piece in enumerate(pieces):
            at = pl.multiple_of((lon_here() ^ mask) * digits, digits)
            last = piece.shape[0] - span
            full_ref[:OV, pl.ds(at, digits), :] = piece[:span, :].reshape(OV, digits, N2)
            full_ref[OV:ends, pl.ds(at, digits), :] = piece[last:, :].reshape(OV, digits, N2)
        forward_rows(full_ref, ends, *tables_in, mid_ref, spec_ref)
        top, bottom = edge_sums(
            rows_of(spec_ref, groups), rows_of(spec_ref, groups, -OV),
            rows_of(edge_ref, groups), lambda i: edge_ref[(2 * OV - 2 - i) * groups : (2 * OV - 1 - i) * groups, :],
        )
        top_ref[...] = top
        bottom_ref[...] = bottom
        swap_out(parity_here(), top, bottom, even_ref, odd_ref)

    end_spectral, sent_top, sent_bottom, even, odd = call(
        ends_body,
        [(ends * groups, N2)] + [row] * 4,
        [*end_pieces, *forward, around],
        [VMEM] * (levels + 5),
        [vmem(pad_ends, N1, N2), vmem(pad_ends * N1, N2)],
        ends * NLON * 256 * 4,
        "ends",
    )
    even, odd = swap(even, odd)
    backward = [const["first_back"], const["turn"], const["second_back"], const["special_back"]]
    pad_early, pad_late = pad_rows(early), pad_rows(late)

    def spread(full_ref, count, out_refs):
        for mask, out_ref in enumerate(out_refs):
            at = pl.multiple_of((lon_here() ^ mask) * digits, digits)
            out_ref[...] = full_ref[:count, pl.ds(at, digits), :].reshape(count * digits, N2)

    def inner_body(*refs):
        pieces, refs = refs[:levels], refs[levels:]
        tables_in, back_in, refs = refs[:4], refs[4:7], refs[7:]
        ends_ref, even_ref, odd_ref, ratio_ref, inverse_ref, edge_ref = refs[:6]
        late_ref, top_ref, even_out, odd_out = refs[6:10]
        early_refs, refs = refs[10 : 10 + levels], refs[10 + levels :]
        full_ref, mid_ref, spec_ref, sum_ref, back_full_ref, back_mid_ref = refs
        for mask, piece in enumerate(pieces):
            at = pl.multiple_of((lon_here() ^ mask) * digits, digits)
            skip = span if mask == 1 else 0
            full_ref[:inner, pl.ds(at, digits), :] = piece[skip : skip + inner * digits, :].reshape(
                inner, digits, N2
            )
        if pad_inner > inner:
            full_ref[inner:] = jnp.zeros((pad_inner - inner, N1, N2), jnp.float32)
        forward_rows(full_ref, inner, *tables_in, mid_ref, spec_ref)
        low, high = swap_in(parity_here(), even_ref[...], odd_ref[...])

        def spec_row(i):
            if i < OV:
                return rows_of(ends_ref, groups)(i)
            if i >= rows - OV:
                return rows_of(ends_ref, groups, rows - ends)(i)
            return rows_of(spec_ref, groups, OV)(i)

        solve_first(rows, groups, spec_row, low, high, ratio_ref, inverse_ref, edge_ref, sum_ref)
        top = sum_ref[:groups, :]
        top_ref[...] = top
        late_ref[...] = sum_ref[early * groups :, :]
        swap_out(parity_here(), sum_ref[(rows - 1) * groups :, :], top, even_out, odd_out)
        early_sum = sum_ref.at[pl.ds(0, early * groups), :]
        backward_rows(early_sum, early, back_in[0], tables_in[1], back_in[1], back_in[2], back_mid_ref, back_full_ref)
        spread(back_full_ref, early, early_refs)

    late_first, own_top, even2, odd2, *early_pieces = call(
        inner_body,
        [(late * groups, N2), row, row, row] + [(early * digits, N2)] * levels,
        [
            *inner_pieces, *forward, backward[0], backward[2], backward[3],
            end_spectral, even, odd, ratio, inverse, edge,
        ],
        [VMEM] * (levels + 13),
        [
            vmem(pad_inner, N1, N2), vmem(pad_inner * N1, N2), vmem(inner * N1, N2), vmem(rows * groups, N2),
            vmem(pad_early, N1, N2), vmem(pad_early * N1, N2),
        ],
        (inner + early) * NLON * 256 * 4,
        "inner",
    )
    early_pieces = swap_levels(early_pieces)
    even2, odd2 = swap(even2, odd2)

    phi_far, psi_far, token = call(
        functools.partial(partners_kernel, rows, early, far_masks),
        [(len(far_masks) * early * groups, N2)] * 2 + [row],
        [lon_all, couple_all, eigen, own_top],
        [VMEM, VMEM, VMEM, VMEM],
        [vmem(*early_block)] * (2 * len(far_masks)),
        len(far_masks) * rows * groups * N2 * 20,
        "partners",
    )

    def sigma_body(*refs):
        first_ref, own_top_ref, even_ref, odd_ref, even2_ref, odd2_ref, top_ref, bottom_ref = refs[:8]
        ratio_ref, edge_ref, around_ref = refs[8:11]
        sigma_ref = refs[-1]
        got_top, got_bottom = swap_in(parity_here(), even_ref[...], odd_ref[...])
        from_low, from_high = swap_in(parity_here(), even2_ref[...], odd2_ref[...])
        low, high = sigmas(
            around_ref[2 * OV * groups : (2 * OV + 1) * groups, :], around_ref[(2 * OV + 1) * groups :, :], own_top_ref[...], first_ref[(late - 1) * groups :, :],
            got_top, got_bottom, top_ref[...], bottom_ref[...], from_low, from_high,
            ratio_ref[:groups, :], ratio_ref[(rows - 1) * groups :, :], edge_ref,
            around_ref[(OV - 1) * groups : OV * groups, :],
            around_ref[(2 * OV - 1) * groups : 2 * OV * groups, :],
        )
        sigma_ref[:groups, :] = low
        sigma_ref[groups:, :] = high

    (sigma,) = call(
        sigma_body,
        [(2 * groups, N2)],
        [
            late_first, own_top, even, odd, even2, odd2, sent_top, sent_bottom, ratio, edge, around,
            *early_pieces[1:], token,
        ],
        [VMEM] * 11 + [pl.ANY] * levels,
        [],
        groups * N2 * 40,
        "sigma",
    )
    sigma_pieces = swap_levels([sigma] * levels)
    def second_body(*refs):
        sigma_ref, first_ref, ratio_ref, inverse_ref, edge_ref = refs[:5]
        tables_in, refs = refs[5:9], refs[9:]
        late_refs = refs[:levels]
        sum_ref, mid_ref, full_ref = refs[levels:]
        low, high = sigma_ref[:groups, :], sigma_ref[groups:, :]

        def at(ref, index):
            return ref[index * groups : (index + 1) * groups, :]

        for i in range(half):
            j = rows - 1 - i
            if i:
                low = at(ratio_ref, i) * low
                high = at(ratio_ref, j) * high
            mid_ref[(j - half) * groups : (j - half + 1) * groups, :] = high
        x_high = at(edge_ref, 3) * high + at(edge_ref, 4) * low
        for j in range(half, rows):
            if j > half:
                x_high = at(mid_ref, j - half) * at(inverse_ref, j) + at(ratio_ref, j - 1) * x_high
            if j >= early:
                here = slice((j - early) * groups, (j - early + 1) * groups)
                sum_ref[here, :] = first_ref[here, :] + x_high
        backward_rows(sum_ref, late, *tables_in, mid_ref, full_ref)
        spread(full_ref, late, late_refs)

    late_pieces = call(
        second_body,
        [(late * digits, N2)] * levels,
        [sigma, late_first, ratio, inverse, edge, *backward],
        [VMEM] * 9,
        [vmem(late * groups, N2), vmem(max(pad_late, half) * N1, N2), vmem(pad_late, N1, N2)],
        late * NLON * 256 * 4,
        "second",
    )
    late_pieces = swap_levels(late_pieces)
    total = rows * levels * digits
    early_total = early * levels * digits
    part = const["first_back_part"]

    def correct(*refs):
        pieces, sigma_refs, refs = refs[:levels], refs[levels : 2 * levels], refs[2 * levels :]
        responses, refs = refs[:6], refs[6:]
        part_ref, turn_ref, second_ref, special_ref = refs[:4]
        out_ref, done_ref, sems, *mid_refs = refs[4:]
        part_rows = part_ref.shape[0] // levels
        mine = part_ref.at[pl.ds(pl.multiple_of(lon_here() * part_rows, part_rows), part_rows), :]
        size = early * groups
        copies = []
        for mask in range(levels):
            level = lon_here() ^ mask
            mid_ref = mid_refs[mask % 2]
            low, high = sigma_refs[mask][:groups, :], sigma_refs[mask][groups:, :]
            phi_ref, psi_ref = responses[2 * min(mask, 2) : 2 * min(mask, 2) + 2]
            first = max(mask - 2, 0) * size
            here = pl.ds(first, size)
            phi_ref, psi_ref = phi_ref.at[here, :], psi_ref.at[here, :]
            phi_all = phi_ref[...].reshape(early, groups, N2)
            psi_all = psi_ref[...].reshape(early, groups, N2)
            value = (phi_all * low[None] + psi_all * high[None]).reshape(size, N2)
            mid_ref[:size, :] = lanes_apart(product_right(lanes_together(value, early), second_ref), early)
            if pad_early > early:
                mid_ref[size:, :] = jnp.zeros((pad_early * groups - size, N2), jnp.float32)
            zeroth_low = jnp.concatenate([low[:1], low[GROUPS : GROUPS + 1]], axis=1)
            zeroth_high = jnp.concatenate([high[:1], high[GROUPS : GROUPS + 1]], axis=1)
            zeroth = load_zeroth(phi_ref, early) * zeroth_low + load_zeroth(psi_ref, early) * zeroth_high
            store_zeroth(mid_ref, early, product_right(zeroth, special_ref))
            for pair in range(pad_early // (2 * BLOCK)):
                value = digits_back(mid_ref, pair, turn_ref, mine)
                for side in range(2):
                    begin = (2 * pair + side) * BLOCK
                    count = min(BLOCK, early - begin)
                    if count <= 0:
                        continue
                    lines = count * digits
                    whole = pieces[mask][begin * digits : begin * digits + lines, :]
                    done_ref[pl.ds(level + begin * digits * levels, lines, stride=levels), :] = (
                        whole + value[:lines, side * N2 : (side + 1) * N2]
                    )
                if mask == levels - 1:
                    begin = 2 * pair * BLOCK * digits * levels
                    lines = min(2 * BLOCK * digits * levels, early_total - begin)
                    there = pl.ds(begin, lines)
                    copy = pltpu.make_async_copy(done_ref.at[there, :], out_ref.at[there, :], sems.at[pair])
                    copy.start()
                    copies.append(copy)
        for copy in copies:
            copy.wait()

    (out,) = call(
        correct,
        [(total, N2)],
        [
            *early_pieces, *sigma_pieces, phi, psi, phi_near, psi_near, phi_far, psi_far,
            part, const["turn"], *backward[2:],
        ],
        [VMEM] * (2 * levels + 10),
        [
            vmem(early_total, N2), pltpu.SemaphoreType.DMA((pad_early // (2 * BLOCK),)),
            vmem(pad_early * N1, N2), vmem(pad_early * N1, N2),
        ],
        levels * early * NLON * 256 * 40,
        "correct",
        out_spaces=[pl.ANY],
    )

    chunks = 4

    def unpack(*refs):
        pieces = refs[:levels]
        out_ref, done_ref, sems = refs[levels + 1 :]
        lines = late * digits // chunks
        copies = []
        for chunk in range(chunks):
            for mask in range(levels):
                first = (lon_here() ^ mask) + chunk * lines * levels
                done_ref[pl.ds(first, lines, stride=levels), :] = pieces[mask][chunk * lines : (chunk + 1) * lines, :]
            here = pl.ds(chunk * lines * levels, lines * levels)
            there = pl.ds(early_total + chunk * lines * levels, lines * levels)
            copy = pltpu.make_async_copy(done_ref.at[here, :], out_ref.at[there, :], sems.at[chunk])
            copy.start()
            copies.append(copy)
        for copy in copies:
            copy.wait()

    (out,) = call(
        unpack,
        [(total, N2)],
        [*late_pieces, out],
        [VMEM] * levels + [pl.ANY],
        [vmem(total - early_total, N2), pltpu.SemaphoreType.DMA((chunks,))],
        0,
        "unpack",
        out_spaces=[pl.ANY],
        aliases={levels: 0},
    )
    return out.reshape(rows, digits, levels, N2).transpose(0, 2, 1, 3).reshape(right_side.shape)


def second_part(
    rows, groups, parity, couple_ref, first_ref, even_ref, odd_ref, even2_ref, odd2_ref, top_ref, bottom_ref,
    ratio_ref, inverse_ref, edge_ref, out_ref, mid_ref,
):
    got_top, got_bottom = swap_in(parity, even_ref[...], odd_ref[...])
    low, high = swap_in(parity, even2_ref[...], odd2_ref[...])
    solve_second(
        rows, groups, couple_ref[OV], couple_ref[OV + rows],
        first_ref[:groups, :], first_ref[(rows - 1) * groups :, :],
        got_top, got_bottom, top_ref[...], bottom_ref[...], low, high,
        ratio_ref, inverse_ref, edge_ref, first_ref, out_ref, mid_ref,
    )


def shared_levels(const, right_side, lon_coef, lat_coef, level_scale):
    rows, levels, lon_count = right_side.shape
    lon_size = lax.axis_size("lon")
    assert lon_size % levels == 0 and GROUPS % (lon_size // levels) == 0 and rows % (lon_size // levels) == 0
    sharers = lon_size // levels
    groups = 2 * GROUPS // sharers
    part_rows = rows // sharers
    digits = N1 // lon_size
    lon_at = lax.axis_index("lon")
    parity = (lax.axis_index("lat") % 2).astype(jnp.int32).reshape(1)
    lon_window, couple = operator_parts(rows, lon_coef, lat_coef, level_scale)
    lon_window = lax.dynamic_index_in_dim(lon_window, lon_at // sharers, 0, False)
    couple = lax.dynamic_index_in_dim(couple, lon_at // sharers, 0, False)
    eigen = lax.dynamic_slice_in_dim(
        const["eigen"], (lon_at % sharers) * (groups // 2), groups // 2, axis=1
    ).reshape(groups, N2)
    ratio, inverse, edge = factor(rows, groups, lon_window, couple, eigen)
    block = (rows * groups, N2)
    row = (groups, N2)
    send = right_side.reshape(sharers, part_rows, levels, lon_count).transpose(2, 0, 1, 3)
    send = send.reshape(lon_size, part_rows, digits, N2)
    got = lax.all_to_all(send, "lon", 0, 0, tiled=True)
    points = got.transpose(1, 0, 2, 3).reshape(part_rows, N1, N2)
    padded = pad_rows(part_rows)

    def transform(points_ref, first_ref, turn_ref, second_ref, special_ref, out_ref, full_ref, mid_ref):
        full_ref[:part_rows] = points_ref[...]
        if padded > part_rows:
            full_ref[part_rows:] = jnp.zeros((padded - part_rows, N1, N2), jnp.float32)
        forward_rows(full_ref, part_rows, first_ref, turn_ref, second_ref, special_ref, mid_ref, out_ref)

    (spectral,) = call(
        transform,
        [(part_rows * N1, N2)],
        [points, const["first"], const["turn"], const["second"], const["special"]],
        [VMEM] * 5,
        [vmem(padded, N1, N2), vmem(padded * N1, N2)],
        part_rows * NLON * 256 * 4,
        "transform",
    )
    spectral = to_coefs(spectral, sharers, part_rows, groups)

    def edges(parity_ref, spec_ref, edge_ref, top_ref, bottom_ref, even_ref, odd_ref):
        top, bottom = edge_sums(
            rows_of(spec_ref, groups), rows_of(spec_ref, groups, OV - rows),
            rows_of(edge_ref, groups, -7), rows_of(edge_ref, groups, -14),
        )
        top_ref[...] = top
        bottom_ref[...] = bottom
        swap_out(parity_ref[0], top, bottom, even_ref, odd_ref)

    sent_top, sent_bottom, even, odd = call(
        edges, [row] * 4, [parity, spectral, edge], [SMEM, VMEM, VMEM], [], groups * N2 * 32, "edges"
    )
    even, odd = swap(even, odd)

    def first(parity_ref, spec_ref, even_ref, odd_ref, ratio_ref, inverse_ref, edge_ref, out_ref, e_ref, o_ref):
        low, high = swap_in(parity_ref[0], even_ref[...], odd_ref[...])
        solve_first(
            rows, groups, rows_of(spec_ref, groups), low, high, ratio_ref, inverse_ref, edge_ref, out_ref
        )
        swap_out(parity_ref[0], out_ref[(rows - 1) * groups :, :], out_ref[:groups, :], e_ref, o_ref)

    iterate, even2, odd2 = call(
        first,
        [block, row, row],
        [parity, spectral, even, odd, ratio, inverse, edge],
        [SMEM] + [VMEM] * 6,
        [],
        rows * groups * N2 * 8,
        "first_solve",
    )
    even2, odd2 = swap(even2, odd2)

    def second(parity_ref, *refs):
        second_part(rows, groups, parity_ref[0], *refs)

    (iterate,) = call(
        second,
        [block],
        [parity, couple, iterate, even, odd, even2, odd2, sent_top, sent_bottom, ratio, inverse, edge],
        [SMEM, SMEM] + [VMEM] * 10,
        [vmem(*block)],
        rows * groups * N2 * 8,
        "second_solve",
    )
    iterate = to_rows(iterate, sharers, part_rows, groups)

    def back(spec_ref, first_ref, turn_ref, second_ref, special_ref, out_ref, mid_ref, full_ref):
        backward_rows(spec_ref, part_rows, first_ref, turn_ref, second_ref, special_ref, mid_ref, full_ref)
        out_ref[...] = full_ref[:part_rows]

    (points,) = call(
        back,
        [(part_rows, N1, N2)],
        [iterate, const["first_back"], const["turn"], const["second_back"], const["special_back"]],
        [VMEM] * 5,
        [vmem(padded * N1, N2), vmem(padded, N1, N2)],
        part_rows * NLON * 256 * 4,
        "back_transform",
    )
    send = points.reshape(part_rows, lon_size, digits, N2).transpose(1, 0, 2, 3)
    got = lax.all_to_all(send, "lon", 0, 0, tiled=True)
    got = got.reshape(levels, sharers, part_rows, lon_count).transpose(1, 2, 0, 3)
    return got.reshape(rows, levels, lon_count)


def level_groups(sharers):
    size = lax.axis_size("lon")
    return [[first + i for i in range(sharers)] for first in range(0, size, sharers)]


def to_coefs(spectral, sharers, part_rows, groups):
    send = spectral.reshape(part_rows, 2, sharers, groups // 2, N2).transpose(2, 0, 1, 3, 4)
    got = lax.all_to_all(
        send, "lon", 0, 0, tiled=True, axis_index_groups=level_groups(sharers)
    )
    return got.reshape(sharers * part_rows * groups, N2)


def to_rows(values, sharers, part_rows, groups):
    send = values.reshape(sharers, part_rows, 2, groups // 2, N2)
    got = lax.all_to_all(
        send, "lon", 0, 0, tiled=True, axis_index_groups=level_groups(sharers)
    )
    return got.transpose(1, 2, 0, 3, 4).reshape(part_rows * N1, N2)


def solution(mesh):
    return jax.shard_map(
        on_device,
        mesh=mesh,
        in_specs=(P("lat", None, "lon"), P(), P(), P()),
        out_specs=P("lat", None, "lon"),
        check_vma=False,
    )
```

```python
import functools
import math

import jax
import jax.numpy as jnp
import numpy as np
from jax import lax
from jax.experimental import pallas as pl
from jax.experimental.pallas import tpu as pltpu
from jax.sharding import PartitionSpec as P

NLON = 4096
OV = 8
N1 = 32
N2 = 128
GROUPS = 16
BLOCK = 8

VMEM = pltpu.VMEM
SMEM = pltpu.SMEM


def numpy_split(table):
    import ml_dtypes

    table = np.asarray(table, np.float32)
    high = table.astype(ml_dtypes.bfloat16)
    low = (table - high.astype(np.float32)).astype(ml_dtypes.bfloat16)
    return high, low


def tables(levels):
    j1 = np.arange(N1)
    j2 = np.arange(N2)
    k2 = np.arange(N2)
    digit = np.arange(GROUPS)
    small = np.zeros((N1, N1))
    small[:GROUPS] = np.cos(2 * np.pi * np.outer(digit, j1) / N1)
    small[GROUPS] = np.cos(np.pi * j1)
    small[GROUPS + 1 :] = -np.sin(2 * np.pi * np.outer(digit[1:], j1) / N1)
    first = np.kron(np.eye(BLOCK), small)
    angle = 2 * np.pi * np.outer(digit, j2) / NLON
    turn_cos = np.cos(angle)
    turn_sin = np.sin(angle)
    phase = 2 * np.pi * (np.outer(j2, k2) % N2) / N2
    cosine, sine = np.cos(phase), np.sin(phase)
    second = np.block([[cosine, -sine], [sine, cosine]])
    special = np.zeros((2 * N2, 2 * N2))
    half = N2 // 2
    special[:N2, : half + 1] = np.cos(2 * np.pi * np.outer(j2, np.arange(half + 1)) / N2)
    special[:N2, half + 1 : N2] = -np.sin(2 * np.pi * np.outer(j2, np.arange(1, half)) / N2)
    odd = 2 * np.pi * np.outer(j2, 1 + 2 * np.arange(half)) / (2 * N2)
    special[N2:, N2 : N2 + half] = np.cos(odd)
    special[N2:, N2 + half :] = -np.sin(odd)
    weight = np.full(2 * N2, 2.0 / NLON)
    weight[0] = 1.0 / NLON
    weight[half] = 1.0 / NLON
    second_back = second.T * (2.0 / NLON)
    special_back = weight[:, None] * special.T
    wave = np.zeros((GROUPS, 2 * N2))
    wave[:, :N2] = digit[:, None] + N1 * k2[None, :]
    wave[:, N2:] = wave[:, :N2]
    lane = np.arange(N2)
    wave[0, :N2] = np.where(lane <= half, N1 * lane, N1 * (lane - half))
    wave[0, N2:] = 16 + N1 * (lane % half)
    eigen = 2.0 - 2.0 * np.cos(2 * np.pi * wave / NLON)
    pair = lambda t: np.concatenate(numpy_split(t), axis=0)
    width = N1 // levels
    part = [pair(np.kron(np.eye(BLOCK), small.T[at : at + width])) for at in range(0, N1, width)]
    return dict(
        first_back_part=np.concatenate(part, axis=0),
        first=pair(first),
        first_back=pair(first.T),
        second=pair(second),
        second_back=pair(second_back),
        special=pair(special),
        special_back=pair(special_back),
        turn=np.concatenate([turn_cos, turn_sin], axis=0).astype(np.float32),
        eigen=np.stack([eigen[:, :N2], eigen[:, N2:]]).astype(np.float32),
    )


def halves(value):
    high = value.astype(jnp.bfloat16)
    low = (value - high.astype(jnp.float32)).astype(jnp.bfloat16)
    return high, low


def dot(a, b):
    return lax.dot_general(a, b, (((1,), (0,)), ((), ())), preferred_element_type=jnp.float32)


def product_right(value, table_ref):
    size = table_ref.shape[0] // 2
    high, low = halves(value)
    table_high = table_ref[:size, :]
    return dot(high, table_high) + dot(low, table_high) + dot(high, table_ref[size:, :])


def product_left(table_ref, value):
    size = table_ref.shape[0] // 2
    high, low = halves(value)
    both = dot(table_ref[...], high)
    return both[:size] + both[size:] + dot(table_ref[:size, :], low)


def lanes_apart(value, rows):
    real = value[:, :N2].reshape(rows, GROUPS, N2)
    imag = value[:, N2:].reshape(rows, GROUPS, N2)
    return jnp.concatenate([real, imag], axis=1).reshape(rows * 2 * GROUPS, N2)


def lanes_together(value, rows):
    both = value.reshape(rows, 2 * GROUPS, N2)
    return jnp.concatenate([both[:, :GROUPS], both[:, GROUPS:]], axis=2).reshape(rows * GROUPS, 2 * N2)


def load_zeroth(ref, rows):
    return jnp.concatenate(
        [ref[pl.ds(0, rows, stride=2 * GROUPS), :], ref[pl.ds(GROUPS, rows, stride=2 * GROUPS), :]], axis=1
    )


def store_zeroth(ref, rows, value):
    ref[pl.ds(0, rows, stride=2 * GROUPS), :] = value[:, :N2]
    ref[pl.ds(GROUPS, rows, stride=2 * GROUPS), :] = value[:, N2:]


def forward_rows(points_ref, rows, first_ref, turn_ref, second_ref, special_ref, mid_ref, out_ref):
    padded = points_ref.shape[0]
    turn_cos = turn_ref[:GROUPS, :][None]
    turn_sin = turn_ref[GROUPS:, :][None]
    for pair in range(padded // (2 * BLOCK)):
        base = pair * 2 * BLOCK
        left = points_ref[base : base + BLOCK].reshape(BLOCK * N1, N2)
        right = points_ref[base + BLOCK : base + 2 * BLOCK].reshape(BLOCK * N1, N2)
        value = product_left(first_ref, jnp.concatenate([left, right], axis=1))
        for side in range(2):
            digits = value[:, side * N2 : (side + 1) * N2].reshape(BLOCK, N1, N2)
            real, imag = digits[:, :GROUPS], digits[:, GROUPS:]
            turned = jnp.concatenate(
                [real * turn_cos + imag * turn_sin, imag * turn_cos - real * turn_sin], axis=1
            )
            at = (base + side * BLOCK) * N1
            mid_ref[at : at + BLOCK * N1, :] = turned.reshape(BLOCK * N1, N2)
    result = product_right(lanes_together(mid_ref[...], padded), second_ref)
    out_ref[...] = lanes_apart(result, padded)[: rows * N1]
    store_zeroth(out_ref, rows, product_right(load_zeroth(mid_ref, padded), special_ref)[:rows])


def spectral_back(spec_ref, rows, padded, second_ref, special_ref, mid_ref):
    result = product_right(lanes_together(spec_ref[...], rows), second_ref)
    mid_ref[: rows * N1, :] = lanes_apart(result, rows)
    if padded > rows:
        mid_ref[rows * N1 : padded * N1, :] = jnp.zeros(((padded - rows) * N1, N2), jnp.float32)
    store_zeroth(mid_ref, rows, product_right(load_zeroth(spec_ref, rows), special_ref))


def digits_back(mid_ref, pair, turn_ref, first_ref):
    turn_cos = turn_ref[:GROUPS, :][None]
    turn_sin = turn_ref[GROUPS:, :][None]
    sides = []
    for side in range(2):
        at = (2 * pair + side) * BLOCK * N1
        both = mid_ref[at : at + BLOCK * N1, :].reshape(BLOCK, N1, N2)
        real, imag = both[:, :GROUPS], both[:, GROUPS:]
        turned = jnp.concatenate(
            [real * turn_cos - imag * turn_sin, imag * turn_cos + real * turn_sin], axis=1
        )
        sides.append(turned.reshape(BLOCK * N1, N2))
    return product_left(first_ref, jnp.concatenate(sides, axis=1))


def backward_rows(spec_ref, rows, first_ref, turn_ref, second_ref, special_ref, mid_ref, out_ref):
    padded = out_ref.shape[0]
    spectral_back(spec_ref, rows, padded, second_ref, special_ref, mid_ref)
    for pair in range(padded // (2 * BLOCK)):
        base = pair * 2 * BLOCK
        value = digits_back(mid_ref, pair, turn_ref, first_ref)
        out_ref[base : base + BLOCK] = value[:, :N2].reshape(BLOCK, N1, N2)
        out_ref[base + BLOCK : base + 2 * BLOCK] = value[:, N2:].reshape(BLOCK, N1, N2)


def factor_kernel(rows, lon_ref, couple_ref, eigen_ref, ratio_ref, inverse_ref, edge_ref):
    eigen = eigen_ref[...]
    groups = eigen.shape[0]
    half = rows // 2
    last = rows + 2 * OV - 1

    def plain(e):
        return 1.0 + lon_ref[e] * eigen

    def put(ref, index, value):
        ref[index * groups : (index + 1) * groups, :] = value

    def chain(start, stop, step, into):
        excess = inverse = None
        for e in range(start, stop + step, step):
            before = couple_ref[e] if step > 0 else couple_ref[e + 1]
            after = couple_ref[e + 1] if step > 0 else couple_ref[e]
            if inverse is None:
                ratio = None
                excess = plain(e) + before
            else:
                ratio = before * inverse
                excess = plain(e) + ratio * excess
            divisor = after + excess
            inverse = 1.0 / divisor
            into(e, ratio, inverse, excess, divisor)

    kept = {}

    def top(e, ratio, inverse, excess, divisor):
        if e == OV - 1:
            put(edge_ref, 0, inverse)
        if e >= OV:
            put(ratio_ref, e - OV, ratio)
            put(inverse_ref, e - OV, inverse)
        if e == OV + half - 1:
            kept["top"] = excess, divisor

    def bottom(e, ratio, inverse, excess, divisor):
        if e == OV + rows:
            put(edge_ref, 1, inverse)
        if e < OV + rows:
            put(ratio_ref, e - OV, ratio)
            put(inverse_ref, e - OV, inverse)
        if e == OV + half:
            kept["bottom"] = excess, divisor

    def next_band(e, ratio, inverse, excess, divisor):
        if ratio is not None:
            put(edge_ref, 7 + e - rows - 1, ratio)
        if e == OV + rows - 1:
            put(edge_ref, 5, inverse)

    def previous_band(e, ratio, inverse, excess, divisor):
        if ratio is not None:
            put(edge_ref, 14 + e - OV, ratio)
        if e == OV:
            put(edge_ref, 6, inverse)

    chain(rows, OV + rows - 1, 1, next_band)
    chain(2 * OV - 1, OV, -1, previous_band)
    chain(0, OV + half - 1, 1, top)
    chain(last, OV + half, -1, bottom)
    excess_top, divisor_top = kept["top"]
    excess_bottom, divisor_bottom = kept["bottom"]
    between = couple_ref[OV + half]
    inverse = 1.0 / (between * (excess_top + excess_bottom) + excess_top * excess_bottom)
    put(edge_ref, 2, divisor_bottom * inverse)
    put(edge_ref, 3, divisor_top * inverse)
    put(edge_ref, 4, between * inverse)


def edge_sums(low_rows, high_rows, next_ratio, previous_ratio):
    top = high_rows(0)
    for i in range(1, OV):
        top = high_rows(i) + next_ratio(i - 1) * top
    bottom = low_rows(OV - 1)
    for i in range(OV - 2, -1, -1):
        bottom = low_rows(i) + previous_ratio(i) * bottom
    return top, bottom


def swap_out(parity, up, down, even_ref, odd_ref):
    is_even = parity == 0
    even_ref[...] = jnp.where(is_even, up, down)
    odd_ref[...] = jnp.where(is_even, down, up)


def swap_in(parity, even, odd):
    is_even = parity == 0
    return jnp.where(is_even, odd, even), jnp.where(is_even, even, odd)


def solve_first(rows, groups, right_side_row, from_low, from_high, ratio_ref, inverse_ref, edge_ref, out_ref):
    half = rows // 2

    def at(ref, index):
        return ref[index * groups : (index + 1) * groups, :]

    def put(index, value):
        out_ref[index * groups : (index + 1) * groups, :] = value

    low, high = from_low, from_high
    for i in range(half):
        j = rows - 1 - i
        low = right_side_row(i) + at(ratio_ref, i) * low
        high = right_side_row(j) + at(ratio_ref, j) * high
        put(i, low)
        put(j, high)
    meet(rows, groups, low, high, ratio_ref, inverse_ref, edge_ref, at, lambda i: at(out_ref, i), put)


def meet(rows, groups, low, high, ratio_ref, inverse_ref, edge_ref, at, value, put):
    half = rows // 2
    between = at(edge_ref, 4)
    x_low = at(edge_ref, 2) * low + between * high
    x_high = at(edge_ref, 3) * high + between * low
    put(half - 1, x_low)
    put(half, x_high)
    for i in range(half - 2, -1, -1):
        j = rows - 1 - i
        x_low = value(i) * at(inverse_ref, i) + at(ratio_ref, i + 1) * x_low
        x_high = value(j) * at(inverse_ref, j) + at(ratio_ref, j - 1) * x_high
        put(i, x_low)
        put(j, x_high)


def sigmas(
    couple_low, couple_high, own_top, own_bottom, got_top, got_bottom, sent_top, sent_bottom, from_low, from_high,
    ratio_first, ratio_last, edge_ref, next_inverse, previous_inverse,
):
    groups = own_top.shape[0]

    def edge(index):
        return edge_ref[index * groups : (index + 1) * groups, :]

    beyond_low = (got_top + couple_low * own_top) * edge(0)
    beyond_high = (got_bottom + couple_high * own_bottom) * edge(1)
    theirs_low = (sent_bottom + couple_low * from_low) * previous_inverse
    theirs_high = (sent_top + couple_high * from_high) * next_inverse
    low = ratio_first * (couple_low * (own_top - theirs_low)) + couple_low * (from_low - beyond_low)
    high = ratio_last * (couple_high * (own_bottom - theirs_high)) + couple_high * (from_high - beyond_high)
    return low, high


def solve_second(
    rows, groups, couple_low, couple_high, own_top, own_bottom, got_top, got_bottom, sent_top, sent_bottom,
    from_low, from_high, ratio_ref, inverse_ref, edge_ref, first_ref, out_ref, mid_ref,
):
    half = rows // 2

    def at(ref, index):
        return ref[index * groups : (index + 1) * groups, :]

    low, high = sigmas(
        couple_low, couple_high, own_top, own_bottom, got_top, got_bottom, sent_top, sent_bottom,
        from_low, from_high, at(ratio_ref, 0), at(ratio_ref, rows - 1), edge_ref, at(edge_ref, 5), at(edge_ref, 6),
    )
    for i in range(half):
        j = rows - 1 - i
        if i:
            low = at(ratio_ref, i) * low
            high = at(ratio_ref, j) * high
        mid_ref[i * groups : (i + 1) * groups, :] = low
        mid_ref[j * groups : (j + 1) * groups, :] = high

    def put(index, value):
        rows_at = slice(index * groups, (index + 1) * groups)
        out_ref[rows_at, :] = first_ref[rows_at, :] + value

    meet(rows, groups, low, high, ratio_ref, inverse_ref, edge_ref, at, lambda i: at(mid_ref, i), put)


def call(body, outs, ins, spaces, scratch, flops, name, out_spaces=None, aliases=None):
    nbytes = sum(x.size * x.dtype.itemsize for x in ins) + sum(4 * math.prod(s) for s in outs)
    out = pl.pallas_call(
        body,
        out_shape=[jax.ShapeDtypeStruct(s, jnp.float32) for s in outs],
        in_specs=[pl.BlockSpec(memory_space=s) for s in spaces],
        out_specs=[pl.BlockSpec(memory_space=s) for s in out_spaces or [VMEM] * len(outs)],
        input_output_aliases=aliases or {},
        scratch_shapes=scratch,
        compiler_params=pltpu.CompilerParams(vmem_limit_bytes=32 << 20),
        cost_estimate=pl.CostEstimate(flops=flops, bytes_accessed=nbytes, transcendentals=0),
        name=name,
    )(*ins)
    return out


def pad_rows(rows):
    return -(-rows // (2 * BLOCK)) * 2 * BLOCK


def swap(value_even, value_odd):
    count = lax.axis_size("lat")
    even = [(i, i ^ 1) for i in range(count) if (i ^ 1) < count]
    odd = [(i, ((i + 1) ^ 1) - 1) for i in range(1, count) if ((i + 1) ^ 1) - 1 < count]
    value_odd = lax.ppermute(value_odd, "lat", odd)
    return lax.ppermute(value_even, "lat", even), value_odd


def send_level(piece, mask, size):
    return lax.ppermute(piece, "lon", [(d, d ^ mask) for d in range(size)])


def swap_levels(pieces):
    return [pieces[0]] + [send_level(pieces[mask], mask, len(pieces)) for mask in range(1, len(pieces))]


def operator_parts(rows, lon_coef, lat_coef, level_scale):
    row_first = lax.axis_index("lat") * rows
    extent = rows + 2 * OV
    lon_window = lax.dynamic_slice_in_dim(jnp.pad(lon_coef, (OV, OV)), row_first, extent)
    couple = lax.dynamic_slice_in_dim(jnp.pad(lat_coef, (OV + 1, OV + 2)), row_first, extent + 1)
    return level_scale[:, None] * lon_window[None], level_scale[:, None] * couple[None]


def factor(rows, groups, lon_window, couple, eigen):
    block = (rows * groups, N2)
    return call(
        functools.partial(factor_kernel, rows),
        [block, block, (21 * groups, N2)],
        [lon_window, couple, eigen],
        [SMEM, SMEM, VMEM],
        [],
        rows * groups * N2 * 20,
        "factor",
    )


def vmem(*shape):
    return pltpu.VMEM(shape, jnp.float32)


def rows_of(ref, groups, first=0):
    return lambda i: ref[(i - first) * groups : (i - first + 1) * groups, :]


def on_device(right_side, lon_coef, lat_coef, level_scale):
    const = {k: jnp.asarray(v) for k, v in tables(right_side.shape[1]).items()}
    if lax.axis_size("lon") != right_side.shape[1]:
        return shared_levels(const, right_side, lon_coef, lat_coef, level_scale)
    return whole_levels(const, right_side, lon_coef, lat_coef, level_scale)


def early_rows(rows):
    return rows // 2 + 6


def lon_here():
    return lax.axis_index("lon").astype(jnp.int32)


def parity_here():
    return lax.axis_index("lat").astype(jnp.int32) % 2


def edge_kernel(rows, lon_ref, couple_ref, eigen_ref, out_ref):
    eigen = eigen_ref[...]
    groups = eigen.shape[0]
    level = lon_here()
    low = high = low_inverse = high_inverse = None
    for i in range(OV):
        e, f = rows + i, 2 * OV - 1 - i
        if i == 0:
            low = 1.0 + lon_ref[level, e : e + 1, :] * eigen + couple_ref[level, e : e + 1, :]
            high = 1.0 + lon_ref[level, f : f + 1, :] * eigen + couple_ref[level, f + 1 : f + 2, :]
        else:
            low_ratio = couple_ref[level, e : e + 1, :] * low_inverse
            high_ratio = couple_ref[level, f + 1 : f + 2, :] * high_inverse
            out_ref[(i - 1) * groups : i * groups, :] = low_ratio
            out_ref[(OV + i - 1) * groups : (OV + i) * groups, :] = high_ratio
            low = 1.0 + lon_ref[level, e : e + 1, :] * eigen + low_ratio * low
            high = 1.0 + lon_ref[level, f : f + 1, :] * eigen + high_ratio * high
        low_inverse = 1.0 / (couple_ref[level, e + 1 : e + 2, :] + low)
        high_inverse = 1.0 / (couple_ref[level, f : f + 1, :] + high)
    out_ref[(OV - 1) * groups : OV * groups, :] = low_inverse
    out_ref[(2 * OV - 1) * groups : 2 * OV * groups, :] = high_inverse
    out_ref[2 * OV * groups : (2 * OV + 1) * groups, :] = jnp.broadcast_to(couple_ref[level, OV : OV + 1, :], eigen.shape)
    out_ref[(2 * OV + 1) * groups :, :] = jnp.broadcast_to(
        couple_ref[level, OV + rows : OV + rows + 1, :], eigen.shape
    )


def level_response(rows, early, level, lon_ref, couple_ref, eigen, put_ratio, put_inverse, keep, tables):
    half = rows // 2
    ratio_at, value_at, put_value, put_phi, put_psi = tables

    def plain(e):
        return 1.0 + lon_ref[level, e : e + 1, :] * eigen

    low = high = None
    low_inverse = high_inverse = low_value = high_value = None
    for i in range(-OV, half):
        j = rows - 1 - i
        e, f = i + OV, j + OV
        if low is None:
            low = plain(e) + couple_ref[level, e : e + 1, :]
            high = plain(f) + couple_ref[level, f + 1 : f + 2, :]
        else:
            low_ratio = couple_ref[level, e : e + 1, :] * low_inverse
            high_ratio = couple_ref[level, f + 1 : f + 2, :] * high_inverse
            low = plain(e) + low_ratio * low
            high = plain(f) + high_ratio * high
        low_divisor = couple_ref[level, e + 1 : e + 2, :] + low
        high_divisor = couple_ref[level, f : f + 1, :] + high
        low_inverse = 1.0 / low_divisor
        high_inverse = 1.0 / high_divisor
        yield
        if i == -1:
            keep(0, low_inverse)
            keep(1, high_inverse)
        if i == 0:
            low_value = high_value = jnp.ones_like(eigen)
        elif i > 0:
            low_value = low_ratio * low_value
            high_value = high_ratio * high_value
        if i >= 0:
            put_ratio(i, low_ratio)
            put_ratio(j, high_ratio)
            put_inverse(i, low_inverse)
            put_inverse(j, high_inverse)
            put_value(i, low_value * low_inverse)
            if j < early:
                put_value(j, high_value * high_inverse)
    between = couple_ref[level, OV + half : OV + half + 1, :]
    inverse = 1.0 / (between * (low + high) + low * high)
    across = between * inverse
    high_inverse = high_divisor * inverse
    low_inverse = low_divisor * inverse
    keep(2, high_inverse)
    keep(3, low_inverse)
    keep(4, across)
    phi = high_inverse * low_value
    psi = across * high_value
    phi_down = across * low_value
    psi_down = low_inverse * high_value
    put_phi(half - 1, phi)
    put_psi(half - 1, psi)
    for i in range(half - 2, -1, -1):
        yield
        ratio = ratio_at(i + 1)
        phi = value_at(i) + ratio * phi
        psi = ratio * psi
        put_phi(i, phi)
        put_psi(i, psi)
    put_phi(half, phi_down)
    put_psi(half, psi_down)
    for j in range(half + 1, early):
        ratio = ratio_at(j - 1)
        phi_down = ratio * phi_down
        psi_down = value_at(j) + ratio * psi_down
        put_phi(j, phi_down)
        put_psi(j, psi_down)


def getter(ref, groups):
    return lambda index: ref[index * groups : (index + 1) * groups, :]


def putter(ref, groups, first=0):
    def put(index, value):
        at = first + index * groups
        ref[pl.ds(at if isinstance(at, int) else pl.multiple_of(at, groups), groups), :] = value

    return put


def together(*steps):
    steps = list(steps)
    while steps:
        steps = [step for step in steps if next(step, steps) is not steps]


def partner_response(rows, early, lon_ref, couple_ref, eigen, masks, phi_ref, psi_ref, kept_refs, value_refs):
    groups = eigen.shape[0]

    def nothing(index, value):
        pass

    def one(n, mask):
        put_kept = putter(kept_refs[n], groups)

        def put_ratio(index, value):
            if index < early:
                put_kept(index, value)

        first = n * early * groups
        return level_response(
            rows, early, lon_here() ^ mask, lon_ref, couple_ref, eigen, put_ratio, nothing, nothing,
            (
                getter(kept_refs[n], groups), getter(value_refs[n], groups), putter(value_refs[n], groups),
                putter(phi_ref, groups, first), putter(psi_ref, groups, first),
            ),
        )

    return [one(n, mask) for n, mask in enumerate(masks)]


def own_kernel(
    rows, early, masks, lon_ref, couple_ref, eigen_ref, ratio_ref, inverse_ref, edge_ref, phi_ref, psi_ref,
    phi_near_ref, psi_near_ref, value_ref, *refs,
):
    eigen = eigen_ref[...]
    groups = eigen.shape[0]
    own = level_response(
        rows, early, lon_here(), lon_ref, couple_ref, eigen, putter(ratio_ref, groups),
        putter(inverse_ref, groups), putter(edge_ref, groups),
        (
            getter(ratio_ref, groups), getter(value_ref, groups), putter(value_ref, groups),
            putter(phi_ref, groups), putter(psi_ref, groups),
        ),
    )
    count = len(masks)
    together(
        own,
        *partner_response(
            rows, early, lon_ref, couple_ref, eigen, masks, phi_near_ref, psi_near_ref,
            refs[:count], refs[count:],
        ),
    )


def partners_kernel(
    rows, early, masks, lon_ref, couple_ref, eigen_ref, after_ref, phi_ref, psi_ref, token_ref, *refs
):
    token_ref[...] = after_ref[...]
    count = len(masks)
    together(
        *partner_response(
            rows, early, lon_ref, couple_ref, eigen_ref[...], masks, phi_ref, psi_ref,
            refs[:count], refs[count:],
        )
    )


def whole_levels(const, right_side, lon_coef, lat_coef, level_scale):
    rows, levels, lon_count = right_side.shape
    digits = N1 // levels
    groups = 2 * GROUPS
    half = rows // 2
    early = early_rows(rows)
    late = rows - early
    eigen = const["eigen"].reshape(groups, N2)
    lon_all, couple_all = operator_parts(rows, lon_coef, lat_coef, level_scale)
    lon_all = jnp.broadcast_to(lon_all[:, :, None], (*lon_all.shape, N2))
    couple_all = jnp.broadcast_to(couple_all[:, :, None], (*couple_all.shape, N2))
    (around,) = call(
        functools.partial(edge_kernel, rows),
        [((2 * OV + 2) * groups, N2)],
        [lon_all, couple_all, eigen],
        [VMEM, VMEM, VMEM],
        [],
        16 * groups * N2 * 20,
        "edge",
    )
    block = (rows * groups, N2)
    early_block = (early * groups, N2)
    early_block = (early * groups, N2)
    near_masks, far_masks = [1], list(range(2, levels))
    ratio, inverse, edge, phi, psi, phi_near, psi_near = call(
        functools.partial(own_kernel, rows, early, near_masks),
        [block, block, (5 * groups, N2)] + [early_block] * 4,
        [lon_all, couple_all, eigen],
        [VMEM, VMEM, VMEM],
        [vmem(*early_block)] * 3,
        2 * rows * groups * N2 * 20,
        "own",
    )
    row = (groups, N2)
    ends = 2 * OV
    inner = rows - ends
    span = OV * digits
    by_row = right_side.reshape(rows, levels, digits, N2).transpose(0, 2, 1, 3).reshape(-1, N2)

    far = list(range(2, levels))

    def pack_ends(in_ref, *refs):
        for end_ref, mask in zip(refs, [0] + far):
            level = lon_here() ^ mask
            end_ref[:span, :] = in_ref[pl.ds(level, span, stride=levels), :]
            end_ref[span:, :] = in_ref[pl.ds(level + levels * (rows - OV) * digits, span, stride=levels), :]

    end_packed = call(
        pack_ends,
        [(ends * digits, N2)] * (levels - 1),
        [by_row],
        [VMEM],
        [],
        0,
        "pack_ends",
    )

    def pack(in_ref, after_ref, *refs):
        del after_ref
        for mask, out_ref in enumerate(refs):
            level = lon_here() ^ mask
            skip = 0 if mask == 1 else levels * span
            out_ref[...] = in_ref[pl.ds(level + skip, out_ref.shape[0], stride=levels), :]

    packed = call(
        pack,
        [((rows if mask == 1 else inner) * digits, N2) for mask in range(levels)],
        [by_row, end_packed[0]],
        [VMEM, pl.ANY],
        [],
        0,
        "pack",
    )
    end_pieces = [end_packed[0], None] + [send_level(p, m, levels) for p, m in zip(end_packed[1:], far)]
    near = send_level(packed[1], 1, levels)
    end_pieces[1] = near
    inner_pieces = [packed[0], near] + [send_level(packed[m], m, levels) for m in far]
    forward = [const["first"], const["turn"], const["second"], const["special"]]
    pad_ends, pad_inner = pad_rows(ends), pad_rows(inner)

    def ends_body(*refs):
        pieces, refs = refs[:levels], refs[levels:]
        tables_in, edge_ref = refs[:4], refs[4]
        spec_ref, top_ref, bottom_ref, even_ref, odd_ref, full_ref, mid_ref = refs[5:]
        for mask, piece in enumerate(pieces):
            at = pl.multiple_of((lon_here() ^ mask) * digits, digits)
            last = piece.shape[0] - span
            full_ref[:OV, pl.ds(at, digits), :] = piece[:span, :].reshape(OV, digits, N2)
            full_ref[OV:ends, pl.ds(at, digits), :] = piece[last:, :].reshape(OV, digits, N2)
        forward_rows(full_ref, ends, *tables_in, mid_ref, spec_ref)
        top, bottom = edge_sums(
            rows_of(spec_ref, groups), rows_of(spec_ref, groups, -OV),
            rows_of(edge_ref, groups), lambda i: edge_ref[(2 * OV - 2 - i) * groups : (2 * OV - 1 - i) * groups, :],
        )
        top_ref[...] = top
        bottom_ref[...] = bottom
        swap_out(parity_here(), top, bottom, even_ref, odd_ref)

    end_spectral, sent_top, sent_bottom, even, odd = call(
        ends_body,
        [(ends * groups, N2)] + [row] * 4,
        [*end_pieces, *forward, around],
        [VMEM] * (levels + 5),
        [vmem(pad_ends, N1, N2), vmem(pad_ends * N1, N2)],
        ends * NLON * 256 * 4,
        "ends",
    )
    even, odd = swap(even, odd)
    backward = [const["first_back"], const["turn"], const["second_back"], const["special_back"]]
    pad_early, pad_late = pad_rows(early), pad_rows(late)

    def spread(full_ref, count, out_refs):
        for mask, out_ref in enumerate(out_refs):
            at = pl.multiple_of((lon_here() ^ mask) * digits, digits)
            out_ref[...] = full_ref[:count, pl.ds(at, digits), :].reshape(count * digits, N2)

    def inner_body(*refs):
        pieces, refs = refs[:levels], refs[levels:]
        tables_in, back_in, refs = refs[:4], refs[4:7], refs[7:]
        ends_ref, even_ref, odd_ref, ratio_ref, inverse_ref, edge_ref = refs[:6]
        late_ref, top_ref, even_out, odd_out = refs[6:10]
        early_refs, refs = refs[10 : 10 + levels], refs[10 + levels :]
        full_ref, mid_ref, spec_ref, sum_ref, back_full_ref, back_mid_ref = refs
        for mask, piece in enumerate(pieces):
            at = pl.multiple_of((lon_here() ^ mask) * digits, digits)
            skip = span if mask == 1 else 0
            full_ref[:inner, pl.ds(at, digits), :] = piece[skip : skip + inner * digits, :].reshape(
                inner, digits, N2
            )
        if pad_inner > inner:
            full_ref[inner:] = jnp.zeros((pad_inner - inner, N1, N2), jnp.float32)
        forward_rows(full_ref, inner, *tables_in, mid_ref, spec_ref)
        low, high = swap_in(parity_here(), even_ref[...], odd_ref[...])

        def spec_row(i):
            if i < OV:
                return rows_of(ends_ref, groups)(i)
            if i >= rows - OV:
                return rows_of(ends_ref, groups, rows - ends)(i)
            return rows_of(spec_ref, groups, OV)(i)

        solve_first(rows, groups, spec_row, low, high, ratio_ref, inverse_ref, edge_ref, sum_ref)
        top = sum_ref[:groups, :]
        top_ref[...] = top
        late_ref[...] = sum_ref[early * groups :, :]
        swap_out(parity_here(), sum_ref[(rows - 1) * groups :, :], top, even_out, odd_out)
        early_sum = sum_ref.at[pl.ds(0, early * groups), :]
        backward_rows(early_sum, early, back_in[0], tables_in[1], back_in[1], back_in[2], back_mid_ref, back_full_ref)
        spread(back_full_ref, early, early_refs)

    late_first, own_top, even2, odd2, *early_pieces = call(
        inner_body,
        [(late * groups, N2), row, row, row] + [(early * digits, N2)] * levels,
        [
            *inner_pieces, *forward, backward[0], backward[2], backward[3],
            end_spectral, even, odd, ratio, inverse, edge,
        ],
        [VMEM] * (levels + 13),
        [
            vmem(pad_inner, N1, N2), vmem(pad_inner * N1, N2), vmem(inner * N1, N2), vmem(rows * groups, N2),
            vmem(pad_early, N1, N2), vmem(pad_early * N1, N2),
        ],
        (inner + early) * NLON * 256 * 4,
        "inner",
    )
    early_pieces = swap_levels(early_pieces)
    even2, odd2 = swap(even2, odd2)

    phi_far, psi_far, token = call(
        functools.partial(partners_kernel, rows, early, far_masks),
        [(len(far_masks) * early * groups, N2)] * 2 + [row],
        [lon_all, couple_all, eigen, own_top],
        [VMEM, VMEM, VMEM, VMEM],
        [vmem(*early_block)] * (2 * len(far_masks)),
        len(far_masks) * rows * groups * N2 * 20,
        "partners",
    )

    def sigma_body(*refs):
        first_ref, own_top_ref, even_ref, odd_ref, even2_ref, odd2_ref, top_ref, bottom_ref = refs[:8]
        ratio_ref, edge_ref, around_ref = refs[8:11]
        sigma_ref = refs[-1]
        got_top, got_bottom = swap_in(parity_here(), even_ref[...], odd_ref[...])
        from_low, from_high = swap_in(parity_here(), even2_ref[...], odd2_ref[...])
        low, high = sigmas(
            around_ref[2 * OV * groups : (2 * OV + 1) * groups, :], around_ref[(2 * OV + 1) * groups :, :], own_top_ref[...], first_ref[(late - 1) * groups :, :],
            got_top, got_bottom, top_ref[...], bottom_ref[...], from_low, from_high,
            ratio_ref[:groups, :], ratio_ref[(rows - 1) * groups :, :], edge_ref,
            around_ref[(OV - 1) * groups : OV * groups, :],
            around_ref[(2 * OV - 1) * groups : 2 * OV * groups, :],
        )
        sigma_ref[:groups, :] = low
        sigma_ref[groups:, :] = high

    (sigma,) = call(
        sigma_body,
        [(2 * groups, N2)],
        [
            late_first, own_top, even, odd, even2, odd2, sent_top, sent_bottom, ratio, edge, around,
            *early_pieces[1:], token,
        ],
        [VMEM] * 11 + [pl.ANY] * levels,
        [],
        groups * N2 * 40,
        "sigma",
    )
    sigma_pieces = swap_levels([sigma] * levels)
    def second_body(*refs):
        sigma_ref, first_ref, ratio_ref, inverse_ref, edge_ref = refs[:5]
        tables_in, refs = refs[5:9], refs[9:]
        late_refs = refs[:levels]
        sum_ref, mid_ref, full_ref = refs[levels:]
        low, high = sigma_ref[:groups, :], sigma_ref[groups:, :]

        def at(ref, index):
            return ref[index * groups : (index + 1) * groups, :]

        for i in range(half):
            j = rows - 1 - i
            if i:
                low = at(ratio_ref, i) * low
                high = at(ratio_ref, j) * high
            mid_ref[(j - half) * groups : (j - half + 1) * groups, :] = high
        x_high = at(edge_ref, 3) * high + at(edge_ref, 4) * low
        for j in range(half, rows):
            if j > half:
                x_high = at(mid_ref, j - half) * at(inverse_ref, j) + at(ratio_ref, j - 1) * x_high
            if j >= early:
                here = slice((j - early) * groups, (j - early + 1) * groups)
                sum_ref[here, :] = first_ref[here, :] + x_high
        backward_rows(sum_ref, late, *tables_in, mid_ref, full_ref)
        spread(full_ref, late, late_refs)

    late_pieces = call(
        second_body,
        [(late * digits, N2)] * levels,
        [sigma, late_first, ratio, inverse, edge, *backward],
        [VMEM] * 9,
        [vmem(late * groups, N2), vmem(max(pad_late, half) * N1, N2), vmem(pad_late, N1, N2)],
        late * NLON * 256 * 4,
        "second",
    )
    late_pieces = swap_levels(late_pieces)
    total = rows * levels * digits
    early_total = early * levels * digits
    part = const["first_back_part"]

    def correct(*refs):
        pieces, sigma_refs, refs = refs[:levels], refs[levels : 2 * levels], refs[2 * levels :]
        responses, refs = refs[:6], refs[6:]
        part_ref, turn_ref, second_ref, special_ref = refs[:4]
        out_ref, done_ref, sems, *mid_refs = refs[4:]
        part_rows = part_ref.shape[0] // levels
        mine = part_ref.at[pl.ds(pl.multiple_of(lon_here() * part_rows, part_rows), part_rows), :]
        size = early * groups
        copies = []
        for mask in range(levels):
            level = lon_here() ^ mask
            mid_ref = mid_refs[mask % 2]
            low, high = sigma_refs[mask][:groups, :], sigma_refs[mask][groups:, :]
            phi_ref, psi_ref = responses[2 * min(mask, 2) : 2 * min(mask, 2) + 2]
            first = max(mask - 2, 0) * size
            here = pl.ds(first, size)
            phi_ref, psi_ref = phi_ref.at[here, :], psi_ref.at[here, :]
            phi_all = phi_ref[...].reshape(early, groups, N2)
            psi_all = psi_ref[...].reshape(early, groups, N2)
            value = (phi_all * low[None] + psi_all * high[None]).reshape(size, N2)
            mid_ref[:size, :] = lanes_apart(product_right(lanes_together(value, early), second_ref), early)
            if pad_early > early:
                mid_ref[size:, :] = jnp.zeros((pad_early * groups - size, N2), jnp.float32)
            zeroth_low = jnp.concatenate([low[:1], low[GROUPS : GROUPS + 1]], axis=1)
            zeroth_high = jnp.concatenate([high[:1], high[GROUPS : GROUPS + 1]], axis=1)
            zeroth = load_zeroth(phi_ref, early) * zeroth_low + load_zeroth(psi_ref, early) * zeroth_high
            store_zeroth(mid_ref, early, product_right(zeroth, special_ref))
            for pair in range(pad_early // (2 * BLOCK)):
                value = digits_back(mid_ref, pair, turn_ref, mine)
                for side in range(2):
                    begin = (2 * pair + side) * BLOCK
                    count = min(BLOCK, early - begin)
                    if count <= 0:
                        continue
                    lines = count * digits
                    whole = pieces[mask][begin * digits : begin * digits + lines, :]
                    done_ref[pl.ds(level + begin * digits * levels, lines, stride=levels), :] = (
                        whole + value[:lines, side * N2 : (side + 1) * N2]
                    )
                if mask == levels - 1:
                    begin = 2 * pair * BLOCK * digits * levels
                    lines = min(2 * BLOCK * digits * levels, early_total - begin)
                    there = pl.ds(begin, lines)
                    copy = pltpu.make_async_copy(done_ref.at[there, :], out_ref.at[there, :], sems.at[pair])
                    copy.start()
                    copies.append(copy)
        for copy in copies:
            copy.wait()

    (out,) = call(
        correct,
        [(total, N2)],
        [
            *early_pieces, *sigma_pieces, phi, psi, phi_near, psi_near, phi_far, psi_far,
            part, const["turn"], *backward[2:],
        ],
        [VMEM] * (2 * levels + 10),
        [
            vmem(early_total, N2), pltpu.SemaphoreType.DMA((pad_early // (2 * BLOCK),)),
            vmem(pad_early * N1, N2), vmem(pad_early * N1, N2),
        ],
        levels * early * NLON * 256 * 40,
        "correct",
        out_spaces=[pl.ANY],
    )

    chunks = 2

    def unpack(*refs):
        pieces = refs[:levels]
        out_ref, done_ref, sems = refs[levels + 1 :]
        lines = late * digits // chunks
        copies = []
        for chunk in range(chunks):
            for mask in range(levels):
                first = (lon_here() ^ mask) + chunk * lines * levels
                done_ref[pl.ds(first, lines, stride=levels), :] = pieces[mask][chunk * lines : (chunk + 1) * lines, :]
            here = pl.ds(chunk * lines * levels, lines * levels)
            there = pl.ds(early_total + chunk * lines * levels, lines * levels)
            copy = pltpu.make_async_copy(done_ref.at[here, :], out_ref.at[there, :], sems.at[chunk])
            copy.start()
            copies.append(copy)
        for copy in copies:
            copy.wait()

    (out,) = call(
        unpack,
        [(total, N2)],
        [*late_pieces, out],
        [VMEM] * levels + [pl.ANY],
        [vmem(total - early_total, N2), pltpu.SemaphoreType.DMA((chunks,))],
        0,
        "unpack",
        out_spaces=[pl.ANY],
        aliases={levels: 0},
    )
    return out.reshape(rows, digits, levels, N2).transpose(0, 2, 1, 3).reshape(right_side.shape)


def second_part(
    rows, groups, parity, couple_ref, first_ref, even_ref, odd_ref, even2_ref, odd2_ref, top_ref, bottom_ref,
    ratio_ref, inverse_ref, edge_ref, out_ref, mid_ref,
):
    got_top, got_bottom = swap_in(parity, even_ref[...], odd_ref[...])
    low, high = swap_in(parity, even2_ref[...], odd2_ref[...])
    solve_second(
        rows, groups, couple_ref[OV], couple_ref[OV + rows],
        first_ref[:groups, :], first_ref[(rows - 1) * groups :, :],
        got_top, got_bottom, top_ref[...], bottom_ref[...], low, high,
        ratio_ref, inverse_ref, edge_ref, first_ref, out_ref, mid_ref,
    )


def shared_levels(const, right_side, lon_coef, lat_coef, level_scale):
    rows, levels, lon_count = right_side.shape
    lon_size = lax.axis_size("lon")
    assert lon_size % levels == 0 and GROUPS % (lon_size // levels) == 0 and rows % (lon_size // levels) == 0
    sharers = lon_size // levels
    groups = 2 * GROUPS // sharers
    part_rows = rows // sharers
    digits = N1 // lon_size
    lon_at = lax.axis_index("lon")
    parity = (lax.axis_index("lat") % 2).astype(jnp.int32).reshape(1)
    lon_window, couple = operator_parts(rows, lon_coef, lat_coef, level_scale)
    lon_window = lax.dynamic_index_in_dim(lon_window, lon_at // sharers, 0, False)
    couple = lax.dynamic_index_in_dim(couple, lon_at // sharers, 0, False)
    eigen = lax.dynamic_slice_in_dim(
        const["eigen"], (lon_at % sharers) * (groups // 2), groups // 2, axis=1
    ).reshape(groups, N2)
    ratio, inverse, edge = factor(rows, groups, lon_window, couple, eigen)
    block = (rows * groups, N2)
    row = (groups, N2)
    send = right_side.reshape(sharers, part_rows, levels, lon_count).transpose(2, 0, 1, 3)
    send = send.reshape(lon_size, part_rows, digits, N2)
    got = lax.all_to_all(send, "lon", 0, 0, tiled=True)
    points = got.transpose(1, 0, 2, 3).reshape(part_rows, N1, N2)
    padded = pad_rows(part_rows)

    def transform(points_ref, first_ref, turn_ref, second_ref, special_ref, out_ref, full_ref, mid_ref):
        full_ref[:part_rows] = points_ref[...]
        if padded > part_rows:
            full_ref[part_rows:] = jnp.zeros((padded - part_rows, N1, N2), jnp.float32)
        forward_rows(full_ref, part_rows, first_ref, turn_ref, second_ref, special_ref, mid_ref, out_ref)

    (spectral,) = call(
        transform,
        [(part_rows * N1, N2)],
        [points, const["first"], const["turn"], const["second"], const["special"]],
        [VMEM] * 5,
        [vmem(padded, N1, N2), vmem(padded * N1, N2)],
        part_rows * NLON * 256 * 4,
        "transform",
    )
    spectral = to_coefs(spectral, sharers, part_rows, groups)

    def edges(parity_ref, spec_ref, edge_ref, top_ref, bottom_ref, even_ref, odd_ref):
        top, bottom = edge_sums(
            rows_of(spec_ref, groups), rows_of(spec_ref, groups, OV - rows),
            rows_of(edge_ref, groups, -7), rows_of(edge_ref, groups, -14),
        )
        top_ref[...] = top
        bottom_ref[...] = bottom
        swap_out(parity_ref[0], top, bottom, even_ref, odd_ref)

    sent_top, sent_bottom, even, odd = call(
        edges, [row] * 4, [parity, spectral, edge], [SMEM, VMEM, VMEM], [], groups * N2 * 32, "edges"
    )
    even, odd = swap(even, odd)

    def first(parity_ref, spec_ref, even_ref, odd_ref, ratio_ref, inverse_ref, edge_ref, out_ref, e_ref, o_ref):
        low, high = swap_in(parity_ref[0], even_ref[...], odd_ref[...])
        solve_first(
            rows, groups, rows_of(spec_ref, groups), low, high, ratio_ref, inverse_ref, edge_ref, out_ref
        )
        swap_out(parity_ref[0], out_ref[(rows - 1) * groups :, :], out_ref[:groups, :], e_ref, o_ref)

    iterate, even2, odd2 = call(
        first,
        [block, row, row],
        [parity, spectral, even, odd, ratio, inverse, edge],
        [SMEM] + [VMEM] * 6,
        [],
        rows * groups * N2 * 8,
        "first_solve",
    )
    even2, odd2 = swap(even2, odd2)

    def second(parity_ref, *refs):
        second_part(rows, groups, parity_ref[0], *refs)

    (iterate,) = call(
        second,
        [block],
        [parity, couple, iterate, even, odd, even2, odd2, sent_top, sent_bottom, ratio, inverse, edge],
        [SMEM, SMEM] + [VMEM] * 10,
        [vmem(*block)],
        rows * groups * N2 * 8,
        "second_solve",
    )
    iterate = to_rows(iterate, sharers, part_rows, groups)

    def back(spec_ref, first_ref, turn_ref, second_ref, special_ref, out_ref, mid_ref, full_ref):
        backward_rows(spec_ref, part_rows, first_ref, turn_ref, second_ref, special_ref, mid_ref, full_ref)
        out_ref[...] = full_ref[:part_rows]

    (points,) = call(
        back,
        [(part_rows, N1, N2)],
        [iterate, const["first_back"], const["turn"], const["second_back"], const["special_back"]],
        [VMEM] * 5,
        [vmem(padded * N1, N2), vmem(padded, N1, N2)],
        part_rows * NLON * 256 * 4,
        "back_transform",
    )
    send = points.reshape(part_rows, lon_size, digits, N2).transpose(1, 0, 2, 3)
    got = lax.all_to_all(send, "lon", 0, 0, tiled=True)
    got = got.reshape(levels, sharers, part_rows, lon_count).transpose(1, 2, 0, 3)
    return got.reshape(rows, levels, lon_count)


def level_groups(sharers):
    size = lax.axis_size("lon")
    return [[first + i for i in range(sharers)] for first in range(0, size, sharers)]


def to_coefs(spectral, sharers, part_rows, groups):
    send = spectral.reshape(part_rows, 2, sharers, groups // 2, N2).transpose(2, 0, 1, 3, 4)
    got = lax.all_to_all(
        send, "lon", 0, 0, tiled=True, axis_index_groups=level_groups(sharers)
    )
    return got.reshape(sharers * part_rows * groups, N2)


def to_rows(values, sharers, part_rows, groups):
    send = values.reshape(sharers, part_rows, 2, groups // 2, N2)
    got = lax.all_to_all(
        send, "lon", 0, 0, tiled=True, axis_index_groups=level_groups(sharers)
    )
    return got.transpose(1, 2, 0, 3, 4).reshape(part_rows * N1, N2)


def solution(mesh):
    return jax.shard_map(
        on_device,
        mesh=mesh,
        in_specs=(P("lat", None, "lon"), P(), P(), P()),
        out_specs=P("lat", None, "lon"),
        check_vma=False,
    )
```
